32 devices in a mesh: dp: 16 (over z, x, core), head: 2 (over y).
Axes of the slice: x: 2, y: 2, z: 4, core: 2. Of those that a mesh axis runs over, the one named last changes fastest.
Arguments:
- hidden: bfloat16 [32, 512, 768], P('dp'), may hold values from -6 to 6
- lengths: int32 [32, 4], P('dp'), may hold values from 1 to 256, 512 in all within a row
- padding: int32 [32, 512], P('dp'), may hold values 0 or 1
- bucket_line: int32 [32, 512, 512], P('dp'), may hold values from 0 to 31
- bucket_horizontal: int32 [32, 512, 512], P('dp'), may hold values from 0 to 63
- bucket_vertical: int32 [32, 512, 512], P('dp'), may hold values from 0 to 63
- attn_project: bfloat16 [3, 768, 768], P(None, None, 'head'), may hold values from -0.21875 to 0.21875
- attn_bias: bfloat16 [2, 768], P(None, 'head'), may hold values from -4 to 4
- table_line: bfloat16 [32, 12], P(None, 'head'), may hold values from -6 to 6
- table_horizontal: bfloat16 [64, 12], P(None, 'head'), may hold values from -6 to 6
- table_vertical: bfloat16 [64, 12], P(None, 'head'), may hold values from -6 to 6
- out_project: bfloat16 [768, 768], P('head'), may hold values from -0.875 to 0.875
- out_bias: bfloat16 [768], replicated, may hold values from -4 to 4
- attn_gain: bfloat16 [768], replicated, may hold values from 0.5 to 1.5
- attn_shift: bfloat16 [768], replicated, may hold values from -4 to 4
- hidden_project: bfloat16 [768, 3072], P(None, 'head'), may hold values from -0.21875 to 0.21875
- hidden_bias: bfloat16 [3072], P('head'), may hold values from -4 to 4
- down_project: bfloat16 [3072, 768], P('head'), may hold values from -0.21875 to 0.21875
- down_bias: bfloat16 [768], replicated, may hold values from -4 to 4
- final_gain: bfloat16 [768], replicated, may hold values from 0.5 to 1.5
- final_shift: bfloat16 [768], replicated, may hold values from -4 to 4
- cotangent: bfloat16 [32, 512, 768], P('dp', 'head'), may hold values from -6 to 6
Outputs:
- output: bfloat16 [32, 512, 768], P('dp', 'head')
- grad_hidden: float32 [32, 512, 768], P('dp', 'head')
- grad_attn_project: float32 [3, 768, 768], P(None, None, 'head')
- grad_attn_bias: float32 [2, 768], P(None, 'head')
- grad_table_line: float32 [32, 12], P(None, 'head')
- grad_table_horizontal: float32 [64, 12], P(None, 'head')
- grad_table_vertical: float32 [64, 12], P(None, 'head')
- grad_out_project: float32 [768, 768], P('head')
- grad_out_bias: float32 [768], replicated
- grad_attn_gain: float32 [768], replicated
- grad_attn_shift: float32 [768], replicated
- grad_hidden_project: float32 [768, 3072], P(None, 'head')
- grad_hidden_bias: float32 [3072], P('head')
- grad_down_project: float32 [3072, 768], P('head')
- grad_down_bias: float32 [768], replicated
- grad_final_gain: float32 [768], replicated
- grad_final_shift: float32 [768], replicated
The draws below stay inside these ranges and needn't reach their ends.
Inputs may be any that keep to these rules, and one draw needn't show every extreme that they name: The 4 lengths of a row sum to 512.
All inputs are finite; a program needn't handle non-finite values. No bound on the sum of `padding` on one device may be relied on, other than what follows from the above.
Results may differ from the reference program's by a relative error of at most 0.013.
The reference program's roundings to bfloat16 on the way count: a program that leaves them out, or rounds other values in their place, can miss the bound.
Values may be sent and summed in bfloat16 or wider, within the bound.
No kernel may reach another device: no remote copies, remote signals or barrier semaphores. Data moves between devices by JAX's collectives and lax.ppermute only.
A program may use at most 192 MiB of HBM per device.

```python
import math
import jax
import jax.numpy as jnp
import numpy as np
from jax import lax

D = 768
FF = 3072
HEADS = 12
HEAD_DIM = 64
LINE_BINS = 32
PLANE_BINS = 64
SLOTS = 512
DOCS = 4
ROWS = 32
MOST_DOC = 256


def touch_ends(entries, rng, least, largest):
    shape = entries.shape
    index_at = [jax.random.randint(jax.random.fold_in(rng, axis), (), 0, shape[axis]) for axis in range(len(shape))]
    entries = entries.at[tuple(index_at)].set(least)
    longest = shape.index(max(shape))
    index_at[longest] = (index_at[longest] + 1) % shape[longest]
    return entries.at[tuple(index_at)].set(largest)


def block_levels(own_key, dims, shards, low, top_value):
    loudness, own = 1.0, jax.random.fold_in(own_key, 6)
    for dim, blocks in shards:
        draws = jnp.exp(jax.random.uniform(jax.random.fold_in(own, dim), (blocks,), jnp.float32, low / len(shards), top_value / len(shards)))
        loudness = loudness * jnp.repeat(draws, dims[dim] // blocks).reshape([-1 if axis == dim else 1 for axis in range(len(dims))])
    return loudness


def length_profile(number_of, total, most, slope):
    weights = [(1 << 20) // math.isqrt(standing ** slope) + 1 for standing in range(2, number_of + 1)]
    spare, given = total - most - (number_of - 1), [1] * (number_of - 1)
    while spare > 0:
        movable = [i for i in range(number_of - 1) if given[i] < most]
        whole, remaining = sum([weights[i] for i in movable]), spare
        for i in movable:
            addition = min(most - given[i], max(1, remaining * weights[i] // whole), spare)
            given[i] = given[i] + addition
            spare = spare - addition
    return np.array([most] + given)


def uneven(stream_key, count, total, bound, lean):
    if count == 2:
        one = jax.random.randint(stream_key, (), max(1, total - bound), min(bound, total - 1) + 1)
        return jnp.stack([one, total - one])
    sizes = jnp.asarray(length_profile(count, total, bound, lean), jnp.int32)
    twos = (count - 1) // 2
    source_of, receiver = sizes[1:1 + 2 * twos:2], sizes[2:2 + 2 * twos:2]
    slack = jnp.minimum(source_of - 1, bound - receiver)
    passed = jax.random.randint(jax.random.fold_in(stream_key, 1), (twos,), 0, 1 << 20) % (slack + 1)
    sizes = sizes.at[1:1 + 2 * twos:2].set(source_of - passed).at[2:2 + 2 * twos:2].set(receiver + passed)
    return sizes[jax.random.permutation(jax.random.fold_in(stream_key, 2), count)]


def scatter_about(stream_key, extent, width, bound, shards=(), kind=jnp.bfloat16):
    level = block_levels(stream_key, extent, shards, -0.22, 0.18) if shards else 1.0
    values = jax.random.normal(stream_key, extent, jnp.float32) * width * level
    return jnp.minimum(jnp.maximum(values, -bound), bound).astype(kind)


def setup_inputs(seed: int = 0) -> dict:
    key_list = jax.random.split(jax.random.key(seed), 23)
    return {
        "hidden": scatter_about(key_list[0], (ROWS, SLOTS, D), 1.0, 6.0, ((0, 16),)),
        "lengths": jax.vmap(lambda own: uneven(own, DOCS, SLOTS, MOST_DOC, 2))(jax.random.split(key_list[1], ROWS)).reshape((ROWS, DOCS)).astype(jnp.int32),
        "padding": touch_ends((jax.random.randint(key_list[2], (ROWS, SLOTS), 0, 8) < 7).astype(jnp.int32), jax.random.fold_in(key_list[2], 1), 0, 1),
        "bucket_line": touch_ends(jax.random.randint(key_list[3], (ROWS, SLOTS, SLOTS), 0, LINE_BINS), jax.random.fold_in(key_list[3], 1), 0, LINE_BINS - 1).astype(jnp.int32),
        "bucket_horizontal": touch_ends(jax.random.randint(key_list[4], (ROWS, SLOTS, SLOTS), 0, PLANE_BINS), jax.random.fold_in(key_list[4], 1), 0, PLANE_BINS - 1).astype(jnp.int32),
        "bucket_vertical": touch_ends(jax.random.randint(key_list[5], (ROWS, SLOTS, SLOTS), 0, PLANE_BINS), jax.random.fold_in(key_list[5], 1), 0, PLANE_BINS - 1).astype(jnp.int32),
        "attn_project": scatter_about(key_list[6], (3, D, D), D ** -0.5, 0.21875, ((2, 2),)),
        "attn_bias": scatter_about(key_list[7], (2, D), 0.3, 4.0, ((1, 2),)),
        "table_line": scatter_about(key_list[8], (LINE_BINS, HEADS), 0.5, 6.0, ((1, 2),)),
        "table_horizontal": scatter_about(key_list[9], (PLANE_BINS, HEADS), 0.5, 6.0, ((1, 2),)),
        "table_vertical": scatter_about(key_list[10], (PLANE_BINS, HEADS), 0.5, 6.0, ((1, 2),)),
        "out_project": scatter_about(key_list[11], (D, D), (D // 16) ** -0.5, 0.875, ((0, 2),)),
        "out_bias": scatter_about(key_list[12], (D,), 0.3, 4.0),
        "attn_gain": jnp.clip(1.0 + 0.1 * jax.random.normal(key_list[13], (D,), jnp.float32), 0.5, 1.5).astype(jnp.bfloat16),
        "attn_shift": scatter_about(key_list[14], (D,), 0.3, 4.0),
        "hidden_project": scatter_about(key_list[15], (D, FF), D ** -0.5, 0.21875, ((1, 2),)),
        "hidden_bias": scatter_about(key_list[16], (FF,), 0.3, 4.0, ((0, 2),)),
        "down_project": scatter_about(key_list[17], (FF, D), (FF // 4) ** -0.5, 0.21875, ((0, 2),)),
        "down_bias": scatter_about(key_list[18], (D,), 0.3, 4.0),
        "final_gain": jnp.clip(1.0 + 0.1 * jax.random.normal(key_list[19], (D,), jnp.float32), 0.5, 1.5).astype(jnp.bfloat16),
        "final_shift": scatter_about(key_list[20], (D,), 0.3, 4.0),
        "cotangent": scatter_about(key_list[21], (ROWS, SLOTS, D), 1.0, 6.0, ((0, 16), (1, 2))),
    }


@jax.custom_vjp
def low(v):
    return lax.optimization_barrier(v.astype(jnp.bfloat16)).astype(jnp.float32)

@jax.custom_vjp
def low_back(v):
    return v

def low_keep(v):
    return (low(v), None)

def low_pass(kept, grad):
    return (grad,)

def back_keep(v):
    return (v, None)

def back_low(kept, grad):
    return (low(grad),)
low.defvjp(low_keep, low_pass)
low_back.defvjp(back_keep, back_low)

def matmul(left, right):
    return jnp.dot(left, right, precision=lax.Precision.HIGHEST, preferred_element_type=jnp.float32)

def norm_rows(values, gain, shift):
    mean = lax.optimization_barrier(jnp.mean(values, axis=-1, keepdims=True))
    centered = values - mean
    variance = lax.optimization_barrier(jnp.mean(centered * centered, axis=-1, keepdims=True))
    return centered * lax.rsqrt(variance + 1e-12) * gain + shift

def relative(bucket, table, bins):
    selector = (bucket[:, :, None] == jnp.arange(bins, dtype=jnp.int32)[None, None, :]).astype(jnp.float32)
    return jnp.einsum('ijb,bh->hij', selector, table, precision=lax.Precision.HIGHEST)

def row_forward(params, inputs):
    attn_project, attn_bias, table_line, table_horizontal, table_vertical, out_project, out_bias, attn_gain, attn_shift, hidden_project, hidden_bias, down_project, down_bias, final_gain, final_shift = params
    tokens, allowed, bucket_line, bucket_horizontal, bucket_vertical = inputs
    query = low(low_back(matmul(tokens, attn_project[0]) + attn_bias[0]))
    key = low(low_back(matmul(tokens, attn_project[1])))
    value = low(low_back(matmul(tokens, attn_project[2]) + attn_bias[1]))
    query_heads = query.reshape(SLOTS, HEADS, HEAD_DIM)
    key_heads = key.reshape(SLOTS, HEADS, HEAD_DIM)
    value_heads = value.reshape(SLOTS, HEADS, HEAD_DIM)
    raw = jnp.einsum('ihd,jhd->hij', query_heads, key_heads, precision=lax.Precision.HIGHEST) * (1.0 / math.sqrt(HEAD_DIM))
    rel = relative(bucket_line, table_line, LINE_BINS) + relative(bucket_horizontal, table_horizontal, PLANE_BINS) + relative(bucket_vertical, table_vertical, PLANE_BINS)
    scores = low_back(raw + rel)
    scores = jnp.where(allowed[None], scores, -1000000000.0)
    probs = low(jax.nn.softmax(scores, axis=-1))
    context = jnp.einsum('hij,jhd->ihd', probs, value_heads, precision=lax.Precision.HIGHEST).reshape(SLOTS, D)
    context = low(low_back(context))
    pre_attn = tokens + (low_back(matmul(context, out_project)) + out_bias)
    mid = norm_rows(pre_attn, attn_gain, attn_shift)
    inner = low_back(matmul(low(mid), hidden_project) + hidden_bias)
    active = low(jax.nn.gelu(inner, approximate=False))
    pre_final = mid + (low_back(matmul(active, down_project)) + down_bias)
    return norm_rows(pre_final, final_gain, final_shift)

def reference(hidden, lengths, padding, bucket_line, bucket_horizontal, bucket_vertical, attn_project, attn_bias, table_line, table_horizontal, table_vertical, out_project, out_bias, attn_gain, attn_shift, hidden_project, hidden_bias, down_project, down_bias, final_gain, final_shift, cotangent):
    bounds = jnp.cumsum(lengths, axis=1)
    place = jnp.arange(SLOTS, dtype=jnp.int32)
    segment = lax.optimization_barrier(jnp.sum((place[None, :, None] >= bounds[:, None, :]).astype(jnp.int32), axis=-1))
    diagonal = place[:, None] == place[None, :]
    allowed = (segment[:, :, None] == segment[:, None, :]) & ((padding[:, None, :] > 0) | diagonal[None])
    params = tuple((weight.astype(jnp.float32) for weight in (attn_project, attn_bias, table_line, table_horizontal, table_vertical, out_project, out_bias, attn_gain, attn_shift, hidden_project, hidden_bias, down_project, down_bias, final_gain, final_shift)))

    def forward(weights, tokens_all):

        def step(carry, inputs):
            return (carry, jax.checkpoint(row_forward)(weights, inputs))
        start = jnp.zeros((), jnp.float32)
        return lax.scan(step, start, (tokens_all, allowed, bucket_line, bucket_horizontal, bucket_vertical))[1]
    result, pullback = jax.vjp(forward, params, hidden.astype(jnp.float32))
    grads, grad_hidden = pullback(cotangent.astype(jnp.float32))
    return (result.astype(jnp.bfloat16), grad_hidden, grads[0], grads[1], grads[2], grads[3], grads[4], grads[5], grads[6], grads[7], grads[8], grads[9], grads[10], grads[11], grads[12], grads[13], grads[14])
```

```python
import functools
import math

import jax
import jax.numpy as jnp
from jax import lax
from jax.experimental import pallas as pl
from jax.experimental.pallas import tpu as pltpu
from jax.sharding import PartitionSpec as P

B = 128

ROWS_PICK = lax.GatherDimensionNumbers(
    offset_dims=(), collapsed_slice_dims=(0,), start_index_map=(0,),
    operand_batching_dims=(1,), start_indices_batching_dims=(1,))
PACK = 16

def pick(table, index):
    return lax.gather(table, index[:, :, None], ROWS_PICK, (1, 1),
                      mode=lax.GatherScatterMode.PROMISE_IN_BOUNDS)

def lookup(tab_ref, h, at, place, masks):
    found = pick(tab_ref[h, at:at + PACK, :], place)
    for step, mask in enumerate(masks):
        low = at + PACK * (step + 1)
        found = jnp.where(mask, pick(tab_ref[h, low:low + PACK, :], place), found)
    return found.astype(jnp.float32)

def doc_span(len_ref, row, first, last):
    edge = 0
    start = 0
    stop = 0
    for k in range(len_ref.shape[1]):
        begin = edge
        edge = edge + len_ref[row, k]
        start = jnp.where(begin <= first, begin, start)
        stop = jnp.where(begin <= last, edge, stop)
    return start // B, (stop + (B - 1)) // B

def fwd_kernel(row, len_ref, q_ref, k_ref, v_ref, pad_ref, bl_ref, bh_ref, bv_ref, tab_ref,
               probs_ref, ctx_ref, kst, vst, sc):
    qb = pl.program_id(0)
    pairs = kst.shape[0]
    heads = 2 * pairs
    tiles = kst.shape[1]
    lane = lax.broadcasted_iota(jnp.int32, (B, B), 1)
    left = lane < (B // 2)

    @pl.when(qb == 0)
    def _():
        for p in range(pairs):
            for t in range(tiles):
                kt = k_ref[t * B:(t + 1) * B, p * B:(p + 1) * B]
                vt = v_ref[t * B:(t + 1) * B, p * B:(p + 1) * B]
                zero = jnp.zeros_like(kt)
                kst[p, t, 0:B, :] = jnp.where(left, kt, zero)
                kst[p, t, B:2 * B, :] = jnp.where(left, zero, kt)
                vst[p, t, 0:B, :] = jnp.where(left, vt, zero)
                vst[p, t, B:2 * B, :] = jnp.where(left, zero, vt)

    first = qb * B
    low, high = doc_span(len_ref, row, first, first + B - 1)
    sub = lax.broadcasted_iota(jnp.int32, (B, B), 0) + first
    count = len_ref.shape[1]
    edges = []
    edge = 0
    for k in range(count):
        edge = edge + len_ref[row, k]
        edges.append(edge)
    seg_q = sum(((sub >= e).astype(jnp.int32) for e in edges))

    def scores(t, top):
        key_at = lane + t * B
        seg_k = sum(((key_at >= e).astype(jnp.int32) for e in edges))
        real = jnp.broadcast_to(pad_ref[:, pl.ds(pl.multiple_of(t * B, B), B)], (B, B)) > 0
        allowed = ((seg_q == seg_k) & real) | (sub == key_at)
        at = pl.ds(pl.multiple_of(t * B, B), B)
        parts = []
        for g in range(B // PACK):
            rows = slice(g * PACK, g * PACK + PACK)
            group = []
            for ref, tiles_of in ((bl_ref, 2), (bh_ref, 4), (bv_ref, 4)):
                index = ref[rows, at].astype(jnp.int16)
                group.append((index & jnp.int16(PACK - 1),
                              [index >= jnp.int16(PACK * a) for a in range(1, tiles_of)]))
            parts.append(group)
        out = []
        for p in range(pairs):
            raw = lax.dot_general(q_ref[:, p * B:(p + 1) * B], kst[p, t], (((1,), (1,)), ((), ())),
                                  preferred_element_type=jnp.float32)
            for s in range(2):
                h = 2 * p + s
                rel = jnp.concatenate(
                    [(lookup(tab_ref, h, 0, *group[0]) + lookup(tab_ref, h, 32, *group[1]))
                     + lookup(tab_ref, h, 96, *group[2]) for group in parts], axis=0)
                val = jnp.where(allowed, raw[:, s * B:(s + 1) * B] + rel, -1000000000.0)
                sc[t, h] = val
                out.append(jnp.maximum(top[h], val))
        return tuple(out)

    start = jnp.full((B, B), -3.0e38, jnp.float32)
    top = lax.fori_loop(low, high, scores, tuple(start for _ in range(heads)))
    top = [jnp.max(x, axis=-1, keepdims=True) for x in top]

    def expo(t, tot):
        out = []
        for h in range(heads):
            e = jnp.exp(sc[t, h] - top[h])
            sc[t, h] = e
            out.append(tot[h] + e)
        return tuple(out)

    zero = jnp.zeros((B, B), jnp.float32)
    tot = lax.fori_loop(low, high, expo, tuple(zero for _ in range(heads)))
    inv = [1.0 / jnp.sum(x, axis=-1, keepdims=True) for x in tot]

    def mix(t, acc):
        out = []
        for p in range(pairs):
            low_pair = []
            for s in range(2):
                h = 2 * p + s
                pr = sc[t, h] * inv[h]
                probs_ref[t, h] = pr
                low_pair.append(pr.astype(jnp.bfloat16))
            out.append(acc[p] + jnp.dot(jnp.concatenate(low_pair, axis=1), vst[p, t],
                                        preferred_element_type=jnp.float32))
        return tuple(out)

    acc = lax.fori_loop(low, high, mix, tuple(zero for _ in range(pairs)))
    for p in range(pairs):
        ctx_ref[:, p * B:(p + 1) * B] = acc[p].astype(jnp.bfloat16)

def attn_fwd(row, lengths, q, k, v, pad, bl, bh, bv, tab):
    slots, width = q.shape[1:]
    pairs = width // B
    tiles = slots // B
    row_block = lambda n: pl.BlockSpec((None, B, n), lambda i, L: (row, i, 0))
    return pl.pallas_call(
        functools.partial(fwd_kernel, row),
        grid_spec=pltpu.PrefetchScalarGridSpec(
            num_scalar_prefetch=1, grid=(tiles,),
            in_specs=[
                row_block(width),
                pl.BlockSpec((None, slots, width), lambda i, L: (row, 0, 0)),
                pl.BlockSpec((None, slots, width), lambda i, L: (row, 0, 0)),
                pl.BlockSpec((None, 1, slots), lambda i, L: (row, 0, 0)),
                row_block(slots), row_block(slots), row_block(slots),
                pl.BlockSpec(tab.shape, lambda i, L: (0, 0, 0)),
            ],
            out_specs=[
                pl.BlockSpec((None, tiles, 2 * pairs, B, B), lambda i, L: (i, 0, 0, 0, 0)),
                pl.BlockSpec((B, width), lambda i, L: (i, 0)),
            ],
            scratch_shapes=[
                pltpu.VMEM((pairs, tiles, 2 * B, B), jnp.bfloat16),
                pltpu.VMEM((pairs, tiles, 2 * B, B), jnp.bfloat16),
                pltpu.VMEM((tiles, 2 * pairs, B, B), jnp.float32),
            ]),
        out_shape=[
            jax.ShapeDtypeStruct((tiles, tiles, 2 * pairs, B, B), jnp.float32),
            jax.ShapeDtypeStruct((slots, width), jnp.bfloat16),
        ],
        compiler_params=pltpu.CompilerParams(vmem_limit_bytes=48 << 20),
        cost_estimate=pl.CostEstimate(
            flops=4 * slots * slots * width * 8, transcendentals=0, bytes_accessed=16 << 20),
        name="attn_forward",
    )(lengths, q, k, v, pad, bl, bh, bv, tab)


NT = (((1,), (1,)), ((), ()))
TN = (((0,), (0,)), ((), ()))

def bwd_kernel(row, factor, len_ref, q_ref, k_ref, v_ref, gctx_ref, ctx_ref, probs_ref,
               ds_ref, dq_ref, dk_ref, dv_ref, kst, vst, dkst, dvst):
    qb = pl.program_id(0)
    pairs, tiles = kst.shape[0], kst.shape[1]
    lane = lax.broadcasted_iota(jnp.int32, (B, B), 1)
    left = lane < (B // 2)

    @pl.when(qb == 0)
    def _():
        dkst[...] = jnp.zeros_like(dkst)
        dvst[...] = jnp.zeros_like(dvst)
        for p in range(pairs):
            for t in range(tiles):
                kt = k_ref[t * B:(t + 1) * B, p * B:(p + 1) * B]
                vt = v_ref[t * B:(t + 1) * B, p * B:(p + 1) * B]
                zero = jnp.zeros_like(kt)
                kst[p, t, 0:B, :] = jnp.where(left, kt, zero)
                kst[p, t, B:2 * B, :] = jnp.where(left, zero, kt)
                vst[p, t, 0:B, :] = jnp.where(left, vt, zero)
                vst[p, t, B:2 * B, :] = jnp.where(left, zero, vt)

    first = qb * B
    low, high = doc_span(len_ref, row, first, first + B - 1)
    for p in range(pairs):
        cols = slice(p * B, (p + 1) * B)
        gctx = gctx_ref[:, cols]
        q = q_ref[:, cols]
        prod = gctx.astype(jnp.float32) * ctx_ref[:, cols].astype(jnp.float32)
        zero = jnp.zeros_like(prod)
        inner = [jnp.sum(jnp.where(left, prod, zero), axis=-1, keepdims=True),
                 jnp.sum(jnp.where(left, zero, prod), axis=-1, keepdims=True)]

        def tile(t, dq, p=p, gctx=gctx, q=q, inner=inner):
            gp = lax.dot_general(gctx, vst[p, t], NT, preferred_element_type=jnp.float32)
            probs_low, g_scores = [], []
            for s in range(2):
                pr = probs_ref[t, 2 * p + s]
                ds = (pr * (gp[:, s * B:(s + 1) * B] - inner[s])).astype(jnp.bfloat16)
                ds_ref[t, 2 * p + s] = ds
                g_scores.append(ds)
                probs_low.append(pr.astype(jnp.bfloat16))
            ds = jnp.concatenate(g_scores, axis=1)
            pl_ = jnp.concatenate(probs_low, axis=1)
            dkst[p, t] += lax.dot_general(ds, q, TN, preferred_element_type=jnp.float32)
            dvst[p, t] += lax.dot_general(pl_, gctx, TN, preferred_element_type=jnp.float32)
            return dq + jnp.dot(ds, kst[p, t], preferred_element_type=jnp.float32)

        dq = lax.fori_loop(low, high, tile, jnp.zeros((B, B), jnp.float32))
        dq_ref[:, cols] = (dq * factor).astype(jnp.bfloat16)

    @pl.when(qb == tiles - 1)
    def _():
        for p in range(pairs):
            for t in range(tiles):
                dk_ref[t * B:(t + 1) * B, p * B:(p + 1) * B] = jnp.where(
                    left, dkst[p, t, 0:B, :], dkst[p, t, B:2 * B, :]).astype(jnp.bfloat16)
                dv_ref[t * B:(t + 1) * B, p * B:(p + 1) * B] = jnp.where(
                    left, dvst[p, t, 0:B, :], dvst[p, t, B:2 * B, :]).astype(jnp.bfloat16)

def attn_bwd(row, factor, lengths, q, k, v, gctx, ctx, probs):
    slots, width = q.shape[1:]
    pairs, tiles = width // B, slots // B
    part = pl.BlockSpec((B, width), lambda i, L: (i, 0))
    full = pl.BlockSpec((slots, width), lambda i, L: (0, 0))
    mine = pl.BlockSpec((None, B, width), lambda i, L: (row, i, 0))
    whole = pl.BlockSpec((None, slots, width), lambda i, L: (row, 0, 0))
    pairs_of = pl.BlockSpec((None, tiles, 2 * pairs, B, B), lambda i, L: (i, 0, 0, 0, 0))
    flat = jax.ShapeDtypeStruct((slots, width), jnp.bfloat16)
    return pl.pallas_call(
        functools.partial(bwd_kernel, row, factor),
        grid_spec=pltpu.PrefetchScalarGridSpec(
            num_scalar_prefetch=1, grid=(tiles,),
            in_specs=[mine, whole, whole, part, part, pairs_of],
            out_specs=[pairs_of, part, full, full],
            scratch_shapes=[
                pltpu.VMEM((pairs, tiles, 2 * B, B), jnp.bfloat16),
                pltpu.VMEM((pairs, tiles, 2 * B, B), jnp.bfloat16),
                pltpu.VMEM((pairs, tiles, 2 * B, B), jnp.float32),
                pltpu.VMEM((pairs, tiles, 2 * B, B), jnp.float32),
            ]),
        out_shape=[jax.ShapeDtypeStruct(probs.shape, jnp.bfloat16), flat, flat, flat],
        compiler_params=pltpu.CompilerParams(vmem_limit_bytes=48 << 20),
        cost_estimate=pl.CostEstimate(
            flops=8 * slots * slots * width * 8, transcendentals=0, bytes_accessed=16 << 20),
        name="attn_backward",
    )(lengths, q, k, v, gctx, ctx, probs)

BINS = 160

def hist_kernel(row, len_ref, bl_ref, bh_ref, bv_ref, ds_ref, out_ref, spread, weights, hot, acc):
    qb = pl.program_id(0)
    tiles, heads = ds_ref.shape[0], ds_ref.shape[1]
    first = qb * B
    low, high = doc_span(len_ref, row, first, first + B - 1)

    @pl.when(qb == 0)
    def _():
        acc[...] = jnp.zeros_like(acc)
        spread[...] = jnp.zeros_like(spread)

    lane_row = lax.broadcasted_iota(jnp.int32, (BINS, B), 1) // 8

    def window(w, carry):
        t0 = low + 2 * w

        def group(g, carry):
            rows = pl.ds(pl.multiple_of(g * PACK, PACK), PACK)
            for part in range(2):
                t = jnp.minimum(t0 + part, tiles - 1)
                live = t0 + part < high
                for h in range(heads):
                    val = ds_ref[t, h, rows, :].astype(jnp.float32)
                    spread[part, pl.ds(h, PACK, stride=8), :] = jnp.where(live, val, 0.0)
            weights[:, 0:B] = spread[0].astype(jnp.bfloat16)
            weights[:, B:2 * B] = spread[1].astype(jnp.bfloat16)
            idx = []
            for ref in (bl_ref, bh_ref, bv_ref):
                pieces = []
                for part in range(2):
                    t = jnp.minimum(t0 + part, tiles - 1)
                    pieces.append(ref[rows, pl.ds(pl.multiple_of(t * B, B), B)])
                idx.append(jnp.concatenate(pieces, axis=1))
            for half in range(2):
                for i in range(8):
                    r = half * 8 + i
                    at = i * BINS
                    for ix, n in zip(idx, (32, 64, 64)):
                        bins = lax.broadcasted_iota(jnp.int16, (n, 2 * B), 0)
                        line = jnp.broadcast_to(ix[r:r + 1, :], (n, 2 * B)).astype(jnp.int16)
                        hot[at:at + n, :] = jnp.where(bins == line, jnp.ones((), jnp.bfloat16),
                                                      jnp.zeros((), jnp.bfloat16))
                        at += n
                res = lax.dot_general(hot[...], weights[...], NT, preferred_element_type=jnp.float32)
                tot = acc[...]
                for i in range(8):
                    tot = tot + jnp.where(lane_row == half * 8 + i, res[i * BINS:(i + 1) * BINS, :], 0.0)
                acc[...] = tot
            return carry

        return lax.fori_loop(0, B // PACK, group, carry)

    lax.fori_loop(0, (high - low + 1) // 2, window, 0)

    @pl.when(qb == pl.num_programs(0) - 1)
    def _():
        out_ref[...] = acc[...]

def table_grads(row, lengths, bl, bh, bv, ds):
    slots = bl.shape[1]
    tiles, heads = ds.shape[0], ds.shape[2]
    block = pl.BlockSpec((None, B, slots), lambda i, L: (row, i, 0))
    return pl.pallas_call(
        functools.partial(hist_kernel, row),
        grid_spec=pltpu.PrefetchScalarGridSpec(
            num_scalar_prefetch=1, grid=(tiles,),
            in_specs=[block, block, block,
                      pl.BlockSpec((None, tiles, heads, B, B), lambda i, L: (i, 0, 0, 0, 0))],
            out_specs=pl.BlockSpec((BINS, B), lambda i, L: (0, 0)),
            scratch_shapes=[
                pltpu.VMEM((2, 8 * PACK, B), jnp.float32),
                pltpu.VMEM((8 * PACK, 2 * B), jnp.bfloat16),
                pltpu.VMEM((8 * BINS, 2 * B), jnp.bfloat16),
                pltpu.VMEM((BINS, B), jnp.float32),
            ]),
        out_shape=jax.ShapeDtypeStruct((BINS, B), jnp.float32),
        compiler_params=pltpu.CompilerParams(vmem_limit_bytes=48 << 20),
        cost_estimate=pl.CostEstimate(
            flops=16 * slots * slots * 384 * 8, transcendentals=0, bytes_accessed=16 << 20),
        name="table_grads",
    )(lengths, bl, bh, bv, ds)


def normalize(values):
    mean = jnp.mean(values, axis=-1, keepdims=True)
    centered = values - mean
    scale = lax.rsqrt(jnp.mean(centered * centered, axis=-1, keepdims=True) + 1e-12)
    return centered * scale, scale


def normalize_back(grad, normed, scale, gain):
    scaled = grad * gain
    first = jnp.mean(scaled, axis=-1, keepdims=True)
    second = jnp.mean(scaled * normed, axis=-1, keepdims=True)
    return scale * (scaled - first - normed * second)


def times(left, right, dims):
    return lax.dot_general(left, right, (dims, ((), ())), preferred_element_type=jnp.float32)


def flips(count, bit):
    return [(i, i ^ (1 << bit)) for i in range(count)]


def sum_all(values, count):
    for bit in range(count.bit_length() - 1):
        values = values + lax.ppermute(values, "dp", flips(count, bit))
    return values


def scatter_sum(values, count):
    index = lax.axis_index("dp")
    for bit in range(count.bit_length() - 1):
        half = values.shape[0] // 2
        mine = (index >> bit) & 1
        send = lax.dynamic_slice_in_dim(values, (1 - mine) * half, half, 0)
        keep = lax.dynamic_slice_in_dim(values, mine * half, half, 0)
        got = lax.ppermute(send, "dp", flips(count, bit))
        values = (keep.astype(jnp.float32) + got.astype(jnp.float32)).astype(jnp.bfloat16)
    return values


def gather_parts(values, count):
    index = lax.axis_index("dp")
    for bit in reversed(range(count.bit_length() - 1)):
        got = lax.ppermute(values, "dp", flips(count, bit))
        mine = ((index >> bit) & 1) == jnp.arange(2, dtype=jnp.int32)
        both = jnp.where(mine[:, None, None], values[None], got[None])
        values = both.reshape((2 * values.shape[0],) + values.shape[1:])
    return values.astype(jnp.float32)


def reduce_rows(values, count):
    return gather_parts(scatter_sum(values.astype(jnp.bfloat16), count), count)


def body(
    count,
    hidden,
    lengths,
    padding,
    bucket_line,
    bucket_horizontal,
    bucket_vertical,
    attn_project,
    attn_bias,
    table_line,
    table_horizontal,
    table_vertical,
    out_project,
    out_bias,
    attn_gain,
    attn_shift,
    hidden_project,
    hidden_bias,
    down_project,
    down_bias,
    final_gain,
    final_shift,
    cotangent,
):
    f32, low = jnp.float32, jnp.bfloat16
    rows, slots, width = hidden.shape
    half = cotangent.shape[1]
    heads = table_line.shape[1]
    local = attn_project.shape[2]
    factor = 1.0 / math.sqrt(local // heads)
    head = lax.axis_index("head")
    offset = head * half
    swap = [(0, 1), (1, 0)]

    def exchange(part):
        part = part.astype(low)
        return part.astype(f32) + lax.ppermute(part, "head", swap).astype(f32)

    other = lax.ppermute(cotangent, "head", swap)
    is_mine = (head == jnp.arange(2, dtype=jnp.int32))[None, :, None, None]
    incoming = jnp.where(is_mine, cotangent[:, None], other[:, None]).reshape(rows, slots, width)

    tables = jnp.concatenate([table_line, table_horizontal, table_vertical], axis=0)
    tables = jnp.broadcast_to(tables.T[:, :, None], (heads, tables.shape[0], B))
    pad = padding[:, None, :]

    flat = hidden.reshape(rows * slots, width)
    project = lax.dot_general(flat, attn_project, (((1,), (1,)), ((), ())), preferred_element_type=f32)
    query = ((project[:, 0] + attn_bias[0].astype(f32)).astype(low) * jnp.asarray(factor, low))
    key = project[:, 1].astype(low)
    value = (project[:, 2] + attn_bias[1].astype(f32)).astype(low)
    query, key, value = (x.reshape(rows, slots, local) for x in (query, key, value))

    gain_first = attn_gain.astype(f32)
    shift_first = attn_shift.astype(f32)
    gain_last = final_gain.astype(f32)
    shift_last = final_shift.astype(f32)
    down_bias = down_bias.astype(f32)
    out_bias = out_bias.astype(f32)
    hidden_bias = hidden_bias.astype(f32)

    outputs, grads_in, tail = [], [], []
    sums = {}
    weights = {}

    def add(store, name, term):
        store[name] = term if name not in store else store[name] + term

    fronts = []
    for r in range(rows):
        probs, context = attn_fwd(r, lengths, query, key, value, pad, bucket_line,
                                  bucket_horizontal, bucket_vertical, tables)
        fronts.append((probs, context))
    mids = []
    for r in range(rows):
        probs, context = fronts[r]
        pre = hidden[r].astype(f32) + exchange(times(context, out_project, ((1,), (0,)))) + out_bias
        normed, scale = normalize(pre)
        mid = normed * gain_first + shift_first
        mid_low = mid.astype(low)
        inner = times(mid_low, hidden_project, ((1,), (0,))) + hidden_bias
        bell = 0.5 * (1.0 + lax.erf(inner * math.sqrt(0.5)))
        active = (inner * bell).astype(low)
        slope = bell + inner * (jnp.exp(-0.5 * inner * inner) * (1.0 / math.sqrt(2.0 * math.pi)))
        pre = mid + exchange(times(active, down_project, ((1,), (0,)))) + down_bias
        mids.append((normed, scale, mid_low, active, slope, pre))
    backs = []
    for r in range(rows):
        normed, scale, mid_low, active, slope, pre = mids[r]
        normed_final, scale_final = normalize(pre)
        result = (normed_final * gain_last + shift_last).astype(low)
        outputs.append(lax.dynamic_slice_in_dim(result, offset, half, 0))
        above = incoming[r].astype(f32)
        add(sums, "final_gain", jnp.sum(above * normed_final, axis=0))
        add(sums, "final_shift", jnp.sum(above, axis=0))
        g_final = normalize_back(above, normed_final, scale_final, gain_last)
        add(sums, "down_bias", jnp.sum(g_final, axis=0))
        g_low = g_final.astype(low)
        add(weights, "down", times(active, g_low, ((0,), (0,))))
        g_inner = (times(g_low, down_project, ((1,), (1,))) * slope).astype(low)
        g_mid = g_final + exchange(times(g_inner, hidden_project, ((1,), (1,))))
        add(sums, "hidden_bias", jnp.sum(g_inner.astype(f32), axis=0))
        add(weights, "hidden", times(mid_low, g_inner, ((0,), (0,))))
        backs.append(g_mid)
    marks = []
    for r in range(rows):
        normed, scale = mids[r][:2]
        probs, context = fronts[r]
        g_mid = backs[r]
        add(sums, "attn_gain", jnp.sum(g_mid * normed, axis=0))
        add(sums, "attn_shift", jnp.sum(g_mid, axis=0))
        g_attn = normalize_back(g_mid, normed, scale, gain_first)
        add(sums, "out_bias", jnp.sum(g_attn, axis=0))
        g_low = g_attn.astype(low)
        add(weights, "out", times(context, g_low, ((0,), (0,))))
        g_context = times(g_low, out_project, ((1,), (1,))).astype(low)
        g_scores, *g_three = attn_bwd(r, factor, lengths, query, key, value, g_context, context, probs)
        marks.append(g_scores)
        add(sums, "query_bias", jnp.sum(g_three[0].astype(f32), axis=0))
        add(sums, "value_bias", jnp.sum(g_three[2].astype(f32), axis=0))
        add(weights, "attn", jnp.stack([times(hidden[r], g, ((0,), (0,))) for g in g_three]))
        part = sum(times(g, attn_project[c], ((1,), (1,))) for c, g in enumerate(g_three))
        send = lax.dynamic_slice_in_dim(part, half - offset, half, 0).astype(low)
        mine = lax.dynamic_slice_in_dim(part + g_attn, offset, half, 0)
        grads_in.append(mine + lax.ppermute(send, "head", swap).astype(f32))
    for r in range(rows):
        add(sums, "tables", table_grads(r, lengths, bucket_line, bucket_horizontal,
                                        bucket_vertical, marks[r]))

    grad_down = reduce_rows(weights["down"], count)
    grad_hidden_project = reduce_rows(weights["hidden"], count)
    grad_out = reduce_rows(weights["out"], count)
    grad_attn = reduce_rows(weights["attn"].reshape(-1, local), count).reshape(attn_project.shape)

    bins = sums["tables"].shape[0]
    sums["tables"] = jnp.sum(sums["tables"].reshape(bins, B // 8, 8), axis=1)[:, :heads].reshape(-1)
    names = list(sums)
    packed = sum_all(jnp.concatenate([sums[n] for n in names]), count)
    edge = 0
    for n in names:
        size = sums[n].shape[0]
        sums[n] = packed[edge:edge + size]
        edge += size
    grad_tables = sums["tables"].reshape(bins, heads)
    first, second = table_line.shape[0], table_horizontal.shape[0]
    return (
        jnp.stack(outputs),
        jnp.stack(grads_in),
        grad_attn,
        jnp.stack([sums["query_bias"], sums["value_bias"]]),
        grad_tables[:first],
        grad_tables[first:first + second],
        grad_tables[first + second:],
        grad_out,
        sums["out_bias"],
        sums["attn_gain"],
        sums["attn_shift"],
        grad_hidden_project,
        sums["hidden_bias"],
        grad_down,
        sums["down_bias"],
        sums["final_gain"],
        sums["final_shift"],
    )


def solution(mesh):
    return jax.shard_map(
        functools.partial(body, mesh.shape["dp"]),
        mesh=mesh,
        in_specs=(
            P("dp", None, None),
            P("dp", None),
            P("dp", None),
            P("dp", None, None),
            P("dp", None, None),
            P("dp", None, None),
            P(None, None, "head"),
            P(None, "head"),
            P(None, "head"),
            P(None, "head"),
            P(None, "head"),
            P("head", None),
            P(),
            P(),
            P(),
            P(None, "head"),
            P("head"),
            P("head", None),
            P(),
            P(),
            P(),
            P("dp", "head", None),
        ),
        out_specs=(
            P("dp", "head", None),
            P("dp", "head", None),
            P(None, None, "head"),
            P(None, "head"),
            P(None, "head"),
            P(None, "head"),
            P(None, "head"),
            P("head", None),
            P(),
            P(),
            P(),
            P(None, "head"),
            P("head"),
            P("head", None),
            P(),
            P(),
            P(),
        ),
        check_vma=False,
    )
```

```python
import functools
import math

import jax
import jax.numpy as jnp
from jax import lax
from jax.experimental import pallas as pl
from jax.experimental.pallas import tpu as pltpu
from jax.sharding import PartitionSpec as P

B = 128

ROWS_PICK = lax.GatherDimensionNumbers(
    offset_dims=(), collapsed_slice_dims=(0,), start_index_map=(0,),
    operand_batching_dims=(1,), start_indices_batching_dims=(1,))
PACK = 16

def pick(table, index):
    return lax.gather(table, index[:, :, None], ROWS_PICK, (1, 1),
                      mode=lax.GatherScatterMode.PROMISE_IN_BOUNDS)

def lookup(tab_ref, h, at, place, masks):
    found = pick(tab_ref[h, at:at + PACK, :], place)
    for step, mask in enumerate(masks):
        low = at + PACK * (step + 1)
        found = jnp.where(mask, pick(tab_ref[h, low:low + PACK, :], place), found)
    return found.astype(jnp.float32)

def doc_span(len_ref, row, first, last):
    edge = 0
    start = 0
    stop = 0
    for k in range(len_ref.shape[1]):
        begin = edge
        edge = edge + len_ref[row, k]
        start = jnp.where(begin <= first, begin, start)
        stop = jnp.where(begin <= last, edge, stop)
    return start // B, (stop + (B - 1)) // B

def fwd_kernel(row, len_ref, q_ref, k_ref, v_ref, pad_ref, bl_ref, bh_ref, bv_ref, tab_ref,
               probs_ref, ctx_ref, kst, vst, sc):
    qb = pl.program_id(0)
    pairs = kst.shape[0]
    heads = 2 * pairs
    tiles = kst.shape[1]
    lane = lax.broadcasted_iota(jnp.int32, (B, B), 1)
    left = lane < (B // 2)

    @pl.when(qb == 0)
    def _():
        for p in range(pairs):
            for t in range(tiles):
                kt = k_ref[t * B:(t + 1) * B, p * B:(p + 1) * B]
                vt = v_ref[t * B:(t + 1) * B, p * B:(p + 1) * B]
                zero = jnp.zeros_like(kt)
                kst[p, t, 0:B, :] = jnp.where(left, kt, zero)
                kst[p, t, B:2 * B, :] = jnp.where(left, zero, kt)
                vst[p, t, 0:B, :] = jnp.where(left, vt, zero)
                vst[p, t, B:2 * B, :] = jnp.where(left, zero, vt)

    first = qb * B
    low, high = doc_span(len_ref, row, first, first + B - 1)
    sub = lax.broadcasted_iota(jnp.int32, (B, B), 0) + first
    count = len_ref.shape[1]
    edges = []
    edge = 0
    for k in range(count):
        edge = edge + len_ref[row, k]
        edges.append(edge)
    seg_q = sum(((sub >= e).astype(jnp.int32) for e in edges))

    def scores(t, top):
        key_at = lane + t * B
        seg_k = sum(((key_at >= e).astype(jnp.int32) for e in edges))
        real = jnp.broadcast_to(pad_ref[:, pl.ds(pl.multiple_of(t * B, B), B)], (B, B)) > 0
        allowed = ((seg_q == seg_k) & real) | (sub == key_at)
        at = pl.ds(pl.multiple_of(t * B, B), B)
        parts = []
        for g in range(B // PACK):
            rows = slice(g * PACK, g * PACK + PACK)
            group = []
            for ref, tiles_of in ((bl_ref, 2), (bh_ref, 4), (bv_ref, 4)):
                index = ref[rows, at].astype(jnp.int16)
                group.append((index & jnp.int16(PACK - 1),
                              [index >= jnp.int16(PACK * a) for a in range(1, tiles_of)]))
            parts.append(group)
        out = []
        for p in range(pairs):
            raw = lax.dot_general(q_ref[:, p * B:(p + 1) * B], kst[p, t], (((1,), (1,)), ((), ())),
                                  preferred_element_type=jnp.float32)
            for s in range(2):
                h = 2 * p + s
                rel = jnp.concatenate(
                    [(lookup(tab_ref, h, 0, *group[0]) + lookup(tab_ref, h, 32, *group[1]))
                     + lookup(tab_ref, h, 96, *group[2]) for group in parts], axis=0)
                val = jnp.where(allowed, raw[:, s * B:(s + 1) * B] + rel, -1000000000.0)
                sc[t, h] = val
                out.append(jnp.maximum(top[h], val))
        return tuple(out)

    start = jnp.full((B, B), -3.0e38, jnp.float32)
    top = lax.fori_loop(low, high, scores, tuple(start for _ in range(heads)))
    top = [jnp.max(x, axis=-1, keepdims=True) for x in top]

    def expo(t, tot):
        out = []
        for h in range(heads):
            e = jnp.exp(sc[t, h] - top[h])
            sc[t, h] = e
            out.append(tot[h] + e)
        return tuple(out)

    zero = jnp.zeros((B, B), jnp.float32)
    tot = lax.fori_loop(low, high, expo, tuple(zero for _ in range(heads)))
    inv = [1.0 / jnp.sum(x, axis=-1, keepdims=True) for x in tot]

    def mix(t, acc):
        out = []
        for p in range(pairs):
            low_pair = []
            for s in range(2):
                h = 2 * p + s
                pr = sc[t, h] * inv[h]
                probs_ref[t, h] = pr
                low_pair.append(pr.astype(jnp.bfloat16))
            out.append(acc[p] + jnp.dot(jnp.concatenate(low_pair, axis=1), vst[p, t],
                                        preferred_element_type=jnp.float32))
        return tuple(out)

    acc = lax.fori_loop(low, high, mix, tuple(zero for _ in range(pairs)))
    for p in range(pairs):
        ctx_ref[:, p * B:(p + 1) * B] = acc[p].astype(jnp.bfloat16)

def attn_fwd(row, lengths, q, k, v, pad, bl, bh, bv, tab):
    slots, width = q.shape[1:]
    pairs = width // B
    tiles = slots // B
    row_block = lambda n: pl.BlockSpec((None, B, n), lambda i, L: (row, i, 0))
    return pl.pallas_call(
        functools.partial(fwd_kernel, row),
        grid_spec=pltpu.PrefetchScalarGridSpec(
            num_scalar_prefetch=1, grid=(tiles,),
            in_specs=[
                row_block(width),
                pl.BlockSpec((None, slots, width), lambda i, L: (row, 0, 0)),
                pl.BlockSpec((None, slots, width), lambda i, L: (row, 0, 0)),
                pl.BlockSpec((None, 1, slots), lambda i, L: (row, 0, 0)),
                row_block(slots), row_block(slots), row_block(slots),
                pl.BlockSpec(tab.shape, lambda i, L: (0, 0, 0)),
            ],
            out_specs=[
                pl.BlockSpec((None, tiles, 2 * pairs, B, B), lambda i, L: (i, 0, 0, 0, 0)),
                pl.BlockSpec((B, width), lambda i, L: (i, 0)),
            ],
            scratch_shapes=[
                pltpu.VMEM((pairs, tiles, 2 * B, B), jnp.bfloat16),
                pltpu.VMEM((pairs, tiles, 2 * B, B), jnp.bfloat16),
                pltpu.VMEM((tiles, 2 * pairs, B, B), jnp.float32),
            ]),
        out_shape=[
            jax.ShapeDtypeStruct((tiles, tiles, 2 * pairs, B, B), jnp.float32),
            jax.ShapeDtypeStruct((slots, width), jnp.bfloat16),
        ],
        compiler_params=pltpu.CompilerParams(vmem_limit_bytes=48 << 20),
        cost_estimate=pl.CostEstimate(
            flops=4 * slots * slots * width * 8, transcendentals=0, bytes_accessed=16 << 20),
        name="attn_forward",
    )(lengths, q, k, v, pad, bl, bh, bv, tab)


NT = (((1,), (1,)), ((), ()))
TN = (((0,), (0,)), ((), ()))

def bwd_kernel(row, factor, len_ref, q_ref, k_ref, v_ref, gctx_ref, ctx_ref, probs_ref,
               ds_ref, dq_ref, dk_ref, dv_ref, kst, vst, dkst, dvst):
    qb = pl.program_id(0)
    pairs, tiles = kst.shape[0], kst.shape[1]
    lane = lax.broadcasted_iota(jnp.int32, (B, B), 1)
    left = lane < (B // 2)

    @pl.when(qb == 0)
    def _():
        dkst[...] = jnp.zeros_like(dkst)
        dvst[...] = jnp.zeros_like(dvst)
        for p in range(pairs):
            for t in range(tiles):
                kt = k_ref[t * B:(t + 1) * B, p * B:(p + 1) * B]
                vt = v_ref[t * B:(t + 1) * B, p * B:(p + 1) * B]
                zero = jnp.zeros_like(kt)
                kst[p, t, 0:B, :] = jnp.where(left, kt, zero)
                kst[p, t, B:2 * B, :] = jnp.where(left, zero, kt)
                vst[p, t, 0:B, :] = jnp.where(left, vt, zero)
                vst[p, t, B:2 * B, :] = jnp.where(left, zero, vt)

    first = qb * B
    low, high = doc_span(len_ref, row, first, first + B - 1)
    for p in range(pairs):
        cols = slice(p * B, (p + 1) * B)
        gctx = gctx_ref[:, cols]
        q = q_ref[:, cols]
        prod = gctx.astype(jnp.float32) * ctx_ref[:, cols].astype(jnp.float32)
        zero = jnp.zeros_like(prod)
        inner = [jnp.sum(jnp.where(left, prod, zero), axis=-1, keepdims=True),
                 jnp.sum(jnp.where(left, zero, prod), axis=-1, keepdims=True)]

        def tile(t, dq, p=p, gctx=gctx, q=q, inner=inner):
            gp = lax.dot_general(gctx, vst[p, t], NT, preferred_element_type=jnp.float32)
            probs_low, g_scores = [], []
            for s in range(2):
                pr = probs_ref[t, 2 * p + s]
                ds = (pr * (gp[:, s * B:(s + 1) * B] - inner[s])).astype(jnp.bfloat16)
                ds_ref[t, 2 * p + s] = ds
                g_scores.append(ds)
                probs_low.append(pr.astype(jnp.bfloat16))
            ds = jnp.concatenate(g_scores, axis=1)
            pl_ = jnp.concatenate(probs_low, axis=1)
            dkst[p, t] += lax.dot_general(ds, q, TN, preferred_element_type=jnp.float32)
            dvst[p, t] += lax.dot_general(pl_, gctx, TN, preferred_element_type=jnp.float32)
            return dq + jnp.dot(ds, kst[p, t], preferred_element_type=jnp.float32)

        dq = lax.fori_loop(low, high, tile, jnp.zeros((B, B), jnp.float32))
        dq_ref[:, cols] = (dq * factor).astype(jnp.bfloat16)

    @pl.when(qb == tiles - 1)
    def _():
        for p in range(pairs):
            for t in range(tiles):
                dk_ref[t * B:(t + 1) * B, p * B:(p + 1) * B] = jnp.where(
                    left, dkst[p, t, 0:B, :], dkst[p, t, B:2 * B, :]).astype(jnp.bfloat16)
                dv_ref[t * B:(t + 1) * B, p * B:(p + 1) * B] = jnp.where(
                    left, dvst[p, t, 0:B, :], dvst[p, t, B:2 * B, :]).astype(jnp.bfloat16)

def attn_bwd(row, factor, lengths, q, k, v, gctx, ctx, probs):
    slots, width = q.shape[1:]
    pairs, tiles = width // B, slots // B
    part = pl.BlockSpec((B, width), lambda i, L: (i, 0))
    full = pl.BlockSpec((slots, width), lambda i, L: (0, 0))
    mine = pl.BlockSpec((None, B, width), lambda i, L: (row, i, 0))
    whole = pl.BlockSpec((None, slots, width), lambda i, L: (row, 0, 0))
    pairs_of = pl.BlockSpec((None, tiles, 2 * pairs, B, B), lambda i, L: (i, 0, 0, 0, 0))
    flat = jax.ShapeDtypeStruct((slots, width), jnp.bfloat16)
    return pl.pallas_call(
        functools.partial(bwd_kernel, row, factor),
        grid_spec=pltpu.PrefetchScalarGridSpec(
            num_scalar_prefetch=1, grid=(tiles,),
            in_specs=[mine, whole, whole, part, part, pairs_of],
            out_specs=[pairs_of, part, full, full],
            scratch_shapes=[
                pltpu.VMEM((pairs, tiles, 2 * B, B), jnp.bfloat16),
                pltpu.VMEM((pairs, tiles, 2 * B, B), jnp.bfloat16),
                pltpu.VMEM((pairs, tiles, 2 * B, B), jnp.float32),
                pltpu.VMEM((pairs, tiles, 2 * B, B), jnp.float32),
            ]),
        out_shape=[jax.ShapeDtypeStruct(probs.shape, jnp.bfloat16), flat, flat, flat],
        compiler_params=pltpu.CompilerParams(vmem_limit_bytes=48 << 20),
        cost_estimate=pl.CostEstimate(
            flops=8 * slots * slots * width * 8, transcendentals=0, bytes_accessed=16 << 20),
        name="attn_backward",
    )(lengths, q, k, v, gctx, ctx, probs)

BINS = 160

def hist_kernel(row, len_ref, bl_ref, bh_ref, bv_ref, ds_ref, out_ref, spread, weights, hot, acc):
    qb = pl.program_id(0)
    tiles, heads = ds_ref.shape[0], ds_ref.shape[1]
    first = qb * B
    low, high = doc_span(len_ref, row, first, first + B - 1)

    @pl.when(qb == 0)
    def _():
        acc[...] = jnp.zeros_like(acc)
        spread[...] = jnp.zeros_like(spread)

    lane_row = lax.broadcasted_iota(jnp.int32, (BINS, B), 1) // 8

    def window(w, carry):
        t0 = low + 2 * w

        def group(g, carry):
            rows = pl.ds(pl.multiple_of(g * PACK, PACK), PACK)
            for part in range(2):
                t = jnp.minimum(t0 + part, tiles - 1)
                live = t0 + part < high
                for h in range(heads):
                    val = ds_ref[t, h, rows, :].astype(jnp.float32)
                    spread[part, pl.ds(h, PACK, stride=8), :] = jnp.where(live, val, 0.0)
            weights[:, 0:B] = spread[0].astype(jnp.bfloat16)
            weights[:, B:2 * B] = spread[1].astype(jnp.bfloat16)
            idx = []
            for ref in (bl_ref, bh_ref, bv_ref):
                pieces = []
                for part in range(2):
                    t = jnp.minimum(t0 + part, tiles - 1)
                    pieces.append(ref[rows, pl.ds(pl.multiple_of(t * B, B), B)])
                idx.append(jnp.concatenate(pieces, axis=1))
            for half in range(2):
                for i in range(8):
                    r = half * 8 + i
                    at = i * BINS
                    for ix, n in zip(idx, (32, 64, 64)):
                        bins = lax.broadcasted_iota(jnp.int16, (n, 2 * B), 0)
                        line = jnp.broadcast_to(ix[r:r + 1, :], (n, 2 * B)).astype(jnp.int16)
                        hot[at:at + n, :] = jnp.where(bins == line, jnp.ones((), jnp.bfloat16),
                                                      jnp.zeros((), jnp.bfloat16))
                        at += n
                res = lax.dot_general(hot[...], weights[...], NT, preferred_element_type=jnp.float32)
                tot = acc[...]
                for i in range(8):
                    tot = tot + jnp.where(lane_row == half * 8 + i, res[i * BINS:(i + 1) * BINS, :], 0.0)
                acc[...] = tot
            return carry

        return lax.fori_loop(0, B // PACK, group, carry)

    lax.fori_loop(0, (high - low + 1) // 2, window, 0)

    @pl.when(qb == pl.num_programs(0) - 1)
    def _():
        out_ref[...] = acc[...]

def table_grads(row, lengths, bl, bh, bv, ds):
    slots = bl.shape[1]
    tiles, heads = ds.shape[0], ds.shape[2]
    block = pl.BlockSpec((None, B, slots), lambda i, L: (row, i, 0))
    return pl.pallas_call(
        functools.partial(hist_kernel, row),
        grid_spec=pltpu.PrefetchScalarGridSpec(
            num_scalar_prefetch=1, grid=(tiles,),
            in_specs=[block, block, block,
                      pl.BlockSpec((None, tiles, heads, B, B), lambda i, L: (i, 0, 0, 0, 0))],
            out_specs=pl.BlockSpec((BINS, B), lambda i, L: (0, 0)),
            scratch_shapes=[
                pltpu.VMEM((2, 8 * PACK, B), jnp.float32),
                pltpu.VMEM((8 * PACK, 2 * B), jnp.bfloat16),
                pltpu.VMEM((8 * BINS, 2 * B), jnp.bfloat16),
                pltpu.VMEM((BINS, B), jnp.float32),
            ]),
        out_shape=jax.ShapeDtypeStruct((BINS, B), jnp.float32),
        compiler_params=pltpu.CompilerParams(vmem_limit_bytes=48 << 20),
        cost_estimate=pl.CostEstimate(
            flops=16 * slots * slots * 384 * 8, transcendentals=0, bytes_accessed=16 << 20),
        name="table_grads",
    )(lengths, bl, bh, bv, ds)


f32, low = jnp.float32, jnp.bfloat16
SWAP = [(0, 1), (1, 0)]


def normalize(values):
    mean = jnp.mean(values, axis=-1, keepdims=True)
    centered = values - mean
    scale = lax.rsqrt(jnp.mean(centered * centered, axis=-1, keepdims=True) + 1e-12)
    return centered * scale, scale


def normalize_back(grad, normed, scale, gain):
    scaled = grad * gain
    first = jnp.mean(scaled, axis=-1, keepdims=True)
    second = jnp.mean(scaled * normed, axis=-1, keepdims=True)
    return scale * (scaled - first - normed * second)


def times(left, right, left_dim, right_dim):
    return lax.dot_general(left, right, (((left_dim,), (right_dim,)), ((), ())),
                           preferred_element_type=f32)


def flips(count, bit):
    return [(i, i ^ (1 << bit)) for i in range(count)]


def to_peer(values):
    return lax.ppermute(values, "head", SWAP)


def plus(left, right):
    return (left.astype(f32) + right.astype(f32)).astype(low)


def scatter_sum(values, count, bits):
    index = lax.axis_index("dp")
    for bit in bits:
        half = values.shape[0] // 2
        mine = (index >> bit) & 1
        send = lax.dynamic_slice_in_dim(values, (1 - mine) * half, half, 0)
        keep = lax.dynamic_slice_in_dim(values, mine * half, half, 0)
        values = plus(keep, lax.ppermute(send, "dp", flips(count, bit)))
    return values


def in_order(bit_value, mine, other):
    return jnp.where(bit_value == 0, jnp.stack([mine, other]), jnp.stack([other, mine]))


def gather_parts(values, count, bits):
    index = lax.axis_index("dp")
    for bit in reversed(bits):
        got = lax.ppermute(values, "dp", flips(count, bit))
        both = in_order((index >> bit) & 1, values, got)
        values = both.reshape((2 * values.shape[0],) + values.shape[1:])
    return values


def body(
    count,
    hidden,
    lengths,
    padding,
    bucket_line,
    bucket_horizontal,
    bucket_vertical,
    attn_project,
    attn_bias,
    table_line,
    table_horizontal,
    table_vertical,
    out_project,
    out_bias,
    attn_gain,
    attn_shift,
    hidden_project,
    hidden_bias,
    down_project,
    down_bias,
    final_gain,
    final_shift,
    cotangent,
):
    rows, slots, width = hidden.shape
    half = cotangent.shape[1]
    heads = table_line.shape[1]
    local = attn_project.shape[2]
    units = hidden_project.shape[1]
    part = units // 2
    factor = 1.0 / math.sqrt(local // heads)
    head = lax.axis_index("head")
    index = lax.axis_index("dp")
    core = index & 1
    offset = head * half
    every = list(range(count.bit_length() - 1))

    def split(values, dim):
        return [lax.dynamic_slice_in_dim(values, c * part, part, dim) for c in (core, 1 - core)]

    ups = split(hidden_project, 1)
    downs = split(down_project, 0)
    for group in (ups, downs):
        got = to_peer(group[0])
        group += [got, lax.ppermute(got, "dp", flips(count, 0))]
    biases = split(hidden_bias, 0) + split(to_peer(hidden_bias), 0)

    tables = jnp.concatenate([table_line, table_horizontal, table_vertical], axis=0)
    bins = tables.shape[0]
    tables = jnp.broadcast_to(tables.T[:, :, None], (heads, bins, B))
    pad = padding[:, None, :]

    flat = hidden.reshape(rows * slots, width)
    project = times(flat, attn_project, 1, 1)
    query = (project[:, 0] + attn_bias[0].astype(f32)).astype(low) * jnp.asarray(factor, low)
    key = project[:, 1].astype(low)
    value = (project[:, 2] + attn_bias[1].astype(f32)).astype(low)
    query, key, value = (x.reshape(rows, slots, local) for x in (query, key, value))

    gain_first = attn_gain.astype(f32)
    shift_first = attn_shift.astype(f32)
    gain_last = final_gain.astype(f32)
    shift_last = final_shift.astype(f32)

    def own(values):
        return lax.dynamic_slice_in_dim(values, offset, half, 0)

    def others(values):
        return lax.dynamic_slice_in_dim(values, half - offset, half, 0)

    fronts, attn_out = [], []
    for r in range(rows):
        probs, context = attn_fwd(r, lengths, query, key, value, pad, bucket_line,
                                  bucket_horizontal, bucket_vertical, tables)
        fronts.append((probs, context))
        got = to_peer(times(others(context), out_project, 1, 0).astype(low))
        attn_out.append(times(own(context), out_project, 1, 0) + got.astype(f32))
    tokens = lax.dynamic_slice_in_dim(hidden, offset, half, 1).reshape(rows * half, width).astype(f32)
    normed, scale = normalize(tokens + jnp.concatenate(attn_out, axis=0) + out_bias.astype(f32))
    mid = normed * gain_first + shift_first
    mid_low = mid.astype(low)

    actives, slopes = [], []
    total = None
    for up, down, bias in zip(ups, downs, biases):
        inner = times(mid_low, up, 1, 0) + bias.astype(f32)
        bell = 0.5 * (1.0 + lax.erf(inner * math.sqrt(0.5)))
        actives.append((inner * bell).astype(low))
        slopes.append(bell + inner * (jnp.exp(-0.5 * inner * inner) * (1.0 / math.sqrt(2.0 * math.pi))))
        term = times(actives[-1], down, 1, 0)
        total = term if total is None else total + term
    normed_final, scale_final = normalize(mid + total + down_bias.astype(f32))
    output = (normed_final * gain_last + shift_last).astype(low).reshape(rows, half, width)

    above = cotangent.reshape(rows * half, width).astype(f32)
    g_final = normalize_back(above, normed_final, scale_final, gain_last)
    g_low = g_final.astype(low)
    grads_down = [times(active, g_low, 0, 0).astype(low) for active in actives]
    total = None
    grads_up, grads_bias = [], []
    for up, down, slope in zip(ups, downs, slopes):
        g_inner = (times(g_low, down, 1, 1) * slope).astype(low)
        grads_bias.append(jnp.sum(g_inner.astype(f32), axis=0))
        grads_up.append(times(mid_low, g_inner, 0, 0).astype(low))
        term = times(g_inner, up, 1, 1)
        total = term if total is None else total + term
    g_mid = g_final + total
    g_attn = normalize_back(g_mid, normed, scale, gain_first)

    def reduce_units(grads):
        got = lax.ppermute(jnp.stack([grads[1], grads[3]]), "dp", flips(count, 0))
        mine = plus(grads[0], got[0])
        mine = plus(mine, to_peer(plus(grads[2], got[1])))
        mine = gather_parts(scatter_sum(mine, count, every[1:]), count, every[1:])
        return mine, lax.ppermute(mine, "dp", flips(count, 0))

    grad_down = in_order(core, *reduce_units(grads_down)).reshape(down_project.shape).astype(f32)
    mine, other = reduce_units(grads_up)
    grad_up = jnp.where(core == 0, jnp.concatenate([mine, other], axis=1),
                        jnp.concatenate([other, mine], axis=1)).astype(f32)

    g_low = g_attn.astype(low).reshape(rows, half, width)
    g_attn = g_attn.reshape(rows, half, width)
    grads_in, marks = [], []
    sums = {"query_bias": 0.0, "value_bias": 0.0}
    grad_out, grad_attn = 0.0, [0.0, 0.0, 0.0]
    for r in range(rows):
        probs, context = fronts[r]
        g_all = in_order(head, g_low[r], to_peer(g_low[r])).reshape(slots, width)
        g_context = times(g_all, out_project, 1, 1).astype(low)
        g_scores, *g_three = attn_bwd(r, factor, lengths, query, key, value, g_context, context, probs)
        marks.append(g_scores)
        grad_out = grad_out + times(context, g_all, 0, 0)
        sums["query_bias"] += jnp.sum(g_three[0].astype(f32), axis=0)
        sums["value_bias"] += jnp.sum(g_three[2].astype(f32), axis=0)
        for c in range(3):
            grad_attn[c] = grad_attn[c] + times(hidden[r], g_three[c], 0, 0)
        give = sum(times(others(g), attn_project[c], 1, 1) for c, g in enumerate(g_three))
        got = to_peer(give.astype(low))
        mine = sum(times(own(g), attn_project[c], 1, 1) for c, g in enumerate(g_three))
        grads_in.append(mine + g_attn[r] + got.astype(f32))

    buffer = jnp.concatenate([g.astype(low) for g in grad_attn]
                             + [grad_out[:, :local].astype(low), grad_out[:, local:].astype(low)], axis=0)
    buffer = gather_parts(scatter_sum(buffer, count, every), count, every).astype(f32)
    grad_attn = buffer[:3 * width].reshape(attn_project.shape)
    grad_out = jnp.concatenate([buffer[3 * width:3 * width + local], buffer[3 * width + local:]], axis=1)

    marks = [table_grads(r, lengths, bucket_line, bucket_horizontal, bucket_vertical, m)
             for r, m in enumerate(marks)]
    marks = jnp.sum(sum(marks).reshape(bins, B // 8, 8), axis=1)[:, :heads]

    def placed(pieces):
        mine = jnp.concatenate(pieces)
        return jnp.where(jnp.arange(2, dtype=jnp.int32)[:, None] == head, mine[None], 0.0).reshape(-1)

    bias_pieces = lax.dynamic_update_slice(
        lax.dynamic_update_slice(jnp.zeros((units,), f32), grads_bias[0], (core * part,)),
        grads_bias[1], ((1 - core) * part,))
    bias_other = lax.dynamic_update_slice(
        lax.dynamic_update_slice(jnp.zeros((units,), f32), grads_bias[2], (core * part,)),
        grads_bias[3], ((1 - core) * part,))
    bias_both = in_order(head, bias_pieces, bias_other).reshape(-1)
    packed = jnp.concatenate([
        jnp.sum(g_attn, axis=(0, 1)),
        jnp.sum(g_mid * normed, axis=0),
        jnp.sum(g_mid, axis=0),
        jnp.sum(g_final, axis=0),
        jnp.sum(above * normed_final, axis=0),
        jnp.sum(above, axis=0),
        bias_both,
        placed([marks.reshape(-1), sums["query_bias"], sums["value_bias"]]),
    ])
    packed = packed + to_peer(packed)
    for bit in every:
        packed = packed + lax.ppermute(packed, "dp", flips(count, bit))
    shared = packed[:6 * width].reshape(6, width)
    grad_bias = lax.dynamic_slice_in_dim(packed, 6 * width + head * units, units, 0)
    size = marks.size + 2 * local
    mine = lax.dynamic_slice_in_dim(packed, 6 * width + 2 * units + head * size, size, 0)
    marks = mine[:bins * heads].reshape(bins, heads)
    first, second = table_line.shape[0], table_horizontal.shape[0]
    return (
        output,
        jnp.stack(grads_in),
        grad_attn,
        mine[bins * heads:].reshape(2, local),
        marks[:first],
        marks[first:first + second],
        marks[first + second:],
        grad_out,
        shared[0],
        shared[1],
        shared[2],
        grad_up,
        grad_bias,
        grad_down,
        shared[3],
        shared[4],
        shared[5],
    )


def solution(mesh):
    return jax.shard_map(
        functools.partial(body, mesh.shape["dp"]),
        mesh=mesh,
        in_specs=(
            P("dp", None, None),
            P("dp", None),
            P("dp", None),
            P("dp", None, None),
            P("dp", None, None),
            P("dp", None, None),
            P(None, None, "head"),
            P(None, "head"),
            P(None, "head"),
            P(None, "head"),
            P(None, "head"),
            P("head", None),
            P(),
            P(),
            P(),
            P(None, "head"),
            P("head"),
            P("head", None),
            P(),
            P(),
            P(),
            P("dp", "head", None),
        ),
        out_specs=(
            P("dp", "head", None),
            P("dp", "head", None),
            P(None, None, "head"),
            P(None, "head"),
            P(None, "head"),
            P(None, "head"),
            P(None, "head"),
            P("head", None),
            P(),
            P(),
            P(),
            P(None, "head"),
            P("head"),
            P("head", None),
            P(),
            P(),
            P(),
        ),
        check_vma=False,
    )
```

```python
import functools
import math

import jax
import jax.numpy as jnp
from jax import lax
from jax.experimental import pallas as pl
from jax.experimental.pallas import tpu as pltpu
from jax.sharding import PartitionSpec as P

B = 128

ROWS_PICK = lax.GatherDimensionNumbers(
    offset_dims=(), collapsed_slice_dims=(0,), start_index_map=(0,),
    operand_batching_dims=(1,), start_indices_batching_dims=(1,))
PACK = 16

def pick(table, index):
    return lax.gather(table, index[:, :, None], ROWS_PICK, (1, 1),
                      mode=lax.GatherScatterMode.PROMISE_IN_BOUNDS)

def lookup(tab_ref, h, at, place, masks):
    found = pick(tab_ref[h, at:at + PACK, :], place)
    for step, mask in enumerate(masks):
        low = at + PACK * (step + 1)
        found = jnp.where(mask, pick(tab_ref[h, low:low + PACK, :], place), found)
    return found.astype(jnp.float32)

def doc_span(len_ref, row, first, last):
    edge = 0
    start = 0
    stop = 0
    for k in range(len_ref.shape[1]):
        begin = edge
        edge = edge + len_ref[row, k]
        start = jnp.where(begin <= first, begin, start)
        stop = jnp.where(begin <= last, edge, stop)
    return start // B, (stop + (B - 1)) // B

def fwd_kernel(row, len_ref, q_ref, k_ref, v_ref, pad_ref, bl_ref, bh_ref, bv_ref, tab_ref,
               probs_ref, ctx_ref, kst, vst, sc):
    qb = pl.program_id(0)
    pairs = kst.shape[0]
    heads = 2 * pairs
    tiles = kst.shape[1]
    lane = lax.broadcasted_iota(jnp.int32, (B, B), 1)
    left = lane < (B // 2)

    @pl.when(qb == 0)
    def _():
        for p in range(pairs):
            for t in range(tiles):
                kt = k_ref[t * B:(t + 1) * B, p * B:(p + 1) * B]
                vt = v_ref[t * B:(t + 1) * B, p * B:(p + 1) * B]
                zero = jnp.zeros_like(kt)
                kst[p, t, 0:B, :] = jnp.where(left, kt, zero)
                kst[p, t, B:2 * B, :] = jnp.where(left, zero, kt)
                vst[p, t, 0:B, :] = jnp.where(left, vt, zero)
                vst[p, t, B:2 * B, :] = jnp.where(left, zero, vt)

    first = qb * B
    low, high = doc_span(len_ref, row, first, first + B - 1)
    sub = lax.broadcasted_iota(jnp.int32, (B, B), 0) + first
    count = len_ref.shape[1]
    edges = []
    edge = 0
    for k in range(count):
        edge = edge + len_ref[row, k]
        edges.append(edge)
    seg_q = sum(((sub >= e).astype(jnp.int32) for e in edges))

    def scores(t, top):
        key_at = lane + t * B
        seg_k = sum(((key_at >= e).astype(jnp.int32) for e in edges))
        real = jnp.broadcast_to(pad_ref[:, pl.ds(pl.multiple_of(t * B, B), B)], (B, B)) > 0
        allowed = ((seg_q == seg_k) & real) | (sub == key_at)
        at = pl.ds(pl.multiple_of(t * B, B), B)
        parts = []
        for g in range(B // PACK):
            rows = slice(g * PACK, g * PACK + PACK)
            group = []
            for ref, tiles_of in ((bl_ref, 2), (bh_ref, 4), (bv_ref, 4)):
                index = ref[rows, at].astype(jnp.int16)
                group.append((index & jnp.int16(PACK - 1),
                              [index >= jnp.int16(PACK * a) for a in range(1, tiles_of)]))
            parts.append(group)
        out = []
        for p in range(pairs):
            raw = lax.dot_general(q_ref[:, p * B:(p + 1) * B], kst[p, t], (((1,), (1,)), ((), ())),
                                  preferred_element_type=jnp.float32)
            for s in range(2):
                h = 2 * p + s
                rel = jnp.concatenate(
                    [(lookup(tab_ref, h, 0, *group[0]) + lookup(tab_ref, h, 32, *group[1]))
                     + lookup(tab_ref, h, 96, *group[2]) for group in parts], axis=0)
                val = jnp.where(allowed, raw[:, s * B:(s + 1) * B] + rel, -1000000000.0)
                sc[t, h] = val
                out.append(jnp.maximum(top[h], val))
        return tuple(out)

    start = jnp.full((B, B), -3.0e38, jnp.float32)
    top = lax.fori_loop(low, high, scores, tuple(start for _ in range(heads)))
    top = [jnp.max(x, axis=-1, keepdims=True) for x in top]

    def expo(t, tot):
        out = []
        for h in range(heads):
            e = jnp.exp(sc[t, h] - top[h])
            sc[t, h] = e
            out.append(tot[h] + e)
        return tuple(out)

    zero = jnp.zeros((B, B), jnp.float32)
    tot = lax.fori_loop(low, high, expo, tuple(zero for _ in range(heads)))
    inv = [1.0 / jnp.sum(x, axis=-1, keepdims=True) for x in tot]

    def mix(t, acc):
        out = []
        for p in range(pairs):
            low_pair = []
            for s in range(2):
                h = 2 * p + s
                pr = sc[t, h] * inv[h]
                probs_ref[t, h] = pr
                low_pair.append(pr.astype(jnp.bfloat16))
            out.append(acc[p] + jnp.dot(jnp.concatenate(low_pair, axis=1), vst[p, t],
                                        preferred_element_type=jnp.float32))
        return tuple(out)

    acc = lax.fori_loop(low, high, mix, tuple(zero for _ in range(pairs)))
    for p in range(pairs):
        ctx_ref[:, p * B:(p + 1) * B] = acc[p].astype(jnp.bfloat16)

def attn_fwd(row, lengths, q, k, v, pad, bl, bh, bv, tab):
    slots, width = q.shape[1:]
    pairs = width // B
    tiles = slots // B
    row_block = lambda n: pl.BlockSpec((None, B, n), lambda i, L: (row, i, 0))
    return pl.pallas_call(
        functools.partial(fwd_kernel, row),
        grid_spec=pltpu.PrefetchScalarGridSpec(
            num_scalar_prefetch=1, grid=(tiles,),
            in_specs=[
                row_block(width),
                pl.BlockSpec((None, slots, width), lambda i, L: (row, 0, 0)),
                pl.BlockSpec((None, slots, width), lambda i, L: (row, 0, 0)),
                pl.BlockSpec((None, 1, slots), lambda i, L: (row, 0, 0)),
                row_block(slots), row_block(slots), row_block(slots),
                pl.BlockSpec(tab.shape, lambda i, L: (0, 0, 0)),
            ],
            out_specs=[
                pl.BlockSpec((None, tiles, 2 * pairs, B, B), lambda i, L: (i, 0, 0, 0, 0)),
                pl.BlockSpec((B, width), lambda i, L: (i, 0)),
            ],
            scratch_shapes=[
                pltpu.VMEM((pairs, tiles, 2 * B, B), jnp.bfloat16),
                pltpu.VMEM((pairs, tiles, 2 * B, B), jnp.bfloat16),
                pltpu.VMEM((tiles, 2 * pairs, B, B), jnp.float32),
            ]),
        out_shape=[
            jax.ShapeDtypeStruct((tiles, tiles, 2 * pairs, B, B), jnp.float32),
            jax.ShapeDtypeStruct((slots, width), jnp.bfloat16),
        ],
        compiler_params=pltpu.CompilerParams(vmem_limit_bytes=48 << 20),
        cost_estimate=pl.CostEstimate(
            flops=4 * slots * slots * width * 8, transcendentals=0, bytes_accessed=16 << 20),
        name="attn_forward",
    )(lengths, q, k, v, pad, bl, bh, bv, tab)


NT = (((1,), (1,)), ((), ()))
TN = (((0,), (0,)), ((), ()))

def bwd_kernel(row, factor, len_ref, q_ref, k_ref, v_ref, gctx_ref, ctx_ref, probs_ref,
               ds_ref, dq_ref, dk_ref, dv_ref, kst, vst, dkst, dvst):
    qb = pl.program_id(0)
    pairs, tiles = kst.shape[0], kst.shape[1]
    lane = lax.broadcasted_iota(jnp.int32, (B, B), 1)
    left = lane < (B // 2)

    @pl.when(qb == 0)
    def _():
        dkst[...] = jnp.zeros_like(dkst)
        dvst[...] = jnp.zeros_like(dvst)
        for p in range(pairs):
            for t in range(tiles):
                kt = k_ref[t * B:(t + 1) * B, p * B:(p + 1) * B]
                vt = v_ref[t * B:(t + 1) * B, p * B:(p + 1) * B]
                zero = jnp.zeros_like(kt)
                kst[p, t, 0:B, :] = jnp.where(left, kt, zero)
                kst[p, t, B:2 * B, :] = jnp.where(left, zero, kt)
                vst[p, t, 0:B, :] = jnp.where(left, vt, zero)
                vst[p, t, B:2 * B, :] = jnp.where(left, zero, vt)

    first = qb * B
    low, high = doc_span(len_ref, row, first, first + B - 1)
    for p in range(pairs):
        cols = slice(p * B, (p + 1) * B)
        gctx = gctx_ref[:, cols]
        q = q_ref[:, cols]
        prod = gctx.astype(jnp.float32) * ctx_ref[:, cols].astype(jnp.float32)
        zero = jnp.zeros_like(prod)
        inner = [jnp.sum(jnp.where(left, prod, zero), axis=-1, keepdims=True),
                 jnp.sum(jnp.where(left, zero, prod), axis=-1, keepdims=True)]

        def tile(t, dq, p=p, gctx=gctx, q=q, inner=inner):
            gp = lax.dot_general(gctx, vst[p, t], NT, preferred_element_type=jnp.float32)
            probs_low, g_scores = [], []
            for s in range(2):
                pr = probs_ref[t, 2 * p + s]
                ds = (pr * (gp[:, s * B:(s + 1) * B] - inner[s])).astype(jnp.bfloat16)
                ds_ref[t, 2 * p + s] = ds
                g_scores.append(ds)
                probs_low.append(pr.astype(jnp.bfloat16))
            ds = jnp.concatenate(g_scores, axis=1)
            pl_ = jnp.concatenate(probs_low, axis=1)
            dkst[p, t] += lax.dot_general(ds, q, TN, preferred_element_type=jnp.float32)
            dvst[p, t] += lax.dot_general(pl_, gctx, TN, preferred_element_type=jnp.float32)
            return dq + jnp.dot(ds, kst[p, t], preferred_element_type=jnp.float32)

        dq = lax.fori_loop(low, high, tile, jnp.zeros((B, B), jnp.float32))
        dq_ref[:, cols] = (dq * factor).astype(jnp.bfloat16)

    @pl.when(qb == tiles - 1)
    def _():
        for p in range(pairs):
            for t in range(tiles):
                dk_ref[t * B:(t + 1) * B, p * B:(p + 1) * B] = jnp.where(
                    left, dkst[p, t, 0:B, :], dkst[p, t, B:2 * B, :]).astype(jnp.bfloat16)
                dv_ref[t * B:(t + 1) * B, p * B:(p + 1) * B] = jnp.where(
                    left, dvst[p, t, 0:B, :], dvst[p, t, B:2 * B, :]).astype(jnp.bfloat16)

def attn_bwd(row, factor, lengths, q, k, v, gctx, ctx, probs):
    slots, width = q.shape[1:]
    pairs, tiles = width // B, slots // B
    part = pl.BlockSpec((B, width), lambda i, L: (i, 0))
    full = pl.BlockSpec((slots, width), lambda i, L: (0, 0))
    mine = pl.BlockSpec((None, B, width), lambda i, L: (row, i, 0))
    whole = pl.BlockSpec((None, slots, width), lambda i, L: (row, 0, 0))
    pairs_of = pl.BlockSpec((None, tiles, 2 * pairs, B, B), lambda i, L: (i, 0, 0, 0, 0))
    flat = jax.ShapeDtypeStruct((slots, width), jnp.bfloat16)
    return pl.pallas_call(
        functools.partial(bwd_kernel, row, factor),
        grid_spec=pltpu.PrefetchScalarGridSpec(
            num_scalar_prefetch=1, grid=(tiles,),
            in_specs=[mine, whole, whole, part, part, pairs_of],
            out_specs=[pairs_of, part, full, full],
            scratch_shapes=[
                pltpu.VMEM((pairs, tiles, 2 * B, B), jnp.bfloat16),
                pltpu.VMEM((pairs, tiles, 2 * B, B), jnp.bfloat16),
                pltpu.VMEM((pairs, tiles, 2 * B, B), jnp.float32),
                pltpu.VMEM((pairs, tiles, 2 * B, B), jnp.float32),
            ]),
        out_shape=[jax.ShapeDtypeStruct(probs.shape, jnp.bfloat16), flat, flat, flat],
        compiler_params=pltpu.CompilerParams(vmem_limit_bytes=48 << 20),
        cost_estimate=pl.CostEstimate(
            flops=8 * slots * slots * width * 8, transcendentals=0, bytes_accessed=16 << 20),
        name="attn_backward",
    )(lengths, q, k, v, gctx, ctx, probs)

BINS = 160

def hist_kernel(row, start, len_ref, bl_ref, bh_ref, bv_ref, ds_ref, out_ref, spread, weights, hot, acc):
    qb = pl.program_id(0)
    tiles, heads = ds_ref.shape[0], ds_ref.shape[1]
    first = (start + qb) * B
    low, high = doc_span(len_ref, row, first, first + B - 1)

    @pl.when(qb == 0)
    def _():
        acc[...] = jnp.zeros_like(acc)
        spread[...] = jnp.zeros_like(spread)

    lane_row = lax.broadcasted_iota(jnp.int32, (BINS, B), 1) // 8

    def window(w, carry):
        t0 = low + 2 * w

        def group(g, carry):
            rows = pl.ds(pl.multiple_of(g * PACK, PACK), PACK)
            for part in range(2):
                t = jnp.minimum(t0 + part, tiles - 1)
                live = t0 + part < high
                for h in range(heads):
                    val = ds_ref[t, h, rows, :].astype(jnp.float32)
                    spread[part, pl.ds(h, PACK, stride=8), :] = jnp.where(live, val, 0.0)
            weights[:, 0:B] = spread[0].astype(jnp.bfloat16)
            weights[:, B:2 * B] = spread[1].astype(jnp.bfloat16)
            idx = []
            for ref in (bl_ref, bh_ref, bv_ref):
                pieces = []
                for part in range(2):
                    t = jnp.minimum(t0 + part, tiles - 1)
                    pieces.append(ref[rows, pl.ds(pl.multiple_of(t * B, B), B)])
                idx.append(jnp.concatenate(pieces, axis=1))
            for half in range(2):
                for i in range(8):
                    r = half * 8 + i
                    at = i * BINS
                    for ix, n in zip(idx, (32, 64, 64)):
                        bins = lax.broadcasted_iota(jnp.int16, (n, 2 * B), 0)
                        line = jnp.broadcast_to(ix[r:r + 1, :], (n, 2 * B)).astype(jnp.int16)
                        hot[at:at + n, :] = jnp.where(bins == line, jnp.ones((), jnp.bfloat16),
                                                      jnp.zeros((), jnp.bfloat16))
                        at += n
                res = lax.dot_general(hot[...], weights[...], NT, preferred_element_type=jnp.float32)
                tot = acc[...]
                for i in range(8):
                    tot = tot + jnp.where(lane_row == half * 8 + i, res[i * BINS:(i + 1) * BINS, :], 0.0)
                acc[...] = tot
            return carry

        return lax.fori_loop(0, B // PACK, group, carry)

    lax.fori_loop(0, (high - low + 1) // 2, window, 0)

    @pl.when(qb == pl.num_programs(0) - 1)
    def _():
        out_ref[...] = acc[...]

def table_grads(row, start, blocks, lengths, bl, bh, bv, ds):
    slots = bl.shape[1]
    tiles, heads = ds.shape[0], ds.shape[2]
    block = pl.BlockSpec((None, B, slots), lambda i, L: (row, start + i, 0))
    return pl.pallas_call(
        functools.partial(hist_kernel, row, start),
        grid_spec=pltpu.PrefetchScalarGridSpec(
            num_scalar_prefetch=1, grid=(blocks,),
            in_specs=[block, block, block,
                      pl.BlockSpec((None, tiles, heads, B, B), lambda i, L: (start + i, 0, 0, 0, 0))],
            out_specs=pl.BlockSpec((BINS, B), lambda i, L: (0, 0)),
            scratch_shapes=[
                pltpu.VMEM((2, 8 * PACK, B), jnp.float32),
                pltpu.VMEM((8 * PACK, 2 * B), jnp.bfloat16),
                pltpu.VMEM((8 * BINS, 2 * B), jnp.bfloat16),
                pltpu.VMEM((BINS, B), jnp.float32),
            ]),
        out_shape=jax.ShapeDtypeStruct((BINS, B), jnp.float32),
        compiler_params=pltpu.CompilerParams(vmem_limit_bytes=48 << 20),
        cost_estimate=pl.CostEstimate(
            flops=16 * slots * slots * 384 * 8, transcendentals=0, bytes_accessed=16 << 20),
        name="table_grads",
    )(lengths, bl, bh, bv, ds)


f32, low = jnp.float32, jnp.bfloat16
SWAP = [(0, 1), (1, 0)]


def normalize(values):
    mean = jnp.mean(values, axis=-1, keepdims=True)
    centered = values - mean
    scale = lax.rsqrt(jnp.mean(centered * centered, axis=-1, keepdims=True) + 1e-12)
    return centered * scale, scale


def normalize_back(grad, normed, scale, gain):
    scaled = grad * gain
    first = jnp.mean(scaled, axis=-1, keepdims=True)
    second = jnp.mean(scaled * normed, axis=-1, keepdims=True)
    return scale * (scaled - first - normed * second)


def times(left, right, left_dim, right_dim):
    return lax.dot_general(left, right, (((left_dim,), (right_dim,)), ((), ())),
                           preferred_element_type=f32)


def flips(count, bit):
    return [(i, i ^ (1 << bit)) for i in range(count)]


def to_peer(values):
    return lax.ppermute(values, "head", SWAP)


def plus(left, right):
    return (left.astype(f32) + right.astype(f32)).astype(low)


def in_order(bit_value, mine, other):
    return jnp.where(bit_value == 0, jnp.stack([mine, other]), jnp.stack([other, mine]))


class Order:
    def __init__(self):
        self.last = None

    def tie(self, values):
        if self.last is None:
            return values
        values, self.last = lax.optimization_barrier((values, self.last))
        return values

    def mark(self, values):
        self.last = values


def scatter_steps(order, values, count, bits):
    index = lax.axis_index("dp")
    for bit in bits:
        half = values.shape[0] // 2
        mine = (index >> bit) & 1
        send = lax.dynamic_slice_in_dim(values, (1 - mine) * half, half, 0)
        keep = lax.dynamic_slice_in_dim(values, mine * half, half, 0)
        order.mark(send)
        got = lax.ppermute(send, "dp", flips(count, bit))
        yield
        values = plus(keep, order.tie(got))
    return values


def gather_steps(order, values, count, bits):
    index = lax.axis_index("dp")
    for bit in reversed(bits):
        order.mark(values)
        got = lax.ppermute(values, "dp", flips(count, bit))
        yield
        both = in_order((index >> bit) & 1, values, order.tie(got))
        values = both.reshape((2 * values.shape[0],) + values.shape[1:])
    return values


def unit_steps(order, grads, count, out):
    bits = list(range(1, count.bit_length() - 1))
    order.mark(grads[3])
    near = lax.ppermute(grads[3], "dp", flips(count, 0))
    got = lax.ppermute(grads[1], "dp", flips(count, 0))
    yield
    send = plus(grads[2], order.tie(near))
    order.mark(send)
    far = to_peer(send)
    mine = plus(grads[0], got)
    yield
    mine = plus(mine, order.tie(far))
    mine = yield from scatter_steps(order, mine, count, bits)
    mine = yield from gather_steps(order, mine, count, bits)
    order.mark(mine)
    other = lax.ppermute(mine, "dp", flips(count, 0))
    yield
    out += [mine, order.tie(other)]


def buffer_steps(order, values, count, out):
    bits = list(range(count.bit_length() - 1))
    values = yield from scatter_steps(order, values, count, bits)
    values = yield from gather_steps(order, values, count, bits)
    order.mark(values)
    out.append(values)


def advance(*chains):
    for chain in chains:
        next(chain, None)


def finish(*chains):
    left = list(chains)
    while left:
        for chain in list(left):
            try:
                next(chain)
            except StopIteration:
                left.remove(chain)


def body(
    count,
    hidden,
    lengths,
    padding,
    bucket_line,
    bucket_horizontal,
    bucket_vertical,
    attn_project,
    attn_bias,
    table_line,
    table_horizontal,
    table_vertical,
    out_project,
    out_bias,
    attn_gain,
    attn_shift,
    hidden_project,
    hidden_bias,
    down_project,
    down_bias,
    final_gain,
    final_shift,
    cotangent,
):
    rows, slots, width = hidden.shape
    half = cotangent.shape[1]
    heads = table_line.shape[1]
    local = attn_project.shape[2]
    units = hidden_project.shape[1]
    part = units // 2
    factor = 1.0 / math.sqrt(local // heads)
    head = lax.axis_index("head")
    index = lax.axis_index("dp")
    core = index & 1
    offset = head * half
    every = list(range(count.bit_length() - 1))

    def split(values, dim):
        return [lax.dynamic_slice_in_dim(values, c * part, part, dim) for c in (core, 1 - core)]

    ups = split(hidden_project, 1)
    downs = split(down_project, 0)
    got = to_peer(ups[0])
    ups += [got, lax.ppermute(got, "dp", flips(count, 0))]
    biases = split(hidden_bias, 0) + split(to_peer(hidden_bias), 0)

    tables = jnp.concatenate([table_line, table_horizontal, table_vertical], axis=0)
    bins = tables.shape[0]
    tables = jnp.broadcast_to(tables.T[:, :, None], (heads, bins, B))
    pad = padding[:, None, :]

    flat = hidden.reshape(rows * slots, width)
    query = ((times(flat, attn_project[0], 1, 0) + attn_bias[0].astype(f32)).astype(low)
             * jnp.asarray(factor, low))
    key = times(flat, attn_project[1], 1, 0).astype(low)
    value = (times(flat, attn_project[2], 1, 0) + attn_bias[1].astype(f32)).astype(low)
    query, key, value = (x.reshape(rows, slots, local) for x in (query, key, value))

    gain_first = attn_gain.astype(f32)
    shift_first = attn_shift.astype(f32)
    gain_last = final_gain.astype(f32)
    shift_last = final_shift.astype(f32)

    def own(values):
        return lax.dynamic_slice_in_dim(values, offset, half, 0)

    def others(values):
        return lax.dynamic_slice_in_dim(values, half - offset, half, 0)

    fronts, attn_sum = [], []
    for r in range(rows):
        probs, context = attn_fwd(r, lengths, query, key, value, pad, bucket_line,
                                  bucket_horizontal, bucket_vertical, tables)
        fronts.append((probs, context))
        send = times(others(context), out_project, 1, 0).astype(low)
        got = to_peer(send)
        attn_sum.append(times(own(context), out_project, 1, 0) + got.astype(f32))
    send, downs[0] = lax.optimization_barrier((send, downs[0]))
    got = to_peer(downs[0])
    downs += [got, lax.ppermute(got, "dp", flips(count, 0))]
    tokens = lax.dynamic_slice_in_dim(hidden, offset, half, 1).reshape(rows * half, width).astype(f32)
    normed, scale = normalize(tokens + jnp.concatenate(attn_sum, axis=0) + out_bias.astype(f32))
    mid = normed * gain_first + shift_first
    mid_low = mid.astype(low)

    actives, slopes = [], []
    total = None
    for up, down, bias in zip(ups, downs, biases):
        inner = times(mid_low, up, 1, 0) + bias.astype(f32)
        bell = 0.5 * (1.0 + lax.erf(inner * math.sqrt(0.5)))
        actives.append((inner * bell).astype(low))
        slopes.append(bell + inner * (jnp.exp(-0.5 * inner * inner) * (1.0 / math.sqrt(2.0 * math.pi))))
        term = times(actives[-1], down, 1, 0)
        total = term if total is None else total + term
    normed_final, scale_final = normalize(mid + total + down_bias.astype(f32))
    output = (normed_final * gain_last + shift_last).astype(low).reshape(rows, half, width)

    above = cotangent.reshape(rows * half, width).astype(f32)
    g_final = normalize_back(above, normed_final, scale_final, gain_last)
    g_low = g_final.astype(low)
    order = Order()
    grads_down = [times(active, g_low, 0, 0).astype(low) for active in actives]
    down_out, up_out, attn_out = [], [], []
    down_chain = unit_steps(order, grads_down, count, down_out)
    advance(down_chain)
    total = None
    grads_bias, inners = [], []
    g_low = order.tie(g_low)
    for up, down, slope in zip(ups, downs, slopes):
        g_inner = (times(g_low, down, 1, 1) * slope).astype(low)
        inners.append(g_inner)
        grads_bias.append(jnp.sum(g_inner.astype(f32), axis=0))
        term = times(g_inner, up, 1, 1)
        total = term if total is None else total + term
    g_mid = g_final + total
    g_attn = normalize_back(g_mid, normed, scale, gain_first)
    g_low = g_attn.astype(low).reshape(rows, half, width)
    g_others = [to_peer(g_low[r]) for r in range(rows)]
    order.mark(g_low)
    advance(down_chain)
    mid_low = order.tie(mid_low)
    grads_up = [times(mid_low, g_inner, 0, 0).astype(low) for g_inner in inners]
    up_chain = unit_steps(order, grads_up, count, up_out)
    advance(up_chain)
    g_attn = g_attn.reshape(rows, half, width)

    grads_in, marks, g_rows = [], [], []
    for r in range(rows):
        probs, context = fronts[r]
        g_all = in_order(head, g_low[r], order.tie(g_others[r])).reshape(slots, width)
        g_context = times(g_all, out_project, 1, 1).astype(low)
        g_scores, *g_three = attn_bwd(r, factor, lengths, query, key, value, g_context, context, probs)
        order.mark(g_three[0])
        g_rows.append((context, g_all, g_three))
        marks.append(g_scores)
        advance(down_chain, up_chain)
    sums = {"query_bias": 0.0, "value_bias": 0.0}
    grad_out, grad_attn = 0.0, [0.0, 0.0, 0.0]
    for r, (context, g_all, g_three) in enumerate(g_rows):
        grad_out = grad_out + times(context, g_all, 0, 0)
        sums["query_bias"] += jnp.sum(g_three[0].astype(f32), axis=0)
        sums["value_bias"] += jnp.sum(g_three[2].astype(f32), axis=0)
        for c in range(3):
            grad_attn[c] = grad_attn[c] + times(hidden[r], g_three[c], 0, 0)
    buffer = jnp.concatenate([g.astype(low) for g in grad_attn]
                             + [grad_out[:, :local].astype(low), grad_out[:, local:].astype(low)], axis=0)
    attn_chain = buffer_steps(order, buffer, count, attn_out)
    advance(attn_chain)
    gives, mines = [], []
    for r, (context, g_all, g_three) in enumerate(g_rows):
        gives.append(sum(times(others(order.tie(g)), attn_project[c], 1, 1)
                         for c, g in enumerate(g_three)).astype(low))
    order.mark(gives[-1])
    for r, (context, g_all, g_three) in enumerate(g_rows):
        mine = sum(times(own(order.tie(g)), attn_project[c], 1, 1) for c, g in enumerate(g_three))
        mines.append(mine + g_attn[r])
    order.mark(mines[-1])
    advance(attn_chain, down_chain, up_chain)
    tables_out = 0.0
    for r in range(rows):
        for block in range(2):
            tables_out = tables_out + table_grads(r, 2 * block, 2, order.tie(lengths), bucket_line,
                                                  bucket_horizontal, bucket_vertical, marks[r])
            order.mark(tables_out)
            advance(attn_chain, down_chain, up_chain)
    grads_in = [mine + to_peer(give).astype(f32) for mine, give in zip(mines, gives)]
    marks = jnp.sum(tables_out.reshape(bins, B // 8, 8), axis=1)[:, :heads]
    finish(attn_chain, down_chain, up_chain)
    grad_down = in_order(core, *down_out).reshape(down_project.shape).astype(f32)
    mine, other = up_out
    grad_up = jnp.where(core == 0, jnp.concatenate([mine, other], axis=1),
                        jnp.concatenate([other, mine], axis=1)).astype(f32)
    buffer = attn_out[0].astype(f32)
    grad_attn = buffer[:3 * width].reshape(attn_project.shape)
    grad_out = jnp.concatenate([buffer[3 * width:3 * width + local], buffer[3 * width + local:]], axis=1)

    def placed(pieces):
        mine = jnp.concatenate(pieces)
        return jnp.where(jnp.arange(2, dtype=jnp.int32)[:, None] == head, mine[None], 0.0).reshape(-1)

    bias_pieces = lax.dynamic_update_slice(
        lax.dynamic_update_slice(jnp.zeros((units,), f32), grads_bias[0], (core * part,)),
        grads_bias[1], ((1 - core) * part,))
    bias_other = lax.dynamic_update_slice(
        lax.dynamic_update_slice(jnp.zeros((units,), f32), grads_bias[2], (core * part,)),
        grads_bias[3], ((1 - core) * part,))
    bias_both = in_order(head, bias_pieces, bias_other).reshape(-1)
    packed = jnp.concatenate([
        jnp.sum(g_attn, axis=(0, 1)),
        jnp.sum(g_mid * normed, axis=0),
        jnp.sum(g_mid, axis=0),
        jnp.sum(g_final, axis=0),
        jnp.sum(above * normed_final, axis=0),
        jnp.sum(above, axis=0),
        bias_both,
        placed([marks.reshape(-1), sums["query_bias"], sums["value_bias"]]),
    ])
    packed = packed + to_peer(packed)
    for bit in every:
        packed = packed + lax.ppermute(packed, "dp", flips(count, bit))
    shared = packed[:6 * width].reshape(6, width)
    grad_bias = lax.dynamic_slice_in_dim(packed, 6 * width + head * units, units, 0)
    size = marks.size + 2 * local
    mine = lax.dynamic_slice_in_dim(packed, 6 * width + 2 * units + head * size, size, 0)
    marks = mine[:bins * heads].reshape(bins, heads)
    first, second = table_line.shape[0], table_horizontal.shape[0]
    return (
        output,
        jnp.stack(grads_in),
        grad_attn,
        mine[bins * heads:].reshape(2, local),
        marks[:first],
        marks[first:first + second],
        marks[first + second:],
        grad_out,
        shared[0],
        shared[1],
        shared[2],
        grad_up,
        grad_bias,
        grad_down,
        shared[3],
        shared[4],
        shared[5],
    )


def solution(mesh):
    return jax.shard_map(
        functools.partial(body, mesh.shape["dp"]),
        mesh=mesh,
        in_specs=(
            P("dp", None, None),
            P("dp", None),
            P("dp", None),
            P("dp", None, None),
            P("dp", None, None),
            P("dp", None, None),
            P(None, None, "head"),
            P(None, "head"),
            P(None, "head"),
            P(None, "head"),
            P(None, "head"),
            P("head", None),
            P(),
            P(),
            P(),
            P(None, "head"),
            P("head"),
            P("head", None),
            P(),
            P(),
            P(),
            P("dp", "head", None),
        ),
        out_specs=(
            P("dp", "head", None),
            P("dp", "head", None),
            P(None, None, "head"),
            P(None, "head"),
            P(None, "head"),
            P(None, "head"),
            P(None, "head"),
            P("head", None),
            P(),
            P(),
            P(),
            P(None, "head"),
            P("head"),
            P("head", None),
            P(),
            P(),
            P(),
        ),
        check_vma=False,
    )
```

```python
import functools
import math

import jax
import jax.numpy as jnp
from jax import lax
from jax.experimental import pallas as pl
from jax.experimental.pallas import tpu as pltpu
from jax.sharding import PartitionSpec as P

B = 128

ROWS_PICK = lax.GatherDimensionNumbers(
    offset_dims=(), collapsed_slice_dims=(0,), start_index_map=(0,),
    operand_batching_dims=(1,), start_indices_batching_dims=(1,))
PACK = 16

def pick(table, index):
    return lax.gather(table, index[:, :, None], ROWS_PICK, (1, 1),
                      mode=lax.GatherScatterMode.PROMISE_IN_BOUNDS)

def lookup(tab_ref, h, at, place, masks):
    found = pick(tab_ref[h, at:at + PACK, :], place)
    for step, mask in enumerate(masks):
        low = at + PACK * (step + 1)
        found = jnp.where(mask, pick(tab_ref[h, low:low + PACK, :], place), found)
    return found.astype(jnp.float32)

def doc_span(len_ref, row, first, last):
    edge = 0
    start = 0
    stop = 0
    for k in range(len_ref.shape[1]):
        begin = edge
        edge = edge + len_ref[row, k]
        start = jnp.where(begin <= first, begin, start)
        stop = jnp.where(begin <= last, edge, stop)
    return start // B, (stop + (B - 1)) // B

def fwd_kernel(row, len_ref, q_ref, k_ref, v_ref, pad_ref, bl_ref, bh_ref, bv_ref, tab_ref,
               probs_ref, ctx_ref, kst, vst, sc):
    qb = pl.program_id(0)
    pairs = kst.shape[0]
    heads = 2 * pairs
    tiles = kst.shape[1]
    lane = lax.broadcasted_iota(jnp.int32, (B, B), 1)
    left = lane < (B // 2)

    @pl.when(qb == 0)
    def _():
        for p in range(pairs):
            for t in range(tiles):
                kt = k_ref[t * B:(t + 1) * B, p * B:(p + 1) * B]
                vt = v_ref[t * B:(t + 1) * B, p * B:(p + 1) * B]
                zero = jnp.zeros_like(kt)
                kst[p, t, 0:B, :] = jnp.where(left, kt, zero)
                kst[p, t, B:2 * B, :] = jnp.where(left, zero, kt)
                vst[p, t, 0:B, :] = jnp.where(left, vt, zero)
                vst[p, t, B:2 * B, :] = jnp.where(left, zero, vt)

    first = qb * B
    low, high = doc_span(len_ref, row, first, first + B - 1)
    sub = lax.broadcasted_iota(jnp.int32, (B, B), 0) + first
    count = len_ref.shape[1]
    edges = []
    edge = 0
    for k in range(count):
        edge = edge + len_ref[row, k]
        edges.append(edge)
    seg_q = sum(((sub >= e).astype(jnp.int32) for e in edges))

    def scores(t, top):
        key_at = lane + t * B
        seg_k = sum(((key_at >= e).astype(jnp.int32) for e in edges))
        real = jnp.broadcast_to(pad_ref[:, pl.ds(pl.multiple_of(t * B, B), B)], (B, B)) > 0
        allowed = ((seg_q == seg_k) & real) | (sub == key_at)
        at = pl.ds(pl.multiple_of(t * B, B), B)
        parts = []
        for g in range(B // PACK):
            rows = slice(g * PACK, g * PACK + PACK)
            group = []
            for ref, tiles_of in ((bl_ref, 2), (bh_ref, 4), (bv_ref, 4)):
                index = ref[rows, at].astype(jnp.int16)
                group.append((index & jnp.int16(PACK - 1),
                              [index >= jnp.int16(PACK * a) for a in range(1, tiles_of)]))
            parts.append(group)
        out = []
        for p in range(pairs):
            raw = lax.dot_general(q_ref[:, p * B:(p + 1) * B], kst[p, t], (((1,), (1,)), ((), ())),
                                  preferred_element_type=jnp.float32)
            for s in range(2):
                h = 2 * p + s
                rel = jnp.concatenate(
                    [(lookup(tab_ref, h, 0, *group[0]) + lookup(tab_ref, h, 32, *group[1]))
                     + lookup(tab_ref, h, 96, *group[2]) for group in parts], axis=0)
                val = jnp.where(allowed, raw[:, s * B:(s + 1) * B] + rel, -1000000000.0)
                sc[t, h] = val
                out.append(jnp.maximum(top[h], val))
        return tuple(out)

    start = jnp.full((B, B), -3.0e38, jnp.float32)
    top = lax.fori_loop(low, high, scores, tuple(start for _ in range(heads)))
    top = [jnp.max(x, axis=-1, keepdims=True) for x in top]

    def expo(t, tot):
        out = []
        for h in range(heads):
            e = jnp.exp(sc[t, h] - top[h])
            sc[t, h] = e
            out.append(tot[h] + e)
        return tuple(out)

    zero = jnp.zeros((B, B), jnp.float32)
    tot = lax.fori_loop(low, high, expo, tuple(zero for _ in range(heads)))
    inv = [1.0 / jnp.sum(x, axis=-1, keepdims=True) for x in tot]

    def mix(t, acc):
        out = []
        for p in range(pairs):
            low_pair = []
            for s in range(2):
                h = 2 * p + s
                pr = sc[t, h] * inv[h]
                probs_ref[t, h] = pr
                low_pair.append(pr.astype(jnp.bfloat16))
            out.append(acc[p] + jnp.dot(jnp.concatenate(low_pair, axis=1), vst[p, t],
                                        preferred_element_type=jnp.float32))
        return tuple(out)

    acc = lax.fori_loop(low, high, mix, tuple(zero for _ in range(pairs)))
    for p in range(pairs):
        ctx_ref[:, p * B:(p + 1) * B] = acc[p].astype(jnp.bfloat16)

def attn_fwd(row, lengths, q, k, v, pad, bl, bh, bv, tab):
    slots, width = q.shape[1:]
    pairs = width // B
    tiles = slots // B
    row_block = lambda n: pl.BlockSpec((None, B, n), lambda i, L: (row, i, 0))
    return pl.pallas_call(
        functools.partial(fwd_kernel, row),
        grid_spec=pltpu.PrefetchScalarGridSpec(
            num_scalar_prefetch=1, grid=(tiles,),
            in_specs=[
                row_block(width),
                pl.BlockSpec((None, slots, width), lambda i, L: (row, 0, 0)),
                pl.BlockSpec((None, slots, width), lambda i, L: (row, 0, 0)),
                pl.BlockSpec((None, 1, slots), lambda i, L: (row, 0, 0)),
                row_block(slots), row_block(slots), row_block(slots),
                pl.BlockSpec(tab.shape, lambda i, L: (0, 0, 0)),
            ],
            out_specs=[
                pl.BlockSpec((None, tiles, 2 * pairs, B, B), lambda i, L: (i, 0, 0, 0, 0)),
                pl.BlockSpec((B, width), lambda i, L: (i, 0)),
            ],
            scratch_shapes=[
                pltpu.VMEM((pairs, tiles, 2 * B, B), jnp.bfloat16),
                pltpu.VMEM((pairs, tiles, 2 * B, B), jnp.bfloat16),
                pltpu.VMEM((tiles, 2 * pairs, B, B), jnp.float32),
            ]),
        out_shape=[
            jax.ShapeDtypeStruct((tiles, tiles, 2 * pairs, B, B), jnp.float32),
            jax.ShapeDtypeStruct((slots, width), jnp.bfloat16),
        ],
        compiler_params=pltpu.CompilerParams(vmem_limit_bytes=48 << 20),
        cost_estimate=pl.CostEstimate(
            flops=4 * slots * slots * width * 8, transcendentals=0, bytes_accessed=16 << 20),
        name="attn_forward",
    )(lengths, q, k, v, pad, bl, bh, bv, tab)


NT = (((1,), (1,)), ((), ()))
TN = (((0,), (0,)), ((), ()))

def bwd_kernel(row, factor, len_ref, q_ref, k_ref, v_ref, gctx_ref, ctx_ref, probs_ref,
               *rest):
    ds_ref, three_ref, kst, vst, dkst, dvst, inner, dqs = rest[-8:]
    qb = pl.program_id(0)
    pairs, tiles = kst.shape[0], kst.shape[1]
    lane = lax.broadcasted_iota(jnp.int32, (B, B), 1)
    left = lane < (B // 2)

    @pl.when(qb == 0)
    def _():
        dkst[...] = jnp.zeros_like(dkst)
        dvst[...] = jnp.zeros_like(dvst)
        for p in range(pairs):
            for t in range(tiles):
                kt = k_ref[t * B:(t + 1) * B, p * B:(p + 1) * B]
                vt = v_ref[t * B:(t + 1) * B, p * B:(p + 1) * B]
                zero = jnp.zeros_like(kt)
                kst[p, t, 0:B, :] = jnp.where(left, kt, zero)
                kst[p, t, B:2 * B, :] = jnp.where(left, zero, kt)
                vst[p, t, 0:B, :] = jnp.where(left, vt, zero)
                vst[p, t, B:2 * B, :] = jnp.where(left, zero, vt)

    first = qb * B
    low, high = doc_span(len_ref, row, first, first + B - 1)
    sides = []
    for p in range(pairs):
        cols = slice(p * B, (p + 1) * B)
        gctx = gctx_ref[:, cols]
        prod = gctx.astype(jnp.float32) * ctx_ref[:, cols].astype(jnp.float32)
        zero = jnp.zeros_like(prod)
        for side in (jnp.where(left, prod, zero), jnp.where(left, zero, prod)):
            inner[len(sides)] = jnp.broadcast_to(jnp.sum(side, axis=-1, keepdims=True), (B, B))
            sides.append(0)
    dqs[...] = jnp.zeros_like(dqs)

    def tile(t, carry):
        for p in range(pairs):
            cols = slice(p * B, (p + 1) * B)
            gctx = gctx_ref[:, cols]
            gp = lax.dot_general(gctx, vst[p, t], NT, preferred_element_type=jnp.float32)
            probs_low, g_scores = [], []
            for s in range(2):
                pr = probs_ref[t, 2 * p + s]
                ds = (pr * (gp[:, s * B:(s + 1) * B] - inner[2 * p + s])).astype(jnp.bfloat16)
                ds_ref[t, 2 * p + s] = ds
                g_scores.append(ds)
                probs_low.append(pr.astype(jnp.bfloat16))
            ds = jnp.concatenate(g_scores, axis=1)
            mix = jnp.concatenate(probs_low, axis=1)
            dvst[p, t] += lax.dot_general(mix, gctx, TN, preferred_element_type=jnp.float32)
            dkst[p, t] += lax.dot_general(ds, q_ref[:, cols], TN, preferred_element_type=jnp.float32)
            dqs[p] += jnp.dot(ds, kst[p, t], preferred_element_type=jnp.float32)
        return carry

    lax.fori_loop(low, high, tile, 0)
    for p in range(pairs):
        three_ref[pl.ds(pl.multiple_of(first, B), B), p * B:(p + 1) * B] = (dqs[p] * factor).astype(jnp.bfloat16)

    @pl.when(qb == tiles - 1)
    def _():
        for p in range(pairs):
            for t in range(tiles):
                three_ref[t * B:(t + 1) * B, (pairs + p) * B:(pairs + p + 1) * B] = jnp.where(
                    left, dkst[p, t, 0:B, :], dkst[p, t, B:2 * B, :]).astype(jnp.bfloat16)
                three_ref[t * B:(t + 1) * B, (2 * pairs + p) * B:(2 * pairs + p + 1) * B] = jnp.where(
                    left, dvst[p, t, 0:B, :], dvst[p, t, B:2 * B, :]).astype(jnp.bfloat16)

def attn_bwd(row, factor, lengths, q, k, v, gctx, ctx, probs, kept=None):
    slots, width = q.shape[1:]
    pairs, tiles = width // B, slots // B
    part = pl.BlockSpec((B, width), lambda i, L: (i, 0))
    three = pl.BlockSpec((None, slots, 3 * width), lambda i, L: (row, 0, 0))
    mine = pl.BlockSpec((None, B, width), lambda i, L: (row, i, 0))
    whole = pl.BlockSpec((None, slots, width), lambda i, L: (row, 0, 0))
    pairs_of = pl.BlockSpec((None, tiles, 2 * pairs, B, B), lambda i, L: (i, 0, 0, 0, 0))
    kept = () if kept is None else (kept,)
    return pl.pallas_call(
        functools.partial(bwd_kernel, row, factor),
        grid_spec=pltpu.PrefetchScalarGridSpec(
            num_scalar_prefetch=1, grid=(tiles,),
            in_specs=[mine, whole, whole, part, part, pairs_of]
            + [pl.BlockSpec(memory_space=pl.ANY)] * len(kept),
            out_specs=[pairs_of, three],
            scratch_shapes=[
                pltpu.VMEM((pairs, tiles, 2 * B, B), jnp.bfloat16),
                pltpu.VMEM((pairs, tiles, 2 * B, B), jnp.bfloat16),
                pltpu.VMEM((pairs, tiles, 2 * B, B), jnp.float32),
                pltpu.VMEM((pairs, tiles, 2 * B, B), jnp.float32),
                pltpu.VMEM((2 * pairs, B, B), jnp.float32),
                pltpu.VMEM((pairs, B, B), jnp.float32),
            ]),
        out_shape=[jax.ShapeDtypeStruct(probs.shape, jnp.bfloat16),
                   jax.ShapeDtypeStruct((q.shape[0], slots, 3 * width), jnp.bfloat16)],
        input_output_aliases={7: 1} if kept else {},
        compiler_params=pltpu.CompilerParams(vmem_limit_bytes=48 << 20),
        cost_estimate=pl.CostEstimate(
            flops=8 * slots * slots * width * 8, transcendentals=0, bytes_accessed=16 << 20),
        name="attn_backward",
    )(lengths, q, k, v, gctx, ctx, probs, *kept)

BINS = 160


def hist_kernel(row, len_ref, bl_ref, bh_ref, bv_ref, ds_ref, out_ref, even, odd):
    tiles, heads = ds_ref.shape[1], ds_ref.shape[2]
    docs = len_ref.shape[1]
    lane = lax.broadcasted_iota(jnp.int32, (PACK, B), 1)
    sub = lax.broadcasted_iota(jnp.int32, (PACK, B), 0)
    even[...] = jnp.zeros_like(even)
    odd[...] = jnp.zeros_like(odd)

    starts, ends, upto = [], [], []
    edge, count = 0, 0
    for d in range(docs):
        starts.append(edge)
        edge = edge + len_ref[row, d]
        ends.append(edge)
        count = count + ((edge + (PACK - 1)) // PACK - starts[d] // PACK)
        upto.append(count)

    def group(g, spread):
        start, end, block = starts[0], ends[0], starts[0] // PACK + g
        for d in range(1, docs):
            past = g >= upto[d - 1]
            start = jnp.where(past, starts[d], start)
            end = jnp.where(past, ends[d], end)
            block = jnp.where(past, starts[d] // PACK + (g - upto[d - 1]), block)
        end = jnp.where(g < count, end, start)
        block = jnp.minimum(block, tiles * B // PACK - 1)
        tile = start // B
        left = start - tile * B
        turn = jnp.where(left == 0, 0, B - left)
        qb = block // (B // PACK)
        rows = pl.ds(pl.multiple_of((block - qb * (B // PACK)) * PACK, PACK), PACK)
        all_rows = pl.ds(pl.multiple_of(block * PACK, PACK), PACK)
        token = sub + block * PACK
        inside = (token >= start) & (token < end)
        lives = [inside & (lane + part * B < end - start) for part in range(2)]
        first = lane < B - left
        spots = [jnp.minimum(tile + part, tiles - 1) for part in range(3)]

        def moved(parts):
            parts = [pltpu.roll(p, turn, 1) for p in parts]
            return [jnp.where(first, parts[part], parts[part + 1]) for part in range(2)]

        for h in range(heads):
            vals = moved([ds_ref[qb, s, h, rows, :].astype(jnp.float32) for s in spots])
            for part in range(2):
                spread[part, pl.ds(h, PACK, stride=8), :] = jnp.where(lives[part], vals[part], 0.0)
        codes = []
        for s in spots:
            at = pl.ds(pl.multiple_of(s * B, B), B)
            codes.append(bl_ref[all_rows, at] + 32 * bh_ref[all_rows, at] + 2048 * bv_ref[all_rows, at])
        code = jnp.concatenate(moved(codes), axis=1)
        index = [(code & 31).astype(jnp.int16), ((code >> 5) & 63).astype(jnp.int16),
                 (code >> 11).astype(jnp.int16)]
        one, zero = jnp.ones((), jnp.bfloat16), jnp.zeros((), jnp.bfloat16)
        grads, hots = [], []
        for r in range(PACK):
            hot = []
            for ix, n in zip(index, (32, 64, 64)):
                bins = lax.broadcasted_iota(jnp.int16, (n, 2 * B), 0)
                line = jnp.broadcast_to(ix[r:r + 1, :], (n, 2 * B))
                hot.append(jnp.where(bins == line, one, zero))
            hots.append(jnp.concatenate(hot, axis=0))
            grads += [spread[part, r * 8:r * 8 + 8, :].astype(jnp.bfloat16) for part in range(2)]
        return lax.dot_general(jnp.concatenate(grads, axis=1), jnp.concatenate(hots, axis=1), NT,
                               preferred_element_type=jnp.float32)

    def two(step, sums):
        return sums[0] + group(2 * step, even), sums[1] + group(2 * step + 1, odd)

    none = jnp.zeros((8, BINS), jnp.float32)
    sums = lax.fori_loop(0, (count + 1) // 2, two, (none, none))
    out_ref[...] = sums[0] + sums[1]


def table_grads(row, lengths, bl, bh, bv, ds):
    slots = bl.shape[1]
    tiles, heads = ds.shape[0], ds.shape[2]
    block = pl.BlockSpec((None, slots, slots), lambda i, L: (row, 0, 0))
    return pl.pallas_call(
        functools.partial(hist_kernel, row),
        grid_spec=pltpu.PrefetchScalarGridSpec(
            num_scalar_prefetch=1, grid=(1,),
            in_specs=[block, block, block,
                      pl.BlockSpec(ds.shape, lambda i, L: (0, 0, 0, 0, 0))],
            out_specs=pl.BlockSpec((8, BINS), lambda i, L: (0, 0)),
            scratch_shapes=[
                pltpu.VMEM((2, 8 * PACK, B), jnp.float32),
                pltpu.VMEM((2, 8 * PACK, B), jnp.float32),
            ]),
        out_shape=jax.ShapeDtypeStruct((8, BINS), jnp.float32),
        compiler_params=pltpu.CompilerParams(vmem_limit_bytes=48 << 20),
        cost_estimate=pl.CostEstimate(
            flops=16 * slots * slots * 384 * 8, transcendentals=0, bytes_accessed=16 << 20),
        name="table_grads",
    )(lengths, bl, bh, bv, ds)


f32, low = jnp.float32, jnp.bfloat16
SWAP = [(0, 1), (1, 0)]


def normalize(values):
    mean = jnp.mean(values, axis=-1, keepdims=True)
    centered = values - mean
    scale = lax.rsqrt(jnp.mean(centered * centered, axis=-1, keepdims=True) + 1e-12)
    return centered * scale, scale


def normalize_back(grad, normed, scale, gain):
    scaled = grad * gain
    first = jnp.mean(scaled, axis=-1, keepdims=True)
    second = jnp.mean(scaled * normed, axis=-1, keepdims=True)
    return scale * (scaled - first - normed * second)


def times(left, right, left_dim, right_dim):
    return lax.dot_general(left, right, (((left_dim,), (right_dim,)), ((), ())),
                           preferred_element_type=f32)


def flips(count, bit):
    return [(i, i ^ (1 << bit)) for i in range(count)]


def to_peer(values):
    return lax.ppermute(values, "head", SWAP)


def plus(left, right):
    return (left.astype(f32) + right.astype(f32)).astype(low)


def in_order(bit_value, mine, other):
    return jnp.where(bit_value == 0, jnp.stack([mine, other]), jnp.stack([other, mine]))


class Order:
    def __init__(self):
        self.last = None

    def tie(self, values):
        if self.last is None:
            return values
        values, self.last = lax.optimization_barrier((values, self.last))
        return values

    def mark(self, values):
        self.last = values


def scatter_steps(order, values, count, bits):
    index = lax.axis_index("dp")
    for bit in bits:
        half = values.shape[0] // 2
        mine = (index >> bit) & 1
        send = lax.dynamic_slice_in_dim(values, (1 - mine) * half, half, 0)
        keep = lax.dynamic_slice_in_dim(values, mine * half, half, 0)
        order.mark(send)
        got = lax.ppermute(send, "dp", flips(count, bit))
        yield
        values = plus(keep, order.tie(got))
    return values


def gather_steps(order, values, count, bits):
    index = lax.axis_index("dp")
    for bit in reversed(bits):
        order.mark(values)
        got = lax.ppermute(values, "dp", flips(count, bit))
        yield
        both = in_order((index >> bit) & 1, values, order.tie(got))
        values = both.reshape((2 * values.shape[0],) + values.shape[1:])
    return values


def unit_steps(order, kept, given, count, split, head_first, out):
    bits = list(range(1, count.bit_length() - 1))
    order.mark(given)
    got = lax.ppermute(given, "dp", flips(count, 0))
    yield
    got = order.tie(got)
    if head_first:
        (mine, other), (mine_got, other_got) = split(kept), split(got)
        send = plus(other, other_got)
        order.mark(send)
        far = to_peer(send)
        mine = plus(mine, mine_got)
        yield
        mine = plus(mine, order.tie(far))
        mine = yield from scatter_steps(order, mine, count, bits)
    else:
        both = yield from scatter_steps(order, plus(kept, got), count, bits)
        mine, send = split(both)
        order.mark(send)
        far = to_peer(send)
        yield
        mine = plus(mine, order.tie(far))
    mine = yield from gather_steps(order, mine, count, bits)
    order.mark(mine)
    other = lax.ppermute(mine, "dp", flips(count, 0))
    yield
    out += [mine, order.tie(other)]


def buffer_steps(order, values, count, out):
    bits = list(range(count.bit_length() - 1))
    values = yield from scatter_steps(order, values, count, bits)
    values = yield from gather_steps(order, values, count, bits)
    order.mark(values)
    out.append(values)


def advance(*chains):
    for chain in chains:
        next(chain, None)


def finish(*chains):
    left = list(chains)
    while left:
        for chain in list(left):
            try:
                next(chain)
            except StopIteration:
                left.remove(chain)


def body(
    count,
    hidden,
    lengths,
    padding,
    bucket_line,
    bucket_horizontal,
    bucket_vertical,
    attn_project,
    attn_bias,
    table_line,
    table_horizontal,
    table_vertical,
    out_project,
    out_bias,
    attn_gain,
    attn_shift,
    hidden_project,
    hidden_bias,
    down_project,
    down_bias,
    final_gain,
    final_shift,
    cotangent,
):
    rows, slots, width = hidden.shape
    half = cotangent.shape[1]
    heads = table_line.shape[1]
    local = attn_project.shape[2]
    units = hidden_project.shape[1]
    part = units // 2
    factor = 1.0 / math.sqrt(local // heads)
    head = lax.axis_index("head")
    index = lax.axis_index("dp")
    core = index & 1
    offset = head * half
    every = list(range(count.bit_length() - 1))

    def split(values, dim):
        return [lax.dynamic_slice_in_dim(values, c * part, part, dim) for c in (core, 1 - core)]

    def joined(own_parts, got, dim):
        mine, rest = own_parts
        beside = lax.ppermute(got, "dp", flips(count, 0))
        return [jnp.concatenate([mine, got], axis=dim), jnp.concatenate([rest, beside], axis=dim)]

    up_parts, down_parts = split(hidden_project, 1), split(down_project, 0)
    up_got, down_got = to_peer(up_parts[0]), to_peer(down_parts[0])
    bias_got = to_peer(hidden_bias)
    biases = [jnp.concatenate([x, y]) for x, y in zip(split(hidden_bias, 0), split(bias_got, 0))]

    tables = jnp.concatenate([table_line, table_horizontal, table_vertical], axis=0)
    bins = tables.shape[0]
    tables = jnp.broadcast_to(tables.T[:, :, None], (heads, bins, B))
    pad = padding[:, None, :]

    flat = hidden.reshape(rows * slots, width)
    query = ((times(flat, attn_project[0], 1, 0) + attn_bias[0].astype(f32)).astype(low)
             * jnp.asarray(factor, low))
    key = times(flat, attn_project[1], 1, 0).astype(low)
    value = (times(flat, attn_project[2], 1, 0) + attn_bias[1].astype(f32)).astype(low)
    query, key, value = (x.reshape(rows, slots, local) for x in (query, key, value))

    gain_first = attn_gain.astype(f32)
    shift_first = attn_shift.astype(f32)
    gain_last = final_gain.astype(f32)
    shift_last = final_shift.astype(f32)

    def own(values):
        return lax.dynamic_slice_in_dim(values, offset, half, 0)

    def others(values):
        return lax.dynamic_slice_in_dim(values, half - offset, half, 0)

    fronts, attn_sum = [], []
    for r in range(rows):
        if r == 1:
            lengths, up_got = lax.optimization_barrier((lengths, up_got))
        probs, context = attn_fwd(r, lengths, query, key, value, pad, bucket_line,
                                  bucket_horizontal, bucket_vertical, tables)
        fronts.append((probs, context))
        send = times(others(context), out_project, 1, 0).astype(low)
        got = to_peer(send)
        attn_sum.append(times(own(context), out_project, 1, 0) + got.astype(f32))
    ups, downs = joined(up_parts, up_got, 1), joined(down_parts, down_got, 0)
    tokens = lax.dynamic_slice_in_dim(hidden, offset, half, 1).reshape(rows * half, width).astype(f32)
    normed, scale = normalize(tokens + jnp.concatenate(attn_sum, axis=0) + out_bias.astype(f32))
    mid = normed * gain_first + shift_first
    mid_low = mid.astype(low)

    actives, slopes = [], []
    total = None
    for up, down, bias in zip(ups, downs, biases):
        inner = times(mid_low, up, 1, 0) + bias.astype(f32)
        bell = 0.5 * (1.0 + lax.erf(inner * math.sqrt(0.5)))
        actives.append((inner * bell).astype(low))
        slopes.append(bell + inner * (jnp.exp(-0.5 * inner * inner) * (1.0 / math.sqrt(2.0 * math.pi))))
        term = times(actives[-1], down, 1, 0)
        total = term if total is None else total + term
    normed_final, scale_final = normalize(mid + total + down_bias.astype(f32))
    output = (normed_final * gain_last + shift_last).astype(low).reshape(rows, half, width)

    above = cotangent.reshape(rows * half, width).astype(f32)
    g_final = normalize_back(above, normed_final, scale_final, gain_last)
    g_low = g_final.astype(low)
    order = Order()
    total = None
    grads_bias, inners = [], []
    for up, down, slope in zip(ups, downs, slopes):
        g_inner = (times(g_low, down, 1, 1) * slope).astype(low)
        inners.append(g_inner)
        grads_bias.append(jnp.sum(g_inner.astype(f32), axis=0))
        term = times(g_inner, up, 1, 1)
        total = term if total is None else total + term
    g_mid = g_final + total
    g_attn = normalize_back(g_mid, normed, scale, gain_first)
    g_attn_low = g_attn.astype(low).reshape(rows, half, width)
    g_others = [to_peer(g_attn_low[r]) for r in range(rows)]
    order.mark(g_attn_low)
    down_out, up_out, attn_out = [], [], []
    g_low = order.tie(g_low)
    kept, given = (times(active, g_low, 0, 0).astype(low) for active in actives)
    down_chain = unit_steps(order, kept, given, count, lambda v: (v[:part], v[part:]), True, down_out)
    advance(down_chain)
    mid_low = order.tie(mid_low)
    kept, given = (times(mid_low, g_inner, 0, 0).astype(low) for g_inner in inners)
    up_chain = unit_steps(order, kept, given, count, lambda v: (v[:, :part], v[:, part:]), False, up_out)
    advance(up_chain, down_chain)
    g_attn = g_attn.reshape(rows, half, width)

    marks, three, grad_out = [], None, 0.0
    for r in range(rows):
        probs, context = fronts[r]
        g_all = in_order(head, g_attn_low[r], order.tie(g_others[r])).reshape(slots, width)
        g_context = times(g_all, out_project, 1, 1).astype(low)
        g_scores, three = attn_bwd(r, factor, lengths, query, key, value, g_context, context, probs, three)
        order.mark(g_scores)
        marks.append(g_scores)
        grad_out = grad_out + times(context, g_all, 0, 0)
        advance(up_chain, down_chain)
    grad_attn = times(flat, three.reshape(rows * slots, 3 * local), 0, 0).astype(low)
    grad_out = jnp.concatenate([grad_out[:, :local], grad_out[:, local:]], axis=0).astype(low)
    attn_chain = buffer_steps(order, jnp.concatenate([grad_attn, grad_out], axis=1), count, attn_out)
    advance(attn_chain)
    every_project = jnp.concatenate([attn_project[c] for c in range(3)], axis=1)
    theirs = lax.dynamic_slice_in_dim(order.tie(three), half - offset, half, 1)
    give = times(theirs.reshape(rows * half, 3 * local), every_project, 1, 1).astype(low)
    mine = lax.dynamic_slice_in_dim(three, offset, half, 1)
    mine = times(mine.reshape(rows * half, 3 * local), every_project, 1, 1)
    grads_in = mine.reshape(rows, half, width) + g_attn
    give, grads_in = lax.optimization_barrier((give, grads_in))
    order.mark(grads_in)
    grads_in = grads_in + to_peer(give).astype(f32).reshape(rows, half, width)
    advance(attn_chain, up_chain, down_chain)
    bias_sums = jnp.sum(three.astype(f32), axis=(0, 1))
    tables_out = 0.0
    for r in range(rows):
        tables_out = tables_out + table_grads(r, order.tie(lengths), bucket_line,
                                              bucket_horizontal, bucket_vertical, marks[r])
        order.mark(tables_out)
        advance(attn_chain, up_chain, down_chain)
    marks = tables_out[:heads].T
    finish(attn_chain, up_chain, down_chain)
    grad_down = in_order(core, *down_out).reshape(down_project.shape).astype(f32)
    mine, other = up_out
    grad_up = jnp.where(core == 0, jnp.concatenate([mine, other], axis=1),
                        jnp.concatenate([other, mine], axis=1)).astype(f32)
    buffer = attn_out[0].astype(f32)
    grad_attn = jnp.stack([buffer[:, c * local:(c + 1) * local] for c in range(3)])
    grad_out = jnp.concatenate([buffer[:local, 3 * local:], buffer[local:, 3 * local:]], axis=1)

    def placed(pieces):
        mine = jnp.concatenate(pieces)
        return jnp.where(jnp.arange(2, dtype=jnp.int32)[:, None] == head, mine[None], 0.0).reshape(-1)

    bias_sets = in_order(core, *grads_bias)
    mine, other = bias_sets[:, :part].reshape(-1), bias_sets[:, part:].reshape(-1)
    bias_both = in_order(head, mine, other).reshape(-1)
    packed = jnp.concatenate([
        jnp.sum(g_attn, axis=(0, 1)),
        jnp.sum(g_mid * normed, axis=0),
        jnp.sum(g_mid, axis=0),
        jnp.sum(g_final, axis=0),
        jnp.sum(above * normed_final, axis=0),
        jnp.sum(above, axis=0),
        bias_both,
        placed([marks.reshape(-1), bias_sums[:local], bias_sums[2 * local:]]),
    ])
    packed = packed + to_peer(packed)
    for bit in every:
        packed = packed + lax.ppermute(packed, "dp", flips(count, bit))
    shared = packed[:6 * width].reshape(6, width)
    grad_bias = lax.dynamic_slice_in_dim(packed, 6 * width + head * units, units, 0)
    size = marks.size + 2 * local
    mine = lax.dynamic_slice_in_dim(packed, 6 * width + 2 * units + head * size, size, 0)
    marks = mine[:bins * heads].reshape(bins, heads)
    first, second = table_line.shape[0], table_horizontal.shape[0]
    return (
        output,
        grads_in,
        grad_attn,
        mine[bins * heads:].reshape(2, local),
        marks[:first],
        marks[first:first + second],
        marks[first + second:],
        grad_out,
        shared[0],
        shared[1],
        shared[2],
        grad_up,
        grad_bias,
        grad_down,
        shared[3],
        shared[4],
        shared[5],
    )


def solution(mesh):
    return jax.shard_map(
        functools.partial(body, mesh.shape["dp"]),
        mesh=mesh,
        in_specs=(
            P("dp", None, None),
            P("dp", None),
            P("dp", None),
            P("dp", None, None),
            P("dp", None, None),
            P("dp", None, None),
            P(None, None, "head"),
            P(None, "head"),
            P(None, "head"),
            P(None, "head"),
            P(None, "head"),
            P("head", None),
            P(),
            P(),
            P(),
            P(None, "head"),
            P("head"),
            P("head", None),
            P(),
            P(),
            P(),
            P("dp", "head", None),
        ),
        out_specs=(
            P("dp", "head", None),
            P("dp", "head", None),
            P(None, None, "head"),
            P(None, "head"),
            P(None, "head"),
            P(None, "head"),
            P(None, "head"),
            P("head", None),
            P(),
            P(),
            P(),
            P(None, "head"),
            P("head"),
            P("head", None),
            P(),
            P(),
            P(),
        ),
        check_vma=False,
    )
```

```python
import functools
import math

import jax
import jax.numpy as jnp
from jax import lax
from jax.experimental import pallas as pl
from jax.experimental.pallas import tpu as pltpu
from jax.sharding import PartitionSpec as P

B = 128

ROWS_PICK = lax.GatherDimensionNumbers(
    offset_dims=(), collapsed_slice_dims=(0,), start_index_map=(0,),
    operand_batching_dims=(1,), start_indices_batching_dims=(1,))
PACK = 16

def pick(table, index):
    return lax.gather(table, index[:, :, None], ROWS_PICK, (1, 1),
                      mode=lax.GatherScatterMode.PROMISE_IN_BOUNDS)

def lookup(tab_ref, h, at, place, masks):
    found = pick(tab_ref[h, at:at + PACK, :], place)
    for step, mask in enumerate(masks):
        low = at + PACK * (step + 1)
        found = jnp.where(mask, pick(tab_ref[h, low:low + PACK, :], place), found)
    return found.astype(jnp.float32)

def doc_span(len_ref, row, first, last):
    edge = 0
    start = 0
    stop = 0
    for k in range(len_ref.shape[1]):
        begin = edge
        edge = edge + len_ref[row, k]
        start = jnp.where(begin <= first, begin, start)
        stop = jnp.where(begin <= last, edge, stop)
    return start // B, (stop + (B - 1)) // B

def fwd_kernel(row, len_ref, q_ref, k_ref, v_ref, pad_ref, bl_ref, bh_ref, bv_ref, tab_ref,
               probs_ref, ctx_ref, kst, vst, sc):
    qb = pl.program_id(0)
    pairs = kst.shape[0]
    heads = 2 * pairs
    tiles = kst.shape[1]
    lane = lax.broadcasted_iota(jnp.int32, (B, B), 1)
    left = lane < (B // 2)

    @pl.when(qb == 0)
    def _():
        for p in range(pairs):
            for t in range(tiles):
                kt = k_ref[t * B:(t + 1) * B, p * B:(p + 1) * B]
                vt = v_ref[t * B:(t + 1) * B, p * B:(p + 1) * B]
                zero = jnp.zeros_like(kt)
                kst[p, t, 0:B, :] = jnp.where(left, kt, zero)
                kst[p, t, B:2 * B, :] = jnp.where(left, zero, kt)
                vst[p, t, 0:B, :] = jnp.where(left, vt, zero)
                vst[p, t, B:2 * B, :] = jnp.where(left, zero, vt)

    first = qb * B
    low, high = doc_span(len_ref, row, first, first + B - 1)
    sub = lax.broadcasted_iota(jnp.int32, (B, B), 0) + first
    count = len_ref.shape[1]
    edges = []
    edge = 0
    for k in range(count):
        edge = edge + len_ref[row, k]
        edges.append(edge)
    seg_q = sum(((sub >= e).astype(jnp.int32) for e in edges))

    def scores(t, top):
        key_at = lane + t * B
        seg_k = sum(((key_at >= e).astype(jnp.int32) for e in edges))
        real = jnp.broadcast_to(pad_ref[:, pl.ds(pl.multiple_of(t * B, B), B)], (B, B)) > 0
        allowed = ((seg_q == seg_k) & real) | (sub == key_at)
        at = pl.ds(pl.multiple_of(t * B, B), B)
        parts = []
        for g in range(B // PACK):
            rows = slice(g * PACK, g * PACK + PACK)
            group = []
            for ref, tiles_of in ((bl_ref, 2), (bh_ref, 4), (bv_ref, 4)):
                index = ref[rows, at].astype(jnp.int16)
                group.append((index & jnp.int16(PACK - 1),
                              [index >= jnp.int16(PACK * a) for a in range(1, tiles_of)]))
            parts.append(group)
        out = []
        for p in range(pairs):
            raw = lax.dot_general(q_ref[:, p * B:(p + 1) * B], kst[p, t], (((1,), (1,)), ((), ())),
                                  preferred_element_type=jnp.float32)
            for s in range(2):
                h = 2 * p + s
                rel = jnp.concatenate(
                    [(lookup(tab_ref, h, 0, *group[0]) + lookup(tab_ref, h, 32, *group[1]))
                     + lookup(tab_ref, h, 96, *group[2]) for group in parts], axis=0)
                val = jnp.where(allowed, raw[:, s * B:(s + 1) * B] + rel, -1000000000.0)
                sc[t, h] = val
                out.append(jnp.maximum(top[h], val))
        return tuple(out)

    start = jnp.full((B, B), -3.0e38, jnp.float32)
    top = lax.fori_loop(low, high, scores, tuple(start for _ in range(heads)))
    top = [jnp.max(x, axis=-1, keepdims=True) for x in top]

    def expo(t, tot):
        out = []
        for h in range(heads):
            e = jnp.exp(sc[t, h] - top[h])
            sc[t, h] = e
            out.append(tot[h] + e)
        return tuple(out)

    zero = jnp.zeros((B, B), jnp.float32)
    tot = lax.fori_loop(low, high, expo, tuple(zero for _ in range(heads)))
    inv = [1.0 / jnp.sum(x, axis=-1, keepdims=True) for x in tot]

    def mix(t, acc):
        out = []
        for p in range(pairs):
            low_pair = []
            for s in range(2):
                h = 2 * p + s
                pr = sc[t, h] * inv[h]
                probs_ref[t, h] = pr
                low_pair.append(pr.astype(jnp.bfloat16))
            out.append(acc[p] + jnp.dot(jnp.concatenate(low_pair, axis=1), vst[p, t],
                                        preferred_element_type=jnp.float32))
        return tuple(out)

    acc = lax.fori_loop(low, high, mix, tuple(zero for _ in range(pairs)))
    for p in range(pairs):
        ctx_ref[:, p * B:(p + 1) * B] = acc[p].astype(jnp.bfloat16)

def attn_fwd(row, lengths, q, k, v, pad, bl, bh, bv, tab):
    slots, width = q.shape[1:]
    pairs = width // B
    tiles = slots // B
    row_block = lambda n: pl.BlockSpec((None, B, n), lambda i, L: (row, i, 0))
    return pl.pallas_call(
        functools.partial(fwd_kernel, row),
        grid_spec=pltpu.PrefetchScalarGridSpec(
            num_scalar_prefetch=1, grid=(tiles,),
            in_specs=[
                row_block(width),
                pl.BlockSpec((None, slots, width), lambda i, L: (row, 0, 0)),
                pl.BlockSpec((None, slots, width), lambda i, L: (row, 0, 0)),
                pl.BlockSpec((None, 1, slots), lambda i, L: (row, 0, 0)),
                row_block(slots), row_block(slots), row_block(slots),
                pl.BlockSpec(tab.shape, lambda i, L: (0, 0, 0)),
            ],
            out_specs=[
                pl.BlockSpec((None, tiles, 2 * pairs, B, B), lambda i, L: (i, 0, 0, 0, 0)),
                pl.BlockSpec((B, width), lambda i, L: (i, 0)),
            ],
            scratch_shapes=[
                pltpu.VMEM((pairs, tiles, 2 * B, B), jnp.bfloat16),
                pltpu.VMEM((pairs, tiles, 2 * B, B), jnp.bfloat16),
                pltpu.VMEM((tiles, 2 * pairs, B, B), jnp.float32),
            ]),
        out_shape=[
            jax.ShapeDtypeStruct((tiles, tiles, 2 * pairs, B, B), jnp.float32),
            jax.ShapeDtypeStruct((slots, width), jnp.bfloat16),
        ],
        compiler_params=pltpu.CompilerParams(vmem_limit_bytes=48 << 20),
        cost_estimate=pl.CostEstimate(
            flops=4 * slots * slots * width * 8, transcendentals=0, bytes_accessed=16 << 20),
        name="attn_forward",
    )(lengths, q, k, v, pad, bl, bh, bv, tab)


NT = (((1,), (1,)), ((), ()))
TN = (((0,), (0,)), ((), ()))

def bwd_kernel(row, factor, len_ref, q_ref, k_ref, v_ref, gctx_ref, ctx_ref, probs_ref,
               *rest):
    ds_ref, three_ref, kst, vst, dkst, dvst, inner, dqs = rest[-8:]
    qb = pl.program_id(0)
    pairs, tiles = kst.shape[0], kst.shape[1]
    lane = lax.broadcasted_iota(jnp.int32, (B, B), 1)
    left = lane < (B // 2)

    @pl.when(qb == 0)
    def _():
        dkst[...] = jnp.zeros_like(dkst)
        dvst[...] = jnp.zeros_like(dvst)
        for p in range(pairs):
            for t in range(tiles):
                kt = k_ref[t * B:(t + 1) * B, p * B:(p + 1) * B]
                vt = v_ref[t * B:(t + 1) * B, p * B:(p + 1) * B]
                zero = jnp.zeros_like(kt)
                kst[p, t, 0:B, :] = jnp.where(left, kt, zero)
                kst[p, t, B:2 * B, :] = jnp.where(left, zero, kt)
                vst[p, t, 0:B, :] = jnp.where(left, vt, zero)
                vst[p, t, B:2 * B, :] = jnp.where(left, zero, vt)

    first = qb * B
    low, high = doc_span(len_ref, row, first, first + B - 1)
    sides = []
    for p in range(pairs):
        cols = slice(p * B, (p + 1) * B)
        gctx = gctx_ref[:, cols]
        prod = gctx.astype(jnp.float32) * ctx_ref[:, cols].astype(jnp.float32)
        zero = jnp.zeros_like(prod)
        for side in (jnp.where(left, prod, zero), jnp.where(left, zero, prod)):
            inner[len(sides)] = jnp.broadcast_to(jnp.sum(side, axis=-1, keepdims=True), (B, B))
            sides.append(0)
    dqs[...] = jnp.zeros_like(dqs)

    def tile(t, carry):
        for p in range(pairs):
            cols = slice(p * B, (p + 1) * B)
            gctx = gctx_ref[:, cols]
            gp = lax.dot_general(gctx, vst[p, t], NT, preferred_element_type=jnp.float32)
            probs_low, g_scores = [], []
            for s in range(2):
                pr = probs_ref[t, 2 * p + s]
                ds = (pr * (gp[:, s * B:(s + 1) * B] - inner[2 * p + s])).astype(jnp.bfloat16)
                ds_ref[t, 2 * p + s] = ds
                g_scores.append(ds)
                probs_low.append(pr.astype(jnp.bfloat16))
            ds = jnp.concatenate(g_scores, axis=1)
            mix = jnp.concatenate(probs_low, axis=1)
            dvst[p, t] += lax.dot_general(mix, gctx, TN, preferred_element_type=jnp.float32)
            dkst[p, t] += lax.dot_general(ds, q_ref[:, cols], TN, preferred_element_type=jnp.float32)
            dqs[p] += jnp.dot(ds, kst[p, t], preferred_element_type=jnp.float32)
        return carry

    lax.fori_loop(low, high, tile, 0)
    for p in range(pairs):
        three_ref[pl.ds(pl.multiple_of(first, B), B), p * B:(p + 1) * B] = (dqs[p] * factor).astype(jnp.bfloat16)

    @pl.when(qb == tiles - 1)
    def _():
        for p in range(pairs):
            for t in range(tiles):
                three_ref[t * B:(t + 1) * B, (pairs + p) * B:(pairs + p + 1) * B] = jnp.where(
                    left, dkst[p, t, 0:B, :], dkst[p, t, B:2 * B, :]).astype(jnp.bfloat16)
                three_ref[t * B:(t + 1) * B, (2 * pairs + p) * B:(2 * pairs + p + 1) * B] = jnp.where(
                    left, dvst[p, t, 0:B, :], dvst[p, t, B:2 * B, :]).astype(jnp.bfloat16)

def attn_bwd(row, factor, lengths, q, k, v, gctx, ctx, probs, kept=None):
    slots, width = q.shape[1:]
    pairs, tiles = width // B, slots // B
    part = pl.BlockSpec((B, width), lambda i, L: (i, 0))
    three = pl.BlockSpec((None, slots, 3 * width), lambda i, L: (row, 0, 0))
    mine = pl.BlockSpec((None, B, width), lambda i, L: (row, i, 0))
    whole = pl.BlockSpec((None, slots, width), lambda i, L: (row, 0, 0))
    pairs_of = pl.BlockSpec((None, tiles, 2 * pairs, B, B), lambda i, L: (i, 0, 0, 0, 0))
    kept = () if kept is None else (kept,)
    return pl.pallas_call(
        functools.partial(bwd_kernel, row, factor),
        grid_spec=pltpu.PrefetchScalarGridSpec(
            num_scalar_prefetch=1, grid=(tiles,),
            in_specs=[mine, whole, whole, part, part, pairs_of]
            + [pl.BlockSpec(memory_space=pl.ANY)] * len(kept),
            out_specs=[pairs_of, three],
            scratch_shapes=[
                pltpu.VMEM((pairs, tiles, 2 * B, B), jnp.bfloat16),
                pltpu.VMEM((pairs, tiles, 2 * B, B), jnp.bfloat16),
                pltpu.VMEM((pairs, tiles, 2 * B, B), jnp.float32),
                pltpu.VMEM((pairs, tiles, 2 * B, B), jnp.float32),
                pltpu.VMEM((2 * pairs, B, B), jnp.float32),
                pltpu.VMEM((pairs, B, B), jnp.float32),
            ]),
        out_shape=[jax.ShapeDtypeStruct(probs.shape, jnp.bfloat16),
                   jax.ShapeDtypeStruct((q.shape[0], slots, 3 * width), jnp.bfloat16)],
        input_output_aliases={7: 1} if kept else {},
        compiler_params=pltpu.CompilerParams(vmem_limit_bytes=48 << 20),
        cost_estimate=pl.CostEstimate(
            flops=8 * slots * slots * width * 8, transcendentals=0, bytes_accessed=16 << 20),
        name="attn_backward",
    )(lengths, q, k, v, gctx, ctx, probs, *kept)

BINS = 160


def hist_kernel(row, step, len_ref, bl_ref, bh_ref, bv_ref, ds_ref, out_ref, even, odd):
    tiles, heads = ds_ref.shape[0], ds_ref.shape[1]
    docs = len_ref.shape[1]
    lane = lax.broadcasted_iota(jnp.int32, (PACK, B), 1)
    sub = lax.broadcasted_iota(jnp.int32, (PACK, B), 0)
    even[...] = jnp.zeros_like(even)
    odd[...] = jnp.zeros_like(odd)

    floor, roof = step * B, (step + 1) * B
    starts, ends, firsts, lasts, upto = [], [], [], [], []
    edge, count = 0, 0
    for d in range(docs):
        starts.append(edge)
        edge = edge + len_ref[row, d]
        ends.append(edge)
        firsts.append(jnp.maximum(starts[d], floor))
        lasts.append(jnp.maximum(jnp.minimum(edge, roof), firsts[d]))
        here = (lasts[d] + (PACK - 1)) // PACK - firsts[d] // PACK
        count = count + jnp.where(lasts[d] > firsts[d], here, 0)
        upto.append(count)

    def group(g, spread):
        start, end, first, last = starts[0], ends[0], firsts[0], lasts[0]
        block = firsts[0] // PACK + g
        for d in range(1, docs):
            past = g >= upto[d - 1]
            start, end, first, last, block = (
                jnp.where(past, new, old) for new, old in
                ((starts[d], start), (ends[d], end), (firsts[d], first), (lasts[d], last),
                 (firsts[d] // PACK + (g - upto[d - 1]), block)))
        last = jnp.where(g < count, last, first)
        start = jnp.minimum(start, tiles * B - 1)
        block = jnp.clip(block - step * (B // PACK), 0, B // PACK - 1)
        tile = start // B
        left = start - tile * B
        turn = jnp.where(left == 0, 0, B - left)
        rows = pl.ds(pl.multiple_of(block * PACK, PACK), PACK)
        token = sub + (floor + block * PACK)
        inside = (token >= first) & (token < last)
        lives = [inside & (lane + part * B < end - start) for part in range(2)]
        before = lane < B - left
        spots = [jnp.minimum(tile + part, tiles - 1) for part in range(3)]

        def moved(parts):
            parts = [pltpu.roll(p, turn, 1) for p in parts]
            return [jnp.where(before, parts[part], parts[part + 1]) for part in range(2)]

        for h in range(heads):
            vals = moved([ds_ref[s, h, rows, :].astype(jnp.float32) for s in spots])
            for part in range(2):
                spread[part, pl.ds(h, PACK, stride=8), :] = jnp.where(lives[part], vals[part], 0.0)
        codes = []
        for s in spots:
            at = pl.ds(pl.multiple_of(s * B, B), B)
            codes.append(bl_ref[rows, at] + 32 * bh_ref[rows, at] + 2048 * bv_ref[rows, at])
        code = jnp.concatenate(moved(codes), axis=1)
        index = [(code & 31).astype(jnp.int16), ((code >> 5) & 63).astype(jnp.int16),
                 (code >> 11).astype(jnp.int16)]
        one, zero = jnp.ones((), jnp.bfloat16), jnp.zeros((), jnp.bfloat16)
        grads, hots = [], []
        for r in range(PACK):
            hot = []
            for ix, n in zip(index, (32, 64, 64)):
                bins = lax.broadcasted_iota(jnp.int16, (n, 2 * B), 0)
                line = jnp.broadcast_to(ix[r:r + 1, :], (n, 2 * B))
                hot.append(jnp.where(bins == line, one, zero))
            hots.append(jnp.concatenate(hot, axis=0))
            grads += [spread[part, r * 8:r * 8 + 8, :].astype(jnp.bfloat16) for part in range(2)]
        return lax.dot_general(jnp.concatenate(grads, axis=1), jnp.concatenate(hots, axis=1), NT,
                               preferred_element_type=jnp.float32)

    def two(step, sums):
        return sums[0] + group(2 * step, even), sums[1] + group(2 * step + 1, odd)

    none = jnp.zeros((8, BINS), jnp.float32)
    sums = lax.fori_loop(0, (count + 1) // 2, two, (none, none))
    out_ref[...] = sums[0] + sums[1]


def table_grads(row, step, lengths, bl, bh, bv, ds):
    slots = bl.shape[1]
    tiles, heads = ds.shape[0], ds.shape[2]
    block = pl.BlockSpec((None, B, slots), lambda i, L: (row, step, 0))
    return pl.pallas_call(
        functools.partial(hist_kernel, row, step),
        grid_spec=pltpu.PrefetchScalarGridSpec(
            num_scalar_prefetch=1, grid=(1,),
            in_specs=[block, block, block,
                      pl.BlockSpec((None, tiles, heads, B, B), lambda i, L: (step, 0, 0, 0, 0))],
            out_specs=pl.BlockSpec((8, BINS), lambda i, L: (0, 0)),
            scratch_shapes=[
                pltpu.VMEM((2, 8 * PACK, B), jnp.float32),
                pltpu.VMEM((2, 8 * PACK, B), jnp.float32),
            ]),
        out_shape=jax.ShapeDtypeStruct((8, BINS), jnp.float32),
        compiler_params=pltpu.CompilerParams(vmem_limit_bytes=48 << 20),
        cost_estimate=pl.CostEstimate(
            flops=4 * slots * slots * 384 * 8, transcendentals=0, bytes_accessed=2 << 20),
        name="table_grads",
    )(lengths, bl, bh, bv, ds)


f32, low = jnp.float32, jnp.bfloat16
SWAP = [(0, 1), (1, 0)]


def normalize(values):
    mean = jnp.mean(values, axis=-1, keepdims=True)
    centered = values - mean
    scale = lax.rsqrt(jnp.mean(centered * centered, axis=-1, keepdims=True) + 1e-12)
    return centered * scale, scale


def normalize_back(grad, normed, scale, gain):
    scaled = grad * gain
    first = jnp.mean(scaled, axis=-1, keepdims=True)
    second = jnp.mean(scaled * normed, axis=-1, keepdims=True)
    return scale * (scaled - first - normed * second)


def times(left, right, left_dim, right_dim):
    return lax.dot_general(left, right, (((left_dim,), (right_dim,)), ((), ())),
                           preferred_element_type=f32)


def flips(count, bit):
    return [(i, i ^ (1 << bit)) for i in range(count)]


def to_peer(values):
    return lax.ppermute(values, "head", SWAP)


def plus(left, right):
    return (left.astype(f32) + right.astype(f32)).astype(low)


def in_order(bit_value, mine, other):
    return jnp.where(bit_value == 0, jnp.stack([mine, other]), jnp.stack([other, mine]))


class Order:
    def __init__(self):
        self.last = None

    def tie(self, values):
        if self.last is None:
            return values
        values, self.last = lax.optimization_barrier((values, self.last))
        return values

    def mark(self, values):
        self.last = values


def total(terms, lift, size, axis):
    return sum(lax.dynamic_slice_in_dim(values, start + lift, size, axis).astype(f32)
               for values, start in terms)


def halve(order, terms, size, axis, count, bit):
    half = size // 2
    mine = (lax.axis_index("dp") >> bit) & 1
    send = total(terms, (1 - mine) * half, half, axis).astype(low)
    order.mark(send)
    got = lax.ppermute(send, "dp", flips(count, bit))
    yield
    return [(values, start + mine * half) for values, start in terms] + [(order.tie(got), 0)]


def gather_steps(order, values, count, bits):
    index = lax.axis_index("dp")
    for bit in reversed(bits):
        order.mark(values)
        got = lax.ppermute(values, "dp", flips(count, bit))
        yield
        both = in_order((index >> bit) & 1, values, order.tie(got))
        values = both.reshape((2 * values.shape[0],) + values.shape[1:])
    return values


def unit_steps(order, kept, given, count, axis, split, out):
    bits = list(range(1, count.bit_length() - 1))
    size = kept.shape[axis]
    order.mark(given)
    got = lax.ppermute(given, "dp", flips(count, 0))
    yield
    terms = [(kept, 0), (order.tie(got), 0)]
    terms = yield from halve(order, terms, size, axis, count, bits[0])
    size //= 2
    mine, other = ([(split(values)[c], start) for values, start in terms] for c in range(2))
    send = total(other, 0, size, 0).astype(low)
    order.mark(send)
    got = to_peer(send)
    yield
    terms = mine + [(order.tie(got), 0)]
    for bit in bits[1:]:
        terms = yield from halve(order, terms, size, 0, count, bit)
        size //= 2
    mine = yield from gather_steps(order, total(terms, 0, size, 0).astype(low), count, bits)
    order.mark(mine)
    other = lax.ppermute(mine, "dp", flips(count, 0))
    yield
    out += [mine, order.tie(other)]


def buffer_steps(order, values, count, out):
    bits = list(range(count.bit_length() - 1))
    size = values.shape[0]
    terms = [(values, 0)]
    for bit in bits:
        terms = yield from halve(order, terms, size, 0, count, bit)
        size //= 2
    values = yield from gather_steps(order, total(terms, 0, size, 0).astype(low), count, bits)
    order.mark(values)
    out.append(values)


def advance(*chains):
    for chain in chains:
        next(chain, None)


def finish(*chains):
    left = list(chains)
    while left:
        for chain in list(left):
            try:
                next(chain)
            except StopIteration:
                left.remove(chain)


def body(
    count,
    hidden,
    lengths,
    padding,
    bucket_line,
    bucket_horizontal,
    bucket_vertical,
    attn_project,
    attn_bias,
    table_line,
    table_horizontal,
    table_vertical,
    out_project,
    out_bias,
    attn_gain,
    attn_shift,
    hidden_project,
    hidden_bias,
    down_project,
    down_bias,
    final_gain,
    final_shift,
    cotangent,
):
    rows, slots, width = hidden.shape
    half = cotangent.shape[1]
    heads = table_line.shape[1]
    local = attn_project.shape[2]
    units = hidden_project.shape[1]
    part = units // 2
    factor = 1.0 / math.sqrt(local // heads)
    head = lax.axis_index("head")
    index = lax.axis_index("dp")
    core = index & 1
    offset = head * half
    every = list(range(count.bit_length() - 1))

    def split(values, dim):
        return [lax.dynamic_slice_in_dim(values, c * part, part, dim) for c in (core, 1 - core)]

    def joined(own_parts, got, dim):
        mine, rest = own_parts
        beside = lax.ppermute(got, "dp", flips(count, 0))
        return [jnp.concatenate([mine, got], axis=dim), jnp.concatenate([rest, beside], axis=dim)]

    up_mine = lax.dynamic_slice_in_dim(hidden_project, core * part, part, 1)
    up_got = to_peer(up_mine)
    up_mine, hidden, hidden_project, down_project = lax.optimization_barrier(
        (up_mine, hidden, hidden_project, down_project))
    up_parts = [up_mine, lax.dynamic_slice_in_dim(hidden_project, (1 - core) * part, part, 1)]
    down_parts = split(down_project, 0)
    down_got = to_peer(down_parts[0])
    bias_got = to_peer(hidden_bias)
    biases = [jnp.concatenate([x, y]) for x, y in zip(split(hidden_bias, 0), split(bias_got, 0))]

    tables = jnp.concatenate([table_line, table_horizontal, table_vertical], axis=0)
    bins = tables.shape[0]
    tables = jnp.broadcast_to(tables.T[:, :, None], (heads, bins, B))
    pad = padding[:, None, :]
    bucket_line, bucket_horizontal, bucket_vertical = (
        pltpu.with_memory_space_constraint(x, pltpu.HBM)
        for x in (bucket_line, bucket_horizontal, bucket_vertical))

    flat = hidden.reshape(rows * slots, width)
    query = ((times(flat, attn_project[0], 1, 0) + attn_bias[0].astype(f32)).astype(low)
             * jnp.asarray(factor, low))
    key = times(flat, attn_project[1], 1, 0).astype(low)
    value = (times(flat, attn_project[2], 1, 0) + attn_bias[1].astype(f32)).astype(low)
    query, key, value = (x.reshape(rows, slots, local) for x in (query, key, value))

    gain_first = attn_gain.astype(f32)
    shift_first = attn_shift.astype(f32)
    gain_last = final_gain.astype(f32)
    shift_last = final_shift.astype(f32)

    def own(values):
        return lax.dynamic_slice_in_dim(values, offset, half, 0)

    def others(values):
        return lax.dynamic_slice_in_dim(values, half - offset, half, 0)

    fronts, attn_sum = [], []
    for r in range(rows):
        if r == 1:
            lengths, up_got = lax.optimization_barrier((lengths, up_got))
        probs, context = attn_fwd(r, lengths, query, key, value, pad, bucket_line,
                                  bucket_horizontal, bucket_vertical, tables)
        fronts.append((probs, context))
        send = times(others(context), out_project, 1, 0).astype(low)
        got = to_peer(send)
        attn_sum.append(times(own(context), out_project, 1, 0) + got.astype(f32))
    ups, downs = joined(up_parts, up_got, 1), joined(down_parts, down_got, 0)
    tokens = lax.dynamic_slice_in_dim(hidden, offset, half, 1).reshape(rows * half, width).astype(f32)
    normed, scale = normalize(tokens + jnp.concatenate(attn_sum, axis=0) + out_bias.astype(f32))
    mid = normed * gain_first + shift_first
    mid_low = mid.astype(low)

    actives, slopes = [], []
    total = None
    for up, down, bias in zip(ups, downs, biases):
        inner = times(mid_low, up, 1, 0) + bias.astype(f32)
        bell = 0.5 * (1.0 + lax.erf(inner * math.sqrt(0.5)))
        actives.append((inner * bell).astype(low))
        slopes.append(bell + inner * (jnp.exp(-0.5 * inner * inner) * (1.0 / math.sqrt(2.0 * math.pi))))
        term = times(actives[-1], down, 1, 0)
        total = term if total is None else total + term
    normed_final, scale_final = normalize(mid + total + down_bias.astype(f32))
    output = (normed_final * gain_last + shift_last).astype(low).reshape(rows, half, width)

    above = cotangent.reshape(rows * half, width).astype(f32)
    g_final = normalize_back(above, normed_final, scale_final, gain_last)
    g_low = g_final.astype(low)
    order = Order()
    total = None
    grads_bias, inners = [], []
    for up, down, slope in zip(ups, downs, slopes):
        g_inner = (times(g_low, down, 1, 1) * slope).astype(low)
        inners.append(g_inner)
        grads_bias.append(jnp.sum(g_inner.astype(f32), axis=0))
        term = times(g_inner, up, 1, 1)
        total = term if total is None else total + term
    g_mid = g_final + total
    g_attn = normalize_back(g_mid, normed, scale, gain_first)
    g_attn_low = g_attn.astype(low).reshape(rows, half, width)
    g_others = [to_peer(g_attn_low[r]) for r in range(rows)]
    order.mark(g_attn_low)
    down_out, up_out, attn_out = [], [], []
    g_low = order.tie(g_low)
    kept, given = (times(active, g_low, 0, 0).astype(low) for active in actives)
    down_chain = unit_steps(order, *(x.reshape(2, part, width) for x in (kept, given)), count, 1,
                            lambda v: (v[0], v[1]), down_out)
    advance(down_chain)
    mid_low = order.tie(mid_low)
    kept, given = (times(mid_low, g_inner, 0, 0).astype(low) for g_inner in inners)
    up_chain = unit_steps(order, kept, given, count, 0, lambda v: (v[:, :part], v[:, part:]), up_out)
    advance(up_chain, down_chain)
    g_attn = g_attn.reshape(rows, half, width)

    marks, three, grad_out = [], None, 0.0
    for r in range(rows):
        probs, context = fronts[r]
        g_all = in_order(head, g_attn_low[r], order.tie(g_others[r])).reshape(slots, width)
        g_context = times(g_all, out_project, 1, 1).astype(low)
        g_scores, three = attn_bwd(r, factor, lengths, query, key, value, g_context, context, probs, three)
        order.mark(g_scores)
        marks.append(g_scores)
        grad_out = grad_out + times(context, g_all, 0, 0)
        advance(up_chain if r == 0 else down_chain)
    grad_attn = times(flat, three.reshape(rows * slots, 3 * local), 0, 0).astype(low)
    grad_out = jnp.concatenate([grad_out[:, :local], grad_out[:, local:]], axis=0).astype(low)
    attn_chain = buffer_steps(order, jnp.concatenate([grad_attn, grad_out], axis=1), count, attn_out)
    advance(attn_chain)
    every_project = jnp.concatenate([attn_project[c] for c in range(3)], axis=1)
    theirs = lax.dynamic_slice_in_dim(order.tie(three), half - offset, half, 1)
    give = times(theirs.reshape(rows * half, 3 * local), every_project, 1, 1).astype(low)
    mine = lax.dynamic_slice_in_dim(three, offset, half, 1)
    mine = times(mine.reshape(rows * half, 3 * local), every_project, 1, 1)
    grads_in = mine.reshape(rows, half, width) + g_attn
    give, grads_in = lax.optimization_barrier((give, grads_in))
    order.mark(grads_in)
    grads_in = grads_in + to_peer(give).astype(f32).reshape(rows, half, width)

    tables_out = []
    blocks = [(r, block) for r in range(rows) for block in range(slots // B)]
    chains = {"D": down_chain, "U": up_chain, "A": attn_chain}
    for name in "ADTUTDATTUADTTUTATDUADUADU":
        if name == "T":
            r, block = blocks[len(tables_out)]
            tables_out.append(table_grads(r, block, order.tie(lengths), bucket_line,
                                          bucket_horizontal, bucket_vertical, marks[r]))
            order.mark(tables_out[-1])
        else:
            advance(chains[name])
    bias_sums = jnp.sum(three.astype(f32), axis=(0, 1))
    marks = sum(tables_out)[:heads].T
    finish(down_chain, attn_chain, up_chain)
    grad_down = in_order(core, *down_out).reshape(down_project.shape).astype(f32)
    mine, other = up_out
    grad_up = jnp.where(core == 0, jnp.concatenate([mine, other], axis=1),
                        jnp.concatenate([other, mine], axis=1)).astype(f32)
    buffer = attn_out[0].astype(f32)
    grad_attn = jnp.stack([buffer[:, c * local:(c + 1) * local] for c in range(3)])
    grad_out = jnp.concatenate([buffer[:local, 3 * local:], buffer[local:, 3 * local:]], axis=1)

    def placed(pieces):
        mine = jnp.concatenate(pieces)
        return jnp.where(jnp.arange(2, dtype=jnp.int32)[:, None] == head, mine[None], 0.0).reshape(-1)

    bias_sets = in_order(core, *grads_bias)
    mine, other = bias_sets[:, :part].reshape(-1), bias_sets[:, part:].reshape(-1)
    bias_both = in_order(head, mine, other).reshape(-1)
    packed = jnp.concatenate([
        jnp.sum(g_attn, axis=(0, 1)),
        jnp.sum(g_mid * normed, axis=0),
        jnp.sum(g_mid, axis=0),
        jnp.sum(g_final, axis=0),
        jnp.sum(above * normed_final, axis=0),
        jnp.sum(above, axis=0),
        bias_both,
        placed([marks.reshape(-1), bias_sums[:local], bias_sums[2 * local:]]),
    ])
    packed = packed + to_peer(packed)
    for bit in every:
        packed = packed + lax.ppermute(packed, "dp", flips(count, bit))
    shared = packed[:6 * width].reshape(6, width)
    grad_bias = lax.dynamic_slice_in_dim(packed, 6 * width + head * units, units, 0)
    size = marks.size + 2 * local
    mine = lax.dynamic_slice_in_dim(packed, 6 * width + 2 * units + head * size, size, 0)
    marks = mine[:bins * heads].reshape(bins, heads)
    first, second = table_line.shape[0], table_horizontal.shape[0]
    return (
        output,
        grads_in,
        grad_attn,
        mine[bins * heads:].reshape(2, local),
        marks[:first],
        marks[first:first + second],
        marks[first + second:],
        grad_out,
        shared[0],
        shared[1],
        shared[2],
        grad_up,
        grad_bias,
        grad_down,
        shared[3],
        shared[4],
        shared[5],
    )


def solution(mesh):
    return jax.shard_map(
        functools.partial(body, mesh.shape["dp"]),
        mesh=mesh,
        in_specs=(
            P("dp", None, None),
            P("dp", None),
            P("dp", None),
            P("dp", None, None),
            P("dp", None, None),
            P("dp", None, None),
            P(None, None, "head"),
            P(None, "head"),
            P(None, "head"),
            P(None, "head"),
            P(None, "head"),
            P("head", None),
            P(),
            P(),
            P(),
            P(None, "head"),
            P("head"),
            P("head", None),
            P(),
            P(),
            P(),
            P("dp", "head", None),
        ),
        out_specs=(
            P("dp", "head", None),
            P("dp", "head", None),
            P(None, None, "head"),
            P(None, "head"),
            P(None, "head"),
            P(None, "head"),
            P(None, "head"),
            P("head", None),
            P(),
            P(),
            P(),
            P(None, "head"),
            P("head"),
            P("head", None),
            P(),
            P(),
            P(),
        ),
        check_vma=False,
    )
```

```python
import functools
import math

import jax
import jax.numpy as jnp
from jax import lax
from jax.experimental import pallas as pl
from jax.experimental.pallas import tpu as pltpu
from jax.sharding import PartitionSpec as P

B = 128

ROWS_PICK = lax.GatherDimensionNumbers(
    offset_dims=(), collapsed_slice_dims=(0,), start_index_map=(0,),
    operand_batching_dims=(1,), start_indices_batching_dims=(1,))
PACK = 16

def pick(table, index):
    return lax.gather(table, index[:, :, None], ROWS_PICK, (1, 1),
                      mode=lax.GatherScatterMode.PROMISE_IN_BOUNDS)

def lookup(tab_ref, h, at, place, masks):
    found = pick(tab_ref[h, at:at + PACK, :], place)
    for step, mask in enumerate(masks):
        low = at + PACK * (step + 1)
        found = jnp.where(mask, pick(tab_ref[h, low:low + PACK, :], place), found)
    return found.astype(jnp.float32)

def doc_span(len_ref, row, first, last):
    edge = 0
    start = 0
    stop = 0
    for k in range(len_ref.shape[1]):
        begin = edge
        edge = edge + len_ref[row, k]
        start = jnp.where(begin <= first, begin, start)
        stop = jnp.where(begin <= last, edge, stop)
    return start // B, (stop + (B - 1)) // B

def fwd_kernel(row, len_ref, q_ref, k_ref, v_ref, pad_ref, bl_ref, bh_ref, bv_ref, tab_ref,
               probs_ref, ctx_ref, kst, vst, sc):
    qb = pl.program_id(0)
    pairs = kst.shape[0]
    heads = 2 * pairs
    tiles = kst.shape[1]
    lane = lax.broadcasted_iota(jnp.int32, (B, B), 1)
    left = lane < (B // 2)

    @pl.when(qb == 0)
    def _():
        for p in range(pairs):
            for t in range(tiles):
                kt = k_ref[t * B:(t + 1) * B, p * B:(p + 1) * B]
                vt = v_ref[t * B:(t + 1) * B, p * B:(p + 1) * B]
                zero = jnp.zeros_like(kt)
                kst[p, t, 0:B, :] = jnp.where(left, kt, zero)
                kst[p, t, B:2 * B, :] = jnp.where(left, zero, kt)
                vst[p, t, 0:B, :] = jnp.where(left, vt, zero)
                vst[p, t, B:2 * B, :] = jnp.where(left, zero, vt)

    first = qb * B
    low, high = doc_span(len_ref, row, first, first + B - 1)
    sub = lax.broadcasted_iota(jnp.int32, (B, B), 0) + first
    count = len_ref.shape[1]
    edges = []
    edge = 0
    for k in range(count):
        edge = edge + len_ref[row, k]
        edges.append(edge)
    seg_q = sum(((sub >= e).astype(jnp.int32) for e in edges))

    def scores(t, top):
        key_at = lane + t * B
        seg_k = sum(((key_at >= e).astype(jnp.int32) for e in edges))
        real = jnp.broadcast_to(pad_ref[:, pl.ds(pl.multiple_of(t * B, B), B)], (B, B)) > 0
        allowed = ((seg_q == seg_k) & real) | (sub == key_at)
        at = pl.ds(pl.multiple_of(t * B, B), B)
        parts = []
        for g in range(B // PACK):
            rows = slice(g * PACK, g * PACK + PACK)
            group = []
            for ref, tiles_of in ((bl_ref, 2), (bh_ref, 4), (bv_ref, 4)):
                index = ref[rows, at].astype(jnp.int16)
                group.append((index & jnp.int16(PACK - 1),
                              [index >= jnp.int16(PACK * a) for a in range(1, tiles_of)]))
            parts.append(group)
        out = []
        for p in range(pairs):
            raw = lax.dot_general(q_ref[:, p * B:(p + 1) * B], kst[p, t], (((1,), (1,)), ((), ())),
                                  preferred_element_type=jnp.float32)
            for s in range(2):
                h = 2 * p + s
                rel = jnp.concatenate(
                    [(lookup(tab_ref, h, 0, *group[0]) + lookup(tab_ref, h, 32, *group[1]))
                     + lookup(tab_ref, h, 96, *group[2]) for group in parts], axis=0)
                val = jnp.where(allowed, raw[:, s * B:(s + 1) * B] + rel, -1000000000.0)
                sc[t, h] = val
                out.append(jnp.maximum(top[h], val))
        return tuple(out)

    start = jnp.full((B, B), -3.0e38, jnp.float32)
    top = lax.fori_loop(low, high, scores, tuple(start for _ in range(heads)))
    top = [jnp.max(x, axis=-1, keepdims=True) for x in top]

    def expo(t, tot):
        out = []
        for h in range(heads):
            e = jnp.exp(sc[t, h] - top[h])
            sc[t, h] = e
            out.append(tot[h] + e)
        return tuple(out)

    zero = jnp.zeros((B, B), jnp.float32)
    tot = lax.fori_loop(low, high, expo, tuple(zero for _ in range(heads)))
    inv = [1.0 / jnp.sum(x, axis=-1, keepdims=True) for x in tot]

    def mix(t, acc):
        out = []
        for p in range(pairs):
            low_pair = []
            for s in range(2):
                h = 2 * p + s
                pr = sc[t, h] * inv[h]
                probs_ref[t, h] = pr
                low_pair.append(pr.astype(jnp.bfloat16))
            out.append(acc[p] + jnp.dot(jnp.concatenate(low_pair, axis=1), vst[p, t],
                                        preferred_element_type=jnp.float32))
        return tuple(out)

    acc = lax.fori_loop(low, high, mix, tuple(zero for _ in range(pairs)))
    for p in range(pairs):
        ctx_ref[:, p * B:(p + 1) * B] = acc[p].astype(jnp.bfloat16)

def attn_fwd(row, lengths, q, k, v, pad, bl, bh, bv, tab):
    slots, width = q.shape[1:]
    pairs = width // B
    tiles = slots // B
    row_block = lambda n: pl.BlockSpec((None, B, n), lambda i, L: (row, i, 0))
    return pl.pallas_call(
        functools.partial(fwd_kernel, row),
        grid_spec=pltpu.PrefetchScalarGridSpec(
            num_scalar_prefetch=1, grid=(tiles,),
            in_specs=[
                row_block(width),
                pl.BlockSpec((None, slots, width), lambda i, L: (row, 0, 0)),
                pl.BlockSpec((None, slots, width), lambda i, L: (row, 0, 0)),
                pl.BlockSpec((None, 1, slots), lambda i, L: (row, 0, 0)),
                row_block(slots), row_block(slots), row_block(slots),
                pl.BlockSpec(tab.shape, lambda i, L: (0, 0, 0)),
            ],
            out_specs=[
                pl.BlockSpec((None, tiles, 2 * pairs, B, B), lambda i, L: (i, 0, 0, 0, 0)),
                pl.BlockSpec((B, width), lambda i, L: (i, 0)),
            ],
            scratch_shapes=[
                pltpu.VMEM((pairs, tiles, 2 * B, B), jnp.bfloat16),
                pltpu.VMEM((pairs, tiles, 2 * B, B), jnp.bfloat16),
                pltpu.VMEM((tiles, 2 * pairs, B, B), jnp.float32),
            ]),
        out_shape=[
            jax.ShapeDtypeStruct((tiles, tiles, 2 * pairs, B, B), jnp.float32),
            jax.ShapeDtypeStruct((slots, width), jnp.bfloat16),
        ],
        compiler_params=pltpu.CompilerParams(vmem_limit_bytes=48 << 20),
        cost_estimate=pl.CostEstimate(flops=1, transcendentals=0, bytes_accessed=1),
        name="attn_forward",
    )(lengths, q, k, v, pad, bl, bh, bv, tab)


NT = (((1,), (1,)), ((), ()))
TN = (((0,), (0,)), ((), ()))

def bwd_kernel(row, factor, len_ref, q_ref, k_ref, v_ref, gctx_ref, ctx_ref, probs_ref,
               *rest):
    ds_ref, three_ref, kst, vst, dkst, dvst, inner, dqs = rest[-8:]
    qb = pl.program_id(0)
    pairs, tiles = kst.shape[0], kst.shape[1]
    lane = lax.broadcasted_iota(jnp.int32, (B, B), 1)
    left = lane < (B // 2)

    @pl.when(qb == 0)
    def _():
        dkst[...] = jnp.zeros_like(dkst)
        dvst[...] = jnp.zeros_like(dvst)
        for p in range(pairs):
            for t in range(tiles):
                kt = k_ref[t * B:(t + 1) * B, p * B:(p + 1) * B]
                vt = v_ref[t * B:(t + 1) * B, p * B:(p + 1) * B]
                zero = jnp.zeros_like(kt)
                kst[p, t, 0:B, :] = jnp.where(left, kt, zero)
                kst[p, t, B:2 * B, :] = jnp.where(left, zero, kt)
                vst[p, t, 0:B, :] = jnp.where(left, vt, zero)
                vst[p, t, B:2 * B, :] = jnp.where(left, zero, vt)

    first = qb * B
    low, high = doc_span(len_ref, row, first, first + B - 1)
    sides = []
    for p in range(pairs):
        cols = slice(p * B, (p + 1) * B)
        gctx = gctx_ref[:, cols]
        prod = gctx.astype(jnp.float32) * ctx_ref[:, cols].astype(jnp.float32)
        zero = jnp.zeros_like(prod)
        for side in (jnp.where(left, prod, zero), jnp.where(left, zero, prod)):
            inner[len(sides)] = jnp.broadcast_to(jnp.sum(side, axis=-1, keepdims=True), (B, B))
            sides.append(0)
    dqs[...] = jnp.zeros_like(dqs)

    def tile(t, carry):
        for p in range(pairs):
            cols = slice(p * B, (p + 1) * B)
            gctx = gctx_ref[:, cols]
            gp = lax.dot_general(gctx, vst[p, t], NT, preferred_element_type=jnp.float32)
            probs_low, g_scores = [], []
            for s in range(2):
                pr = probs_ref[t, 2 * p + s]
                ds = (pr * (gp[:, s * B:(s + 1) * B] - inner[2 * p + s])).astype(jnp.bfloat16)
                ds_ref[t, 2 * p + s] = ds
                g_scores.append(ds)
                probs_low.append(pr.astype(jnp.bfloat16))
            ds = jnp.concatenate(g_scores, axis=1)
            mix = jnp.concatenate(probs_low, axis=1)
            dvst[p, t] += lax.dot_general(mix, gctx, TN, preferred_element_type=jnp.float32)
            dkst[p, t] += lax.dot_general(ds, q_ref[:, cols], TN, preferred_element_type=jnp.float32)
            dqs[p] += jnp.dot(ds, kst[p, t], preferred_element_type=jnp.float32)
        return carry

    lax.fori_loop(low, high, tile, 0)
    for p in range(pairs):
        three_ref[pl.ds(pl.multiple_of(first, B), B), p * B:(p + 1) * B] = (dqs[p] * factor).astype(jnp.bfloat16)

    @pl.when(qb == tiles - 1)
    def _():
        for p in range(pairs):
            for t in range(tiles):
                three_ref[t * B:(t + 1) * B, (pairs + p) * B:(pairs + p + 1) * B] = jnp.where(
                    left, dkst[p, t, 0:B, :], dkst[p, t, B:2 * B, :]).astype(jnp.bfloat16)
                three_ref[t * B:(t + 1) * B, (2 * pairs + p) * B:(2 * pairs + p + 1) * B] = jnp.where(
                    left, dvst[p, t, 0:B, :], dvst[p, t, B:2 * B, :]).astype(jnp.bfloat16)

def attn_bwd(row, factor, lengths, q, k, v, gctx, ctx, probs, kept=None):
    slots, width = q.shape[1:]
    pairs, tiles = width // B, slots // B
    part = pl.BlockSpec((B, width), lambda i, L: (i, 0))
    three = pl.BlockSpec((None, slots, 3 * width), lambda i, L: (row, 0, 0))
    mine = pl.BlockSpec((None, B, width), lambda i, L: (row, i, 0))
    whole = pl.BlockSpec((None, slots, width), lambda i, L: (row, 0, 0))
    pairs_of = pl.BlockSpec((None, tiles, 2 * pairs, B, B), lambda i, L: (i, 0, 0, 0, 0))
    kept = () if kept is None else (kept,)
    return pl.pallas_call(
        functools.partial(bwd_kernel, row, factor),
        grid_spec=pltpu.PrefetchScalarGridSpec(
            num_scalar_prefetch=1, grid=(tiles,),
            in_specs=[mine, whole, whole, part, part, pairs_of]
            + [pl.BlockSpec(memory_space=pl.ANY)] * len(kept),
            out_specs=[pairs_of, three],
            scratch_shapes=[
                pltpu.VMEM((pairs, tiles, 2 * B, B), jnp.bfloat16),
                pltpu.VMEM((pairs, tiles, 2 * B, B), jnp.bfloat16),
                pltpu.VMEM((pairs, tiles, 2 * B, B), jnp.float32),
                pltpu.VMEM((pairs, tiles, 2 * B, B), jnp.float32),
                pltpu.VMEM((2 * pairs, B, B), jnp.float32),
                pltpu.VMEM((pairs, B, B), jnp.float32),
            ]),
        out_shape=[jax.ShapeDtypeStruct(probs.shape, jnp.bfloat16),
                   jax.ShapeDtypeStruct((q.shape[0], slots, 3 * width), jnp.bfloat16)],
        input_output_aliases={7: 1} if kept else {},
        compiler_params=pltpu.CompilerParams(vmem_limit_bytes=48 << 20),
        cost_estimate=pl.CostEstimate(flops=1, transcendentals=0, bytes_accessed=1),
        name="attn_backward",
    )(lengths, q, k, v, gctx, ctx, probs, *kept)

BINS = 160


def hist_kernel(row, step, len_ref, bl_ref, bh_ref, bv_ref, ds_ref, out_ref, even, odd):
    tiles, heads = ds_ref.shape[0], ds_ref.shape[1]
    docs = len_ref.shape[1]
    lane = lax.broadcasted_iota(jnp.int32, (PACK, B), 1)
    sub = lax.broadcasted_iota(jnp.int32, (PACK, B), 0)
    even[...] = jnp.zeros_like(even)
    odd[...] = jnp.zeros_like(odd)

    floor, roof = step * B, (step + 1) * B
    starts, ends, firsts, lasts, upto = [], [], [], [], []
    edge, count = 0, 0
    for d in range(docs):
        starts.append(edge)
        edge = edge + len_ref[row, d]
        ends.append(edge)
        firsts.append(jnp.maximum(starts[d], floor))
        lasts.append(jnp.maximum(jnp.minimum(edge, roof), firsts[d]))
        here = (lasts[d] + (PACK - 1)) // PACK - firsts[d] // PACK
        count = count + jnp.where(lasts[d] > firsts[d], here, 0)
        upto.append(count)

    def group(g, spread):
        start, end, first, last = starts[0], ends[0], firsts[0], lasts[0]
        block = firsts[0] // PACK + g
        for d in range(1, docs):
            past = g >= upto[d - 1]
            start, end, first, last, block = (
                jnp.where(past, new, old) for new, old in
                ((starts[d], start), (ends[d], end), (firsts[d], first), (lasts[d], last),
                 (firsts[d] // PACK + (g - upto[d - 1]), block)))
        last = jnp.where(g < count, last, first)
        start = jnp.minimum(start, tiles * B - 1)
        block = jnp.clip(block - step * (B // PACK), 0, B // PACK - 1)
        tile = start // B
        left = start - tile * B
        turn = jnp.where(left == 0, 0, B - left)
        rows = pl.ds(pl.multiple_of(block * PACK, PACK), PACK)
        token = sub + (floor + block * PACK)
        inside = (token >= first) & (token < last)
        lives = [inside & (lane + part * B < end - start) for part in range(2)]
        before = lane < B - left
        spots = [jnp.minimum(tile + part, tiles - 1) for part in range(3)]

        def moved(parts):
            parts = [pltpu.roll(p, turn, 1) for p in parts]
            return [jnp.where(before, parts[part], parts[part + 1]) for part in range(2)]

        for h in range(heads):
            vals = moved([ds_ref[s, h, rows, :].astype(jnp.float32) for s in spots])
            for part in range(2):
                spread[part, pl.ds(h, PACK, stride=8), :] = jnp.where(lives[part], vals[part], 0.0)
        codes = []
        for s in spots:
            at = pl.ds(pl.multiple_of(s * B, B), B)
            codes.append(bl_ref[rows, at] + 32 * bh_ref[rows, at] + 2048 * bv_ref[rows, at])
        code = jnp.concatenate(moved(codes), axis=1)
        index = [(code & 31).astype(jnp.int16), ((code >> 5) & 63).astype(jnp.int16),
                 (code >> 11).astype(jnp.int16)]
        one, zero = jnp.ones((), jnp.bfloat16), jnp.zeros((), jnp.bfloat16)
        grads, hots = [], []
        for r in range(PACK):
            hot = []
            for ix, n in zip(index, (32, 64, 64)):
                bins = lax.broadcasted_iota(jnp.int16, (n, 2 * B), 0)
                line = jnp.broadcast_to(ix[r:r + 1, :], (n, 2 * B))
                hot.append(jnp.where(bins == line, one, zero))
            hots.append(jnp.concatenate(hot, axis=0))
            grads += [spread[part, r * 8:r * 8 + 8, :].astype(jnp.bfloat16) for part in range(2)]
        return lax.dot_general(jnp.concatenate(grads, axis=1), jnp.concatenate(hots, axis=1), NT,
                               preferred_element_type=jnp.float32)

    def two(step, sums):
        return sums[0] + group(2 * step, even), sums[1] + group(2 * step + 1, odd)

    none = jnp.zeros((8, BINS), jnp.float32)
    sums = lax.fori_loop(0, (count + 1) // 2, two, (none, none))
    out_ref[...] = sums[0] + sums[1]


def table_grads(row, step, lengths, bl, bh, bv, ds):
    slots = bl.shape[1]
    tiles, heads = ds.shape[0], ds.shape[2]
    block = pl.BlockSpec((None, B, slots), lambda i, L: (row, step, 0))
    return pl.pallas_call(
        functools.partial(hist_kernel, row, step),
        grid_spec=pltpu.PrefetchScalarGridSpec(
            num_scalar_prefetch=1, grid=(1,),
            in_specs=[block, block, block,
                      pl.BlockSpec((None, tiles, heads, B, B), lambda i, L: (step, 0, 0, 0, 0))],
            out_specs=pl.BlockSpec((8, BINS), lambda i, L: (0, 0)),
            scratch_shapes=[
                pltpu.VMEM((2, 8 * PACK, B), jnp.float32),
                pltpu.VMEM((2, 8 * PACK, B), jnp.float32),
            ]),
        out_shape=jax.ShapeDtypeStruct((8, BINS), jnp.float32),
        compiler_params=pltpu.CompilerParams(vmem_limit_bytes=48 << 20),
        cost_estimate=pl.CostEstimate(flops=1, transcendentals=0, bytes_accessed=1),
        name="table_grads",
    )(lengths, bl, bh, bv, ds)


f32, low = jnp.float32, jnp.bfloat16
SWAP = [(0, 1), (1, 0)]


def normalize(values):
    mean = jnp.mean(values, axis=-1, keepdims=True)
    centered = values - mean
    scale = lax.rsqrt(jnp.mean(centered * centered, axis=-1, keepdims=True) + 1e-12)
    return centered * scale, scale


def normalize_back(grad, normed, scale, gain):
    scaled = grad * gain
    first = jnp.mean(scaled, axis=-1, keepdims=True)
    second = jnp.mean(scaled * normed, axis=-1, keepdims=True)
    return scale * (scaled - first - normed * second)


def times(left, right, left_dim, right_dim):
    return lax.dot_general(left, right, (((left_dim,), (right_dim,)), ((), ())),
                           preferred_element_type=f32)


def flips(count, bit):
    return [(i, i ^ (1 << bit)) for i in range(count)]


def to_peer(values):
    return lax.ppermute(values, "head", SWAP)


def plus(left, right):
    return (left.astype(f32) + right.astype(f32)).astype(low)


def in_order(bit_value, mine, other):
    return jnp.where(bit_value == 0, jnp.stack([mine, other]), jnp.stack([other, mine]))


class Order:
    def __init__(self):
        self.last = None

    def tie(self, values):
        if self.last is None:
            return values
        values, self.last = lax.optimization_barrier((values, self.last))
        return values

    def mark(self, values):
        self.last = values


def total(terms, lift, size, axis):
    return sum(lax.dynamic_slice_in_dim(values, start + lift, size, axis).astype(f32)
               for values, start in terms)


def halve(order, terms, size, axis, count, bit):
    half = size // 2
    mine = (lax.axis_index("dp") >> bit) & 1
    send = total(terms, (1 - mine) * half, half, axis).astype(low)
    order.mark(send)
    got = lax.ppermute(send, "dp", flips(count, bit))
    yield
    return [(values, start + mine * half) for values, start in terms] + [(order.tie(got), 0)]


def gather_steps(order, values, count, bits):
    index = lax.axis_index("dp")
    for bit in reversed(bits):
        order.mark(values)
        got = lax.ppermute(values, "dp", flips(count, bit))
        yield
        both = in_order((index >> bit) & 1, values, order.tie(got))
        values = both.reshape((2 * values.shape[0],) + values.shape[1:])
    return values


def unit_steps(order, kept, given, count, axis, split, out):
    bits = list(range(1, count.bit_length() - 1))
    size = kept.shape[axis]
    order.mark(given)
    got = lax.ppermute(given, "dp", flips(count, 0))
    yield
    terms = [(kept, 0), (order.tie(got), 0)]
    terms = yield from halve(order, terms, size, axis, count, bits[0])
    size //= 2
    mine, other = ([(split(values)[c], start) for values, start in terms] for c in range(2))
    send = total(other, 0, size, 0).astype(low)
    order.mark(send)
    got = to_peer(send)
    yield
    terms = mine + [(order.tie(got), 0)]
    for bit in bits[1:]:
        terms = yield from halve(order, terms, size, 0, count, bit)
        size //= 2
    mine = yield from gather_steps(order, total(terms, 0, size, 0).astype(low), count, bits)
    order.mark(mine)
    other = lax.ppermute(mine, "dp", flips(count, 0))
    yield
    out += [mine, order.tie(other)]


def buffer_steps(order, values, count, out):
    bits = list(range(count.bit_length() - 1))
    size = values.shape[0]
    terms = [(values, 0)]
    for bit in bits:
        terms = yield from halve(order, terms, size, 0, count, bit)
        size //= 2
    values = yield from gather_steps(order, total(terms, 0, size, 0).astype(low), count, bits)
    order.mark(values)
    out.append(values)


def advance(*chains):
    for chain in chains:
        next(chain, None)


def finish(*chains):
    left = list(chains)
    while left:
        for chain in list(left):
            try:
                next(chain)
            except StopIteration:
                left.remove(chain)


def body(
    count,
    hidden,
    lengths,
    padding,
    bucket_line,
    bucket_horizontal,
    bucket_vertical,
    attn_project,
    attn_bias,
    table_line,
    table_horizontal,
    table_vertical,
    out_project,
    out_bias,
    attn_gain,
    attn_shift,
    hidden_project,
    hidden_bias,
    down_project,
    down_bias,
    final_gain,
    final_shift,
    cotangent,
):
    rows, slots, width = hidden.shape
    half = cotangent.shape[1]
    heads = table_line.shape[1]
    local = attn_project.shape[2]
    units = hidden_project.shape[1]
    part = units // 2
    factor = 1.0 / math.sqrt(local // heads)
    head = lax.axis_index("head")
    index = lax.axis_index("dp")
    core = index & 1
    offset = head * half
    every = list(range(count.bit_length() - 1))

    def split(values, dim):
        return [lax.dynamic_slice_in_dim(values, c * part, part, dim) for c in (core, 1 - core)]

    def joined(own_parts, got, dim):
        mine, rest = own_parts
        beside = lax.ppermute(got, "dp", flips(count, 0))
        return [jnp.concatenate([mine, got], axis=dim), jnp.concatenate([rest, beside], axis=dim)]

    side = (index >> 1) & 1
    down_mine = lax.dynamic_slice_in_dim(down_project, core * part + side * (part // 2), part // 2, 0)
    down_got = to_peer(down_mine)
    down_mine, hidden_project = lax.optimization_barrier((down_mine, hidden_project))
    up_mine = lax.dynamic_slice_in_dim(hidden_project, core * part, part, 1)
    up_got = to_peer(up_mine)
    up_mine, hidden, hidden_project, down_project = lax.optimization_barrier(
        (up_mine, hidden, hidden_project, down_project))
    bias_got = to_peer(hidden_bias)
    biases = [jnp.concatenate([x, y]) for x, y in zip(split(hidden_bias, 0), split(bias_got, 0))]

    tables = jnp.concatenate([table_line, table_horizontal, table_vertical], axis=0)
    bins = tables.shape[0]
    tables = jnp.broadcast_to(tables.T[:, :, None], (heads, bins, B))
    pad = padding[:, None, :]
    bucket_line, bucket_horizontal, bucket_vertical = (
        pltpu.with_memory_space_constraint(x, pltpu.HBM)
        for x in (bucket_line, bucket_horizontal, bucket_vertical))

    flat = hidden.reshape(rows * slots, width)
    query = ((times(flat, attn_project[0], 1, 0) + attn_bias[0].astype(f32)).astype(low)
             * jnp.asarray(factor, low))
    key = times(flat, attn_project[1], 1, 0).astype(low)
    value = (times(flat, attn_project[2], 1, 0) + attn_bias[1].astype(f32)).astype(low)
    query, key, value = (x.reshape(rows, slots, local) for x in (query, key, value))

    gain_first = attn_gain.astype(f32)
    shift_first = attn_shift.astype(f32)
    gain_last = final_gain.astype(f32)
    shift_last = final_shift.astype(f32)

    def own(values):
        return lax.dynamic_slice_in_dim(values, offset, half, 0)

    def others(values):
        return lax.dynamic_slice_in_dim(values, half - offset, half, 0)

    fronts, attn_sum, attn_got = [], [], []
    for r in range(rows):
        if r == 1:
            lengths, down_got = lax.optimization_barrier((lengths, down_got))
            down_beside = lax.ppermute(down_got, "dp", flips(count, 1))
        probs, context = attn_fwd(r, lengths, query, key, value, pad, bucket_line,
                                  bucket_horizontal, bucket_vertical, tables)
        if r == 1:
            context, down_beside = lax.optimization_barrier((context, down_beside))
        fronts.append((probs, context))
        send = times(others(context), out_project, 1, 0).astype(low)
        got = to_peer(send)
        attn_sum.append(times(own(context), out_project, 1, 0))
        attn_got.append(got)
    send, hidden_project, down_project = lax.optimization_barrier((send, hidden_project, down_project))
    up_parts = [up_mine, lax.dynamic_slice_in_dim(hidden_project, (1 - core) * part, part, 1)]
    down_parts = split(down_project, 0)
    up_got, down_beside, attn_got = lax.optimization_barrier((up_got, down_beside, attn_got))
    down_got = in_order(side, down_got, down_beside)
    ups = joined(up_parts, up_got, 1)
    downs = joined(down_parts, down_got.reshape(part, width), 0)
    attn_sum = [x + got.astype(f32) for x, got in zip(attn_sum, attn_got)]
    tokens = lax.dynamic_slice_in_dim(hidden, offset, half, 1).reshape(rows * half, width).astype(f32)
    normed, scale = normalize(tokens + jnp.concatenate(attn_sum, axis=0) + out_bias.astype(f32))
    mid = normed * gain_first + shift_first
    mid_low = mid.astype(low)

    actives, slopes = [], []
    total = None
    for up, down, bias in zip(ups, downs, biases):
        inner = times(mid_low, up, 1, 0) + bias.astype(f32)
        bell = 0.5 * (1.0 + lax.erf(inner * math.sqrt(0.5)))
        actives.append((inner * bell).astype(low))
        slopes.append(bell + inner * (jnp.exp(-0.5 * inner * inner) * (1.0 / math.sqrt(2.0 * math.pi))))
        term = times(actives[-1], down, 1, 0)
        total = term if total is None else total + term
    normed_final, scale_final = normalize(mid + total + down_bias.astype(f32))
    output = (normed_final * gain_last + shift_last).astype(low).reshape(rows, half, width)

    above = cotangent.reshape(rows * half, width).astype(f32)
    g_final = normalize_back(above, normed_final, scale_final, gain_last)
    g_low = g_final.astype(low)
    order = Order()
    total = None
    grads_bias, inners = [], []
    for up, down, slope in zip(ups, downs, slopes):
        g_inner = (times(g_low, down, 1, 1) * slope).astype(low)
        inners.append(g_inner)
        grads_bias.append(jnp.sum(g_inner.astype(f32), axis=0))
        term = times(g_inner, up, 1, 1)
        total = term if total is None else total + term
    g_mid = g_final + total
    g_attn = normalize_back(g_mid, normed, scale, gain_first)
    g_attn_low = g_attn.astype(low).reshape(rows, half, width)
    g_others = [to_peer(g_attn_low[r]) for r in range(rows)]
    order.mark(g_attn_low)
    down_out, up_out, attn_out = [], [], []
    g_low = order.tie(g_low)
    kept, given = (times(active, g_low, 0, 0).astype(low) for active in actives)
    down_chain = unit_steps(order, *(x.reshape(2, part, width) for x in (kept, given)), count, 1,
                            lambda v: (v[0], v[1]), down_out)
    advance(down_chain)
    mid_low = order.tie(mid_low)
    kept, given = (times(mid_low, g_inner, 0, 0).astype(low) for g_inner in inners)
    up_chain = unit_steps(order, kept, given, count, 0, lambda v: (v[:, :part], v[:, part:]), up_out)
    advance(up_chain, down_chain)
    g_attn = g_attn.reshape(rows, half, width)

    marks, three, grad_out = [], None, 0.0
    for r in range(rows):
        probs, context = fronts[r]
        g_all = in_order(head, g_attn_low[r], order.tie(g_others[r])).reshape(slots, width)
        g_context = times(g_all, out_project, 1, 1).astype(low)
        g_scores, three = attn_bwd(r, factor, lengths, query, key, value, g_context, context, probs, three)
        order.mark(g_scores)
        marks.append(g_scores)
        grad_out = grad_out + times(context, g_all, 0, 0)
        advance(up_chain if r == 0 else down_chain)
    grad_attn = times(flat, three.reshape(rows * slots, 3 * local), 0, 0).astype(low)
    grad_out = jnp.concatenate([grad_out[:, :local], grad_out[:, local:]], axis=0).astype(low)
    attn_chain = buffer_steps(order, jnp.concatenate([grad_attn, grad_out], axis=1), count, attn_out)
    advance(attn_chain)
    advance(up_chain, attn_chain)
    every_project = jnp.concatenate([attn_project[c] for c in range(3)], axis=1)
    theirs = lax.dynamic_slice_in_dim(three, half - offset, half, 1)
    give = times(theirs.reshape(rows * half, 3 * local), every_project, 1, 1).astype(low)
    mine = lax.dynamic_slice_in_dim(three, offset, half, 1)
    mine = times(mine.reshape(rows * half, 3 * local), every_project, 1, 1)
    grads_in = mine.reshape(rows, half, width) + g_attn
    give, grads_in = lax.optimization_barrier((give, grads_in))
    grads_in = grads_in + to_peer(give).astype(f32).reshape(rows, half, width)

    tables_out = []
    blocks = [(r, block) for r in range(rows) for block in range(slots // B)]
    chains = {"D": down_chain, "U": up_chain, "A": attn_chain}
    for name in "DTTUATDTUATDTUATDTUDAUDAU":
        if name == "T":
            r, block = blocks[len(tables_out)]
            tables_out.append(table_grads(r, block, order.tie(lengths), bucket_line,
                                          bucket_horizontal, bucket_vertical, marks[r]))
            order.mark(tables_out[-1])
        else:
            advance(chains[name])
    bias_sums = jnp.sum(three.astype(f32), axis=(0, 1))
    marks = sum(tables_out)[:heads].T
    finish(down_chain, attn_chain, up_chain)
    grad_down = in_order(core, *down_out).reshape(down_project.shape).astype(f32)
    mine, other = up_out
    grad_up = jnp.where(core == 0, jnp.concatenate([mine, other], axis=1),
                        jnp.concatenate([other, mine], axis=1)).astype(f32)
    buffer = attn_out[0].astype(f32)
    grad_attn = jnp.stack([buffer[:, c * local:(c + 1) * local] for c in range(3)])
    grad_out = jnp.concatenate([buffer[:local, 3 * local:], buffer[local:, 3 * local:]], axis=1)

    def placed(values):
        return [jnp.where(head == slot, values, 0.0) for slot in range(2)]

    bias_sets = in_order(core, *grads_bias)
    bias_sets = in_order(head, bias_sets[:, :part].reshape(-1), bias_sets[:, part:].reshape(-1))
    early = [jnp.sum(g_attn, axis=(0, 1)), jnp.sum(g_mid * normed, axis=0), jnp.sum(g_mid, axis=0),
             jnp.sum(g_final, axis=0), jnp.sum(above * normed_final, axis=0), jnp.sum(above, axis=0),
             bias_sets, bias_sums]
    early = order.tie(early)
    table_rows = -(-marks.size // width)
    marks = jnp.pad(marks.reshape(-1), (0, table_rows * width - marks.size)).reshape(table_rows, width)
    attn_row = jnp.concatenate([early[7][:local], early[7][2 * local:]])[None]
    packed = jnp.concatenate([jnp.stack(early[:6]), early[6].reshape(-1, width)]
                             + placed(jnp.concatenate([marks, attn_row], axis=0)), axis=0)
    packed = packed + to_peer(packed)
    for bit in every:
        packed = packed + lax.ppermute(packed, "dp", flips(count, bit))
    shared = packed[:6]
    bias_rows = units // width
    grad_bias = lax.dynamic_slice_in_dim(packed, 6 + head * bias_rows, bias_rows, 0).reshape(-1)
    mine = lax.dynamic_slice_in_dim(packed, 6 + 2 * bias_rows + head * (table_rows + 1), table_rows + 1, 0)
    marks = mine[:table_rows].reshape(-1)[:bins * heads].reshape(bins, heads)
    first, second = table_line.shape[0], table_horizontal.shape[0]
    return (
        output,
        grads_in,
        grad_attn,
        mine[table_rows].reshape(2, local),
        marks[:first],
        marks[first:first + second],
        marks[first + second:],
        grad_out,
        shared[0],
        shared[1],
        shared[2],
        grad_up,
        grad_bias,
        grad_down,
        shared[3],
        shared[4],
        shared[5],
    )


def solution(mesh):
    return jax.shard_map(
        functools.partial(body, mesh.shape["dp"]),
        mesh=mesh,
        in_specs=(
            P("dp", None, None),
            P("dp", None),
            P("dp", None),
            P("dp", None, None),
            P("dp", None, None),
            P("dp", None, None),
            P(None, None, "head"),
            P(None, "head"),
            P(None, "head"),
            P(None, "head"),
            P(None, "head"),
            P("head", None),
            P(),
            P(),
            P(),
            P(None, "head"),
            P("head"),
            P("head", None),
            P(),
            P(),
            P(),
            P("dp", "head", None),
        ),
        out_specs=(
            P("dp", "head", None),
            P("dp", "head", None),
            P(None, None, "head"),
            P(None, "head"),
            P(None, "head"),
            P(None, "head"),
            P(None, "head"),
            P("head", None),
            P(),
            P(),
            P(),
            P(None, "head"),
            P("head"),
            P("head", None),
            P(),
            P(),
            P(),
        ),
        check_vma=False,
    )
```

```python
import functools
import math

import jax
import jax.numpy as jnp
from jax import lax
from jax.experimental import pallas as pl
from jax.experimental.pallas import tpu as pltpu
from jax.sharding import PartitionSpec as P

B = 128

ROWS_PICK = lax.GatherDimensionNumbers(
    offset_dims=(), collapsed_slice_dims=(0,), start_index_map=(0,),
    operand_batching_dims=(1,), start_indices_batching_dims=(1,))
PACK = 16

def pick(table, index):
    return lax.gather(table, index[:, :, None], ROWS_PICK, (1, 1),
                      mode=lax.GatherScatterMode.PROMISE_IN_BOUNDS)

def lookup(tab_ref, h, at, place, masks):
    found = pick(tab_ref[h, at:at + PACK, :], place)
    for step, mask in enumerate(masks):
        low = at + PACK * (step + 1)
        found = jnp.where(mask, pick(tab_ref[h, low:low + PACK, :], place), found)
    return found.astype(jnp.float32)

def doc_span(len_ref, row, first, last):
    edge = 0
    start = 0
    stop = 0
    for k in range(len_ref.shape[1]):
        begin = edge
        edge = edge + len_ref[row, k]
        start = jnp.where(begin <= first, begin, start)
        stop = jnp.where(begin <= last, edge, stop)
    return start // B, (stop + (B - 1)) // B

def fwd_kernel(row, len_ref, q_ref, k_ref, v_ref, pad_ref, bl_ref, bh_ref, bv_ref, tab_ref,
               probs_ref, ctx_ref, kst, vst, sc):
    qb = pl.program_id(0)
    pairs = kst.shape[0]
    heads = 2 * pairs
    tiles = kst.shape[1]
    lane = lax.broadcasted_iota(jnp.int32, (B, B), 1)
    left = lane < (B // 2)

    @pl.when(qb == 0)
    def _():
        for p in range(pairs):
            for t in range(tiles):
                kt = k_ref[t * B:(t + 1) * B, p * B:(p + 1) * B]
                vt = v_ref[t * B:(t + 1) * B, p * B:(p + 1) * B]
                zero = jnp.zeros_like(kt)
                kst[p, t, 0:B, :] = jnp.where(left, kt, zero)
                kst[p, t, B:2 * B, :] = jnp.where(left, zero, kt)
                vst[p, t, 0:B, :] = jnp.where(left, vt, zero)
                vst[p, t, B:2 * B, :] = jnp.where(left, zero, vt)

    first = qb * B
    low, high = doc_span(len_ref, row, first, first + B - 1)
    sub = lax.broadcasted_iota(jnp.int32, (B, B), 0) + first
    count = len_ref.shape[1]
    edges = []
    edge = 0
    for k in range(count):
        edge = edge + len_ref[row, k]
        edges.append(edge)
    seg_q = sum(((sub >= e).astype(jnp.int32) for e in edges))

    def scores(t, top):
        key_at = lane + t * B
        seg_k = sum(((key_at >= e).astype(jnp.int32) for e in edges))
        real = jnp.broadcast_to(pad_ref[:, pl.ds(pl.multiple_of(t * B, B), B)], (B, B)) > 0
        allowed = ((seg_q == seg_k) & real) | (sub == key_at)
        at = pl.ds(pl.multiple_of(t * B, B), B)
        parts = []
        for g in range(B // PACK):
            rows = slice(g * PACK, g * PACK + PACK)
            group = []
            for ref, tiles_of in ((bl_ref, 2), (bh_ref, 4), (bv_ref, 4)):
                index = ref[rows, at].astype(jnp.int16)
                group.append((index & jnp.int16(PACK - 1),
                              [index >= jnp.int16(PACK * a) for a in range(1, tiles_of)]))
            parts.append(group)
        out = []
        for p in range(pairs):
            raw = lax.dot_general(q_ref[:, p * B:(p + 1) * B], kst[p, t], (((1,), (1,)), ((), ())),
                                  preferred_element_type=jnp.float32)
            for s in range(2):
                h = 2 * p + s
                rel = jnp.concatenate(
                    [(lookup(tab_ref, h, 0, *group[0]) + lookup(tab_ref, h, 32, *group[1]))
                     + lookup(tab_ref, h, 96, *group[2]) for group in parts], axis=0)
                val = jnp.where(allowed, raw[:, s * B:(s + 1) * B] + rel, -1000000000.0)
                sc[t, h] = val
                out.append(jnp.maximum(top[h], val))
        return tuple(out)

    start = jnp.full((B, B), -3.0e38, jnp.float32)
    top = lax.fori_loop(low, high, scores, tuple(start for _ in range(heads)))
    top = [jnp.max(x, axis=-1, keepdims=True) for x in top]

    def expo(t, tot):
        out = []
        for h in range(heads):
            e = jnp.exp(sc[t, h] - top[h])
            sc[t, h] = e
            out.append(tot[h] + e)
        return tuple(out)

    zero = jnp.zeros((B, B), jnp.float32)
    tot = lax.fori_loop(low, high, expo, tuple(zero for _ in range(heads)))
    inv = [1.0 / jnp.sum(x, axis=-1, keepdims=True) for x in tot]

    def mix(t, acc):
        out = []
        for p in range(pairs):
            low_pair = []
            for s in range(2):
                h = 2 * p + s
                pr = sc[t, h] * inv[h]
                probs_ref[t, h] = pr
                low_pair.append(pr.astype(jnp.bfloat16))
            out.append(acc[p] + jnp.dot(jnp.concatenate(low_pair, axis=1), vst[p, t],
                                        preferred_element_type=jnp.float32))
        return tuple(out)

    acc = lax.fori_loop(low, high, mix, tuple(zero for _ in range(pairs)))
    for p in range(pairs):
        ctx_ref[:, p * B:(p + 1) * B] = acc[p].astype(jnp.bfloat16)

def attn_fwd(row, lengths, q, k, v, pad, bl, bh, bv, tab):
    slots, width = q.shape[1:]
    pairs = width // B
    tiles = slots // B
    row_block = lambda n: pl.BlockSpec((None, B, n), lambda i, L: (row, i, 0))
    return pl.pallas_call(
        functools.partial(fwd_kernel, row),
        grid_spec=pltpu.PrefetchScalarGridSpec(
            num_scalar_prefetch=1, grid=(tiles,),
            in_specs=[
                row_block(width),
                pl.BlockSpec((None, slots, width), lambda i, L: (row, 0, 0)),
                pl.BlockSpec((None, slots, width), lambda i, L: (row, 0, 0)),
                pl.BlockSpec((None, 1, slots), lambda i, L: (row, 0, 0)),
                row_block(slots), row_block(slots), row_block(slots),
                pl.BlockSpec(tab.shape, lambda i, L: (0, 0, 0)),
            ],
            out_specs=[
                pl.BlockSpec((None, tiles, 2 * pairs, B, B), lambda i, L: (i, 0, 0, 0, 0)),
                pl.BlockSpec((B, width), lambda i, L: (i, 0)),
            ],
            scratch_shapes=[
                pltpu.VMEM((pairs, tiles, 2 * B, B), jnp.bfloat16),
                pltpu.VMEM((pairs, tiles, 2 * B, B), jnp.bfloat16),
                pltpu.VMEM((tiles, 2 * pairs, B, B), jnp.float32),
            ]),
        out_shape=[
            jax.ShapeDtypeStruct((tiles, tiles, 2 * pairs, B, B), jnp.float32),
            jax.ShapeDtypeStruct((slots, width), jnp.bfloat16),
        ],
        compiler_params=pltpu.CompilerParams(vmem_limit_bytes=48 << 20),
        cost_estimate=pl.CostEstimate(flops=1, transcendentals=0, bytes_accessed=1),
        name="attn_forward",
    )(lengths, q, k, v, pad, bl, bh, bv, tab)


NT = (((1,), (1,)), ((), ()))
TN = (((0,), (0,)), ((), ()))

def bwd_kernel(row, factor, len_ref, q_ref, k_ref, v_ref, gctx_ref, ctx_ref, probs_ref,
               *rest):
    ds_ref, three_ref, kst, vst, dkst, dvst, inner, dqs = rest[-8:]
    qb = pl.program_id(0)
    pairs, tiles = kst.shape[0], kst.shape[1]
    lane = lax.broadcasted_iota(jnp.int32, (B, B), 1)
    left = lane < (B // 2)

    @pl.when(qb == 0)
    def _():
        dkst[...] = jnp.zeros_like(dkst)
        dvst[...] = jnp.zeros_like(dvst)
        for p in range(pairs):
            for t in range(tiles):
                kt = k_ref[t * B:(t + 1) * B, p * B:(p + 1) * B]
                vt = v_ref[t * B:(t + 1) * B, p * B:(p + 1) * B]
                zero = jnp.zeros_like(kt)
                kst[p, t, 0:B, :] = jnp.where(left, kt, zero)
                kst[p, t, B:2 * B, :] = jnp.where(left, zero, kt)
                vst[p, t, 0:B, :] = jnp.where(left, vt, zero)
                vst[p, t, B:2 * B, :] = jnp.where(left, zero, vt)

    first = qb * B
    low, high = doc_span(len_ref, row, first, first + B - 1)
    sides = []
    for p in range(pairs):
        cols = slice(p * B, (p + 1) * B)
        gctx = gctx_ref[:, cols]
        prod = gctx.astype(jnp.float32) * ctx_ref[:, cols].astype(jnp.float32)
        zero = jnp.zeros_like(prod)
        for side in (jnp.where(left, prod, zero), jnp.where(left, zero, prod)):
            inner[len(sides)] = jnp.broadcast_to(jnp.sum(side, axis=-1, keepdims=True), (B, B))
            sides.append(0)
    dqs[...] = jnp.zeros_like(dqs)

    def tile(t, carry):
        for p in range(pairs):
            cols = slice(p * B, (p + 1) * B)
            gctx = gctx_ref[:, cols]
            gp = lax.dot_general(gctx, vst[p, t], NT, preferred_element_type=jnp.float32)
            probs_low, g_scores = [], []
            for s in range(2):
                pr = probs_ref[t, 2 * p + s]
                ds = (pr * (gp[:, s * B:(s + 1) * B] - inner[2 * p + s])).astype(jnp.bfloat16)
                ds_ref[t, 2 * p + s] = ds
                g_scores.append(ds)
                probs_low.append(pr.astype(jnp.bfloat16))
            ds = jnp.concatenate(g_scores, axis=1)
            mix = jnp.concatenate(probs_low, axis=1)
            dvst[p, t] += lax.dot_general(mix, gctx, TN, preferred_element_type=jnp.float32)
            dkst[p, t] += lax.dot_general(ds, q_ref[:, cols], TN, preferred_element_type=jnp.float32)
            dqs[p] += jnp.dot(ds, kst[p, t], preferred_element_type=jnp.float32)
        return carry

    lax.fori_loop(low, high, tile, 0)
    for p in range(pairs):
        three_ref[pl.ds(pl.multiple_of(first, B), B), p * B:(p + 1) * B] = (dqs[p] * factor).astype(jnp.bfloat16)

    @pl.when(qb == tiles - 1)
    def _():
        for p in range(pairs):
            for t in range(tiles):
                three_ref[t * B:(t + 1) * B, (pairs + p) * B:(pairs + p + 1) * B] = jnp.where(
                    left, dkst[p, t, 0:B, :], dkst[p, t, B:2 * B, :]).astype(jnp.bfloat16)
                three_ref[t * B:(t + 1) * B, (2 * pairs + p) * B:(2 * pairs + p + 1) * B] = jnp.where(
                    left, dvst[p, t, 0:B, :], dvst[p, t, B:2 * B, :]).astype(jnp.bfloat16)

def attn_bwd(row, factor, lengths, q, k, v, gctx, ctx, probs, kept=None):
    slots, width = q.shape[1:]
    pairs, tiles = width // B, slots // B
    part = pl.BlockSpec((B, width), lambda i, L: (i, 0))
    three = pl.BlockSpec((None, slots, 3 * width), lambda i, L: (row, 0, 0))
    mine = pl.BlockSpec((None, B, width), lambda i, L: (row, i, 0))
    whole = pl.BlockSpec((None, slots, width), lambda i, L: (row, 0, 0))
    pairs_of = pl.BlockSpec((None, tiles, 2 * pairs, B, B), lambda i, L: (i, 0, 0, 0, 0))
    kept = () if kept is None else (kept,)
    return pl.pallas_call(
        functools.partial(bwd_kernel, row, factor),
        grid_spec=pltpu.PrefetchScalarGridSpec(
            num_scalar_prefetch=1, grid=(tiles,),
            in_specs=[mine, whole, whole, part, part, pairs_of]
            + [pl.BlockSpec(memory_space=pl.ANY)] * len(kept),
            out_specs=[pairs_of, three],
            scratch_shapes=[
                pltpu.VMEM((pairs, tiles, 2 * B, B), jnp.bfloat16),
                pltpu.VMEM((pairs, tiles, 2 * B, B), jnp.bfloat16),
                pltpu.VMEM((pairs, tiles, 2 * B, B), jnp.float32),
                pltpu.VMEM((pairs, tiles, 2 * B, B), jnp.float32),
                pltpu.VMEM((2 * pairs, B, B), jnp.float32),
                pltpu.VMEM((pairs, B, B), jnp.float32),
            ]),
        out_shape=[jax.ShapeDtypeStruct(probs.shape, jnp.bfloat16),
                   jax.ShapeDtypeStruct((q.shape[0], slots, 3 * width), jnp.bfloat16)],
        input_output_aliases={7: 1} if kept else {},
        compiler_params=pltpu.CompilerParams(vmem_limit_bytes=48 << 20),
        cost_estimate=pl.CostEstimate(flops=1, transcendentals=0, bytes_accessed=1),
        name="attn_backward",
    )(lengths, q, k, v, gctx, ctx, probs, *kept)

BINS = 160


def hist_kernel(row, step, len_ref, bl_ref, bh_ref, bv_ref, ds_ref, out_ref, even, odd):
    tiles, heads = ds_ref.shape[0], ds_ref.shape[1]
    docs = len_ref.shape[1]
    lane = lax.broadcasted_iota(jnp.int32, (PACK, B), 1)
    sub = lax.broadcasted_iota(jnp.int32, (PACK, B), 0)
    even[...] = jnp.zeros_like(even)
    odd[...] = jnp.zeros_like(odd)

    floor, roof = step * B, (step + 1) * B
    starts, ends, firsts, lasts, upto = [], [], [], [], []
    edge, count = 0, 0
    for d in range(docs):
        starts.append(edge)
        edge = edge + len_ref[row, d]
        ends.append(edge)
        firsts.append(jnp.maximum(starts[d], floor))
        lasts.append(jnp.maximum(jnp.minimum(edge, roof), firsts[d]))
        here = (lasts[d] + (PACK - 1)) // PACK - firsts[d] // PACK
        count = count + jnp.where(lasts[d] > firsts[d], here, 0)
        upto.append(count)

    def group(g, spread):
        start, end, first, last = starts[0], ends[0], firsts[0], lasts[0]
        block = firsts[0] // PACK + g
        for d in range(1, docs):
            past = g >= upto[d - 1]
            start, end, first, last, block = (
                jnp.where(past, new, old) for new, old in
                ((starts[d], start), (ends[d], end), (firsts[d], first), (lasts[d], last),
                 (firsts[d] // PACK + (g - upto[d - 1]), block)))
        last = jnp.where(g < count, last, first)
        start = jnp.minimum(start, tiles * B - 1)
        block = jnp.clip(block - step * (B // PACK), 0, B // PACK - 1)
        tile = start // B
        left = start - tile * B
        turn = jnp.where(left == 0, 0, B - left)
        rows = pl.ds(pl.multiple_of(block * PACK, PACK), PACK)
        token = sub + (floor + block * PACK)
        inside = (token >= first) & (token < last)
        lives = [inside & (lane + part * B < end - start) for part in range(2)]
        before = lane < B - left
        spots = [jnp.minimum(tile + part, tiles - 1) for part in range(3)]

        def moved(parts):
            parts = [pltpu.roll(p, turn, 1) for p in parts]
            return [jnp.where(before, parts[part], parts[part + 1]) for part in range(2)]

        for h in range(heads):
            vals = moved([ds_ref[s, h, rows, :].astype(jnp.float32) for s in spots])
            for part in range(2):
                spread[part, pl.ds(h, PACK, stride=8), :] = jnp.where(lives[part], vals[part], 0.0)
        codes = []
        for s in spots:
            at = pl.ds(pl.multiple_of(s * B, B), B)
            codes.append(bl_ref[rows, at] + 32 * bh_ref[rows, at] + 2048 * bv_ref[rows, at])
        code = jnp.concatenate(moved(codes), axis=1)
        index = [(code & 31).astype(jnp.int16), ((code >> 5) & 63).astype(jnp.int16),
                 (code >> 11).astype(jnp.int16)]
        one, zero = jnp.ones((), jnp.bfloat16), jnp.zeros((), jnp.bfloat16)
        grads, hots = [], []
        for r in range(PACK):
            hot = []
            for ix, n in zip(index, (32, 64, 64)):
                bins = lax.broadcasted_iota(jnp.int16, (n, 2 * B), 0)
                line = jnp.broadcast_to(ix[r:r + 1, :], (n, 2 * B))
                hot.append(jnp.where(bins == line, one, zero))
            hots.append(jnp.concatenate(hot, axis=0))
            grads += [spread[part, r * 8:r * 8 + 8, :].astype(jnp.bfloat16) for part in range(2)]
        return lax.dot_general(jnp.concatenate(grads, axis=1), jnp.concatenate(hots, axis=1), NT,
                               preferred_element_type=jnp.float32)

    def two(step, sums):
        return sums[0] + group(2 * step, even), sums[1] + group(2 * step + 1, odd)

    none = jnp.zeros((8, BINS), jnp.float32)
    sums = lax.fori_loop(0, (count + 1) // 2, two, (none, none))
    out_ref[...] = sums[0] + sums[1]


def table_grads(row, step, lengths, bl, bh, bv, ds):
    slots = bl.shape[1]
    tiles, heads = ds.shape[0], ds.shape[2]
    block = pl.BlockSpec((None, B, slots), lambda i, L: (row, step, 0))
    return pl.pallas_call(
        functools.partial(hist_kernel, row, step),
        grid_spec=pltpu.PrefetchScalarGridSpec(
            num_scalar_prefetch=1, grid=(1,),
            in_specs=[block, block, block,
                      pl.BlockSpec((None, tiles, heads, B, B), lambda i, L: (step, 0, 0, 0, 0))],
            out_specs=pl.BlockSpec((8, BINS), lambda i, L: (0, 0)),
            scratch_shapes=[
                pltpu.VMEM((2, 8 * PACK, B), jnp.float32),
                pltpu.VMEM((2, 8 * PACK, B), jnp.float32),
            ]),
        out_shape=jax.ShapeDtypeStruct((8, BINS), jnp.float32),
        compiler_params=pltpu.CompilerParams(vmem_limit_bytes=48 << 20),
        cost_estimate=pl.CostEstimate(flops=1, transcendentals=0, bytes_accessed=1),
        name="table_grads",
    )(lengths, bl, bh, bv, ds)


f32, low = jnp.float32, jnp.bfloat16
SWAP = [(0, 1), (1, 0)]
ORDER = "ATUDTADTUGATDUTATDTUADTPSUASDUSASSU"


def normalize(values):
    mean = jnp.mean(values, axis=-1, keepdims=True)
    centered = values - mean
    scale = lax.rsqrt(jnp.mean(centered * centered, axis=-1, keepdims=True) + 1e-12)
    return centered * scale, scale


def normalize_back(grad, normed, scale, gain):
    scaled = grad * gain
    first = jnp.mean(scaled, axis=-1, keepdims=True)
    second = jnp.mean(scaled * normed, axis=-1, keepdims=True)
    return scale * (scaled - first - normed * second)


def times(left, right, left_dim, right_dim):
    return lax.dot_general(left, right, (((left_dim,), (right_dim,)), ((), ())),
                           preferred_element_type=f32)


def flips(count, bit):
    return [(i, i ^ (1 << bit)) for i in range(count)]


def to_peer(values):
    return lax.ppermute(values, "head", SWAP)


def plus(left, right):
    return (left.astype(f32) + right.astype(f32)).astype(low)


def arranged(bit_value, mine, other):
    return jnp.where(bit_value == 0, mine, other), jnp.where(bit_value == 0, other, mine)


def in_order(bit_value, mine, other):
    return jnp.stack(arranged(bit_value, mine, other))


class Order:
    def __init__(self):
        self.last = None

    def tie(self, values):
        if self.last is None:
            return values
        values, self.last = lax.optimization_barrier((values, self.last))
        return values

    def mark(self, values):
        self.last = values


def total(terms, lift, size, axis):
    return sum(lax.dynamic_slice_in_dim(values, start + lift, size, axis).astype(f32)
               for values, start in terms)


def halve(order, terms, size, axis, count, bit):
    half = size // 2
    mine = (lax.axis_index("dp") >> bit) & 1
    send = total(terms, (1 - mine) * half, half, axis).astype(low)
    order.mark(send)
    got = lax.ppermute(send, "dp", flips(count, bit))
    yield
    return [(values, start + mine * half) for values, start in terms] + [(order.tie(got), 0)]


def gather_steps(order, values, count, bits):
    index = lax.axis_index("dp")
    for bit in reversed(bits):
        order.mark(values)
        got = lax.ppermute(values, "dp", flips(count, bit))
        yield
        both = in_order((index >> bit) & 1, values, order.tie(got))
        values = both.reshape((2 * values.shape[0],) + values.shape[1:])
    return values


def unit_steps(order, kept, given, count, axis, split, out):
    bits = list(range(1, count.bit_length() - 1))
    size = kept.shape[axis]
    given = order.tie(given)
    order.mark(given)
    got = lax.ppermute(given, "dp", flips(count, 0))
    yield
    terms = [(kept, 0), (order.tie(got), 0)]
    terms = yield from halve(order, terms, size, axis, count, bits[0])
    size //= 2
    mine, other = ([(split(values)[c], start) for values, start in terms] for c in range(2))
    send = total(other, 0, size, 0).astype(low)
    order.mark(send)
    got = to_peer(send)
    yield
    terms = mine + [(order.tie(got), 0)]
    for bit in bits[1:]:
        terms = yield from halve(order, terms, size, 0, count, bit)
        size //= 2
    mine = yield from gather_steps(order, total(terms, 0, size, 0).astype(low), count, bits)
    order.mark(mine)
    other = lax.ppermute(mine, "dp", flips(count, 0))
    yield
    out += [mine, order.tie(other)]


def buffer_steps(order, values, count, out):
    bits = list(range(count.bit_length() - 1))
    size = values.shape[0]
    terms = [(order.tie(values), 0)]
    for bit in bits:
        terms = yield from halve(order, terms, size, 0, count, bit)
        size //= 2
    values = yield from gather_steps(order, total(terms, 0, size, 0).astype(low), count, bits)
    order.mark(values)
    out.append(values)


def small_steps(order, values, count, out):
    values = order.tie(values)
    for bit in [None] + list(range(count.bit_length() - 1)):
        order.mark(values)
        got = to_peer(values) if bit is None else lax.ppermute(values, "dp", flips(count, bit))
        yield
        values = values + order.tie(got)
    order.mark(values)
    out.append(values)


def advance(*chains):
    for chain in chains:
        next(chain, None)


def finish(*chains):
    left = list(chains)
    while left:
        for chain in list(left):
            try:
                next(chain)
            except StopIteration:
                left.remove(chain)


def body(
    count,
    hidden,
    lengths,
    padding,
    bucket_line,
    bucket_horizontal,
    bucket_vertical,
    attn_project,
    attn_bias,
    table_line,
    table_horizontal,
    table_vertical,
    out_project,
    out_bias,
    attn_gain,
    attn_shift,
    hidden_project,
    hidden_bias,
    down_project,
    down_bias,
    final_gain,
    final_shift,
    cotangent,
):
    rows, slots, width = hidden.shape
    half = cotangent.shape[1]
    heads = table_line.shape[1]
    local = attn_project.shape[2]
    units = hidden_project.shape[1]
    part = units // 2
    factor = 1.0 / math.sqrt(local // heads)
    head = lax.axis_index("head")
    index = lax.axis_index("dp")
    core = index & 1
    offset = head * half
    every = list(range(count.bit_length() - 1))

    def split(values, dim):
        return [lax.dynamic_slice_in_dim(values, c * part, part, dim) for c in (core, 1 - core)]

    def joined(own_parts, got, dim):
        mine, rest = own_parts
        beside = lax.ppermute(got, "dp", flips(count, 0))
        return [jnp.concatenate([mine, got], axis=dim), jnp.concatenate([rest, beside], axis=dim)]

    side = (index >> 1) & 1
    down_mine = lax.dynamic_slice_in_dim(down_project, core * part + side * (part // 2), part // 2, 0)
    down_got = to_peer(down_mine)
    down_mine, hidden_project = lax.optimization_barrier((down_mine, hidden_project))
    up_mine = lax.dynamic_slice_in_dim(hidden_project, core * part, part, 1)
    up_got = to_peer(up_mine)
    up_mine, hidden, hidden_project, down_project = lax.optimization_barrier(
        (up_mine, hidden, hidden_project, down_project))
    bias_got = to_peer(hidden_bias)

    tables = jnp.concatenate([table_line, table_horizontal, table_vertical], axis=0)
    bins = tables.shape[0]
    tables = jnp.broadcast_to(tables.T[:, :, None], (heads, bins, B))
    pad = padding[:, None, :]
    bucket_line, bucket_horizontal, bucket_vertical = (
        pltpu.with_memory_space_constraint(x, pltpu.HBM)
        for x in (bucket_line, bucket_horizontal, bucket_vertical))

    flat = hidden.reshape(rows * slots, width)
    query = ((times(flat, attn_project[0], 1, 0) + attn_bias[0].astype(f32)).astype(low)
             * jnp.asarray(factor, low))
    key = times(flat, attn_project[1], 1, 0).astype(low)
    value = (times(flat, attn_project[2], 1, 0) + attn_bias[1].astype(f32)).astype(low)
    query, key, value = (pltpu.with_memory_space_constraint(x.reshape(rows, slots, local), pltpu.HBM)
                         for x in (query, key, value))

    def own(values):
        return lax.dynamic_slice_in_dim(values, offset, half, 0)

    def others(values):
        return lax.dynamic_slice_in_dim(values, half - offset, half, 0)

    fronts, attn_sum, attn_got = [], [], []
    for r in range(rows):
        if r == 1:
            lengths, down_got = lax.optimization_barrier((lengths, down_got))
            down_beside = lax.ppermute(down_got, "dp", flips(count, 1))
        probs, context = attn_fwd(r, lengths, query, key, value, pad, bucket_line,
                                  bucket_horizontal, bucket_vertical, tables)
        if r == 1:
            context, down_beside = lax.optimization_barrier((context, down_beside))
        fronts.append((probs, context))
        send = times(others(context), out_project, 1, 0).astype(low)
        got = to_peer(send)
        attn_sum.append(times(own(context), out_project, 1, 0))
        attn_got.append(got)
    (send, hidden_project, down_project, cotangent, norm_rows, out_bias, down_bias, hidden_bias, bias_got,
     hidden) = lax.optimization_barrier(
        (send, hidden_project, down_project, cotangent, (attn_gain, attn_shift, final_gain, final_shift),
         out_bias, down_bias, hidden_bias, bias_got, hidden))
    biases = [jnp.concatenate([x, y]) for x, y in zip(split(hidden_bias, 0), split(bias_got, 0))]
    gain_first, shift_first, gain_last, shift_last = (x.astype(f32) for x in norm_rows)
    up_parts = [up_mine, lax.dynamic_slice_in_dim(hidden_project, (1 - core) * part, part, 1)]
    down_parts = split(down_project, 0)
    up_got, down_beside, attn_got = lax.optimization_barrier((up_got, down_beside, attn_got))
    down_got = in_order(side, down_got, down_beside)
    ups = joined(up_parts, up_got, 1)
    downs = joined(down_parts, down_got.reshape(part, width), 0)
    attn_sum = [x + got.astype(f32) for x, got in zip(attn_sum, attn_got)]
    tokens = lax.dynamic_slice_in_dim(hidden, offset, half, 1).reshape(rows * half, width).astype(f32)
    normed, scale = normalize(tokens + jnp.concatenate(attn_sum, axis=0) + out_bias.astype(f32))
    mid = normed * gain_first + shift_first
    mid_low = mid.astype(low)

    actives, slopes = [], []
    total = None
    for up, down, bias in zip(ups, downs, biases):
        inner = times(mid_low, up, 1, 0) + bias.astype(f32)
        bell = 0.5 * (1.0 + lax.erf(inner * math.sqrt(0.5)))
        actives.append((inner * bell).astype(low))
        slopes.append(bell + inner * (jnp.exp(-0.5 * inner * inner) * (1.0 / math.sqrt(2.0 * math.pi))))
        term = times(actives[-1], down, 1, 0)
        total = term if total is None else total + term
    normed_final, scale_final = normalize(mid + total + down_bias.astype(f32))
    output = (normed_final * gain_last + shift_last).astype(low).reshape(rows, half, width)

    above = cotangent.reshape(rows * half, width).astype(f32)
    g_final = normalize_back(above, normed_final, scale_final, gain_last)
    g_low = g_final.astype(low)
    order = Order()
    total = None
    grads_bias, inners = [], []
    for up, down, slope in zip(ups, downs, slopes):
        g_inner = (times(g_low, down, 1, 1) * slope).astype(low)
        inners.append(g_inner)
        grads_bias.append(jnp.sum(g_inner.astype(f32), axis=0, keepdims=True))
        term = times(g_inner, up, 1, 1)
        total = term if total is None else total + term
    g_mid = g_final + total
    g_attn = normalize_back(g_mid, normed, scale, gain_first)
    g_attn_low = g_attn.astype(low).reshape(rows, half, width)
    g_others = [to_peer(g_attn_low[r]) for r in range(rows)]
    order.mark(g_attn_low)
    down_out, up_out, attn_out = [], [], []
    g_low = order.tie(g_low)
    kept, given = (times(active, g_low, 0, 0).astype(low) for active in actives)
    down_chain = unit_steps(order, *(x.reshape(2, part, width) for x in (kept, given)), count, 1,
                            lambda v: (v[0], v[1]), down_out)
    advance(down_chain)
    mid_low = order.tie(mid_low)
    kept, given = (times(mid_low, g_inner, 0, 0).astype(low) for g_inner in inners)
    up_chain = unit_steps(order, kept, given, count, 0, lambda v: (v[:, :part], v[:, part:]), up_out)
    advance(up_chain, down_chain)
    g_attn = g_attn.reshape(rows, half, width)

    marks, three, grad_out = [], None, 0.0
    for r in range(rows):
        probs, context = fronts[r]
        g_all = in_order(head, g_attn_low[r], order.tie(g_others[r])).reshape(slots, width)
        g_context = times(g_all, out_project, 1, 1).astype(low)
        g_scores, three = attn_bwd(r, factor, lengths, query, key, value, g_context, context, probs, three)
        order.mark(g_scores)
        marks.append(g_scores)
        grad_out = grad_out + times(context, g_all, 0, 0)
        advance(up_chain if r == 0 else down_chain)
    grad_attn = times(flat, three.reshape(rows * slots, 3 * local), 0, 0).astype(low)
    grad_out = jnp.concatenate([grad_out[:, :local], grad_out[:, local:]], axis=0).astype(low)
    attn_chain = buffer_steps(order, jnp.concatenate([grad_attn, grad_out], axis=1), count, attn_out)
    advance(attn_chain)
    every_project = jnp.concatenate([attn_project[c] for c in range(3)], axis=1)
    three = order.tie(three)
    theirs = lax.dynamic_slice_in_dim(three, half - offset, half, 1)
    give = times(theirs.reshape(rows * half, 3 * local), every_project, 1, 1).astype(low)
    mine = lax.dynamic_slice_in_dim(three, offset, half, 1)
    mine = times(mine.reshape(rows * half, 3 * local), every_project, 1, 1)
    grads_in = mine.reshape(rows, half, width) + g_attn
    give, grads_in = lax.optimization_barrier((give, grads_in))
    order.mark(grads_in)

    room = width // 2

    def pack():
        sums = [jnp.sum(x.reshape(rows * half, width), axis=0, keepdims=True) for x in
                (g_attn, g_mid * normed, g_mid, g_final, above * normed_final, above)]
        sums, unit_sums, three_sums, tables = order.tie(
            (sums, grads_bias, jnp.sum(three.astype(f32).reshape(rows * slots, 3 * local), axis=0,
                                       keepdims=True), sum(tables_out)))
        ours, others_ = (jnp.concatenate(arranged(core, *(x[:, c * part:(c + 1) * part] for x in unit_sums)),
                                         axis=0) for c in range(2))
        pair = jnp.concatenate([three_sums[:, :local], three_sums[:, 2 * local:]], axis=1)
        tables = jnp.pad(tables, ((0, 0), (0, room - bins)))
        return jnp.concatenate(
            sums + list(arranged(head, ours, others_))
            + [jnp.where(head == slot, pair, 0.0) for slot in range(2)]
            + [jnp.zeros((4, width), f32),
               jnp.concatenate([jnp.where(head == slot, tables, 0.0) for slot in range(2)], axis=1)], axis=0)

    tables_out, small_out = [], []
    blocks = [(r, block) for r in range(rows) for block in range(slots // B)]
    chains = {"D": down_chain, "U": up_chain, "A": attn_chain}
    for name in ORDER:
        if name == "T":
            r, block = blocks[len(tables_out)]
            tables_out.append(table_grads(r, block, order.tie(lengths), bucket_line,
                                          bucket_horizontal, bucket_vertical, marks[r]))
            order.mark(tables_out[-1])
        elif name == "G":
            give = order.tie(give)
            order.mark(give)
            received = to_peer(give)
        elif name == "P":
            chains["S"] = small_steps(order, pack(), count, small_out)
        else:
            advance(chains[name])
    finish(*chains.values())
    packed = small_out[0]
    grads_in = grads_in + received.astype(f32).reshape(rows, half, width)
    grad_down = in_order(core, *down_out).reshape(down_project.shape).astype(f32)
    mine, other = up_out
    grad_up = jnp.concatenate(arranged(core, mine, other), axis=1).astype(f32)
    buffer = attn_out[0].astype(f32)
    grad_attn = jnp.stack([buffer[:, c * local:(c + 1) * local] for c in range(3)])
    grad_out = jnp.concatenate([buffer[:local, 3 * local:], buffer[local:, 3 * local:]], axis=1)

    rows_of = lambda at, size: lax.dynamic_slice_in_dim(packed, at, size, 0)
    grad_bias = rows_of(6 + 2 * head, 2).reshape(-1)
    grad_attn_bias = rows_of(10 + head, 1).reshape(2, local)
    marks = jnp.where(head == 0, packed[16:, :bins], packed[16:, room:room + bins])[:heads].T
    first, second = table_line.shape[0], table_horizontal.shape[0]
    return (
        output,
        grads_in,
        grad_attn,
        grad_attn_bias,
        marks[:first],
        marks[first:first + second],
        marks[first + second:],
        grad_out,
        packed[0],
        packed[1],
        packed[2],
        grad_up,
        grad_bias,
        grad_down,
        packed[3],
        packed[4],
        packed[5],
    )


def solution(mesh):
    return jax.shard_map(
        functools.partial(body, mesh.shape["dp"]),
        mesh=mesh,
        in_specs=(
            P("dp", None, None),
            P("dp", None),
            P("dp", None),
            P("dp", None, None),
            P("dp", None, None),
            P("dp", None, None),
            P(None, None, "head"),
            P(None, "head"),
            P(None, "head"),
            P(None, "head"),
            P(None, "head"),
            P("head", None),
            P(),
            P(),
            P(),
            P(None, "head"),
            P("head"),
            P("head", None),
            P(),
            P(),
            P(),
            P("dp", "head", None),
        ),
        out_specs=(
            P("dp", "head", None),
            P("dp", "head", None),
            P(None, None, "head"),
            P(None, "head"),
            P(None, "head"),
            P(None, "head"),
            P(None, "head"),
            P("head", None),
            P(),
            P(),
            P(),
            P(None, "head"),
            P("head"),
            P("head", None),
            P(),
            P(),
            P(),
        ),
        check_vma=False,
    )
```

```python
import functools
import math

import jax
import jax.numpy as jnp
from jax import lax
from jax.experimental import pallas as pl
from jax.experimental.pallas import tpu as pltpu
from jax.sharding import PartitionSpec as P

B = 128

PACK = 16


def gather_dims(axis):
    return lax.GatherDimensionNumbers(
        offset_dims=(), collapsed_slice_dims=(axis,), start_index_map=(axis,),
        operand_batching_dims=(1 - axis,), start_indices_batching_dims=(1 - axis,))


def pick(table, index, axis):
    return lax.gather(table, index[:, :, None], gather_dims(axis), (1, 1),
                      mode=lax.GatherScatterMode.PROMISE_IN_BOUNDS)


def two_heads(values, left):
    zero = jnp.zeros_like(values)
    return jnp.concatenate([jnp.where(left, values, zero), jnp.where(left, zero, values)], axis=0)


def doc_span(len_ref, row, first, last):
    edge = 0
    start = 0
    stop = 0
    for k in range(len_ref.shape[1]):
        begin = edge
        edge = edge + len_ref[row, k]
        start = jnp.where(begin <= first, begin, start)
        stop = jnp.where(begin <= last, edge, stop)
    return start // B, (stop + (B - 1)) // B

def fwd_kernel(row, len_ref, q_ref, k_ref, v_ref, pad_ref, bl_ref, bh_ref, bv_ref, line_ref, plane_ref,
               probs_ref, ctx_ref, sc, qs, best, mass, mixed):
    qb = pl.program_id(0)
    heads = sc.shape[1]
    pairs = heads // 2
    lane = lax.broadcasted_iota(jnp.int32, (B, B), 1)
    left = lane < (B // 2)
    first = qb * B
    low, high = doc_span(len_ref, row, first, first + B - 1)
    sub = lax.broadcasted_iota(jnp.int32, (B, B), 0) + first
    edges = []
    edge = 0
    for k in range(len_ref.shape[1]):
        edge = edge + len_ref[row, k]
        edges.append(edge)
    seg_q = sum(((sub >= e).astype(jnp.int32) for e in edges))
    for p in range(pairs):
        qs[p] = two_heads(q_ref[:, p * B:(p + 1) * B], left)

    def scores(t, carry):
        key_at = lane + t * B
        at = pl.ds(pl.multiple_of(t * B, B), B)
        seg_k = sum(((key_at >= e).astype(jnp.int32) for e in edges))
        real = jnp.broadcast_to(pad_ref[:, at], (B, B)) > 0
        allowed = ((seg_q == seg_k) & real) | (sub == key_at)
        parts = []
        for g in range(B // PACK):
            rows = slice(g * PACK, g * PACK + PACK)
            line = bl_ref[rows, at].astype(jnp.int16)
            parts.append((line & jnp.int16(PACK - 1), line >= jnp.int16(PACK),
                          bh_ref[rows, at].astype(jnp.int16), (bv_ref[rows, at] + 64).astype(jnp.int16)))
        for p in range(pairs):
            raw = lax.dot_general(qs[p], k_ref[at, p * B:(p + 1) * B], (((1,), (1,)), ((), ())),
                                  preferred_element_type=jnp.float32)
            for s in range(2):
                h = 2 * p + s
                plane = plane_ref[h]
                for g, (place, upper, horiz, vert) in enumerate(parts):
                    rows = slice(g * PACK, g * PACK + PACK)
                    found = jnp.where(upper, pick(line_ref[h, PACK:2 * PACK, :], place, 0),
                                      pick(line_ref[h, 0:PACK, :], place, 0))
                    rel = ((found.astype(jnp.float32) + pick(plane, horiz, 1).astype(jnp.float32))
                           + pick(plane, vert, 1).astype(jnp.float32))
                    val = jnp.where(allowed[rows], raw[s * B + g * PACK:s * B + (g + 1) * PACK, :] + rel,
                                    -1000000000.0)
                    sc[t, h, rows, :] = val
                    best[h, rows, :] = jnp.maximum(best[h, rows, :], val)
        return carry

    best[...] = jnp.full(best.shape, -3.0e38, jnp.float32)
    mass[...] = jnp.zeros_like(mass)
    mixed[...] = jnp.zeros_like(mixed)
    lax.fori_loop(low, high, scores, 0)
    for h in range(heads):
        best[h] = jnp.broadcast_to(jnp.max(best[h], axis=-1, keepdims=True), (B, B))

    def expo(t, carry):
        for h in range(heads):
            e = jnp.exp(sc[t, h] - best[h])
            sc[t, h] = e
            mass[h] += e
        return carry

    lax.fori_loop(low, high, expo, 0)
    for h in range(heads):
        mass[h] = jnp.broadcast_to(1.0 / jnp.sum(mass[h], axis=-1, keepdims=True), (B, B))

    def mix(t, carry):
        at = pl.ds(pl.multiple_of(t * B, B), B)
        for p in range(pairs):
            low_pair = []
            for s in range(2):
                h = 2 * p + s
                pr = sc[t, h] * mass[h]
                probs_ref[t, h] = pr
                low_pair.append(pr.astype(jnp.bfloat16))
            mixed[p] += jnp.dot(jnp.concatenate(low_pair, axis=0), v_ref[at, p * B:(p + 1) * B],
                                preferred_element_type=jnp.float32)
        return carry

    lax.fori_loop(low, high, mix, 0)
    for p in range(pairs):
        ctx_ref[:, p * B:(p + 1) * B] = jnp.where(left, mixed[p, :B, :], mixed[p, B:, :]).astype(jnp.bfloat16)


def attn_fwd(row, lengths, q, k, v, pad, bl, bh, bv, line, plane):
    slots, width = q.shape[1:]
    pairs = width // B
    tiles = slots // B
    row_block = lambda n: pl.BlockSpec((None, B, n), lambda i, L: (row, i, 0))
    return pl.pallas_call(
        functools.partial(fwd_kernel, row),
        grid_spec=pltpu.PrefetchScalarGridSpec(
            num_scalar_prefetch=1, grid=(tiles,),
            in_specs=[
                row_block(width),
                pl.BlockSpec((None, slots, width), lambda i, L: (row, 0, 0)),
                pl.BlockSpec((None, slots, width), lambda i, L: (row, 0, 0)),
                pl.BlockSpec((None, 1, slots), lambda i, L: (row, 0, 0)),
                row_block(slots), row_block(slots), row_block(slots),
                pl.BlockSpec(line.shape, lambda i, L: (0, 0, 0)),
                pl.BlockSpec(plane.shape, lambda i, L: (0, 0, 0)),
            ],
            out_specs=[
                pl.BlockSpec((None, tiles, 2 * pairs, B, B), lambda i, L: (i, 0, 0, 0, 0)),
                pl.BlockSpec((B, width), lambda i, L: (i, 0)),
            ],
            scratch_shapes=[
                pltpu.VMEM((tiles, 2 * pairs, B, B), jnp.float32),
                pltpu.VMEM((pairs, 2 * B, B), jnp.bfloat16),
                pltpu.VMEM((2 * pairs, B, B), jnp.float32),
                pltpu.VMEM((2 * pairs, B, B), jnp.float32),
                pltpu.VMEM((pairs, 2 * B, B), jnp.float32),
            ]),
        out_shape=[
            jax.ShapeDtypeStruct((tiles, tiles, 2 * pairs, B, B), jnp.float32),
            jax.ShapeDtypeStruct((slots, width), jnp.bfloat16),
        ],
        compiler_params=pltpu.CompilerParams(vmem_limit_bytes=48 << 20),
        cost_estimate=pl.CostEstimate(flops=1, transcendentals=0, bytes_accessed=1),
        name="attn_forward",
    )(lengths, q, k, v, pad, bl, bh, bv, line, plane)


NT = (((1,), (1,)), ((), ()))
TN = (((0,), (0,)), ((), ()))

def bwd_kernel(row, factor, len_ref, q_ref, k_ref, v_ref, gctx_ref, ctx_ref, probs_ref, *rest):
    pairs, tiles = q_ref.shape[1] // B, probs_ref.shape[0]
    ds_ref, three_ref, *scratch = rest[len(rest) - 6 * pairs - 2:]
    dks, dvs, dqs, inner, qs, gs = (scratch[n * pairs:(n + 1) * pairs] for n in range(6))
    qb = pl.program_id(0)
    lane = lax.broadcasted_iota(jnp.int32, (B, B), 1)
    left = lane < (B // 2)

    @pl.when(qb == 0)
    def _():
        for ref in dks + dvs:
            ref[...] = jnp.zeros_like(ref)

    first = qb * B
    low, high = doc_span(len_ref, row, first, first + B - 1)
    for p in range(pairs):
        cols = slice(p * B, (p + 1) * B)
        gctx = gctx_ref[:, cols]
        qs[p][...] = two_heads(q_ref[:, cols], left)
        gs[p][...] = two_heads(gctx, left)
        prod = gctx.astype(jnp.float32) * ctx_ref[:, cols].astype(jnp.float32)
        inner[p][...] = jnp.broadcast_to(jnp.sum(two_heads(prod, left), axis=-1, keepdims=True), (2 * B, B))
        dqs[p][...] = jnp.zeros_like(dqs[p])

    def tile(t, carry):
        at = pl.ds(pl.multiple_of(t * B, B), B)
        for p in range(pairs):
            cols = slice(p * B, (p + 1) * B)
            gp = lax.dot_general(gs[p][...], v_ref[at, cols], NT, preferred_element_type=jnp.float32)
            probs_low, g_scores = [], []
            for s in range(2):
                rows = slice(s * B, (s + 1) * B)
                pr = probs_ref[t, 2 * p + s]
                ds = (pr * (gp[rows, :] - inner[p][rows, :])).astype(jnp.bfloat16)
                ds_ref[t, 2 * p + s] = ds
                g_scores.append(ds)
                probs_low.append(pr.astype(jnp.bfloat16))
            ds = jnp.concatenate(g_scores, axis=0)
            mix = jnp.concatenate(probs_low, axis=0)
            dvs[p][t] += lax.dot_general(mix, gs[p][...], TN, preferred_element_type=jnp.float32)
            dks[p][t] += lax.dot_general(ds, qs[p][...], TN, preferred_element_type=jnp.float32)
            dqs[p][...] += jnp.dot(ds, k_ref[at, cols], preferred_element_type=jnp.float32)
        return carry

    lax.fori_loop(low, high, tile, 0)
    for p in range(pairs):
        dq = jnp.where(left, dqs[p][0:B, :], dqs[p][B:2 * B, :]) * factor
        three_ref[pl.ds(pl.multiple_of(first, B), B), p * B:(p + 1) * B] = dq.astype(jnp.bfloat16)

    @pl.when(qb == tiles - 1)
    def _():
        for p in range(pairs):
            for t in range(tiles):
                rows = slice(t * B, (t + 1) * B)
                three_ref[rows, (pairs + p) * B:(pairs + p + 1) * B] = dks[p][t].astype(jnp.bfloat16)
                three_ref[rows, (2 * pairs + p) * B:(2 * pairs + p + 1) * B] = dvs[p][t].astype(jnp.bfloat16)


def attn_bwd(row, factor, lengths, q, k, v, gctx, ctx, probs, kept=None):
    slots, width = q.shape[1:]
    pairs, tiles = width // B, slots // B
    part = pl.BlockSpec((B, width), lambda i, L: (i, 0))
    three = pl.BlockSpec((None, slots, 3 * width), lambda i, L: (row, 0, 0))
    mine = pl.BlockSpec((None, B, width), lambda i, L: (row, i, 0))
    whole = pl.BlockSpec((None, slots, width), lambda i, L: (row, 0, 0))
    pairs_of = pl.BlockSpec((None, tiles, 2 * pairs, B, B), lambda i, L: (i, 0, 0, 0, 0))
    kept = () if kept is None else (kept,)
    return pl.pallas_call(
        functools.partial(bwd_kernel, row, factor),
        grid_spec=pltpu.PrefetchScalarGridSpec(
            num_scalar_prefetch=1, grid=(tiles,),
            in_specs=[mine, whole, whole, part, part, pairs_of]
            + [pl.BlockSpec(memory_space=pl.ANY)] * len(kept),
            out_specs=[pairs_of, three],
            scratch_shapes=[pltpu.VMEM((tiles, B, B), jnp.float32)] * (2 * pairs)
            + [pltpu.VMEM((2 * B, B), jnp.float32)] * (2 * pairs)
            + [pltpu.VMEM((2 * B, B), jnp.bfloat16)] * (2 * pairs)),
        out_shape=[jax.ShapeDtypeStruct(probs.shape, jnp.bfloat16),
                   jax.ShapeDtypeStruct((q.shape[0], slots, 3 * width), jnp.bfloat16)],
        input_output_aliases={7: 1} if kept else {},
        compiler_params=pltpu.CompilerParams(vmem_limit_bytes=48 << 20),
        cost_estimate=pl.CostEstimate(flops=1, transcendentals=0, bytes_accessed=1),
        name="attn_backward",
    )(lengths, q, k, v, gctx, ctx, probs, *kept)

BINS = 160
SPREADS = 3


def hist_kernel(row, step, len_ref, bl_ref, bh_ref, bv_ref, ds_ref, out_ref, *spreads):
    tiles, heads = ds_ref.shape[0], ds_ref.shape[1]
    docs = len_ref.shape[1]
    lane = lax.broadcasted_iota(jnp.int32, (PACK, B), 1)
    sub = lax.broadcasted_iota(jnp.int32, (PACK, B), 0)
    for spread in spreads:
        spread[...] = jnp.zeros_like(spread)

    floor, roof = step * B, (step + 1) * B
    starts, ends, firsts, lasts, upto = [], [], [], [], []
    edge, count = 0, 0
    for d in range(docs):
        starts.append(edge)
        edge = edge + len_ref[row, d]
        ends.append(edge)
        firsts.append(jnp.maximum(starts[d], floor))
        lasts.append(jnp.maximum(jnp.minimum(edge, roof), firsts[d]))
        here = (lasts[d] + (PACK - 1)) // PACK - firsts[d] // PACK
        count = count + jnp.where(lasts[d] > firsts[d], here, 0)
        upto.append(count)

    def group(g, spread):
        start, end, first, last = starts[0], ends[0], firsts[0], lasts[0]
        block = firsts[0] // PACK + g
        for d in range(1, docs):
            past = g >= upto[d - 1]
            start, end, first, last, block = (
                jnp.where(past, new, old) for new, old in
                ((starts[d], start), (ends[d], end), (firsts[d], first), (lasts[d], last),
                 (firsts[d] // PACK + (g - upto[d - 1]), block)))
        last = jnp.where(g < count, last, first)
        start = jnp.minimum(start, tiles * B - 1)
        block = jnp.clip(block - step * (B // PACK), 0, B // PACK - 1)
        tile = start // B
        left = start - tile * B
        turn = jnp.where(left == 0, 0, B - left)
        rows = pl.ds(pl.multiple_of(block * PACK, PACK), PACK)
        token = sub + (floor + block * PACK)
        inside = (token >= first) & (token < last)
        lives = [inside & (lane + part * B < end - start) for part in range(2)]
        before = lane < B - left
        spots = [jnp.minimum(tile + part, tiles - 1) for part in range(3)]

        def moved(parts):
            parts = [pltpu.roll(p, turn, 1) for p in parts]
            return [jnp.where(before, parts[part], parts[part + 1]) for part in range(2)]

        for h in range(heads):
            vals = moved([ds_ref[s, h, rows, :].astype(jnp.float32) for s in spots])
            for part in range(2):
                spread[part, pl.ds(h, PACK, stride=8), :] = jnp.where(lives[part], vals[part], 0.0)
        codes = []
        for s in spots:
            at = pl.ds(pl.multiple_of(s * B, B), B)
            codes.append(bl_ref[rows, at] + 32 * bh_ref[rows, at] + 2048 * bv_ref[rows, at])
        code = jnp.concatenate(moved(codes), axis=1)
        index = [(code & 31).astype(jnp.int16), ((code >> 5) & 63).astype(jnp.int16),
                 (code >> 11).astype(jnp.int16)]
        one, zero = jnp.ones((), jnp.bfloat16), jnp.zeros((), jnp.bfloat16)
        grads, hots = [], []
        for r in range(PACK):
            hot = []
            for ix, n in zip(index, (32, 64, 64)):
                bins = lax.broadcasted_iota(jnp.int16, (n, 2 * B), 0)
                line = jnp.broadcast_to(ix[r:r + 1, :], (n, 2 * B))
                hot.append(jnp.where(bins == line, one, zero))
            hots.append(jnp.concatenate(hot, axis=0))
            grads += [spread[part, r * 8:r * 8 + 8, :].astype(jnp.bfloat16) for part in range(2)]
        return lax.dot_general(jnp.concatenate(grads, axis=1), jnp.concatenate(hots, axis=1), NT,
                               preferred_element_type=jnp.float32)

    def several(turn, sums):
        return tuple(x + group(len(spreads) * turn + n, spread)
                     for n, (x, spread) in enumerate(zip(sums, spreads)))

    none = jnp.zeros((8, BINS), jnp.float32)
    turns = (count + (len(spreads) - 1)) // len(spreads)
    out_ref[...] = sum(lax.fori_loop(0, turns, several, tuple(none for _ in spreads)))


def table_grads(row, step, lengths, bl, bh, bv, ds):
    slots = bl.shape[1]
    tiles, heads = ds.shape[0], ds.shape[2]
    block = pl.BlockSpec((None, B, slots), lambda i, L: (row, step, 0))
    return pl.pallas_call(
        functools.partial(hist_kernel, row, step),
        grid_spec=pltpu.PrefetchScalarGridSpec(
            num_scalar_prefetch=1, grid=(1,),
            in_specs=[block, block, block,
                      pl.BlockSpec((None, tiles, heads, B, B), lambda i, L: (step, 0, 0, 0, 0))],
            out_specs=pl.BlockSpec((8, BINS), lambda i, L: (0, 0)),
            scratch_shapes=[pltpu.VMEM((2, 8 * PACK, B), jnp.float32)] * SPREADS),
        out_shape=jax.ShapeDtypeStruct((8, BINS), jnp.float32),
        compiler_params=pltpu.CompilerParams(vmem_limit_bytes=48 << 20),
        cost_estimate=pl.CostEstimate(flops=1, transcendentals=0, bytes_accessed=1),
        name="table_grads",
    )(lengths, bl, bh, bv, ds)


f32, low = jnp.float32, jnp.bfloat16
SWAP = [(0, 1), (1, 0)]
ORDER = "UATDTADTUGATDUTATDTUADTPSUASDUSASSU"


def normalize(values):
    mean = jnp.mean(values, axis=-1, keepdims=True)
    centered = values - mean
    scale = lax.rsqrt(jnp.mean(centered * centered, axis=-1, keepdims=True) + 1e-12)
    return centered * scale, scale


def normalize_back(grad, normed, scale, gain):
    scaled = grad * gain
    first = jnp.mean(scaled, axis=-1, keepdims=True)
    second = jnp.mean(scaled * normed, axis=-1, keepdims=True)
    return scale * (scaled - first - normed * second)


def times(left, right, left_dim, right_dim):
    return lax.dot_general(left, right, (((left_dim,), (right_dim,)), ((), ())),
                           preferred_element_type=f32)


def flips(count, bit):
    return [(i, i ^ (1 << bit)) for i in range(count)]


def to_peer(values):
    return lax.ppermute(values, "head", SWAP)


def plus(left, right):
    return (left.astype(f32) + right.astype(f32)).astype(low)


def arranged(bit_value, mine, other):
    return jnp.where(bit_value == 0, mine, other), jnp.where(bit_value == 0, other, mine)


def in_order(bit_value, mine, other):
    return jnp.stack(arranged(bit_value, mine, other))


class Order:
    def __init__(self):
        self.last = None

    def tie(self, values):
        if self.last is None:
            return values
        values, self.last = lax.optimization_barrier((values, self.last))
        return values

    def mark(self, values):
        self.last = values


def total(terms, lift, size, axis):
    return sum(lax.dynamic_slice_in_dim(values, start + lift, size, axis).astype(f32)
               for values, start in terms)


def halve(order, terms, size, axis, count, bit):
    half = size // 2
    mine = (lax.axis_index("dp") >> bit) & 1
    send = total(terms, (1 - mine) * half, half, axis).astype(low)
    order.mark(send)
    got = lax.ppermute(send, "dp", flips(count, bit))
    yield
    return [(values, start + mine * half) for values, start in terms] + [(order.tie(got), 0)]


def gather_steps(order, values, count, bits):
    index = lax.axis_index("dp")
    for bit in reversed(bits):
        order.mark(values)
        got = lax.ppermute(values, "dp", flips(count, bit))
        yield
        both = in_order((index >> bit) & 1, values, order.tie(got))
        values = both.reshape((2 * values.shape[0],) + values.shape[1:])
    return values


def unit_steps(order, kept, given, count, axis, split, out):
    bits = list(range(1, count.bit_length() - 1))
    size = kept.shape[axis]
    given = order.tie(given)
    order.mark(given)
    got = lax.ppermute(given, "dp", flips(count, 0))
    yield
    terms = [(kept, 0), (order.tie(got), 0)]
    terms = yield from halve(order, terms, size, axis, count, bits[0])
    size //= 2
    mine, other = ([(split(values)[c], start) for values, start in terms] for c in range(2))
    send = total(other, 0, size, 0).astype(low)
    order.mark(send)
    got = to_peer(send)
    yield
    terms = mine + [(order.tie(got), 0)]
    for bit in bits[1:]:
        terms = yield from halve(order, terms, size, 0, count, bit)
        size //= 2
    mine = yield from gather_steps(order, total(terms, 0, size, 0).astype(low), count, bits)
    order.mark(mine)
    other = lax.ppermute(mine, "dp", flips(count, 0))
    yield
    out += [mine, order.tie(other)]


def buffer_steps(order, values, count, out):
    bits = list(range(count.bit_length() - 1))
    size = values.shape[0]
    terms = [(order.tie(values), 0)]
    for bit in bits:
        terms = yield from halve(order, terms, size, 0, count, bit)
        size //= 2
    values = yield from gather_steps(order, total(terms, 0, size, 0).astype(low), count, bits)
    order.mark(values)
    out.append(values)


def small_steps(order, values, count, out):
    values = order.tie(values)
    for bit in [None] + list(range(count.bit_length() - 1)):
        order.mark(values)
        got = to_peer(values) if bit is None else lax.ppermute(values, "dp", flips(count, bit))
        yield
        values = values + order.tie(got)
    order.mark(values)
    out.append(values)


def advance(*chains):
    for chain in chains:
        next(chain, None)


def finish(*chains):
    left = list(chains)
    while left:
        for chain in list(left):
            try:
                next(chain)
            except StopIteration:
                left.remove(chain)


def body(
    count,
    hidden,
    lengths,
    padding,
    bucket_line,
    bucket_horizontal,
    bucket_vertical,
    attn_project,
    attn_bias,
    table_line,
    table_horizontal,
    table_vertical,
    out_project,
    out_bias,
    attn_gain,
    attn_shift,
    hidden_project,
    hidden_bias,
    down_project,
    down_bias,
    final_gain,
    final_shift,
    cotangent,
):
    rows, slots, width = hidden.shape
    half = cotangent.shape[1]
    heads = table_line.shape[1]
    local = attn_project.shape[2]
    units = hidden_project.shape[1]
    part = units // 2
    factor = 1.0 / math.sqrt(local // heads)
    head = lax.axis_index("head")
    index = lax.axis_index("dp")
    core = index & 1
    offset = head * half
    every = list(range(count.bit_length() - 1))

    def split(values, dim):
        return [lax.dynamic_slice_in_dim(values, c * part, part, dim) for c in (core, 1 - core)]

    def joined(own_parts, got, dim):
        mine, rest = own_parts
        beside = lax.ppermute(got, "dp", flips(count, 0))
        return [jnp.concatenate([mine, got], axis=dim), jnp.concatenate([rest, beside], axis=dim)]

    side = (index >> 1) & 1
    down_mine = lax.dynamic_slice_in_dim(down_project, core * part + side * (part // 2), part // 2, 0)
    down_got = to_peer(down_mine)
    down_mine, hidden_project = lax.optimization_barrier((down_mine, hidden_project))
    up_mine = lax.dynamic_slice_in_dim(hidden_project, core * part, part, 1)
    up_got = to_peer(up_mine)
    up_mine, hidden, hidden_project, down_project = lax.optimization_barrier(
        (up_mine, hidden, hidden_project, down_project))
    bias_got = to_peer(hidden_bias)

    planes = jnp.concatenate([table_horizontal, table_vertical], axis=0)
    bins = table_line.shape[0] + planes.shape[0]
    lines = jnp.broadcast_to(table_line.T[:, :, None], (heads, table_line.shape[0], B))
    planes = jnp.broadcast_to(planes.T[:, None, :], (heads, PACK, planes.shape[0]))
    pad = padding[:, None, :]
    bucket_line, bucket_horizontal, bucket_vertical = (
        pltpu.with_memory_space_constraint(x, pltpu.HBM)
        for x in (bucket_line, bucket_horizontal, bucket_vertical))

    flat = hidden.reshape(rows * slots, width)
    query = ((times(flat, attn_project[0], 1, 0) + attn_bias[0].astype(f32)).astype(low)
             * jnp.asarray(factor, low))
    key = times(flat, attn_project[1], 1, 0).astype(low)
    value = (times(flat, attn_project[2], 1, 0) + attn_bias[1].astype(f32)).astype(low)
    query, key, value = (pltpu.with_memory_space_constraint(x.reshape(rows, slots, local), pltpu.HBM)
                         for x in (query, key, value))

    def own(values):
        return lax.dynamic_slice_in_dim(values, offset, half, 0)

    def others(values):
        return lax.dynamic_slice_in_dim(values, half - offset, half, 0)

    fronts, attn_sum, attn_got = [], [], []
    for r in range(rows):
        if r == 1:
            lengths, down_got = lax.optimization_barrier((lengths, down_got))
            down_beside = lax.ppermute(down_got, "dp", flips(count, 1))
        probs, context = attn_fwd(r, lengths, query, key, value, pad, bucket_line,
                                  bucket_horizontal, bucket_vertical, lines, planes)
        if r == 1:
            context, down_beside = lax.optimization_barrier((context, down_beside))
        fronts.append((probs, context))
        send = times(others(context), out_project, 1, 0).astype(low)
        got = to_peer(send)
        attn_sum.append(times(own(context), out_project, 1, 0))
        attn_got.append(got)
    (send, hidden_project, down_project, cotangent, norm_rows, out_bias, down_bias, hidden_bias, bias_got,
     hidden) = lax.optimization_barrier(
        (send, hidden_project, down_project, cotangent, (attn_gain, attn_shift, final_gain, final_shift),
         out_bias, down_bias, hidden_bias, bias_got, hidden))
    biases = [jnp.concatenate([x, y]) for x, y in zip(split(hidden_bias, 0), split(bias_got, 0))]
    gain_first, shift_first, gain_last, shift_last = (x.astype(f32) for x in norm_rows)
    up_parts = [up_mine, lax.dynamic_slice_in_dim(hidden_project, (1 - core) * part, part, 1)]
    down_parts = split(down_project, 0)
    up_got, down_beside, attn_got = lax.optimization_barrier((up_got, down_beside, attn_got))
    down_got = in_order(side, down_got, down_beside)
    ups = joined(up_parts, up_got, 1)
    downs = joined(down_parts, down_got.reshape(part, width), 0)
    attn_sum = [x + got.astype(f32) for x, got in zip(attn_sum, attn_got)]
    tokens = lax.dynamic_slice_in_dim(hidden, offset, half, 1).reshape(rows * half, width).astype(f32)
    normed, scale = normalize(tokens + jnp.concatenate(attn_sum, axis=0) + out_bias.astype(f32))
    mid = normed * gain_first + shift_first
    mid_low = mid.astype(low)

    actives, slopes = [], []
    total = None
    for up, down, bias in zip(ups, downs, biases):
        inner = times(mid_low, up, 1, 0) + bias.astype(f32)
        bell = 0.5 * (1.0 + lax.erf(inner * math.sqrt(0.5)))
        actives.append((inner * bell).astype(low))
        slopes.append(bell + inner * (jnp.exp(-0.5 * inner * inner) * (1.0 / math.sqrt(2.0 * math.pi))))
        term = times(actives[-1], down, 1, 0)
        total = term if total is None else total + term
    normed_final, scale_final = normalize(mid + total + down_bias.astype(f32))
    output = (normed_final * gain_last + shift_last).astype(low).reshape(rows, half, width)

    above = cotangent.reshape(rows * half, width).astype(f32)
    g_final = normalize_back(above, normed_final, scale_final, gain_last)
    g_low = g_final.astype(low)
    order = Order()
    total = None
    inners = []
    for up, down, slope in zip(ups, downs, slopes):
        g_inner = (times(g_low, down, 1, 1) * slope).astype(low)
        inners.append(g_inner)
        term = times(g_inner, up, 1, 1)
        total = term if total is None else total + term
    g_mid = g_final + total
    g_attn = normalize_back(g_mid, normed, scale, gain_first)
    g_attn_low = g_attn.astype(low).reshape(rows, half, width)
    g_others = [to_peer(g_attn_low[r]) for r in range(rows)]
    order.mark(g_attn_low)
    down_out, up_out, attn_out = [], [], []
    g_low = order.tie(g_low)
    kept, given = (times(active, g_low, 0, 0).astype(low) for active in actives)
    down_chain = unit_steps(order, *(x.reshape(2, part, width) for x in (kept, given)), count, 1,
                            lambda v: (v[0], v[1]), down_out)
    advance(down_chain)
    mid_low = order.tie(mid_low)
    kept, given = (times(mid_low, g_inner, 0, 0).astype(low) for g_inner in inners)
    up_chain = unit_steps(order, kept, given, count, 0, lambda v: (v[:, :part], v[:, part:]), up_out)
    advance(up_chain, down_chain)
    g_attn = g_attn.reshape(rows, half, width)

    marks, three, grad_out = [], None, 0.0
    for r in range(rows):
        probs, context = fronts[r]
        g_all = in_order(head, g_attn_low[r], order.tie(g_others[r])).reshape(slots, width)
        g_context = times(g_all, out_project, 1, 1).astype(low)
        g_scores, three = attn_bwd(r, factor, lengths, query, key, value, g_context, context, probs, three)
        order.mark(g_scores)
        marks.append(g_scores)
        grad_out = grad_out + times(context, g_all, 0, 0)
        advance(up_chain if r == 0 else down_chain)
    grad_attn = times(flat, three.reshape(rows * slots, 3 * local), 0, 0).astype(low)
    grad_out = jnp.concatenate([grad_out[:, :local], grad_out[:, local:]], axis=0).astype(low)
    attn_chain = buffer_steps(order, jnp.concatenate([grad_attn, grad_out], axis=1), count, attn_out)
    advance(attn_chain)
    every_project = jnp.concatenate([attn_project[c] for c in range(3)], axis=1)
    theirs = lax.dynamic_slice_in_dim(three, half - offset, half, 1)
    give = times(theirs.reshape(rows * half, 3 * local), every_project, 1, 1).astype(low)
    mine = lax.dynamic_slice_in_dim(three, offset, half, 1)
    mine = times(mine.reshape(rows * half, 3 * local), every_project, 1, 1)
    grads_in = mine.reshape(rows, half, width) + g_attn
    give, grads_in = lax.optimization_barrier((give, grads_in))

    room = width // 2

    def pack():
        sums = [jnp.sum(x.reshape(rows * half, width), axis=0, keepdims=True) for x in
                (g_attn, g_mid * normed, g_mid, g_final, above * normed_final, above)]
        sums, units_in, three_sums, tables = order.tie(
            (sums, inners, jnp.sum(three.astype(f32).reshape(rows * slots, 3 * local), axis=0,
                                       keepdims=True), sum(tables_out)))
        unit_sums = [jnp.sum(x.astype(f32), axis=0, keepdims=True) for x in units_in]
        ours, others_ = (jnp.concatenate(arranged(core, *(x[:, c * part:(c + 1) * part] for x in unit_sums)),
                                         axis=0) for c in range(2))
        pair = jnp.concatenate([three_sums[:, :local], three_sums[:, 2 * local:]], axis=1)
        tables = jnp.pad(tables, ((0, 0), (0, room - bins)))
        return jnp.concatenate(
            sums + list(arranged(head, ours, others_))
            + [jnp.where(head == slot, pair, 0.0) for slot in range(2)]
            + [jnp.zeros((4, width), f32),
               jnp.concatenate([jnp.where(head == slot, tables, 0.0) for slot in range(2)], axis=1)], axis=0)

    tables_out, small_out = [], []
    blocks = [(r, block) for r in range(rows) for block in range(slots // B)]
    chains = {"D": down_chain, "U": up_chain, "A": attn_chain}
    for name in ORDER:
        if name == "T":
            r, block = blocks[len(tables_out)]
            tables_out.append(table_grads(r, block, order.tie(lengths), bucket_line,
                                          bucket_horizontal, bucket_vertical, marks[r]))
            order.mark(tables_out[-1])
        elif name == "G":
            give = order.tie(give)
            order.mark(give)
            received = to_peer(give)
        elif name == "P":
            chains["S"] = small_steps(order, pack(), count, small_out)
        else:
            advance(chains[name])
    finish(*chains.values())
    packed = small_out[0]
    grads_in = grads_in + received.astype(f32).reshape(rows, half, width)
    grad_down = in_order(core, *down_out).reshape(down_project.shape).astype(f32)
    mine, other = up_out
    grad_up = jnp.concatenate(arranged(core, mine, other), axis=1).astype(f32)
    buffer = attn_out[0].astype(f32)
    grad_attn = jnp.stack([buffer[:, c * local:(c + 1) * local] for c in range(3)])
    grad_out = jnp.concatenate([buffer[:local, 3 * local:], buffer[local:, 3 * local:]], axis=1)

    rows_of = lambda at, size: lax.dynamic_slice_in_dim(packed, at, size, 0)
    grad_bias = rows_of(6 + 2 * head, 2).reshape(-1)
    grad_attn_bias = rows_of(10 + head, 1).reshape(2, local)
    marks = jnp.where(head == 0, packed[16:, :bins], packed[16:, room:room + bins])[:heads].T
    first, second = table_line.shape[0], table_horizontal.shape[0]
    return (
        output,
        grads_in,
        grad_attn,
        grad_attn_bias,
        marks[:first],
        marks[first:first + second],
        marks[first + second:],
        grad_out,
        packed[0],
        packed[1],
        packed[2],
        grad_up,
        grad_bias,
        grad_down,
        packed[3],
        packed[4],
        packed[5],
    )


def solution(mesh):
    return jax.shard_map(
        functools.partial(body, mesh.shape["dp"]),
        mesh=mesh,
        in_specs=(
            P("dp", None, None),
            P("dp", None),
            P("dp", None),
            P("dp", None, None),
            P("dp", None, None),
            P("dp", None, None),
            P(None, None, "head"),
            P(None, "head"),
            P(None, "head"),
            P(None, "head"),
            P(None, "head"),
            P("head", None),
            P(),
            P(),
            P(),
            P(None, "head"),
            P("head"),
            P("head", None),
            P(),
            P(),
            P(),
            P("dp", "head", None),
        ),
        out_specs=(
            P("dp", "head", None),
            P("dp", "head", None),
            P(None, None, "head"),
            P(None, "head"),
            P(None, "head"),
            P(None, "head"),
            P(None, "head"),
            P("head", None),
            P(),
            P(),
            P(),
            P(None, "head"),
            P("head"),
            P("head", None),
            P(),
            P(),
            P(),
        ),
        check_vma=False,
    )
```

```python
import functools
import math

import jax
import jax.numpy as jnp
from jax import lax
from jax.experimental import pallas as pl
from jax.experimental.pallas import tpu as pltpu
from jax.sharding import PartitionSpec as P

B = 128

PACK = 16


def gather_dims(axis):
    return lax.GatherDimensionNumbers(
        offset_dims=(), collapsed_slice_dims=(axis,), start_index_map=(axis,),
        operand_batching_dims=(1 - axis,), start_indices_batching_dims=(1 - axis,))


def pick(table, index, axis):
    return lax.gather(table, index[:, :, None], gather_dims(axis), (1, 1),
                      mode=lax.GatherScatterMode.PROMISE_IN_BOUNDS)


def two_heads(values, left):
    zero = jnp.zeros_like(values)
    return jnp.concatenate([jnp.where(left, values, zero), jnp.where(left, zero, values)], axis=0)


def doc_span(len_ref, row, first, last):
    edge = 0
    start = 0
    stop = 0
    for k in range(len_ref.shape[1]):
        begin = edge
        edge = edge + len_ref[row, k]
        start = jnp.where(begin <= first, begin, start)
        stop = jnp.where(begin <= last, edge, stop)
    return start // B, (stop + (B - 1)) // B

def fwd_kernel(row, len_ref, q_ref, k_ref, v_ref, pad_ref, bl_ref, bh_ref, bv_ref, line_ref, plane_ref,
               probs_ref, ctx_ref, sc, qs, best, mass, mixed):
    qb = pl.program_id(0)
    heads = sc.shape[1]
    pairs = heads // 2
    lane = lax.broadcasted_iota(jnp.int32, (B, B), 1)
    left = lane < (B // 2)
    first = qb * B
    low, high = doc_span(len_ref, row, first, first + B - 1)
    sub = lax.broadcasted_iota(jnp.int32, (B, B), 0) + first
    edges = []
    edge = 0
    for k in range(len_ref.shape[1]):
        edge = edge + len_ref[row, k]
        edges.append(edge)
    seg_q = sum(((sub >= e).astype(jnp.int32) for e in edges))
    for p in range(pairs):
        qs[p] = two_heads(q_ref[:, p * B:(p + 1) * B], left)

    def scores(t, carry):
        key_at = lane + t * B
        at = pl.ds(pl.multiple_of(t * B, B), B)
        seg_k = sum(((key_at >= e).astype(jnp.int32) for e in edges))
        real = jnp.broadcast_to(pad_ref[:, at], (B, B)) > 0
        allowed = ((seg_q == seg_k) & real) | (sub == key_at)
        parts = []
        for g in range(B // PACK):
            rows = slice(g * PACK, g * PACK + PACK)
            line = bl_ref[rows, at].astype(jnp.int16)
            parts.append((line & jnp.int16(PACK - 1), line >= jnp.int16(PACK),
                          bh_ref[rows, at].astype(jnp.int16), (bv_ref[rows, at] + 64).astype(jnp.int16)))
        for p in range(pairs):
            raw = lax.dot_general(qs[p], k_ref[at, p * B:(p + 1) * B], (((1,), (1,)), ((), ())),
                                  preferred_element_type=jnp.float32)
            for s in range(2):
                h = 2 * p + s
                plane = plane_ref[h]
                for g, (place, upper, horiz, vert) in enumerate(parts):
                    rows = slice(g * PACK, g * PACK + PACK)
                    found = jnp.where(upper, pick(line_ref[h, PACK:2 * PACK, :], place, 0),
                                      pick(line_ref[h, 0:PACK, :], place, 0))
                    rel = ((found.astype(jnp.float32) + pick(plane, horiz, 1).astype(jnp.float32))
                           + pick(plane, vert, 1).astype(jnp.float32))
                    val = jnp.where(allowed[rows], raw[s * B + g * PACK:s * B + (g + 1) * PACK, :] + rel,
                                    -1000000000.0)
                    sc[t, h, rows, :] = val
                    best[h, rows, :] = jnp.maximum(best[h, rows, :], val)
        return carry

    best[...] = jnp.full(best.shape, -3.0e38, jnp.float32)
    mass[...] = jnp.zeros_like(mass)
    mixed[...] = jnp.zeros_like(mixed)
    lax.fori_loop(low, high, scores, 0)
    for h in range(heads):
        best[h] = jnp.broadcast_to(jnp.max(best[h], axis=-1, keepdims=True), (B, B))

    def expo(t, carry):
        for h in range(heads):
            e = jnp.exp(sc[t, h] - best[h])
            sc[t, h] = e
            mass[h] += e
        return carry

    lax.fori_loop(low, high, expo, 0)
    for h in range(heads):
        mass[h] = jnp.broadcast_to(1.0 / jnp.sum(mass[h], axis=-1, keepdims=True), (B, B))

    def mix(t, carry):
        at = pl.ds(pl.multiple_of(t * B, B), B)
        for p in range(pairs):
            low_pair = []
            for s in range(2):
                h = 2 * p + s
                pr = sc[t, h] * mass[h]
                probs_ref[t, h] = pr
                low_pair.append(pr.astype(jnp.bfloat16))
            mixed[p] += jnp.dot(jnp.concatenate(low_pair, axis=0), v_ref[at, p * B:(p + 1) * B],
                                preferred_element_type=jnp.float32)
        return carry

    lax.fori_loop(low, high, mix, 0)
    for p in range(pairs):
        ctx_ref[:, p * B:(p + 1) * B] = jnp.where(left, mixed[p, :B, :], mixed[p, B:, :]).astype(jnp.bfloat16)


def attn_fwd(row, lengths, q, k, v, pad, bl, bh, bv, line, plane):
    slots, width = q.shape[1:]
    pairs = width // B
    tiles = slots // B
    row_block = lambda n: pl.BlockSpec((None, B, n), lambda i, L: (row, i, 0))
    return pl.pallas_call(
        functools.partial(fwd_kernel, row),
        grid_spec=pltpu.PrefetchScalarGridSpec(
            num_scalar_prefetch=1, grid=(tiles,),
            in_specs=[
                row_block(width),
                pl.BlockSpec((None, slots, width), lambda i, L: (row, 0, 0)),
                pl.BlockSpec((None, slots, width), lambda i, L: (row, 0, 0)),
                pl.BlockSpec((None, 1, slots), lambda i, L: (row, 0, 0)),
                row_block(slots), row_block(slots), row_block(slots),
                pl.BlockSpec(line.shape, lambda i, L: (0, 0, 0)),
                pl.BlockSpec(plane.shape, lambda i, L: (0, 0, 0)),
            ],
            out_specs=[
                pl.BlockSpec((None, tiles, 2 * pairs, B, B), lambda i, L: (i, 0, 0, 0, 0)),
                pl.BlockSpec((B, width), lambda i, L: (i, 0)),
            ],
            scratch_shapes=[
                pltpu.VMEM((tiles, 2 * pairs, B, B), jnp.float32),
                pltpu.VMEM((pairs, 2 * B, B), jnp.bfloat16),
                pltpu.VMEM((2 * pairs, B, B), jnp.float32),
                pltpu.VMEM((2 * pairs, B, B), jnp.float32),
                pltpu.VMEM((pairs, 2 * B, B), jnp.float32),
            ]),
        out_shape=[
            jax.ShapeDtypeStruct((tiles, tiles, 2 * pairs, B, B), jnp.float32),
            jax.ShapeDtypeStruct((slots, width), jnp.bfloat16),
        ],
        compiler_params=pltpu.CompilerParams(vmem_limit_bytes=48 << 20),
        cost_estimate=pl.CostEstimate(flops=1, transcendentals=0, bytes_accessed=1),
        name="attn_forward",
    )(lengths, q, k, v, pad, bl, bh, bv, line, plane)


NT = (((1,), (1,)), ((), ()))
TN = (((0,), (0,)), ((), ()))

def bwd_kernel(row, factor, len_ref, q_ref, k_ref, v_ref, gctx_ref, ctx_ref, probs_ref, *rest):
    pairs, tiles = q_ref.shape[1] // B, probs_ref.shape[0]
    ds_ref, three_ref, *scratch = rest[len(rest) - 6 * pairs - 2:]
    dks, dvs, dqs, inner, qs, gs = (scratch[n * pairs:(n + 1) * pairs] for n in range(6))
    qb = pl.program_id(0)
    lane = lax.broadcasted_iota(jnp.int32, (B, B), 1)
    left = lane < (B // 2)

    @pl.when(qb == 0)
    def _():
        for ref in dks + dvs:
            ref[...] = jnp.zeros_like(ref)

    first = qb * B
    low, high = doc_span(len_ref, row, first, first + B - 1)
    for p in range(pairs):
        cols = slice(p * B, (p + 1) * B)
        gctx = gctx_ref[:, cols]
        qs[p][...] = two_heads(q_ref[:, cols], left)
        gs[p][...] = two_heads(gctx, left)
        prod = gctx.astype(jnp.float32) * ctx_ref[:, cols].astype(jnp.float32)
        inner[p][...] = jnp.broadcast_to(jnp.sum(two_heads(prod, left), axis=-1, keepdims=True), (2 * B, B))
        dqs[p][...] = jnp.zeros_like(dqs[p])

    def tile(t, carry):
        at = pl.ds(pl.multiple_of(t * B, B), B)
        for p in range(pairs):
            cols = slice(p * B, (p + 1) * B)
            gp = lax.dot_general(gs[p][...], v_ref[at, cols], NT, preferred_element_type=jnp.float32)
            probs_low, g_scores = [], []
            for s in range(2):
                rows = slice(s * B, (s + 1) * B)
                pr = probs_ref[t, 2 * p + s]
                ds = (pr * (gp[rows, :] - inner[p][rows, :])).astype(jnp.bfloat16)
                ds_ref[t, 2 * p + s] = ds
                g_scores.append(ds)
                probs_low.append(pr.astype(jnp.bfloat16))
            ds = jnp.concatenate(g_scores, axis=0)
            mix = jnp.concatenate(probs_low, axis=0)
            dvs[p][t] += lax.dot_general(mix, gs[p][...], TN, preferred_element_type=jnp.float32)
            dks[p][t] += lax.dot_general(ds, qs[p][...], TN, preferred_element_type=jnp.float32)
            dqs[p][...] += jnp.dot(ds, k_ref[at, cols], preferred_element_type=jnp.float32)
        return carry

    lax.fori_loop(low, high, tile, 0)
    for p in range(pairs):
        dq = jnp.where(left, dqs[p][0:B, :], dqs[p][B:2 * B, :]) * factor
        three_ref[pl.ds(pl.multiple_of(first, B), B), p * B:(p + 1) * B] = dq.astype(jnp.bfloat16)

    @pl.when(qb == tiles - 1)
    def _():
        for p in range(pairs):
            for t in range(tiles):
                rows = slice(t * B, (t + 1) * B)
                three_ref[rows, (pairs + p) * B:(pairs + p + 1) * B] = dks[p][t].astype(jnp.bfloat16)
                three_ref[rows, (2 * pairs + p) * B:(2 * pairs + p + 1) * B] = dvs[p][t].astype(jnp.bfloat16)


def attn_bwd(row, factor, lengths, q, k, v, gctx, ctx, probs, kept=None):
    slots, width = q.shape[1:]
    pairs, tiles = width // B, slots // B
    part = pl.BlockSpec((B, width), lambda i, L: (i, 0))
    three = pl.BlockSpec((None, slots, 3 * width), lambda i, L: (row, 0, 0))
    mine = pl.BlockSpec((None, B, width), lambda i, L: (row, i, 0))
    whole = pl.BlockSpec((None, slots, width), lambda i, L: (row, 0, 0))
    pairs_of = pl.BlockSpec((None, tiles, 2 * pairs, B, B), lambda i, L: (i, 0, 0, 0, 0))
    kept = () if kept is None else (kept,)
    return pl.pallas_call(
        functools.partial(bwd_kernel, row, factor),
        grid_spec=pltpu.PrefetchScalarGridSpec(
            num_scalar_prefetch=1, grid=(tiles,),
            in_specs=[mine, whole, whole, part, part, pairs_of]
            + [pl.BlockSpec(memory_space=pl.ANY)] * len(kept),
            out_specs=[pairs_of, three],
            scratch_shapes=[pltpu.VMEM((tiles, B, B), jnp.float32)] * (2 * pairs)
            + [pltpu.VMEM((2 * B, B), jnp.float32)] * (2 * pairs)
            + [pltpu.VMEM((2 * B, B), jnp.bfloat16)] * (2 * pairs)),
        out_shape=[jax.ShapeDtypeStruct(probs.shape, jnp.bfloat16),
                   jax.ShapeDtypeStruct((q.shape[0], slots, 3 * width), jnp.bfloat16)],
        input_output_aliases={7: 1} if kept else {},
        compiler_params=pltpu.CompilerParams(vmem_limit_bytes=48 << 20),
        cost_estimate=pl.CostEstimate(flops=1, transcendentals=0, bytes_accessed=1),
        name="attn_backward",
    )(lengths, q, k, v, gctx, ctx, probs, *kept)

BINS = 160
SPREADS = 3


def hist_kernel(row, step, len_ref, bl_ref, bh_ref, bv_ref, ds_ref, out_ref, *spreads):
    tiles, heads = ds_ref.shape[0], ds_ref.shape[1]
    docs = len_ref.shape[1]
    lane = lax.broadcasted_iota(jnp.int32, (PACK, B), 1)
    sub = lax.broadcasted_iota(jnp.int32, (PACK, B), 0)
    for spread in spreads:
        spread[...] = jnp.zeros_like(spread)

    floor, roof = step * B, (step + 1) * B
    starts, ends, firsts, lasts, upto, steps = [], [], [], [], [], []
    edge, count = 0, 0
    for d in range(docs):
        starts.append(edge)
        edge = edge + len_ref[row, d]
        ends.append(edge)
        firsts.append(jnp.maximum(starts[d], floor))
        lasts.append(jnp.maximum(jnp.minimum(edge, roof), firsts[d]))
        steps.append(jnp.where(edge - starts[d] <= B, 2, 1))
        here = ((lasts[d] + (PACK - 1)) // PACK - firsts[d] // PACK + (steps[d] - 1)) // steps[d]
        count = count + jnp.where(lasts[d] > firsts[d], here, 0)
        upto.append(count)

    def group(g, spread):
        start, end, first, last, pace = starts[0], ends[0], firsts[0], lasts[0], steps[0]
        block = firsts[0] // PACK + g * steps[0]
        for d in range(1, docs):
            past = g >= upto[d - 1]
            start, end, first, last, pace, block = (
                jnp.where(past, new, old) for new, old in
                ((starts[d], start), (ends[d], end), (firsts[d], first), (lasts[d], last), (steps[d], pace),
                 (firsts[d] // PACK + (g - upto[d - 1]) * steps[d], block)))
        last = jnp.where(g < count, last, first)
        start = jnp.minimum(start, tiles * B - 1)
        tile = start // B
        left = start - tile * B
        turn = jnp.where(left == 0, 0, B - left)
        halves = []
        for part in range(2):
            along, later = part * (pace - 1), part * (2 - pace)
            mine = block + along
            token = sub + mine * PACK
            live = (token >= first) & (token < last) & (lane + later * B < end - start)
            at = jnp.clip(mine - step * (B // PACK), 0, B // PACK - 1)
            halves.append((live, pl.ds(pl.multiple_of(at * PACK, PACK), PACK),
                           [jnp.minimum(tile + later + n, tiles - 1) for n in range(2)]))
        before = lane < B - left

        def moved(here, there):
            return jnp.where(before, pltpu.roll(here, turn, 1), pltpu.roll(there, turn, 1))

        codes = []
        for part, (live, rows, spots) in enumerate(halves):
            for h in range(heads):
                vals = moved(*(ds_ref[s, h, rows, :].astype(jnp.float32) for s in spots))
                spread[part, pl.ds(h, PACK, stride=8), :] = jnp.where(live, vals, 0.0)
            at = [pl.ds(pl.multiple_of(s * B, B), B) for s in spots]
            codes.append(moved(*(bl_ref[rows, x] + 32 * bh_ref[rows, x] + 2048 * bv_ref[rows, x]
                                 for x in at)))
        code = jnp.concatenate(codes, axis=1)
        index = [(code & 31).astype(jnp.int16), ((code >> 5) & 63).astype(jnp.int16),
                 (code >> 11).astype(jnp.int16)]
        one, zero = jnp.ones((), jnp.bfloat16), jnp.zeros((), jnp.bfloat16)
        grads, hots = [], []
        for r in range(PACK):
            hot = []
            for ix, n in zip(index, (32, 64, 64)):
                bins = lax.broadcasted_iota(jnp.int16, (n, 2 * B), 0)
                line = jnp.broadcast_to(ix[r:r + 1, :], (n, 2 * B))
                hot.append(jnp.where(bins == line, one, zero))
            hots.append(jnp.concatenate(hot, axis=0))
            grads += [spread[part, r * 8:r * 8 + 8, :].astype(jnp.bfloat16) for part in range(2)]
        return lax.dot_general(jnp.concatenate(grads, axis=1), jnp.concatenate(hots, axis=1), NT,
                               preferred_element_type=jnp.float32)

    def several(turn, sums):
        return tuple(x + group(len(spreads) * turn + n, spread)
                     for n, (x, spread) in enumerate(zip(sums, spreads)))

    none = jnp.zeros((8, BINS), jnp.float32)
    turns = (count + (len(spreads) - 1)) // len(spreads)
    out_ref[...] = sum(lax.fori_loop(0, turns, several, tuple(none for _ in spreads)))


def table_grads(row, step, lengths, bl, bh, bv, ds):
    slots = bl.shape[1]
    tiles, heads = ds.shape[0], ds.shape[2]
    block = pl.BlockSpec((None, B, slots), lambda i, L: (row, step, 0))
    return pl.pallas_call(
        functools.partial(hist_kernel, row, step),
        grid_spec=pltpu.PrefetchScalarGridSpec(
            num_scalar_prefetch=1, grid=(1,),
            in_specs=[block, block, block,
                      pl.BlockSpec((None, tiles, heads, B, B), lambda i, L: (step, 0, 0, 0, 0))],
            out_specs=pl.BlockSpec((8, BINS), lambda i, L: (0, 0)),
            scratch_shapes=[pltpu.VMEM((2, 8 * PACK, B), jnp.float32)] * SPREADS),
        out_shape=jax.ShapeDtypeStruct((8, BINS), jnp.float32),
        compiler_params=pltpu.CompilerParams(vmem_limit_bytes=48 << 20),
        cost_estimate=pl.CostEstimate(flops=1, transcendentals=0, bytes_accessed=1),
        name="table_grads",
    )(lengths, bl, bh, bv, ds)


f32, low = jnp.float32, jnp.bfloat16
SWAP = [(0, 1), (1, 0)]
ORDER = "UATDTADTUGATDUTATDTUADTPSUASDUSASSU"


def normalize(values):
    mean = jnp.mean(values, axis=-1, keepdims=True)
    centered = values - mean
    scale = lax.rsqrt(jnp.mean(centered * centered, axis=-1, keepdims=True) + 1e-12)
    return centered * scale, scale


def normalize_back(grad, normed, scale, gain):
    scaled = grad * gain
    first = jnp.mean(scaled, axis=-1, keepdims=True)
    second = jnp.mean(scaled * normed, axis=-1, keepdims=True)
    return scale * (scaled - first - normed * second)


def times(left, right, left_dim, right_dim):
    return lax.dot_general(left, right, (((left_dim,), (right_dim,)), ((), ())),
                           preferred_element_type=f32)


def flips(count, bit):
    return [(i, i ^ (1 << bit)) for i in range(count)]


def to_peer(values):
    return lax.ppermute(values, "head", SWAP)


def plus(left, right):
    return (left.astype(f32) + right.astype(f32)).astype(low)


def arranged(bit_value, mine, other):
    return jnp.where(bit_value == 0, mine, other), jnp.where(bit_value == 0, other, mine)


def in_order(bit_value, mine, other):
    return jnp.stack(arranged(bit_value, mine, other))


class Order:
    def __init__(self):
        self.last = None

    def tie(self, values):
        if self.last is None:
            return values
        values, self.last = lax.optimization_barrier((values, self.last))
        return values

    def mark(self, values):
        self.last = values


def total(terms, lift, size, axis):
    return sum(lax.dynamic_slice_in_dim(values, start + lift, size, axis).astype(f32)
               for values, start in terms)


def halve(order, terms, size, axis, count, bit):
    half = size // 2
    mine = (lax.axis_index("dp") >> bit) & 1
    send = total(terms, (1 - mine) * half, half, axis).astype(low)
    order.mark(send)
    got = lax.ppermute(send, "dp", flips(count, bit))
    yield
    return [(values, start + mine * half) for values, start in terms] + [(order.tie(got), 0)]


def gather_steps(order, values, count, bits):
    index = lax.axis_index("dp")
    for bit in reversed(bits):
        order.mark(values)
        got = lax.ppermute(values, "dp", flips(count, bit))
        yield
        both = in_order((index >> bit) & 1, values, order.tie(got))
        values = both.reshape((2 * values.shape[0],) + values.shape[1:])
    return values


def unit_steps(order, kept, given, count, axis, split, out):
    bits = list(range(1, count.bit_length() - 1))
    size = kept.shape[axis]
    given = order.tie(given)
    order.mark(given)
    got = lax.ppermute(given, "dp", flips(count, 0))
    yield
    terms = [(kept, 0), (order.tie(got), 0)]
    terms = yield from halve(order, terms, size, axis, count, bits[0])
    size //= 2
    mine, other = ([(split(values)[c], start) for values, start in terms] for c in range(2))
    send = total(other, 0, size, 0).astype(low)
    order.mark(send)
    got = to_peer(send)
    yield
    terms = mine + [(order.tie(got), 0)]
    for bit in bits[1:]:
        terms = yield from halve(order, terms, size, 0, count, bit)
        size //= 2
    mine = yield from gather_steps(order, total(terms, 0, size, 0).astype(low), count, bits)
    order.mark(mine)
    other = lax.ppermute(mine, "dp", flips(count, 0))
    yield
    out += [mine, order.tie(other)]


def buffer_steps(order, values, count, out):
    bits = list(range(count.bit_length() - 1))
    size = values.shape[0]
    terms = [(order.tie(values), 0)]
    for bit in bits:
        terms = yield from halve(order, terms, size, 0, count, bit)
        size //= 2
    values = yield from gather_steps(order, total(terms, 0, size, 0).astype(low), count, bits)
    order.mark(values)
    out.append(values)


def small_steps(order, values, count, out):
    values = order.tie(values)
    for bit in [None] + list(range(count.bit_length() - 1)):
        order.mark(values)
        got = to_peer(values) if bit is None else lax.ppermute(values, "dp", flips(count, bit))
        yield
        values = values + order.tie(got)
    order.mark(values)
    out.append(values)


def advance(*chains):
    for chain in chains:
        next(chain, None)


def finish(*chains):
    left = list(chains)
    while left:
        for chain in list(left):
            try:
                next(chain)
            except StopIteration:
                left.remove(chain)


def body(
    count,
    hidden,
    lengths,
    padding,
    bucket_line,
    bucket_horizontal,
    bucket_vertical,
    attn_project,
    attn_bias,
    table_line,
    table_horizontal,
    table_vertical,
    out_project,
    out_bias,
    attn_gain,
    attn_shift,
    hidden_project,
    hidden_bias,
    down_project,
    down_bias,
    final_gain,
    final_shift,
    cotangent,
):
    rows, slots, width = hidden.shape
    half = cotangent.shape[1]
    heads = table_line.shape[1]
    local = attn_project.shape[2]
    units = hidden_project.shape[1]
    part = units // 2
    factor = 1.0 / math.sqrt(local // heads)
    head = lax.axis_index("head")
    index = lax.axis_index("dp")
    core = index & 1
    offset = head * half
    every = list(range(count.bit_length() - 1))

    def split(values, dim):
        return [lax.dynamic_slice_in_dim(values, c * part, part, dim) for c in (core, 1 - core)]

    def joined(own_parts, got, dim):
        mine, rest = own_parts
        beside = lax.ppermute(got, "dp", flips(count, 0))
        return [jnp.concatenate([mine, got], axis=dim), jnp.concatenate([rest, beside], axis=dim)]

    side = (index >> 1) & 1
    down_mine = lax.dynamic_slice_in_dim(down_project, core * part + side * (part // 2), part // 2, 0)
    down_got = to_peer(down_mine)
    down_mine, hidden_project = lax.optimization_barrier((down_mine, hidden_project))
    up_mine = lax.dynamic_slice_in_dim(hidden_project, core * part, part, 1)
    up_got = to_peer(up_mine)
    up_mine, hidden, hidden_project, down_project = lax.optimization_barrier(
        (up_mine, hidden, hidden_project, down_project))
    bias_got = to_peer(hidden_bias)

    planes = jnp.concatenate([table_horizontal, table_vertical], axis=0)
    bins = table_line.shape[0] + planes.shape[0]
    lines = jnp.broadcast_to(table_line.T[:, :, None], (heads, table_line.shape[0], B))
    planes = jnp.broadcast_to(planes.T[:, None, :], (heads, PACK, planes.shape[0]))
    pad = padding[:, None, :]
    bucket_line, bucket_horizontal, bucket_vertical = (
        pltpu.with_memory_space_constraint(x, pltpu.HBM)
        for x in (bucket_line, bucket_horizontal, bucket_vertical))

    flat = hidden.reshape(rows * slots, width)
    query = ((times(flat, attn_project[0], 1, 0) + attn_bias[0].astype(f32)).astype(low)
             * jnp.asarray(factor, low))
    key = times(flat, attn_project[1], 1, 0).astype(low)
    value = (times(flat, attn_project[2], 1, 0) + attn_bias[1].astype(f32)).astype(low)
    query, key, value = (pltpu.with_memory_space_constraint(x.reshape(rows, slots, local), pltpu.HBM)
                         for x in (query, key, value))

    def own(values):
        return lax.dynamic_slice_in_dim(values, offset, half, 0)

    def others(values):
        return lax.dynamic_slice_in_dim(values, half - offset, half, 0)

    fronts, attn_sum, attn_got = [], [], []
    for r in range(rows):
        if r == 1:
            lengths, down_got = lax.optimization_barrier((lengths, down_got))
            down_beside = lax.ppermute(down_got, "dp", flips(count, 1))
        probs, context = attn_fwd(r, lengths, query, key, value, pad, bucket_line,
                                  bucket_horizontal, bucket_vertical, lines, planes)
        if r == 1:
            context, down_beside = lax.optimization_barrier((context, down_beside))
        fronts.append((probs, context))
        send = times(others(context), out_project, 1, 0).astype(low)
        got = to_peer(send)
        attn_sum.append(times(own(context), out_project, 1, 0))
        attn_got.append(got)
    (send, hidden_project, down_project, cotangent, norm_rows, out_bias, down_bias, hidden_bias, bias_got,
     hidden) = lax.optimization_barrier(
        (send, hidden_project, down_project, cotangent, (attn_gain, attn_shift, final_gain, final_shift),
         out_bias, down_bias, hidden_bias, bias_got, hidden))
    biases = [jnp.concatenate([x, y]) for x, y in zip(split(hidden_bias, 0), split(bias_got, 0))]
    gain_first, shift_first, gain_last, shift_last = (x.astype(f32) for x in norm_rows)
    up_parts = [up_mine, lax.dynamic_slice_in_dim(hidden_project, (1 - core) * part, part, 1)]
    down_parts = split(down_project, 0)
    up_got, down_beside, attn_got = lax.optimization_barrier((up_got, down_beside, attn_got))
    down_got = in_order(side, down_got, down_beside)
    ups = joined(up_parts, up_got, 1)
    downs = joined(down_parts, down_got.reshape(part, width), 0)
    attn_sum = [x + got.astype(f32) for x, got in zip(attn_sum, attn_got)]
    tokens = lax.dynamic_slice_in_dim(hidden, offset, half, 1).reshape(rows * half, width).astype(f32)
    normed, scale = normalize(tokens + jnp.concatenate(attn_sum, axis=0) + out_bias.astype(f32))
    mid = normed * gain_first + shift_first
    mid_low = mid.astype(low)

    actives, slopes = [], []
    total = None
    for up, down, bias in zip(ups, downs, biases):
        inner = times(mid_low, up, 1, 0) + bias.astype(f32)
        bell = 0.5 * (1.0 + lax.erf(inner * math.sqrt(0.5)))
        actives.append((inner * bell).astype(low))
        slope = bell + inner * (jnp.exp(-0.5 * inner * inner) * (1.0 / math.sqrt(2.0 * math.pi)))
        slopes.append(slope.astype(low))
        term = times(actives[-1], down, 1, 0)
        total = term if total is None else total + term
    normed_final, scale_final = normalize(mid + total + down_bias.astype(f32))
    output = (normed_final * gain_last + shift_last).astype(low).reshape(rows, half, width)

    above = cotangent.reshape(rows * half, width).astype(f32)
    g_final = normalize_back(above, normed_final, scale_final, gain_last)
    g_low = g_final.astype(low)
    order = Order()
    total = None
    inners = []
    for up, down, slope in zip(ups, downs, slopes):
        g_inner = (times(g_low, down, 1, 1) * slope.astype(f32)).astype(low)
        inners.append(g_inner)
        term = times(g_inner, up, 1, 1)
        total = term if total is None else total + term
    g_mid = g_final + total
    g_attn = normalize_back(g_mid, normed, scale, gain_first)
    g_attn_low = g_attn.astype(low).reshape(rows, half, width)
    g_others = [to_peer(g_attn_low[r]) for r in range(rows)]
    order.mark(g_attn_low)
    down_out, up_out, attn_out = [], [], []
    g_low = order.tie(g_low)
    kept, given = (times(active, g_low, 0, 0).astype(low) for active in actives)
    down_chain = unit_steps(order, *(x.reshape(2, part, width) for x in (kept, given)), count, 1,
                            lambda v: (v[0], v[1]), down_out)
    advance(down_chain)
    mid_low = order.tie(mid_low)
    kept, given = (times(mid_low, g_inner, 0, 0).astype(low) for g_inner in inners)
    up_chain = unit_steps(order, kept, given, count, 0, lambda v: (v[:, :part], v[:, part:]), up_out)
    advance(up_chain, down_chain)
    g_attn = g_attn.reshape(rows, half, width)

    marks, three, grad_out = [], None, 0.0
    for r in range(rows):
        probs, context = fronts[r]
        g_all = in_order(head, g_attn_low[r], order.tie(g_others[r])).reshape(slots, width)
        g_context = times(g_all, out_project, 1, 1).astype(low)
        g_scores, three = attn_bwd(r, factor, lengths, query, key, value, g_context, context, probs, three)
        order.mark(g_scores)
        marks.append(g_scores)
        grad_out = grad_out + times(context, g_all, 0, 0)
        advance(up_chain if r == 0 else down_chain)
    grad_attn = times(flat, three.reshape(rows * slots, 3 * local), 0, 0).astype(low)
    grad_out = jnp.concatenate([grad_out[:, :local], grad_out[:, local:]], axis=0).astype(low)
    attn_chain = buffer_steps(order, jnp.concatenate([grad_attn, grad_out], axis=1), count, attn_out)
    advance(attn_chain)
    every_project = jnp.concatenate([attn_project[c] for c in range(3)], axis=1)
    room = width // 2

    def pack():
        sums = [jnp.sum(x.reshape(rows * half, width), axis=0, keepdims=True) for x in
                (g_attn, g_mid * normed, g_mid, g_final, above * normed_final, above)]
        sums, units_in, three_sums, tables = order.tie(
            (sums, inners, jnp.sum(three.astype(f32).reshape(rows * slots, 3 * local), axis=0,
                                       keepdims=True), sum(tables_out)))
        unit_sums = [jnp.sum(x.astype(f32), axis=0, keepdims=True) for x in units_in]
        ours, others_ = (jnp.concatenate(arranged(core, *(x[:, c * part:(c + 1) * part] for x in unit_sums)),
                                         axis=0) for c in range(2))
        pair = jnp.concatenate([three_sums[:, :local], three_sums[:, 2 * local:]], axis=1)
        tables = jnp.pad(tables, ((0, 0), (0, room - bins)))
        return jnp.concatenate(
            sums + list(arranged(head, ours, others_))
            + [jnp.where(head == slot, pair, 0.0) for slot in range(2)]
            + [jnp.zeros((4, width), f32),
               jnp.concatenate([jnp.where(head == slot, tables, 0.0) for slot in range(2)], axis=1)], axis=0)

    tables_out, small_out = [], []
    blocks = [(r, block) for r in range(rows) for block in range(slots // B)]
    chains = {"D": down_chain, "U": up_chain, "A": attn_chain}
    for name in ORDER:
        if name == "T":
            r, block = blocks[len(tables_out)]
            tables_out.append(table_grads(r, block, order.tie(lengths), bucket_line,
                                          bucket_horizontal, bucket_vertical, marks[r]))
            order.mark(tables_out[-1])
        elif name == "G":
            three = order.tie(three)
            theirs = lax.dynamic_slice_in_dim(three, half - offset, half, 1)
            give = times(theirs.reshape(rows * half, 3 * local), every_project, 1, 1).astype(low)
            order.mark(give)
            received = to_peer(give)
            mine = lax.dynamic_slice_in_dim(three, offset, half, 1)
            mine = times(mine.reshape(rows * half, 3 * local), every_project, 1, 1)
        elif name == "P":
            chains["S"] = small_steps(order, pack(), count, small_out)
        else:
            advance(chains[name])
    finish(*chains.values())
    packed = small_out[0]
    grads_in = (mine + received.astype(f32)).reshape(rows, half, width) + g_attn
    grad_down = in_order(core, *down_out).reshape(down_project.shape).astype(f32)
    mine, other = up_out
    grad_up = jnp.concatenate(arranged(core, mine, other), axis=1).astype(f32)
    buffer = attn_out[0].astype(f32)
    grad_attn = jnp.stack([buffer[:, c * local:(c + 1) * local] for c in range(3)])
    grad_out = jnp.concatenate([buffer[:local, 3 * local:], buffer[local:, 3 * local:]], axis=1)

    rows_of = lambda at, size: lax.dynamic_slice_in_dim(packed, at, size, 0)
    grad_bias = rows_of(6 + 2 * head, 2).reshape(-1)
    grad_attn_bias = rows_of(10 + head, 1).reshape(2, local)
    marks = jnp.where(head == 0, packed[16:, :bins], packed[16:, room:room + bins])[:heads].T
    first, second = table_line.shape[0], table_horizontal.shape[0]
    return (
        output,
        grads_in,
        grad_attn,
        grad_attn_bias,
        marks[:first],
        marks[first:first + second],
        marks[first + second:],
        grad_out,
        packed[0],
        packed[1],
        packed[2],
        grad_up,
        grad_bias,
        grad_down,
        packed[3],
        packed[4],
        packed[5],
    )


def solution(mesh):
    return jax.shard_map(
        functools.partial(body, mesh.shape["dp"]),
        mesh=mesh,
        in_specs=(
            P("dp", None, None),
            P("dp", None),
            P("dp", None),
            P("dp", None, None),
            P("dp", None, None),
            P("dp", None, None),
            P(None, None, "head"),
            P(None, "head"),
            P(None, "head"),
            P(None, "head"),
            P(None, "head"),
            P("head", None),
            P(),
            P(),
            P(),
            P(None, "head"),
            P("head"),
            P("head", None),
            P(),
            P(),
            P(),
            P("dp", "head", None),
        ),
        out_specs=(
            P("dp", "head", None),
            P("dp", "head", None),
            P(None, None, "head"),
            P(None, "head"),
            P(None, "head"),
            P(None, "head"),
            P(None, "head"),
            P("head", None),
            P(),
            P(),
            P(),
            P(None, "head"),
            P("head"),
            P("head", None),
            P(),
            P(),
            P(),
        ),
        check_vma=False,
    )
```

```python
import functools
import math

import jax
import jax.numpy as jnp
from jax import lax
from jax.experimental import pallas as pl
from jax.experimental.pallas import tpu as pltpu
from jax.sharding import PartitionSpec as P

B = 128

PACK = 16


def gather_dims(axis):
    return lax.GatherDimensionNumbers(
        offset_dims=(), collapsed_slice_dims=(axis,), start_index_map=(axis,),
        operand_batching_dims=(1 - axis,), start_indices_batching_dims=(1 - axis,))


def pick(table, index, axis):
    return lax.gather(table, index[:, :, None], gather_dims(axis), (1, 1),
                      mode=lax.GatherScatterMode.PROMISE_IN_BOUNDS)


def two_heads(values, left):
    zero = jnp.zeros_like(values)
    return jnp.concatenate([jnp.where(left, values, zero), jnp.where(left, zero, values)], axis=0)


def doc_span(len_ref, row, first, last):
    edge = 0
    start = 0
    stop = 0
    for k in range(len_ref.shape[1]):
        begin = edge
        edge = edge + len_ref[row, k]
        start = jnp.where(begin <= first, begin, start)
        stop = jnp.where(begin <= last, edge, stop)
    return start // B, (stop + (B - 1)) // B

def fwd_kernel(row, len_ref, q_ref, k_ref, v_ref, pad_ref, bl_ref, bh_ref, bv_ref, line_ref, plane_ref,
               probs_ref, ctx_ref, sc, qs, best, mass, mixed):
    qb = pl.program_id(0)
    heads = sc.shape[1]
    pairs = heads // 2
    lane = lax.broadcasted_iota(jnp.int32, (B, B), 1)
    left = lane < (B // 2)
    first = qb * B
    low, high = doc_span(len_ref, row, first, first + B - 1)
    sub = lax.broadcasted_iota(jnp.int32, (B, B), 0) + first
    edges = []
    edge = 0
    for k in range(len_ref.shape[1]):
        edge = edge + len_ref[row, k]
        edges.append(edge)
    seg_q = sum(((sub >= e).astype(jnp.int32) for e in edges))
    for p in range(pairs):
        qs[p] = two_heads(q_ref[:, p * B:(p + 1) * B], left)

    def scores(t, carry):
        key_at = lane + t * B
        at = pl.ds(pl.multiple_of(t * B, B), B)
        seg_k = sum(((key_at >= e).astype(jnp.int32) for e in edges))
        real = jnp.broadcast_to(pad_ref[:, at], (B, B)) > 0
        allowed = ((seg_q == seg_k) & real) | (sub == key_at)
        parts = []
        for g in range(B // PACK):
            rows = slice(g * PACK, g * PACK + PACK)
            line = bl_ref[rows, at].astype(jnp.int16)
            parts.append((line & jnp.int16(PACK - 1), line >= jnp.int16(PACK),
                          bh_ref[rows, at].astype(jnp.int16), (bv_ref[rows, at] + 64).astype(jnp.int16)))
        for p in range(pairs):
            raw = lax.dot_general(qs[p], k_ref[at, p * B:(p + 1) * B], (((1,), (1,)), ((), ())),
                                  preferred_element_type=jnp.float32)
            for s in range(2):
                h = 2 * p + s
                plane = plane_ref[h]
                for g, (place, upper, horiz, vert) in enumerate(parts):
                    rows = slice(g * PACK, g * PACK + PACK)
                    found = jnp.where(upper, pick(line_ref[h, PACK:2 * PACK, :], place, 0),
                                      pick(line_ref[h, 0:PACK, :], place, 0))
                    rel = ((found.astype(jnp.float32) + pick(plane, horiz, 1).astype(jnp.float32))
                           + pick(plane, vert, 1).astype(jnp.float32))
                    val = jnp.where(allowed[rows], raw[s * B + g * PACK:s * B + (g + 1) * PACK, :] + rel,
                                    -1000000000.0)
                    sc[t, h, rows, :] = val
                    best[h, rows, :] = jnp.maximum(best[h, rows, :], val)
        return carry

    best[...] = jnp.full(best.shape, -3.0e38, jnp.float32)
    mass[...] = jnp.zeros_like(mass)
    mixed[...] = jnp.zeros_like(mixed)
    lax.fori_loop(low, high, scores, 0)
    for h in range(heads):
        best[h] = jnp.broadcast_to(jnp.max(best[h], axis=-1, keepdims=True), (B, B))

    def expo(t, carry):
        for h in range(heads):
            e = jnp.exp(sc[t, h] - best[h])
            sc[t, h] = e
            mass[h] += e
        return carry

    lax.fori_loop(low, high, expo, 0)
    for h in range(heads):
        mass[h] = jnp.broadcast_to(1.0 / jnp.sum(mass[h], axis=-1, keepdims=True), (B, B))

    def mix(t, carry):
        at = pl.ds(pl.multiple_of(t * B, B), B)
        for p in range(pairs):
            low_pair = []
            for s in range(2):
                h = 2 * p + s
                pr = sc[t, h] * mass[h]
                probs_ref[t, h] = pr
                low_pair.append(pr.astype(jnp.bfloat16))
            mixed[p] += jnp.dot(jnp.concatenate(low_pair, axis=0), v_ref[at, p * B:(p + 1) * B],
                                preferred_element_type=jnp.float32)
        return carry

    lax.fori_loop(low, high, mix, 0)
    for p in range(pairs):
        ctx_ref[:, p * B:(p + 1) * B] = jnp.where(left, mixed[p, :B, :], mixed[p, B:, :]).astype(jnp.bfloat16)


def attn_fwd(row, lengths, q, k, v, pad, bl, bh, bv, line, plane):
    slots, width = q.shape[1:]
    pairs = width // B
    tiles = slots // B
    row_block = lambda n: pl.BlockSpec((None, B, n), lambda i, L: (row, i, 0))
    return pl.pallas_call(
        functools.partial(fwd_kernel, row),
        grid_spec=pltpu.PrefetchScalarGridSpec(
            num_scalar_prefetch=1, grid=(tiles,),
            in_specs=[
                row_block(width),
                pl.BlockSpec((None, slots, width), lambda i, L: (row, 0, 0)),
                pl.BlockSpec((None, slots, width), lambda i, L: (row, 0, 0)),
                pl.BlockSpec((None, 1, slots), lambda i, L: (row, 0, 0)),
                row_block(slots), row_block(slots), row_block(slots),
                pl.BlockSpec(line.shape, lambda i, L: (0, 0, 0)),
                pl.BlockSpec(plane.shape, lambda i, L: (0, 0, 0)),
            ],
            out_specs=[
                pl.BlockSpec((None, tiles, 2 * pairs, B, B), lambda i, L: (i, 0, 0, 0, 0)),
                pl.BlockSpec((B, width), lambda i, L: (i, 0)),
            ],
            scratch_shapes=[
                pltpu.VMEM((tiles, 2 * pairs, B, B), jnp.float32),
                pltpu.VMEM((pairs, 2 * B, B), jnp.bfloat16),
                pltpu.VMEM((2 * pairs, B, B), jnp.float32),
                pltpu.VMEM((2 * pairs, B, B), jnp.float32),
                pltpu.VMEM((pairs, 2 * B, B), jnp.float32),
            ]),
        out_shape=[
            jax.ShapeDtypeStruct((tiles, tiles, 2 * pairs, B, B), jnp.float32),
            jax.ShapeDtypeStruct((slots, width), jnp.bfloat16),
        ],
        compiler_params=pltpu.CompilerParams(vmem_limit_bytes=48 << 20),
        cost_estimate=pl.CostEstimate(flops=1, transcendentals=0, bytes_accessed=1),
        name="attn_forward",
    )(lengths, q, k, v, pad, bl, bh, bv, line, plane)


NT = (((1,), (1,)), ((), ()))
TN = (((0,), (0,)), ((), ()))

def bwd_kernel(row, factor, len_ref, q_ref, k_ref, v_ref, gctx_ref, ctx_ref, probs_ref, *rest):
    pairs, tiles = q_ref.shape[1] // B, probs_ref.shape[0]
    ds_ref, three_ref, *scratch = rest[len(rest) - 6 * pairs - 2:]
    dks, dvs, dqs, inner, qs, gs = (scratch[n * pairs:(n + 1) * pairs] for n in range(6))
    qb = pl.program_id(0)
    lane = lax.broadcasted_iota(jnp.int32, (B, B), 1)
    left = lane < (B // 2)

    @pl.when(qb == 0)
    def _():
        for ref in dks + dvs:
            ref[...] = jnp.zeros_like(ref)

    first = qb * B
    low, high = doc_span(len_ref, row, first, first + B - 1)
    for p in range(pairs):
        cols = slice(p * B, (p + 1) * B)
        gctx = gctx_ref[:, cols]
        qs[p][...] = two_heads(q_ref[:, cols], left)
        gs[p][...] = two_heads(gctx, left)
        prod = gctx.astype(jnp.float32) * ctx_ref[:, cols].astype(jnp.float32)
        inner[p][...] = jnp.broadcast_to(jnp.sum(two_heads(prod, left), axis=-1, keepdims=True), (2 * B, B))
        dqs[p][...] = jnp.zeros_like(dqs[p])

    def tile(t, carry):
        at = pl.ds(pl.multiple_of(t * B, B), B)
        for p in range(pairs):
            cols = slice(p * B, (p + 1) * B)
            gp = lax.dot_general(gs[p][...], v_ref[at, cols], NT, preferred_element_type=jnp.float32)
            probs_low, g_scores = [], []
            for s in range(2):
                rows = slice(s * B, (s + 1) * B)
                pr = probs_ref[t, 2 * p + s]
                ds = (pr * (gp[rows, :] - inner[p][rows, :])).astype(jnp.bfloat16)
                ds_ref[t, 2 * p + s] = ds
                g_scores.append(ds)
                probs_low.append(pr.astype(jnp.bfloat16))
            ds = jnp.concatenate(g_scores, axis=0)
            mix = jnp.concatenate(probs_low, axis=0)
            dvs[p][t] += lax.dot_general(mix, gs[p][...], TN, preferred_element_type=jnp.float32)
            dks[p][t] += lax.dot_general(ds, qs[p][...], TN, preferred_element_type=jnp.float32)
            dqs[p][...] += jnp.dot(ds, k_ref[at, cols], preferred_element_type=jnp.float32)
        return carry

    lax.fori_loop(low, high, tile, 0)
    for p in range(pairs):
        dq = jnp.where(left, dqs[p][0:B, :], dqs[p][B:2 * B, :]) * factor
        three_ref[pl.ds(pl.multiple_of(first, B), B), p * B:(p + 1) * B] = dq.astype(jnp.bfloat16)

    @pl.when(qb == tiles - 1)
    def _():
        for p in range(pairs):
            for t in range(tiles):
                rows = slice(t * B, (t + 1) * B)
                three_ref[rows, (pairs + p) * B:(pairs + p + 1) * B] = dks[p][t].astype(jnp.bfloat16)
                three_ref[rows, (2 * pairs + p) * B:(2 * pairs + p + 1) * B] = dvs[p][t].astype(jnp.bfloat16)


def attn_bwd(row, factor, lengths, q, k, v, gctx, ctx, probs, kept=None):
    slots, width = q.shape[1:]
    pairs, tiles = width // B, slots // B
    part = pl.BlockSpec((B, width), lambda i, L: (i, 0))
    three = pl.BlockSpec((None, slots, 3 * width), lambda i, L: (row, 0, 0))
    mine = pl.BlockSpec((None, B, width), lambda i, L: (row, i, 0))
    whole = pl.BlockSpec((None, slots, width), lambda i, L: (row, 0, 0))
    pairs_of = pl.BlockSpec((None, tiles, 2 * pairs, B, B), lambda i, L: (i, 0, 0, 0, 0))
    kept = () if kept is None else (kept,)
    return pl.pallas_call(
        functools.partial(bwd_kernel, row, factor),
        grid_spec=pltpu.PrefetchScalarGridSpec(
            num_scalar_prefetch=1, grid=(tiles,),
            in_specs=[mine, whole, whole, part, part, pairs_of]
            + [pl.BlockSpec(memory_space=pl.ANY)] * len(kept),
            out_specs=[pairs_of, three],
            scratch_shapes=[pltpu.VMEM((tiles, B, B), jnp.float32)] * (2 * pairs)
            + [pltpu.VMEM((2 * B, B), jnp.float32)] * (2 * pairs)
            + [pltpu.VMEM((2 * B, B), jnp.bfloat16)] * (2 * pairs)),
        out_shape=[jax.ShapeDtypeStruct(probs.shape, jnp.bfloat16),
                   jax.ShapeDtypeStruct((q.shape[0], slots, 3 * width), jnp.bfloat16)],
        input_output_aliases={7: 1} if kept else {},
        compiler_params=pltpu.CompilerParams(vmem_limit_bytes=48 << 20),
        cost_estimate=pl.CostEstimate(flops=1, transcendentals=0, bytes_accessed=1),
        name="attn_backward",
    )(lengths, q, k, v, gctx, ctx, probs, *kept)

BINS = 160
SPREADS = 3


def hist_kernel(row, step, len_ref, bl_ref, bh_ref, bv_ref, ds_ref, out_ref, *spreads):
    tiles, heads = ds_ref.shape[0], ds_ref.shape[1]
    docs = len_ref.shape[1]
    lane = lax.broadcasted_iota(jnp.int32, (PACK, B), 1)
    sub = lax.broadcasted_iota(jnp.int32, (PACK, B), 0)
    for spread in spreads:
        spread[...] = jnp.zeros_like(spread)

    floor, roof = step * B, (step + 1) * B
    starts, ends, firsts, lasts, upto, steps = [], [], [], [], [], []
    edge, count = 0, 0
    for d in range(docs):
        starts.append(edge)
        edge = edge + len_ref[row, d]
        ends.append(edge)
        firsts.append(jnp.maximum(starts[d], floor))
        lasts.append(jnp.maximum(jnp.minimum(edge, roof), firsts[d]))
        steps.append(jnp.where(edge - starts[d] <= B, 2, 1))
        here = ((lasts[d] + (PACK - 1)) // PACK - firsts[d] // PACK + (steps[d] - 1)) // steps[d]
        count = count + jnp.where(lasts[d] > firsts[d], here, 0)
        upto.append(count)

    def group(g, spread):
        start, end, first, last, pace = starts[0], ends[0], firsts[0], lasts[0], steps[0]
        block = firsts[0] // PACK + g * steps[0]
        for d in range(1, docs):
            past = g >= upto[d - 1]
            start, end, first, last, pace, block = (
                jnp.where(past, new, old) for new, old in
                ((starts[d], start), (ends[d], end), (firsts[d], first), (lasts[d], last), (steps[d], pace),
                 (firsts[d] // PACK + (g - upto[d - 1]) * steps[d], block)))
        last = jnp.where(g < count, last, first)
        start = jnp.minimum(start, tiles * B - 1)
        tile = start // B
        left = start - tile * B
        turn = jnp.where(left == 0, 0, B - left)
        halves = []
        for part in range(2):
            along, later = part * (pace - 1), part * (2 - pace)
            mine = block + along
            token = sub + mine * PACK
            live = (token >= first) & (token < last) & (lane + later * B < end - start)
            at = jnp.clip(mine - step * (B // PACK), 0, B // PACK - 1)
            halves.append((live, pl.ds(pl.multiple_of(at * PACK, PACK), PACK),
                           [jnp.minimum(tile + later + n, tiles - 1) for n in range(2)]))
        before = lane < B - left

        def moved(here, there):
            return jnp.where(before, pltpu.roll(here, turn, 1), pltpu.roll(there, turn, 1))

        codes = []
        for part, (live, rows, spots) in enumerate(halves):
            for h in range(heads):
                vals = moved(*(ds_ref[s, h, rows, :].astype(jnp.float32) for s in spots))
                spread[part, pl.ds(h, PACK, stride=8), :] = jnp.where(live, vals, 0.0)
            at = [pl.ds(pl.multiple_of(s * B, B), B) for s in spots]
            codes.append(moved(*(bl_ref[rows, x] + 32 * bh_ref[rows, x] + 2048 * bv_ref[rows, x]
                                 for x in at)))
        code = jnp.concatenate(codes, axis=1)
        index = [(code & 31).astype(jnp.int16), ((code >> 5) & 63).astype(jnp.int16),
                 (code >> 11).astype(jnp.int16)]
        one, zero = jnp.ones((), jnp.bfloat16), jnp.zeros((), jnp.bfloat16)
        grads, hots = [], []
        for r in range(PACK):
            hot = []
            for ix, n in zip(index, (32, 64, 64)):
                bins = lax.broadcasted_iota(jnp.int16, (n, 2 * B), 0)
                line = jnp.broadcast_to(ix[r:r + 1, :], (n, 2 * B))
                hot.append(jnp.where(bins == line, one, zero))
            hots.append(jnp.concatenate(hot, axis=0))
            grads += [spread[part, r * 8:r * 8 + 8, :].astype(jnp.bfloat16) for part in range(2)]
        return lax.dot_general(jnp.concatenate(grads, axis=1), jnp.concatenate(hots, axis=1), NT,
                               preferred_element_type=jnp.float32)

    def several(turn, sums):
        return tuple(x + group(len(spreads) * turn + n, spread)
                     for n, (x, spread) in enumerate(zip(sums, spreads)))

    none = jnp.zeros((8, BINS), jnp.float32)
    turns = (count + (len(spreads) - 1)) // len(spreads)
    out_ref[...] = sum(lax.fori_loop(0, turns, several, tuple(none for _ in spreads)))


def table_grads(row, step, lengths, bl, bh, bv, ds):
    slots = bl.shape[1]
    tiles, heads = ds.shape[0], ds.shape[2]
    block = pl.BlockSpec((None, B, slots), lambda i, L: (row, step, 0))
    return pl.pallas_call(
        functools.partial(hist_kernel, row, step),
        grid_spec=pltpu.PrefetchScalarGridSpec(
            num_scalar_prefetch=1, grid=(1,),
            in_specs=[block, block, block,
                      pl.BlockSpec((None, tiles, heads, B, B), lambda i, L: (step, 0, 0, 0, 0))],
            out_specs=pl.BlockSpec((8, BINS), lambda i, L: (0, 0)),
            scratch_shapes=[pltpu.VMEM((2, 8 * PACK, B), jnp.float32)] * SPREADS),
        out_shape=jax.ShapeDtypeStruct((8, BINS), jnp.float32),
        compiler_params=pltpu.CompilerParams(vmem_limit_bytes=48 << 20),
        cost_estimate=pl.CostEstimate(flops=1, transcendentals=0, bytes_accessed=1),
        name="table_grads",
    )(lengths, bl, bh, bv, ds)


f32, low = jnp.float32, jnp.bfloat16
SWAP = [(0, 1), (1, 0)]
ORDER = "UATDTADTUGATDUTATDTURADTUAPSDUSASSSU"


def normalize(values):
    mean = jnp.mean(values, axis=-1, keepdims=True)
    centered = values - mean
    scale = lax.rsqrt(jnp.mean(centered * centered, axis=-1, keepdims=True) + 1e-12)
    return centered * scale, scale


def normalize_back(grad, normed, scale, gain):
    scaled = grad * gain
    first = jnp.mean(scaled, axis=-1, keepdims=True)
    second = jnp.mean(scaled * normed, axis=-1, keepdims=True)
    return scale * (scaled - first - normed * second)


def times(left, right, left_dim, right_dim):
    return lax.dot_general(left, right, (((left_dim,), (right_dim,)), ((), ())),
                           preferred_element_type=f32)


def flips(count, bit):
    return [(i, i ^ (1 << bit)) for i in range(count)]


def to_peer(values):
    return lax.ppermute(values, "head", SWAP)


def plus(left, right):
    return (left.astype(f32) + right.astype(f32)).astype(low)


def arranged(bit_value, mine, other):
    return jnp.where(bit_value == 0, mine, other), jnp.where(bit_value == 0, other, mine)


def in_order(bit_value, mine, other):
    return jnp.stack(arranged(bit_value, mine, other))


NO_COST = pl.CostEstimate(flops=1, transcendentals=0, bytes_accessed=1)


def join_kernel(bit_ref, mine_ref, got_ref, out_ref):
    own = pl.program_id(0) == bit_ref[0]

    @pl.when(own)
    def _():
        out_ref[...] = mine_ref[...]

    @pl.when(jnp.logical_not(own))
    def _():
        out_ref[...] = got_ref[...]


def joined_rows(bit_value, mine, got):
    rows, columns = mine.shape
    whole = pl.BlockSpec((rows, columns), lambda i, b: (0, 0))
    out = pl.pallas_call(
        join_kernel,
        grid_spec=pltpu.PrefetchScalarGridSpec(
            num_scalar_prefetch=1, grid=(2,), in_specs=[whole, whole],
            out_specs=pl.BlockSpec((None, rows, columns), lambda i, b: (i, 0, 0))),
        out_shape=jax.ShapeDtypeStruct((2, rows, columns), mine.dtype),
        compiler_params=pltpu.CompilerParams(vmem_limit_bytes=48 << 20),
        cost_estimate=NO_COST, name="joined_rows",
    )(bit_value.reshape(1), mine, got)
    return out.reshape(2 * rows, columns)


def add_kernel(left_ref, right_ref, out_ref):
    out_ref[...] = left_ref[...] + right_ref[...]


def added(left, right):
    return pl.pallas_call(add_kernel, out_shape=jax.ShapeDtypeStruct(left.shape, left.dtype),
                          cost_estimate=NO_COST, name="added")(left, right)


def nothing(*refs):
    pass


def after(values, earlier):
    anywhere = pl.BlockSpec(memory_space=pl.ANY)
    return pl.pallas_call(
        nothing, in_specs=[anywhere, anywhere], out_specs=anywhere,
        out_shape=jax.ShapeDtypeStruct(values.shape, values.dtype), input_output_aliases={0: 0},
        cost_estimate=NO_COST, name="after")(values, earlier)


class Order:
    def __init__(self):
        self.last = None

    def tie(self, values):
        if self.last is None:
            return values
        values, self.last = lax.optimization_barrier((values, self.last))
        return values

    def mark(self, values):
        self.last = values


def total(terms, lift, size, axis):
    return sum(lax.dynamic_slice_in_dim(values, start + lift, size, axis).astype(f32)
               for values, start in terms)


def halve(order, terms, size, axis, count, bit):
    half = size // 2
    mine = (lax.axis_index("dp") >> bit) & 1
    send = total(terms, (1 - mine) * half, half, axis).astype(low)
    order.mark(send)
    got = lax.ppermute(send, "dp", flips(count, bit))
    yield
    return [(values, start + mine * half) for values, start in terms] + [(order.tie(got), 0)]


def gather_steps(order, values, count, bits):
    index = lax.axis_index("dp")
    for bit in reversed(bits):
        order.mark(values)
        got = lax.ppermute(values, "dp", flips(count, bit))
        yield
        values = joined_rows((index >> bit) & 1, values, order.tie(got))
    return values


def unit_steps(order, kept, given, count, axis, split, out):
    bits = list(range(1, count.bit_length() - 1))
    size = kept.shape[axis]
    given = order.tie(given)
    order.mark(given)
    got = lax.ppermute(given, "dp", flips(count, 0))
    yield
    terms = [(kept, 0), (order.tie(got), 0)]
    terms = yield from halve(order, terms, size, axis, count, bits[0])
    size //= 2
    mine, other = ([(split(values)[c], start) for values, start in terms] for c in range(2))
    send = total(other, 0, size, 0).astype(low)
    order.mark(send)
    got = to_peer(send)
    yield
    terms = mine + [(order.tie(got), 0)]
    for bit in bits[1:]:
        terms = yield from halve(order, terms, size, 0, count, bit)
        size //= 2
    mine = yield from gather_steps(order, total(terms, 0, size, 0).astype(low), count, bits)
    order.mark(mine)
    other = lax.ppermute(mine, "dp", flips(count, 0))
    yield
    out += [mine, order.tie(other)]


def buffer_steps(order, values, count, out):
    bits = list(range(count.bit_length() - 1))
    size = values.shape[0]
    terms = [(order.tie(values), 0)]
    for bit in bits:
        terms = yield from halve(order, terms, size, 0, count, bit)
        size //= 2
    values = yield from gather_steps(order, total(terms, 0, size, 0).astype(low), count, bits)
    order.mark(values)
    out.append(values)


def small_steps(order, values, count, out):
    values = order.tie(values)
    for bit in [None] + list(range(count.bit_length() - 1)):
        order.mark(values)
        got = to_peer(values) if bit is None else lax.ppermute(values, "dp", flips(count, bit))
        yield
        values = added(values, order.tie(got))
    order.mark(values)
    out.append(values)


def advance(*chains):
    for chain in chains:
        next(chain, None)


def finish(*chains):
    left = list(chains)
    while left:
        for chain in list(left):
            try:
                next(chain)
            except StopIteration:
                left.remove(chain)


def body(
    count,
    hidden,
    lengths,
    padding,
    bucket_line,
    bucket_horizontal,
    bucket_vertical,
    attn_project,
    attn_bias,
    table_line,
    table_horizontal,
    table_vertical,
    out_project,
    out_bias,
    attn_gain,
    attn_shift,
    hidden_project,
    hidden_bias,
    down_project,
    down_bias,
    final_gain,
    final_shift,
    cotangent,
):
    rows, slots, width = hidden.shape
    half = cotangent.shape[1]
    heads = table_line.shape[1]
    local = attn_project.shape[2]
    units = hidden_project.shape[1]
    part = units // 2
    factor = 1.0 / math.sqrt(local // heads)
    head = lax.axis_index("head")
    index = lax.axis_index("dp")
    core = index & 1
    offset = head * half
    every = list(range(count.bit_length() - 1))

    def split(values, dim):
        return [lax.dynamic_slice_in_dim(values, c * part, part, dim) for c in (core, 1 - core)]

    def joined(own_parts, got, dim):
        mine, rest = own_parts
        beside = lax.ppermute(got, "dp", flips(count, 0))
        return [jnp.concatenate([mine, got], axis=dim), jnp.concatenate([rest, beside], axis=dim)]

    side = (index >> 1) & 1
    down_mine = lax.dynamic_slice_in_dim(down_project, core * part + side * (part // 2), part // 2, 0)
    down_got = to_peer(down_mine)
    down_mine, hidden_project = lax.optimization_barrier((down_mine, hidden_project))
    up_mine = lax.dynamic_slice_in_dim(hidden_project, core * part, part, 1)
    up_got = to_peer(up_mine)
    up_mine, hidden, hidden_project, down_project = lax.optimization_barrier(
        (up_mine, hidden, hidden_project, down_project))
    bias_got = to_peer(hidden_bias)

    planes = jnp.concatenate([table_horizontal, table_vertical], axis=0)
    bins = table_line.shape[0] + planes.shape[0]
    lines = jnp.broadcast_to(table_line.T[:, :, None], (heads, table_line.shape[0], B))
    planes = jnp.broadcast_to(planes.T[:, None, :], (heads, PACK, planes.shape[0]))
    pad = padding[:, None, :]
    bucket_line, bucket_horizontal, bucket_vertical = (
        pltpu.with_memory_space_constraint(x, pltpu.HBM)
        for x in (bucket_line, bucket_horizontal, bucket_vertical))

    flat = hidden.reshape(rows * slots, width)
    query = ((times(flat, attn_project[0], 1, 0) + attn_bias[0].astype(f32)).astype(low)
             * jnp.asarray(factor, low))
    key = times(flat, attn_project[1], 1, 0).astype(low)
    value = (times(flat, attn_project[2], 1, 0) + attn_bias[1].astype(f32)).astype(low)
    query, key, value = (pltpu.with_memory_space_constraint(x.reshape(rows, slots, local), pltpu.HBM)
                         for x in (query, key, value))

    def own(values):
        return lax.dynamic_slice_in_dim(values, offset, half, 0)

    def others(values):
        return lax.dynamic_slice_in_dim(values, half - offset, half, 0)

    fronts, attn_sum, attn_got = [], [], []
    for r in range(rows):
        if r == 1:
            lengths, down_got = lax.optimization_barrier((lengths, down_got))
            down_beside = lax.ppermute(down_got, "dp", flips(count, 1))
        probs, context = attn_fwd(r, lengths, query, key, value, pad, bucket_line,
                                  bucket_horizontal, bucket_vertical, lines, planes)
        if r == 1:
            context, down_beside = lax.optimization_barrier((context, down_beside))
        fronts.append((probs, context))
        send = times(others(context), out_project, 1, 0).astype(low)
        got = to_peer(send)
        attn_sum.append(times(own(context), out_project, 1, 0))
        attn_got.append(got)
    (send, hidden_project, down_project, cotangent, norm_rows, out_bias, down_bias, hidden_bias, bias_got,
     hidden) = lax.optimization_barrier(
        (send, hidden_project, down_project, cotangent, (attn_gain, attn_shift, final_gain, final_shift),
         out_bias, down_bias, hidden_bias, bias_got, hidden))
    biases = [jnp.concatenate([x, y]) for x, y in zip(split(hidden_bias, 0), split(bias_got, 0))]
    gain_first, shift_first, gain_last, shift_last = (x.astype(f32) for x in norm_rows)
    up_parts = [up_mine, lax.dynamic_slice_in_dim(hidden_project, (1 - core) * part, part, 1)]
    down_parts = split(down_project, 0)
    up_got, down_beside, attn_got = lax.optimization_barrier((up_got, down_beside, attn_got))
    down_got = in_order(side, down_got, down_beside)
    ups = joined(up_parts, up_got, 1)
    downs = joined(down_parts, down_got.reshape(part, width), 0)
    attn_sum = [x + got.astype(f32) for x, got in zip(attn_sum, attn_got)]
    tokens = lax.dynamic_slice_in_dim(hidden, offset, half, 1).reshape(rows * half, width).astype(f32)
    normed, scale = normalize(tokens + jnp.concatenate(attn_sum, axis=0) + out_bias.astype(f32))
    mid = normed * gain_first + shift_first
    mid_low = mid.astype(low)

    actives, slopes = [], []
    total = None
    for up, down, bias in zip(ups, downs, biases):
        inner = times(mid_low, up, 1, 0) + bias.astype(f32)
        bell = 0.5 * (1.0 + lax.erf(inner * math.sqrt(0.5)))
        actives.append((inner * bell).astype(low))
        slope = bell + inner * (jnp.exp(-0.5 * inner * inner) * (1.0 / math.sqrt(2.0 * math.pi)))
        slopes.append(slope.astype(low))
        term = times(actives[-1], down, 1, 0)
        total = term if total is None else total + term
    normed_final, scale_final = normalize(mid + total + down_bias.astype(f32))
    output = (normed_final * gain_last + shift_last).astype(low).reshape(rows, half, width)

    above = cotangent.reshape(rows * half, width).astype(f32)
    g_final = normalize_back(above, normed_final, scale_final, gain_last)
    g_low = g_final.astype(low)
    order = Order()
    total = None
    inners = []
    for up, down, slope in zip(ups, downs, slopes):
        g_inner = (times(g_low, down, 1, 1) * slope.astype(f32)).astype(low)
        inners.append(g_inner)
        term = times(g_inner, up, 1, 1)
        total = term if total is None else total + term
    g_mid = g_final + total
    g_attn = normalize_back(g_mid, normed, scale, gain_first)
    g_attn_low = g_attn.astype(low).reshape(rows, half, width)
    g_others = [to_peer(g_attn_low[r]) for r in range(rows)]
    order.mark(g_attn_low)
    down_out, up_out, attn_out = [], [], []
    g_low = order.tie(g_low)
    kept, given = (times(active, g_low, 0, 0).astype(low) for active in actives)
    down_chain = unit_steps(order, *(x.reshape(2, part, width) for x in (kept, given)), count, 1,
                            lambda v: (v[0], v[1]), down_out)
    advance(down_chain)
    mid_low = order.tie(mid_low)
    kept, given = (times(mid_low, g_inner, 0, 0).astype(low) for g_inner in inners)
    up_chain = unit_steps(order, kept, given, count, 0, lambda v: (v[:, :part], v[:, part:]), up_out)
    advance(up_chain, down_chain)
    g_attn = g_attn.reshape(rows, half, width)

    marks, three, grad_out = [], None, 0.0
    for r in range(rows):
        probs, context = fronts[r]
        g_all = in_order(head, g_attn_low[r], order.tie(g_others[r])).reshape(slots, width)
        g_context = times(g_all, out_project, 1, 1).astype(low)
        g_scores, three = attn_bwd(r, factor, lengths, query, key, value, g_context, context, probs, three)
        order.mark(g_scores)
        marks.append(g_scores)
        grad_out = grad_out + times(context, g_all, 0, 0)
        advance(up_chain if r == 0 else down_chain)
    grad_attn = times(flat, three.reshape(rows * slots, 3 * local), 0, 0).astype(low)
    grad_out = jnp.concatenate([grad_out[:, :local], grad_out[:, local:]], axis=0).astype(low)
    attn_chain = buffer_steps(order, jnp.concatenate([grad_attn, grad_out], axis=1), count, attn_out)
    advance(attn_chain)
    every_project = jnp.concatenate([attn_project[c] for c in range(3)], axis=1)
    room = width // 2

    def pack():
        sums = [jnp.sum(x.reshape(rows * half, width), axis=0, keepdims=True) for x in
                (g_attn, g_mid * normed, g_mid, g_final, above * normed_final, above)]
        sums, units_in, three_sums, tables = order.tie(
            (sums, inners, jnp.sum(three.astype(f32).reshape(rows * slots, 3 * local), axis=0,
                                       keepdims=True), sum(tables_out)))
        unit_sums = [jnp.sum(x.astype(f32), axis=0, keepdims=True) for x in units_in]
        ours, others_ = (jnp.concatenate(arranged(core, *(x[:, c * part:(c + 1) * part] for x in unit_sums)),
                                         axis=0) for c in range(2))
        pair = jnp.concatenate([three_sums[:, :local], three_sums[:, 2 * local:]], axis=1)
        tables = jnp.pad(tables, ((0, 0), (0, room - bins)))
        return jnp.concatenate(
            sums + list(arranged(head, ours, others_))
            + [jnp.where(head == slot, pair, 0.0) for slot in range(2)]
            + [jnp.zeros((4, width), f32),
               jnp.concatenate([jnp.where(head == slot, tables, 0.0) for slot in range(2)], axis=1)], axis=0)

    tables_out, small_out = [], []
    blocks = [(r, block) for r in range(rows) for block in range(slots // B)]
    chains = {"D": down_chain, "U": up_chain, "A": attn_chain}
    for name in ORDER:
        if name == "T":
            r, block = blocks[len(tables_out)]
            tables_out.append(table_grads(r, block, order.tie(lengths), bucket_line,
                                          bucket_horizontal, bucket_vertical, marks[r]))
            order.mark(tables_out[-1])
        elif name == "G":
            three = order.tie(three)
            theirs = lax.dynamic_slice_in_dim(three, half - offset, half, 1)
            give = times(theirs.reshape(rows * half, 3 * local), every_project, 1, 1).astype(low)
            order.mark(give)
            received = to_peer(give)
            mine = lax.dynamic_slice_in_dim(three, offset, half, 1)
            mine = times(mine.reshape(rows * half, 3 * local), every_project, 1, 1)
        elif name == "R":
            grads_in = (mine + order.tie(received).astype(f32)).reshape(rows, half, width) + g_attn
            order.mark(grads_in)
        elif name == "P":
            chains["S"] = small_steps(order, pack(), count, small_out)
        else:
            advance(chains[name])
    finish(*chains.values())
    packed = after(small_out[0], up_out[0])
    grad_down = in_order(core, *down_out).reshape(down_project.shape).astype(f32)
    mine, other = up_out
    grad_up = jnp.concatenate(arranged(core, mine, other), axis=1).astype(f32)
    buffer = attn_out[0].astype(f32)
    grad_attn = jnp.stack([buffer[:, c * local:(c + 1) * local] for c in range(3)])
    grad_out = jnp.concatenate([buffer[:local, 3 * local:], buffer[local:, 3 * local:]], axis=1)

    rows_of = lambda at, size: lax.dynamic_slice_in_dim(packed, at, size, 0)
    grad_bias = rows_of(6 + 2 * head, 2).reshape(-1)
    grad_attn_bias = rows_of(10 + head, 1).reshape(2, local)
    marks = jnp.where(head == 0, packed[16:, :bins], packed[16:, room:room + bins])[:heads].T
    first, second = table_line.shape[0], table_horizontal.shape[0]
    return (
        output,
        grads_in,
        grad_attn,
        grad_attn_bias,
        marks[:first],
        marks[first:first + second],
        marks[first + second:],
        grad_out,
        packed[0],
        packed[1],
        packed[2],
        grad_up,
        grad_bias,
        grad_down,
        packed[3],
        packed[4],
        packed[5],
    )


def solution(mesh):
    return jax.shard_map(
        functools.partial(body, mesh.shape["dp"]),
        mesh=mesh,
        in_specs=(
            P("dp", None, None),
            P("dp", None),
            P("dp", None),
            P("dp", None, None),
            P("dp", None, None),
            P("dp", None, None),
            P(None, None, "head"),
            P(None, "head"),
            P(None, "head"),
            P(None, "head"),
            P(None, "head"),
            P("head", None),
            P(),
            P(),
            P(),
            P(None, "head"),
            P("head"),
            P("head", None),
            P(),
            P(),
            P(),
            P("dp", "head", None),
        ),
        out_specs=(
            P("dp", "head", None),
            P("dp", "head", None),
            P(None, None, "head"),
            P(None, "head"),
            P(None, "head"),
            P(None, "head"),
            P(None, "head"),
            P("head", None),
            P(),
            P(),
            P(),
            P(None, "head"),
            P("head"),
            P("head", None),
            P(),
            P(),
            P(),
        ),
        check_vma=False,
    )
```

```python
import functools
import math

import jax
import jax.numpy as jnp
from jax import lax
from jax.experimental import pallas as pl
from jax.experimental.pallas import tpu as pltpu
from jax.sharding import PartitionSpec as P

B = 128

PACK = 16


def gather_dims(axis):
    return lax.GatherDimensionNumbers(
        offset_dims=(), collapsed_slice_dims=(axis,), start_index_map=(axis,),
        operand_batching_dims=(1 - axis,), start_indices_batching_dims=(1 - axis,))


def pick(table, index, axis):
    return lax.gather(table, index[:, :, None], gather_dims(axis), (1, 1),
                      mode=lax.GatherScatterMode.PROMISE_IN_BOUNDS)


def two_heads(values, left):
    zero = jnp.zeros_like(values)
    return jnp.concatenate([jnp.where(left, values, zero), jnp.where(left, zero, values)], axis=0)


def doc_span(len_ref, row, first, last):
    edge = 0
    start = 0
    stop = 0
    for k in range(len_ref.shape[1]):
        begin = edge
        edge = edge + len_ref[row, k]
        start = jnp.where(begin <= first, begin, start)
        stop = jnp.where(begin <= last, edge, stop)
    return start // B, (stop + (B - 1)) // B

def fwd_kernel(row, len_ref, q_ref, k_ref, v_ref, pad_ref, bl_ref, bh_ref, bv_ref, line_ref, plane_ref,
               probs_ref, ctx_ref, sc, qs, best, mass, mixed):
    qb = pl.program_id(0)
    heads = sc.shape[1]
    pairs = heads // 2
    lane = lax.broadcasted_iota(jnp.int32, (B, B), 1)
    left = lane < (B // 2)
    first = qb * B
    low, high = doc_span(len_ref, row, first, first + B - 1)
    sub = lax.broadcasted_iota(jnp.int32, (B, B), 0) + first
    edges = []
    edge = 0
    for k in range(len_ref.shape[1]):
        edge = edge + len_ref[row, k]
        edges.append(edge)
    seg_q = sum(((sub >= e).astype(jnp.int32) for e in edges))
    for p in range(pairs):
        qs[p] = two_heads(q_ref[:, p * B:(p + 1) * B], left)

    def scores(t, carry):
        key_at = lane + t * B
        at = pl.ds(pl.multiple_of(t * B, B), B)
        seg_k = sum(((key_at >= e).astype(jnp.int32) for e in edges))
        real = jnp.broadcast_to(pad_ref[:, at], (B, B)) > 0
        allowed = ((seg_q == seg_k) & real) | (sub == key_at)
        parts = []
        for g in range(B // PACK):
            rows = slice(g * PACK, g * PACK + PACK)
            line = bl_ref[rows, at].astype(jnp.int16)
            parts.append((line & jnp.int16(PACK - 1), line >= jnp.int16(PACK),
                          bh_ref[rows, at].astype(jnp.int16), (bv_ref[rows, at] + 64).astype(jnp.int16)))
        for p in range(pairs):
            raw = lax.dot_general(qs[p], k_ref[at, p * B:(p + 1) * B], (((1,), (1,)), ((), ())),
                                  preferred_element_type=jnp.float32)
            for s in range(2):
                h = 2 * p + s
                plane = plane_ref[h]
                for g, (place, upper, horiz, vert) in enumerate(parts):
                    rows = slice(g * PACK, g * PACK + PACK)
                    found = jnp.where(upper, pick(line_ref[h, PACK:2 * PACK, :], place, 0),
                                      pick(line_ref[h, 0:PACK, :], place, 0))
                    rel = ((found.astype(jnp.float32) + pick(plane, horiz, 1).astype(jnp.float32))
                           + pick(plane, vert, 1).astype(jnp.float32))
                    val = jnp.where(allowed[rows], raw[s * B + g * PACK:s * B + (g + 1) * PACK, :] + rel,
                                    -1000000000.0)
                    sc[t, h, rows, :] = val
                    best[h, rows, :] = jnp.maximum(best[h, rows, :], val)
        return carry

    best[...] = jnp.full(best.shape, -3.0e38, jnp.float32)
    mass[...] = jnp.zeros_like(mass)
    mixed[...] = jnp.zeros_like(mixed)
    lax.fori_loop(low, high, scores, 0)
    for h in range(heads):
        best[h] = jnp.broadcast_to(jnp.max(best[h], axis=-1, keepdims=True), (B, B))

    def expo(t, carry):
        for h in range(heads):
            e = jnp.exp(sc[t, h] - best[h])
            sc[t, h] = e
            mass[h] += e
        return carry

    lax.fori_loop(low, high, expo, 0)
    for h in range(heads):
        mass[h] = jnp.broadcast_to(1.0 / jnp.sum(mass[h], axis=-1, keepdims=True), (B, B))

    def mix(t, carry):
        at = pl.ds(pl.multiple_of(t * B, B), B)
        for p in range(pairs):
            low_pair = []
            for s in range(2):
                h = 2 * p + s
                pr = sc[t, h] * mass[h]
                probs_ref[t, h] = pr
                low_pair.append(pr.astype(jnp.bfloat16))
            mixed[p] += jnp.dot(jnp.concatenate(low_pair, axis=0), v_ref[at, p * B:(p + 1) * B],
                                preferred_element_type=jnp.float32)
        return carry

    lax.fori_loop(low, high, mix, 0)
    for p in range(pairs):
        ctx_ref[:, p * B:(p + 1) * B] = jnp.where(left, mixed[p, :B, :], mixed[p, B:, :]).astype(jnp.bfloat16)


def attn_fwd(row, lengths, q, k, v, pad, bl, bh, bv, line, plane):
    slots, width = q.shape[1:]
    pairs = width // B
    tiles = slots // B
    row_block = lambda n: pl.BlockSpec((None, B, n), lambda i, L: (row, i, 0))
    return pl.pallas_call(
        functools.partial(fwd_kernel, row),
        grid_spec=pltpu.PrefetchScalarGridSpec(
            num_scalar_prefetch=1, grid=(tiles,),
            in_specs=[
                row_block(width),
                pl.BlockSpec((None, slots, width), lambda i, L: (row, 0, 0)),
                pl.BlockSpec((None, slots, width), lambda i, L: (row, 0, 0)),
                pl.BlockSpec((None, 1, slots), lambda i, L: (row, 0, 0)),
                row_block(slots), row_block(slots), row_block(slots),
                pl.BlockSpec(line.shape, lambda i, L: (0, 0, 0)),
                pl.BlockSpec(plane.shape, lambda i, L: (0, 0, 0)),
            ],
            out_specs=[
                pl.BlockSpec((None, tiles, 2 * pairs, B, B), lambda i, L: (i, 0, 0, 0, 0)),
                pl.BlockSpec((B, width), lambda i, L: (i, 0)),
            ],
            scratch_shapes=[
                pltpu.VMEM((tiles, 2 * pairs, B, B), jnp.float32),
                pltpu.VMEM((pairs, 2 * B, B), jnp.bfloat16),
                pltpu.VMEM((2 * pairs, B, B), jnp.float32),
                pltpu.VMEM((2 * pairs, B, B), jnp.float32),
                pltpu.VMEM((pairs, 2 * B, B), jnp.float32),
            ]),
        out_shape=[
            jax.ShapeDtypeStruct((tiles, tiles, 2 * pairs, B, B), jnp.float32),
            jax.ShapeDtypeStruct((slots, width), jnp.bfloat16),
        ],
        compiler_params=pltpu.CompilerParams(vmem_limit_bytes=48 << 20),
        cost_estimate=pl.CostEstimate(flops=1, transcendentals=0, bytes_accessed=1),
        name="attn_forward",
    )(lengths, q, k, v, pad, bl, bh, bv, line, plane)


NT = (((1,), (1,)), ((), ()))
TN = (((0,), (0,)), ((), ()))

def bwd_kernel(row, factor, len_ref, q_ref, k_ref, v_ref, gctx_ref, ctx_ref, probs_ref, *rest):
    pairs, tiles = q_ref.shape[1] // B, probs_ref.shape[0]
    ds_ref, three_ref, *scratch = rest[len(rest) - 6 * pairs - 2:]
    dks, dvs, dqs, inner, qs, gs = (scratch[n * pairs:(n + 1) * pairs] for n in range(6))
    qb = pl.program_id(0)
    lane = lax.broadcasted_iota(jnp.int32, (B, B), 1)
    left = lane < (B // 2)

    @pl.when(qb == 0)
    def _():
        for ref in dks + dvs:
            ref[...] = jnp.zeros_like(ref)

    first = qb * B
    low, high = doc_span(len_ref, row, first, first + B - 1)
    for p in range(pairs):
        cols = slice(p * B, (p + 1) * B)
        gctx = gctx_ref[:, cols]
        qs[p][...] = two_heads(q_ref[:, cols], left)
        gs[p][...] = two_heads(gctx, left)
        prod = gctx.astype(jnp.float32) * ctx_ref[:, cols].astype(jnp.float32)
        inner[p][...] = jnp.broadcast_to(jnp.sum(two_heads(prod, left), axis=-1, keepdims=True), (2 * B, B))
        dqs[p][...] = jnp.zeros_like(dqs[p])

    def tile(t, carry):
        at = pl.ds(pl.multiple_of(t * B, B), B)
        for p in range(pairs):
            cols = slice(p * B, (p + 1) * B)
            gp = lax.dot_general(gs[p][...], v_ref[at, cols], NT, preferred_element_type=jnp.float32)
            probs_low, g_scores = [], []
            for s in range(2):
                rows = slice(s * B, (s + 1) * B)
                pr = probs_ref[t, 2 * p + s]
                ds = (pr * (gp[rows, :] - inner[p][rows, :])).astype(jnp.bfloat16)
                ds_ref[t, 2 * p + s] = ds
                g_scores.append(ds)
                probs_low.append(pr.astype(jnp.bfloat16))
            ds = jnp.concatenate(g_scores, axis=0)
            mix = jnp.concatenate(probs_low, axis=0)
            dvs[p][t] += lax.dot_general(mix, gs[p][...], TN, preferred_element_type=jnp.float32)
            dks[p][t] += lax.dot_general(ds, qs[p][...], TN, preferred_element_type=jnp.float32)
            dqs[p][...] += jnp.dot(ds, k_ref[at, cols], preferred_element_type=jnp.float32)
        return carry

    lax.fori_loop(low, high, tile, 0)
    for p in range(pairs):
        dq = jnp.where(left, dqs[p][0:B, :], dqs[p][B:2 * B, :]) * factor
        three_ref[pl.ds(pl.multiple_of(first, B), B), p * B:(p + 1) * B] = dq.astype(jnp.bfloat16)

    @pl.when(qb == tiles - 1)
    def _():
        for p in range(pairs):
            for t in range(tiles):
                rows = slice(t * B, (t + 1) * B)
                three_ref[rows, (pairs + p) * B:(pairs + p + 1) * B] = dks[p][t].astype(jnp.bfloat16)
                three_ref[rows, (2 * pairs + p) * B:(2 * pairs + p + 1) * B] = dvs[p][t].astype(jnp.bfloat16)


def attn_bwd(row, factor, lengths, q, k, v, gctx, ctx, probs, kept=None):
    slots, width = q.shape[1:]
    pairs, tiles = width // B, slots // B
    part = pl.BlockSpec((B, width), lambda i, L: (i, 0))
    three = pl.BlockSpec((None, slots, 3 * width), lambda i, L: (row, 0, 0))
    mine = pl.BlockSpec((None, B, width), lambda i, L: (row, i, 0))
    whole = pl.BlockSpec((None, slots, width), lambda i, L: (row, 0, 0))
    pairs_of = pl.BlockSpec((None, tiles, 2 * pairs, B, B), lambda i, L: (i, 0, 0, 0, 0))
    kept = () if kept is None else (kept,)
    return pl.pallas_call(
        functools.partial(bwd_kernel, row, factor),
        grid_spec=pltpu.PrefetchScalarGridSpec(
            num_scalar_prefetch=1, grid=(tiles,),
            in_specs=[mine, whole, whole, part, part, pairs_of]
            + [pl.BlockSpec(memory_space=pl.ANY)] * len(kept),
            out_specs=[pairs_of, three],
            scratch_shapes=[pltpu.VMEM((tiles, B, B), jnp.float32)] * (2 * pairs)
            + [pltpu.VMEM((2 * B, B), jnp.float32)] * (2 * pairs)
            + [pltpu.VMEM((2 * B, B), jnp.bfloat16)] * (2 * pairs)),
        out_shape=[jax.ShapeDtypeStruct(probs.shape, jnp.bfloat16),
                   jax.ShapeDtypeStruct((q.shape[0], slots, 3 * width), jnp.bfloat16)],
        input_output_aliases={7: 1} if kept else {},
        compiler_params=pltpu.CompilerParams(vmem_limit_bytes=48 << 20),
        cost_estimate=pl.CostEstimate(flops=1, transcendentals=0, bytes_accessed=1),
        name="attn_backward",
    )(lengths, q, k, v, gctx, ctx, probs, *kept)

BINS = 160
SPREADS = 3


def hist_kernel(row, step, len_ref, bl_ref, bh_ref, bv_ref, ds_ref, out_ref, *spreads):
    tiles, heads = ds_ref.shape[0], ds_ref.shape[1]
    docs = len_ref.shape[1]
    lane = lax.broadcasted_iota(jnp.int32, (PACK, B), 1)
    sub = lax.broadcasted_iota(jnp.int32, (PACK, B), 0)
    for spread in spreads:
        spread[...] = jnp.zeros_like(spread)

    floor, roof = step * B, (step + 1) * B
    starts, ends, firsts, lasts, upto, steps = [], [], [], [], [], []
    edge, count = 0, 0
    for d in range(docs):
        starts.append(edge)
        edge = edge + len_ref[row, d]
        ends.append(edge)
        firsts.append(jnp.maximum(starts[d], floor))
        lasts.append(jnp.maximum(jnp.minimum(edge, roof), firsts[d]))
        steps.append(jnp.where(edge - starts[d] <= B, 2, 1))
        here = ((lasts[d] + (PACK - 1)) // PACK - firsts[d] // PACK + (steps[d] - 1)) // steps[d]
        count = count + jnp.where(lasts[d] > firsts[d], here, 0)
        upto.append(count)

    def group(g, spread):
        start, end, first, last, pace = starts[0], ends[0], firsts[0], lasts[0], steps[0]
        block = firsts[0] // PACK + g * steps[0]
        for d in range(1, docs):
            past = g >= upto[d - 1]
            start, end, first, last, pace, block = (
                jnp.where(past, new, old) for new, old in
                ((starts[d], start), (ends[d], end), (firsts[d], first), (lasts[d], last), (steps[d], pace),
                 (firsts[d] // PACK + (g - upto[d - 1]) * steps[d], block)))
        last = jnp.where(g < count, last, first)
        start = jnp.minimum(start, tiles * B - 1)
        tile = start // B
        left = start - tile * B
        turn = jnp.where(left == 0, 0, B - left)
        halves = []
        for part in range(2):
            along, later = part * (pace - 1), part * (2 - pace)
            mine = block + along
            token = sub + mine * PACK
            live = (token >= first) & (token < last) & (lane + later * B < end - start)
            at = jnp.clip(mine - step * (B // PACK), 0, B // PACK - 1)
            halves.append((live, pl.ds(pl.multiple_of(at * PACK, PACK), PACK),
                           [jnp.minimum(tile + later + n, tiles - 1) for n in range(2)]))
        before = lane < B - left

        def moved(here, there):
            return jnp.where(before, pltpu.roll(here, turn, 1), pltpu.roll(there, turn, 1))

        codes = []
        for part, (live, rows, spots) in enumerate(halves):
            for h in range(heads):
                vals = moved(*(ds_ref[s, h, rows, :].astype(jnp.float32) for s in spots))
                spread[part, pl.ds(h, PACK, stride=8), :] = jnp.where(live, vals, 0.0)
            at = [pl.ds(pl.multiple_of(s * B, B), B) for s in spots]
            codes.append(moved(*(bl_ref[rows, x] + 32 * bh_ref[rows, x] + 2048 * bv_ref[rows, x]
                                 for x in at)))
        code = jnp.concatenate(codes, axis=1)
        index = [(code & 31).astype(jnp.int16), ((code >> 5) & 63).astype(jnp.int16),
                 (code >> 11).astype(jnp.int16)]
        one, zero = jnp.ones((), jnp.bfloat16), jnp.zeros((), jnp.bfloat16)
        grads, hots = [], []
        for r in range(PACK):
            hot = []
            for ix, n in zip(index, (32, 64, 64)):
                bins = lax.broadcasted_iota(jnp.int16, (n, 2 * B), 0)
                line = jnp.broadcast_to(ix[r:r + 1, :], (n, 2 * B))
                hot.append(jnp.where(bins == line, one, zero))
            hots.append(jnp.concatenate(hot, axis=0))
            grads += [spread[part, r * 8:r * 8 + 8, :].astype(jnp.bfloat16) for part in range(2)]
        return lax.dot_general(jnp.concatenate(grads, axis=1), jnp.concatenate(hots, axis=1), NT,
                               preferred_element_type=jnp.float32)

    def several(turn, sums):
        return tuple(x + group(len(spreads) * turn + n, spread)
                     for n, (x, spread) in enumerate(zip(sums, spreads)))

    none = jnp.zeros((8, BINS), jnp.float32)
    turns = (count + (len(spreads) - 1)) // len(spreads)
    out_ref[...] = sum(lax.fori_loop(0, turns, several, tuple(none for _ in spreads)))


def table_grads(row, step, lengths, bl, bh, bv, ds):
    slots = bl.shape[1]
    tiles, heads = ds.shape[0], ds.shape[2]
    block = pl.BlockSpec((None, B, slots), lambda i, L: (row, step, 0))
    return pl.pallas_call(
        functools.partial(hist_kernel, row, step),
        grid_spec=pltpu.PrefetchScalarGridSpec(
            num_scalar_prefetch=1, grid=(1,),
            in_specs=[block, block, block,
                      pl.BlockSpec((None, tiles, heads, B, B), lambda i, L: (step, 0, 0, 0, 0))],
            out_specs=pl.BlockSpec((8, BINS), lambda i, L: (0, 0)),
            scratch_shapes=[pltpu.VMEM((2, 8 * PACK, B), jnp.float32)] * SPREADS),
        out_shape=jax.ShapeDtypeStruct((8, BINS), jnp.float32),
        compiler_params=pltpu.CompilerParams(vmem_limit_bytes=48 << 20),
        cost_estimate=pl.CostEstimate(flops=1, transcendentals=0, bytes_accessed=1),
        name="table_grads",
    )(lengths, bl, bh, bv, ds)


f32, low = jnp.float32, jnp.bfloat16
SWAP = [(0, 1), (1, 0)]
ORDER = "UATDTADTUGATDUTATDTURADTUAPSDUSASSUSS"


def normalize(values):
    mean = jnp.mean(values, axis=-1, keepdims=True)
    centered = values - mean
    scale = lax.rsqrt(jnp.mean(centered * centered, axis=-1, keepdims=True) + 1e-12)
    return centered * scale, scale


def normalize_back(grad, normed, scale, gain):
    scaled = grad * gain
    first = jnp.mean(scaled, axis=-1, keepdims=True)
    second = jnp.mean(scaled * normed, axis=-1, keepdims=True)
    return scale * (scaled - first - normed * second)


def times(left, right, left_dim, right_dim):
    return lax.dot_general(left, right, (((left_dim,), (right_dim,)), ((), ())),
                           preferred_element_type=f32)


def flips(count, bit):
    return [(i, i ^ (1 << bit)) for i in range(count)]


def to_peer(values):
    return lax.ppermute(values, "head", SWAP)


def plus(left, right):
    return (left.astype(f32) + right.astype(f32)).astype(low)


def arranged(bit_value, mine, other):
    return jnp.where(bit_value == 0, mine, other), jnp.where(bit_value == 0, other, mine)


def in_order(bit_value, mine, other):
    return jnp.stack(arranged(bit_value, mine, other))


NO_COST = pl.CostEstimate(flops=1, transcendentals=0, bytes_accessed=1)


def join_kernel(bit_ref, mine_ref, got_ref, out_ref):
    own = pl.program_id(0) == bit_ref[0]

    @pl.when(own)
    def _():
        out_ref[...] = mine_ref[...]

    @pl.when(jnp.logical_not(own))
    def _():
        out_ref[...] = got_ref[...]


def joined_rows(bit_value, mine, got):
    rows, columns = mine.shape
    whole = pl.BlockSpec((rows, columns), lambda i, b: (0, 0))
    out = pl.pallas_call(
        join_kernel,
        grid_spec=pltpu.PrefetchScalarGridSpec(
            num_scalar_prefetch=1, grid=(2,), in_specs=[whole, whole],
            out_specs=pl.BlockSpec((None, rows, columns), lambda i, b: (i, 0, 0))),
        out_shape=jax.ShapeDtypeStruct((2, rows, columns), mine.dtype),
        compiler_params=pltpu.CompilerParams(vmem_limit_bytes=48 << 20),
        cost_estimate=NO_COST, name="joined_rows",
    )(bit_value.reshape(1), mine, got)
    return out.reshape(2 * rows, columns)


def nothing(*refs):
    pass


def after(values, earlier):
    anywhere = pl.BlockSpec(memory_space=pl.ANY)
    return pl.pallas_call(
        nothing, in_specs=[anywhere, anywhere], out_specs=anywhere,
        out_shape=jax.ShapeDtypeStruct(values.shape, values.dtype), input_output_aliases={0: 0},
        cost_estimate=NO_COST, name="after")(values, earlier)


class Order:
    def __init__(self):
        self.last = None

    def tie(self, values):
        if self.last is None:
            return values
        values, self.last = lax.optimization_barrier((values, self.last))
        return values

    def mark(self, values):
        self.last = values


def total(terms, lift, size, axis):
    return sum(lax.dynamic_slice_in_dim(values, start + lift, size, axis).astype(f32)
               for values, start in terms)


def halve(order, terms, size, axis, count, bit):
    half = size // 2
    mine = (lax.axis_index("dp") >> bit) & 1
    send = total(terms, (1 - mine) * half, half, axis).astype(low)
    order.mark(send)
    got = lax.ppermute(send, "dp", flips(count, bit))
    yield
    return [(values, start + mine * half) for values, start in terms] + [(order.tie(got), 0)]


def gather_steps(order, values, count, bits):
    index = lax.axis_index("dp")
    for bit in reversed(bits):
        order.mark(values)
        got = lax.ppermute(values, "dp", flips(count, bit))
        yield
        values = joined_rows((index >> bit) & 1, values, order.tie(got))
    return values


def unit_steps(order, kept, given, count, axis, split, out):
    bits = list(range(1, count.bit_length() - 1))
    size = kept.shape[axis]
    given = order.tie(given)
    order.mark(given)
    got = lax.ppermute(given, "dp", flips(count, 0))
    yield
    terms = [(kept, 0), (order.tie(got), 0)]
    terms = yield from halve(order, terms, size, axis, count, bits[0])
    size //= 2
    mine, other = ([(split(values)[c], start) for values, start in terms] for c in range(2))
    send = total(other, 0, size, 0).astype(low)
    order.mark(send)
    got = to_peer(send)
    yield
    terms = mine + [(order.tie(got), 0)]
    for bit in bits[1:]:
        terms = yield from halve(order, terms, size, 0, count, bit)
        size //= 2
    mine = yield from gather_steps(order, total(terms, 0, size, 0).astype(low), count, bits)
    order.mark(mine)
    other = lax.ppermute(mine, "dp", flips(count, 0))
    yield
    out += [mine, order.tie(other)]


def buffer_steps(order, values, count, out):
    bits = list(range(count.bit_length() - 1))
    size = values.shape[0]
    terms = [(order.tie(values), 0)]
    for bit in bits:
        terms = yield from halve(order, terms, size, 0, count, bit)
        size //= 2
    values = yield from gather_steps(order, total(terms, 0, size, 0).astype(low), count, bits)
    order.mark(values)
    out.append(values)


def small_steps(order, values, count, out):
    values = order.tie(values)
    for bit in [None] + list(range(count.bit_length() - 1)):
        order.mark(values)
        got = to_peer(values) if bit is None else lax.ppermute(values, "dp", flips(count, bit))
        yield
        values = values + order.tie(got)
    order.mark(values)
    out.append(values)


def advance(*chains):
    for chain in chains:
        next(chain, None)


def finish(*chains):
    left = list(chains)
    while left:
        for chain in list(left):
            try:
                next(chain)
            except StopIteration:
                left.remove(chain)


def body(
    count,
    hidden,
    lengths,
    padding,
    bucket_line,
    bucket_horizontal,
    bucket_vertical,
    attn_project,
    attn_bias,
    table_line,
    table_horizontal,
    table_vertical,
    out_project,
    out_bias,
    attn_gain,
    attn_shift,
    hidden_project,
    hidden_bias,
    down_project,
    down_bias,
    final_gain,
    final_shift,
    cotangent,
):
    rows, slots, width = hidden.shape
    half = cotangent.shape[1]
    heads = table_line.shape[1]
    local = attn_project.shape[2]
    units = hidden_project.shape[1]
    part = units // 2
    factor = 1.0 / math.sqrt(local // heads)
    head = lax.axis_index("head")
    index = lax.axis_index("dp")
    core = index & 1
    offset = head * half
    every = list(range(count.bit_length() - 1))

    def split(values, dim):
        return [lax.dynamic_slice_in_dim(values, c * part, part, dim) for c in (core, 1 - core)]

    def joined(own_parts, got, dim):
        mine, rest = own_parts
        beside = lax.ppermute(got, "dp", flips(count, 0))
        return [jnp.concatenate([mine, got], axis=dim), jnp.concatenate([rest, beside], axis=dim)]

    side = (index >> 1) & 1
    down_mine = lax.dynamic_slice_in_dim(down_project, core * part + side * (part // 2), part // 2, 0)
    down_got = to_peer(down_mine)
    down_mine, hidden_project = lax.optimization_barrier((down_mine, hidden_project))
    up_mine = lax.dynamic_slice_in_dim(hidden_project, core * part, part, 1)
    up_got = to_peer(up_mine)
    up_mine, hidden, hidden_project, down_project = lax.optimization_barrier(
        (up_mine, hidden, hidden_project, down_project))
    bias_got = to_peer(hidden_bias)

    planes = jnp.concatenate([table_horizontal, table_vertical], axis=0)
    bins = table_line.shape[0] + planes.shape[0]
    lines = jnp.broadcast_to(table_line.T[:, :, None], (heads, table_line.shape[0], B))
    planes = jnp.broadcast_to(planes.T[:, None, :], (heads, PACK, planes.shape[0]))
    pad = padding[:, None, :]
    bucket_line, bucket_horizontal, bucket_vertical = (
        pltpu.with_memory_space_constraint(x, pltpu.HBM)
        for x in (bucket_line, bucket_horizontal, bucket_vertical))

    flat = hidden.reshape(rows * slots, width)
    query = ((times(flat, attn_project[0], 1, 0) + attn_bias[0].astype(f32)).astype(low)
             * jnp.asarray(factor, low))
    key = times(flat, attn_project[1], 1, 0).astype(low)
    value = (times(flat, attn_project[2], 1, 0) + attn_bias[1].astype(f32)).astype(low)
    query, key, value = (pltpu.with_memory_space_constraint(x.reshape(rows, slots, local), pltpu.HBM)
                         for x in (query, key, value))

    def own(values):
        return lax.dynamic_slice_in_dim(values, offset, half, 0)

    def others(values):
        return lax.dynamic_slice_in_dim(values, half - offset, half, 0)

    fronts, attn_sum, attn_got = [], [], []
    for r in range(rows):
        if r == 1:
            lengths, down_got = lax.optimization_barrier((lengths, down_got))
            down_beside = lax.ppermute(down_got, "dp", flips(count, 1))
        probs, context = attn_fwd(r, lengths, query, key, value, pad, bucket_line,
                                  bucket_horizontal, bucket_vertical, lines, planes)
        if r == 1:
            context, down_beside = lax.optimization_barrier((context, down_beside))
        fronts.append((probs, context))
        send = times(others(context), out_project, 1, 0).astype(low)
        got = to_peer(send)
        attn_sum.append(times(own(context), out_project, 1, 0))
        attn_got.append(got)
    (send, hidden_project, down_project, cotangent, norm_rows, out_bias, down_bias, hidden_bias, bias_got,
     hidden) = lax.optimization_barrier(
        (send, hidden_project, down_project, cotangent, (attn_gain, attn_shift, final_gain, final_shift),
         out_bias, down_bias, hidden_bias, bias_got, hidden))
    biases = [jnp.concatenate([x, y]) for x, y in zip(split(hidden_bias, 0), split(bias_got, 0))]
    gain_first, shift_first, gain_last, shift_last = (x.astype(f32) for x in norm_rows)
    up_parts = [up_mine, lax.dynamic_slice_in_dim(hidden_project, (1 - core) * part, part, 1)]
    down_parts = split(down_project, 0)
    up_got, down_beside, attn_got = lax.optimization_barrier((up_got, down_beside, attn_got))
    down_got = in_order(side, down_got, down_beside)
    ups = joined(up_parts, up_got, 1)
    downs = joined(down_parts, down_got.reshape(part, width), 0)
    attn_sum = [x + got.astype(f32) for x, got in zip(attn_sum, attn_got)]
    tokens = lax.dynamic_slice_in_dim(hidden, offset, half, 1).reshape(rows * half, width).astype(f32)
    normed, scale = normalize(tokens + jnp.concatenate(attn_sum, axis=0) + out_bias.astype(f32))
    mid = normed * gain_first + shift_first
    mid_low = mid.astype(low)

    actives, slopes = [], []
    total = None
    for up, down, bias in zip(ups, downs, biases):
        inner = times(mid_low, up, 1, 0) + bias.astype(f32)
        bell = 0.5 * (1.0 + lax.erf(inner * math.sqrt(0.5)))
        actives.append((inner * bell).astype(low))
        slope = bell + inner * (jnp.exp(-0.5 * inner * inner) * (1.0 / math.sqrt(2.0 * math.pi)))
        slopes.append(slope.astype(low))
        term = times(actives[-1], down, 1, 0)
        total = term if total is None else total + term
    normed_final, scale_final = normalize(mid + total + down_bias.astype(f32))
    output = (normed_final * gain_last + shift_last).astype(low).reshape(rows, half, width)

    above = cotangent.reshape(rows * half, width).astype(f32)
    g_final = normalize_back(above, normed_final, scale_final, gain_last)
    g_low = g_final.astype(low)
    order = Order()
    total = None
    inners = []
    for up, down, slope in zip(ups, downs, slopes):
        g_inner = (times(g_low, down, 1, 1) * slope.astype(f32)).astype(low)
        inners.append(g_inner)
        term = times(g_inner, up, 1, 1)
        total = term if total is None else total + term
    g_mid = g_final + total
    g_attn = normalize_back(g_mid, normed, scale, gain_first)
    g_attn_low = g_attn.astype(low).reshape(rows, half, width)
    g_others = [to_peer(g_attn_low[r]) for r in range(rows)]
    order.mark(g_attn_low)
    down_out, up_out, attn_out = [], [], []
    g_low = order.tie(g_low)
    kept, given = (times(active, g_low, 0, 0).astype(low) for active in actives)
    down_chain = unit_steps(order, *(x.reshape(2, part, width) for x in (kept, given)), count, 1,
                            lambda v: (v[0], v[1]), down_out)
    advance(down_chain)
    mid_low = order.tie(mid_low)
    kept, given = (times(mid_low, g_inner, 0, 0).astype(low) for g_inner in inners)
    up_chain = unit_steps(order, kept, given, count, 0, lambda v: (v[:, :part], v[:, part:]), up_out)
    advance(up_chain, down_chain)
    g_attn = g_attn.reshape(rows, half, width)

    marks, three, grad_out = [], None, 0.0
    for r in range(rows):
        probs, context = fronts[r]
        g_all = in_order(head, g_attn_low[r], order.tie(g_others[r])).reshape(slots, width)
        g_context = times(g_all, out_project, 1, 1).astype(low)
        g_scores, three = attn_bwd(r, factor, lengths, query, key, value, g_context, context, probs, three)
        order.mark(g_scores)
        marks.append(g_scores)
        grad_out = grad_out + times(context, g_all, 0, 0)
        advance(up_chain if r == 0 else down_chain)
    grad_attn = times(flat, three.reshape(rows * slots, 3 * local), 0, 0).astype(low)
    grad_out = jnp.concatenate([grad_out[:, :local], grad_out[:, local:]], axis=0).astype(low)
    attn_chain = buffer_steps(order, jnp.concatenate([grad_attn, grad_out], axis=1), count, attn_out)
    advance(attn_chain)
    every_project = jnp.concatenate([attn_project[c] for c in range(3)], axis=1)
    room = width // 2

    def pack():
        sums = [jnp.sum(x.reshape(rows * half, width), axis=0, keepdims=True) for x in
                (g_attn, g_mid * normed, g_mid, g_final, above * normed_final, above)]
        sums, units_in, three_sums, tables = order.tie(
            (sums, inners, jnp.sum(three.astype(f32).reshape(rows * slots, 3 * local), axis=0,
                                       keepdims=True), sum(tables_out)))
        unit_sums = [jnp.sum(x.astype(f32), axis=0, keepdims=True) for x in units_in]
        ours, others_ = (jnp.concatenate(arranged(core, *(x[:, c * part:(c + 1) * part] for x in unit_sums)),
                                         axis=0) for c in range(2))
        pair = jnp.concatenate([three_sums[:, :local], three_sums[:, 2 * local:]], axis=1)
        tables = jnp.pad(tables, ((0, 0), (0, room - bins)))
        return jnp.concatenate(
            sums + list(arranged(head, ours, others_))
            + [jnp.where(head == slot, pair, 0.0) for slot in range(2)]
            + [jnp.zeros((4, width), f32),
               jnp.concatenate([jnp.where(head == slot, tables, 0.0) for slot in range(2)], axis=1)], axis=0)

    tables_out, small_out = [], []
    blocks = [(r, block) for r in range(rows) for block in range(slots // B)]
    chains = {"D": down_chain, "U": up_chain, "A": attn_chain}
    for name in ORDER:
        if name == "T":
            r, block = blocks[len(tables_out)]
            tables_out.append(table_grads(r, block, order.tie(lengths), bucket_line,
                                          bucket_horizontal, bucket_vertical, marks[r]))
            order.mark(tables_out[-1])
        elif name == "G":
            three = order.tie(three)
            theirs = lax.dynamic_slice_in_dim(three, half - offset, half, 1)
            give = times(theirs.reshape(rows * half, 3 * local), every_project, 1, 1).astype(low)
            order.mark(give)
            received = to_peer(give)
            mine = lax.dynamic_slice_in_dim(three, offset, half, 1)
            mine = times(mine.reshape(rows * half, 3 * local), every_project, 1, 1)
        elif name == "R":
            grads_in = (mine + order.tie(received).astype(f32)).reshape(rows, half, width) + g_attn
            order.mark(grads_in)
        elif name == "P":
            chains["S"] = small_steps(order, pack(), count, small_out)
        else:
            advance(chains[name])
    finish(*chains.values())
    packed = after(small_out[0], up_out[0])
    grad_down = in_order(core, *down_out).reshape(down_project.shape).astype(f32)
    mine, other = up_out
    grad_up = jnp.concatenate(arranged(core, mine, other), axis=1).astype(f32)
    buffer = attn_out[0].astype(f32)
    grad_attn = jnp.stack([buffer[:, c * local:(c + 1) * local] for c in range(3)])
    grad_out = jnp.concatenate([buffer[:local, 3 * local:], buffer[local:, 3 * local:]], axis=1)

    rows_of = lambda at, size: lax.dynamic_slice_in_dim(packed, at, size, 0)
    grad_bias = rows_of(6 + 2 * head, 2).reshape(-1)
    grad_attn_bias = rows_of(10 + head, 1).reshape(2, local)
    marks = jnp.where(head == 0, packed[16:, :bins], packed[16:, room:room + bins])[:heads].T
    first, second = table_line.shape[0], table_horizontal.shape[0]
    return (
        output,
        grads_in,
        grad_attn,
        grad_attn_bias,
        marks[:first],
        marks[first:first + second],
        marks[first + second:],
        grad_out,
        packed[0],
        packed[1],
        packed[2],
        grad_up,
        grad_bias,
        grad_down,
        packed[3],
        packed[4],
        packed[5],
    )


def solution(mesh):
    return jax.shard_map(
        functools.partial(body, mesh.shape["dp"]),
        mesh=mesh,
        in_specs=(
            P("dp", None, None),
            P("dp", None),
            P("dp", None),
            P("dp", None, None),
            P("dp", None, None),
            P("dp", None, None),
            P(None, None, "head"),
            P(None, "head"),
            P(None, "head"),
            P(None, "head"),
            P(None, "head"),
            P("head", None),
            P(),
            P(),
            P(),
            P(None, "head"),
            P("head"),
            P("head", None),
            P(),
            P(),
            P(),
            P("dp", "head", None),
        ),
        out_specs=(
            P("dp", "head", None),
            P("dp", "head", None),
            P(None, None, "head"),
            P(None, "head"),
            P(None, "head"),
            P(None, "head"),
            P(None, "head"),
            P("head", None),
            P(),
            P(),
            P(),
            P(None, "head"),
            P("head"),
            P("head", None),
            P(),
            P(),
            P(),
        ),
        check_vma=False,
    )
```

```python
import functools
import math

import jax
import jax.numpy as jnp
from jax import lax
from jax.experimental import pallas as pl
from jax.experimental.pallas import tpu as pltpu
from jax.sharding import PartitionSpec as P

B = 128

PACK = 16


def gather_dims(axis):
    return lax.GatherDimensionNumbers(
        offset_dims=(), collapsed_slice_dims=(axis,), start_index_map=(axis,),
        operand_batching_dims=(1 - axis,), start_indices_batching_dims=(1 - axis,))


def pick(table, index, axis):
    return lax.gather(table, index[:, :, None], gather_dims(axis), (1, 1),
                      mode=lax.GatherScatterMode.PROMISE_IN_BOUNDS)


def two_heads(values, left):
    zero = jnp.zeros_like(values)
    return jnp.concatenate([jnp.where(left, values, zero), jnp.where(left, zero, values)], axis=0)


def doc_span(len_ref, row, first, last):
    edge = 0
    start = 0
    stop = 0
    for k in range(len_ref.shape[1]):
        begin = edge
        edge = edge + len_ref[row, k]
        start = jnp.where(begin <= first, begin, start)
        stop = jnp.where(begin <= last, edge, stop)
    return start // B, (stop + (B - 1)) // B

def fwd_kernel(row, len_ref, q_ref, k_ref, v_ref, pad_ref, bl_ref, bh_ref, bv_ref, line_ref, plane_ref,
               probs_ref, ctx_ref, sc, qs, best, mass, mixed):
    qb = pl.program_id(0)
    heads = sc.shape[1]
    pairs = heads // 2
    lane = lax.broadcasted_iota(jnp.int32, (B, B), 1)
    left = lane < (B // 2)
    first = qb * B
    low, high = doc_span(len_ref, row, first, first + B - 1)
    sub = lax.broadcasted_iota(jnp.int32, (B, B), 0) + first
    edges = []
    edge = 0
    for k in range(len_ref.shape[1]):
        edge = edge + len_ref[row, k]
        edges.append(edge)
    seg_q = sum(((sub >= e).astype(jnp.int32) for e in edges))
    for p in range(pairs):
        qs[p] = two_heads(q_ref[:, p * B:(p + 1) * B], left)

    def scores(t, carry):
        key_at = lane + t * B
        at = pl.ds(pl.multiple_of(t * B, B), B)
        seg_k = sum(((key_at >= e).astype(jnp.int32) for e in edges))
        real = jnp.broadcast_to(pad_ref[:, at], (B, B)) > 0
        allowed = ((seg_q == seg_k) & real) | (sub == key_at)
        parts = []
        for g in range(B // PACK):
            rows = slice(g * PACK, g * PACK + PACK)
            line = bl_ref[rows, at].astype(jnp.int16)
            parts.append((line & jnp.int16(PACK - 1), line >= jnp.int16(PACK),
                          bh_ref[rows, at].astype(jnp.int16), (bv_ref[rows, at] + 64).astype(jnp.int16)))
        for p in range(pairs):
            raw = lax.dot_general(qs[p], k_ref[at, p * B:(p + 1) * B], (((1,), (1,)), ((), ())),
                                  preferred_element_type=jnp.float32)
            for s in range(2):
                h = 2 * p + s
                plane = plane_ref[h]
                for g, (place, upper, horiz, vert) in enumerate(parts):
                    rows = slice(g * PACK, g * PACK + PACK)
                    found = jnp.where(upper, pick(line_ref[h, PACK:2 * PACK, :], place, 0),
                                      pick(line_ref[h, 0:PACK, :], place, 0))
                    rel = ((found.astype(jnp.float32) + pick(plane, horiz, 1).astype(jnp.float32))
                           + pick(plane, vert, 1).astype(jnp.float32))
                    val = jnp.where(allowed[rows], raw[s * B + g * PACK:s * B + (g + 1) * PACK, :] + rel,
                                    -1000000000.0)
                    sc[t, h, rows, :] = val
                    best[h, rows, :] = jnp.maximum(best[h, rows, :], val)
        return carry

    best[...] = jnp.full(best.shape, -3.0e38, jnp.float32)
    mass[...] = jnp.zeros_like(mass)
    mixed[...] = jnp.zeros_like(mixed)
    lax.fori_loop(low, high, scores, 0)
    for h in range(heads):
        best[h] = jnp.broadcast_to(jnp.max(best[h], axis=-1, keepdims=True), (B, B))

    def expo(t, carry):
        for h in range(heads):
            e = jnp.exp(sc[t, h] - best[h])
            sc[t, h] = e
            mass[h] += e
        return carry

    lax.fori_loop(low, high, expo, 0)
    for h in range(heads):
        mass[h] = jnp.broadcast_to(1.0 / jnp.sum(mass[h], axis=-1, keepdims=True), (B, B))

    def mix(t, carry):
        at = pl.ds(pl.multiple_of(t * B, B), B)
        for p in range(pairs):
            low_pair = []
            for s in range(2):
                h = 2 * p + s
                pr = sc[t, h] * mass[h]
                probs_ref[t, h] = pr
                low_pair.append(pr.astype(jnp.bfloat16))
            mixed[p] += jnp.dot(jnp.concatenate(low_pair, axis=0), v_ref[at, p * B:(p + 1) * B],
                                preferred_element_type=jnp.float32)
        return carry

    lax.fori_loop(low, high, mix, 0)
    for p in range(pairs):
        ctx_ref[:, p * B:(p + 1) * B] = jnp.where(left, mixed[p, :B, :], mixed[p, B:, :]).astype(jnp.bfloat16)


def attn_fwd(row, lengths, q, k, v, pad, bl, bh, bv, line, plane):
    slots, width = q.shape[1:]
    pairs = width // B
    tiles = slots // B
    row_block = lambda n: pl.BlockSpec((None, B, n), lambda i, L: (row, i, 0))
    return pl.pallas_call(
        functools.partial(fwd_kernel, row),
        grid_spec=pltpu.PrefetchScalarGridSpec(
            num_scalar_prefetch=1, grid=(tiles,),
            in_specs=[
                row_block(width),
                pl.BlockSpec((None, slots, width), lambda i, L: (row, 0, 0)),
                pl.BlockSpec((None, slots, width), lambda i, L: (row, 0, 0)),
                pl.BlockSpec((None, 1, slots), lambda i, L: (row, 0, 0)),
                row_block(slots), row_block(slots), row_block(slots),
                pl.BlockSpec(line.shape, lambda i, L: (0, 0, 0)),
                pl.BlockSpec(plane.shape, lambda i, L: (0, 0, 0)),
            ],
            out_specs=[
                pl.BlockSpec((None, tiles, 2 * pairs, B, B), lambda i, L: (i, 0, 0, 0, 0)),
                pl.BlockSpec((B, width), lambda i, L: (i, 0)),
            ],
            scratch_shapes=[
                pltpu.VMEM((tiles, 2 * pairs, B, B), jnp.float32),
                pltpu.VMEM((pairs, 2 * B, B), jnp.bfloat16),
                pltpu.VMEM((2 * pairs, B, B), jnp.float32),
                pltpu.VMEM((2 * pairs, B, B), jnp.float32),
                pltpu.VMEM((pairs, 2 * B, B), jnp.float32),
            ]),
        out_shape=[
            jax.ShapeDtypeStruct((tiles, tiles, 2 * pairs, B, B), jnp.float32),
            jax.ShapeDtypeStruct((slots, width), jnp.bfloat16),
        ],
        compiler_params=pltpu.CompilerParams(vmem_limit_bytes=48 << 20),
        cost_estimate=pl.CostEstimate(flops=1, transcendentals=0, bytes_accessed=1),
        name="attn_forward",
    )(lengths, q, k, v, pad, bl, bh, bv, line, plane)


NT = (((1,), (1,)), ((), ()))
TN = (((0,), (0,)), ((), ()))

def bwd_kernel(row, factor, len_ref, q_ref, k_ref, v_ref, gctx_ref, ctx_ref, probs_ref, *rest):
    pairs, tiles = q_ref.shape[1] // B, probs_ref.shape[0]
    ds_ref, three_ref, *scratch = rest[len(rest) - 6 * pairs - 2:]
    dks, dvs, dqs, inner, qs, gs = (scratch[n * pairs:(n + 1) * pairs] for n in range(6))
    qb = pl.program_id(0)
    lane = lax.broadcasted_iota(jnp.int32, (B, B), 1)
    left = lane < (B // 2)

    @pl.when(qb == 0)
    def _():
        for ref in dks + dvs:
            ref[...] = jnp.zeros_like(ref)

    first = qb * B
    low, high = doc_span(len_ref, row, first, first + B - 1)
    for p in range(pairs):
        cols = slice(p * B, (p + 1) * B)
        gctx = gctx_ref[:, cols]
        qs[p][...] = two_heads(q_ref[:, cols], left)
        gs[p][...] = two_heads(gctx, left)
        prod = gctx.astype(jnp.float32) * ctx_ref[:, cols].astype(jnp.float32)
        inner[p][...] = jnp.broadcast_to(jnp.sum(two_heads(prod, left), axis=-1, keepdims=True), (2 * B, B))
        dqs[p][...] = jnp.zeros_like(dqs[p])

    def tile(t, carry):
        at = pl.ds(pl.multiple_of(t * B, B), B)
        for p in range(pairs):
            cols = slice(p * B, (p + 1) * B)
            gp = lax.dot_general(gs[p][...], v_ref[at, cols], NT, preferred_element_type=jnp.float32)
            probs_low, g_scores = [], []
            for s in range(2):
                rows = slice(s * B, (s + 1) * B)
                pr = probs_ref[t, 2 * p + s]
                ds = (pr * (gp[rows, :] - inner[p][rows, :])).astype(jnp.bfloat16)
                ds_ref[t, 2 * p + s] = ds
                g_scores.append(ds)
                probs_low.append(pr.astype(jnp.bfloat16))
            ds = jnp.concatenate(g_scores, axis=0)
            mix = jnp.concatenate(probs_low, axis=0)
            dvs[p][t] += lax.dot_general(mix, gs[p][...], TN, preferred_element_type=jnp.float32)
            dks[p][t] += lax.dot_general(ds, qs[p][...], TN, preferred_element_type=jnp.float32)
            dqs[p][...] += jnp.dot(ds, k_ref[at, cols], preferred_element_type=jnp.float32)
        return carry

    lax.fori_loop(low, high, tile, 0)
    for p in range(pairs):
        dq = jnp.where(left, dqs[p][0:B, :], dqs[p][B:2 * B, :]) * factor
        three_ref[pl.ds(pl.multiple_of(first, B), B), p * B:(p + 1) * B] = dq.astype(jnp.bfloat16)

    @pl.when(qb == tiles - 1)
    def _():
        for p in range(pairs):
            for t in range(tiles):
                rows = slice(t * B, (t + 1) * B)
                three_ref[rows, (pairs + p) * B:(pairs + p + 1) * B] = dks[p][t].astype(jnp.bfloat16)
                three_ref[rows, (2 * pairs + p) * B:(2 * pairs + p + 1) * B] = dvs[p][t].astype(jnp.bfloat16)


def attn_bwd(row, factor, lengths, q, k, v, gctx, ctx, probs, kept=None):
    slots, width = q.shape[1:]
    pairs, tiles = width // B, slots // B
    part = pl.BlockSpec((B, width), lambda i, L: (i, 0))
    three = pl.BlockSpec((None, slots, 3 * width), lambda i, L: (row, 0, 0))
    mine = pl.BlockSpec((None, B, width), lambda i, L: (row, i, 0))
    whole = pl.BlockSpec((None, slots, width), lambda i, L: (row, 0, 0))
    pairs_of = pl.BlockSpec((None, tiles, 2 * pairs, B, B), lambda i, L: (i, 0, 0, 0, 0))
    kept = () if kept is None else (kept,)
    return pl.pallas_call(
        functools.partial(bwd_kernel, row, factor),
        grid_spec=pltpu.PrefetchScalarGridSpec(
            num_scalar_prefetch=1, grid=(tiles,),
            in_specs=[mine, whole, whole, part, part, pairs_of]
            + [pl.BlockSpec(memory_space=pl.ANY)] * len(kept),
            out_specs=[pairs_of, three],
            scratch_shapes=[pltpu.VMEM((tiles, B, B), jnp.float32)] * (2 * pairs)
            + [pltpu.VMEM((2 * B, B), jnp.float32)] * (2 * pairs)
            + [pltpu.VMEM((2 * B, B), jnp.bfloat16)] * (2 * pairs)),
        out_shape=[jax.ShapeDtypeStruct(probs.shape, jnp.bfloat16),
                   jax.ShapeDtypeStruct((q.shape[0], slots, 3 * width), jnp.bfloat16)],
        input_output_aliases={7: 1} if kept else {},
        compiler_params=pltpu.CompilerParams(vmem_limit_bytes=48 << 20),
        cost_estimate=pl.CostEstimate(flops=1, transcendentals=0, bytes_accessed=1),
        name="attn_backward",
    )(lengths, q, k, v, gctx, ctx, probs, *kept)

BINS = 160
SPREADS = 3


def hist_kernel(row, step, len_ref, bl_ref, bh_ref, bv_ref, ds_ref, out_ref, *spreads):
    tiles, heads = ds_ref.shape[0], ds_ref.shape[1]
    docs = len_ref.shape[1]
    lane = lax.broadcasted_iota(jnp.int32, (PACK, B), 1)
    sub = lax.broadcasted_iota(jnp.int32, (PACK, B), 0)
    for spread in spreads:
        spread[...] = jnp.zeros_like(spread)

    floor, roof = step * B, (step + 1) * B
    starts, ends, firsts, lasts, upto, steps = [], [], [], [], [], []
    edge, count = 0, 0
    for d in range(docs):
        starts.append(edge)
        edge = edge + len_ref[row, d]
        ends.append(edge)
        firsts.append(jnp.maximum(starts[d], floor))
        lasts.append(jnp.maximum(jnp.minimum(edge, roof), firsts[d]))
        steps.append(jnp.where(edge - starts[d] <= B, 2, 1))
        here = ((lasts[d] + (PACK - 1)) // PACK - firsts[d] // PACK + (steps[d] - 1)) // steps[d]
        count = count + jnp.where(lasts[d] > firsts[d], here, 0)
        upto.append(count)

    def group(g, spread):
        start, end, first, last, pace = starts[0], ends[0], firsts[0], lasts[0], steps[0]
        block = firsts[0] // PACK + g * steps[0]
        for d in range(1, docs):
            past = g >= upto[d - 1]
            start, end, first, last, pace, block = (
                jnp.where(past, new, old) for new, old in
                ((starts[d], start), (ends[d], end), (firsts[d], first), (lasts[d], last), (steps[d], pace),
                 (firsts[d] // PACK + (g - upto[d - 1]) * steps[d], block)))
        last = jnp.where(g < count, last, first)
        start = jnp.minimum(start, tiles * B - 1)
        tile = start // B
        left = start - tile * B
        turn = jnp.where(left == 0, 0, B - left)
        halves = []
        for part in range(2):
            along, later = part * (pace - 1), part * (2 - pace)
            mine = block + along
            token = sub + mine * PACK
            live = (token >= first) & (token < last) & (lane + later * B < end - start)
            at = jnp.clip(mine - step * (B // PACK), 0, B // PACK - 1)
            halves.append((live, pl.ds(pl.multiple_of(at * PACK, PACK), PACK),
                           [jnp.minimum(tile + later + n, tiles - 1) for n in range(2)]))
        before = lane < B - left

        def moved(here, there):
            return jnp.where(before, pltpu.roll(here, turn, 1), pltpu.roll(there, turn, 1))

        codes = []
        for part, (live, rows, spots) in enumerate(halves):
            for h in range(heads):
                vals = moved(*(ds_ref[s, h, rows, :].astype(jnp.float32) for s in spots))
                spread[part, pl.ds(h, PACK, stride=8), :] = jnp.where(live, vals, 0.0)
            at = [pl.ds(pl.multiple_of(s * B, B), B) for s in spots]
            codes.append(moved(*(bl_ref[rows, x] + 32 * bh_ref[rows, x] + 2048 * bv_ref[rows, x]
                                 for x in at)))
        code = jnp.concatenate(codes, axis=1)
        index = [(code & 31).astype(jnp.int16), ((code >> 5) & 63).astype(jnp.int16),
                 (code >> 11).astype(jnp.int16)]
        one, zero = jnp.ones((), jnp.bfloat16), jnp.zeros((), jnp.bfloat16)
        grads, hots = [], []
        for r in range(PACK):
            hot = []
            for ix, n in zip(index, (32, 64, 64)):
                bins = lax.broadcasted_iota(jnp.int16, (n, 2 * B), 0)
                line = jnp.broadcast_to(ix[r:r + 1, :], (n, 2 * B))
                hot.append(jnp.where(bins == line, one, zero))
            hots.append(jnp.concatenate(hot, axis=0))
            grads += [spread[part, r * 8:r * 8 + 8, :].astype(jnp.bfloat16) for part in range(2)]
        return lax.dot_general(jnp.concatenate(grads, axis=1), jnp.concatenate(hots, axis=1), NT,
                               preferred_element_type=jnp.float32)

    def several(turn, sums):
        return tuple(x + group(len(spreads) * turn + n, spread)
                     for n, (x, spread) in enumerate(zip(sums, spreads)))

    none = jnp.zeros((8, BINS), jnp.float32)
    turns = (count + (len(spreads) - 1)) // len(spreads)
    out_ref[...] = sum(lax.fori_loop(0, turns, several, tuple(none for _ in spreads)))


def table_grads(row, step, lengths, bl, bh, bv, ds):
    slots = bl.shape[1]
    tiles, heads = ds.shape[0], ds.shape[2]
    block = pl.BlockSpec((None, B, slots), lambda i, L: (row, step, 0))
    return pl.pallas_call(
        functools.partial(hist_kernel, row, step),
        grid_spec=pltpu.PrefetchScalarGridSpec(
            num_scalar_prefetch=1, grid=(1,),
            in_specs=[block, block, block,
                      pl.BlockSpec((None, tiles, heads, B, B), lambda i, L: (step, 0, 0, 0, 0))],
            out_specs=pl.BlockSpec((8, BINS), lambda i, L: (0, 0)),
            scratch_shapes=[pltpu.VMEM((2, 8 * PACK, B), jnp.float32)] * SPREADS),
        out_shape=jax.ShapeDtypeStruct((8, BINS), jnp.float32),
        compiler_params=pltpu.CompilerParams(vmem_limit_bytes=48 << 20),
        cost_estimate=pl.CostEstimate(flops=1, transcendentals=0, bytes_accessed=1),
        name="table_grads",
    )(lengths, bl, bh, bv, ds)


f32, low = jnp.float32, jnp.bfloat16
SWAP = [(0, 1), (1, 0)]
ORDER = "UATDTADTGUATDTUADTTUADTPSUASDUSASSU"


def normalize(values):
    mean = jnp.mean(values, axis=-1, keepdims=True)
    centered = values - mean
    scale = lax.rsqrt(jnp.mean(centered * centered, axis=-1, keepdims=True) + 1e-12)
    return centered * scale, scale


def normalize_back(grad, normed, scale, gain):
    scaled = grad * gain
    first = jnp.mean(scaled, axis=-1, keepdims=True)
    second = jnp.mean(scaled * normed, axis=-1, keepdims=True)
    return scale * (scaled - first - normed * second)


def times(left, right, left_dim, right_dim):
    return lax.dot_general(left, right, (((left_dim,), (right_dim,)), ((), ())),
                           preferred_element_type=f32)


def flips(count, bit):
    return [(i, i ^ (1 << bit)) for i in range(count)]


def to_peer(values):
    return lax.ppermute(values, "head", SWAP)


def plus(left, right):
    return (left.astype(f32) + right.astype(f32)).astype(low)


def arranged(bit_value, mine, other):
    return jnp.where(bit_value == 0, mine, other), jnp.where(bit_value == 0, other, mine)


def in_order(bit_value, mine, other):
    return jnp.stack(arranged(bit_value, mine, other))


def nothing(*refs):
    pass


def after(values, earlier):
    anywhere = pl.BlockSpec(memory_space=pl.ANY)
    return pl.pallas_call(
        nothing, in_specs=[anywhere, anywhere], out_specs=anywhere,
        out_shape=jax.ShapeDtypeStruct(values.shape, values.dtype), input_output_aliases={0: 0},
        cost_estimate=pl.CostEstimate(flops=1, transcendentals=0, bytes_accessed=1), name="after")(values, earlier)


class Order:
    def __init__(self):
        self.last = None

    def tie(self, values):
        if self.last is None:
            return values
        values, self.last = lax.optimization_barrier((values, self.last))
        return values

    def mark(self, values):
        self.last = values


def total(terms, lift, size, axis):
    return sum(lax.dynamic_slice_in_dim(values, start + lift, size, axis).astype(f32)
               for values, start in terms)


def halve(order, terms, size, axis, count, bit):
    half = size // 2
    mine = (lax.axis_index("dp") >> bit) & 1
    send = total(terms, (1 - mine) * half, half, axis).astype(low)
    order.mark(send)
    got = lax.ppermute(send, "dp", flips(count, bit))
    yield
    return [(values, start + mine * half) for values, start in terms] + [(order.tie(got), 0)]


def gather_steps(order, values, count, bits):
    index = lax.axis_index("dp")
    for bit in reversed(bits):
        order.mark(values)
        got = lax.ppermute(values, "dp", flips(count, bit))
        yield
        both = in_order((index >> bit) & 1, values, order.tie(got))
        values = both.reshape((2 * values.shape[0],) + values.shape[1:])
    return values


def unit_steps(order, kept, given, count, axis, split, out):
    bits = list(range(1, count.bit_length() - 1))
    size = kept.shape[axis]
    given = order.tie(given)
    order.mark(given)
    got = lax.ppermute(given, "dp", flips(count, 0))
    yield
    terms = [(kept, 0), (order.tie(got), 0)]
    terms = yield from halve(order, terms, size, axis, count, bits[0])
    size //= 2
    mine, other = ([(split(values)[c], start) for values, start in terms] for c in range(2))
    send = total(other, 0, size, 0).astype(low)
    order.mark(send)
    got = to_peer(send)
    yield
    terms = mine + [(order.tie(got), 0)]
    for bit in bits[1:]:
        terms = yield from halve(order, terms, size, 0, count, bit)
        size //= 2
    mine = yield from gather_steps(order, total(terms, 0, size, 0).astype(low), count, bits)
    order.mark(mine)
    other = lax.ppermute(mine, "dp", flips(count, 0))
    yield
    out += [mine, order.tie(other)]


def buffer_steps(order, values, count, out):
    bits = list(range(count.bit_length() - 1))
    size = values.shape[0]
    terms = [(order.tie(values), 0)]
    for bit in bits:
        terms = yield from halve(order, terms, size, 0, count, bit)
        size //= 2
    values = yield from gather_steps(order, total(terms, 0, size, 0).astype(low), count, bits)
    order.mark(values)
    out.append(values)


def small_steps(order, values, count, out):
    values = order.tie(values)
    for bit in [None, 0] + list(range(2, count.bit_length() - 1)) + [1]:
        order.mark(values)
        got = to_peer(values) if bit is None else lax.ppermute(values, "dp", flips(count, bit))
        yield
        values = values + order.tie(got)
    order.mark(values)
    out.append(values)


def advance(*chains):
    for chain in chains:
        next(chain, None)


def finish(*chains):
    left = list(chains)
    while left:
        for chain in list(left):
            try:
                next(chain)
            except StopIteration:
                left.remove(chain)


def body(
    count,
    hidden,
    lengths,
    padding,
    bucket_line,
    bucket_horizontal,
    bucket_vertical,
    attn_project,
    attn_bias,
    table_line,
    table_horizontal,
    table_vertical,
    out_project,
    out_bias,
    attn_gain,
    attn_shift,
    hidden_project,
    hidden_bias,
    down_project,
    down_bias,
    final_gain,
    final_shift,
    cotangent,
):
    rows, slots, width = hidden.shape
    half = cotangent.shape[1]
    heads = table_line.shape[1]
    local = attn_project.shape[2]
    units = hidden_project.shape[1]
    part = units // 2
    factor = 1.0 / math.sqrt(local // heads)
    head = lax.axis_index("head")
    index = lax.axis_index("dp")
    core = index & 1
    offset = head * half
    every = list(range(count.bit_length() - 1))

    def split(values, dim):
        return [lax.dynamic_slice_in_dim(values, c * part, part, dim) for c in (core, 1 - core)]

    def joined(own_parts, got, dim):
        mine, rest = own_parts
        beside = lax.ppermute(got, "dp", flips(count, 0))
        return [jnp.concatenate([mine, got], axis=dim), jnp.concatenate([rest, beside], axis=dim)]

    side = (index >> 1) & 1
    down_mine = lax.dynamic_slice_in_dim(down_project, core * part + side * (part // 2), part // 2, 0)
    down_got = to_peer(down_mine)
    down_mine, hidden_project = lax.optimization_barrier((down_mine, hidden_project))
    up_mine = lax.dynamic_slice_in_dim(hidden_project, core * part, part, 1)
    up_got = to_peer(up_mine)
    up_mine, hidden, hidden_project, down_project = lax.optimization_barrier(
        (up_mine, hidden, hidden_project, down_project))
    bias_got = to_peer(hidden_bias)

    planes = jnp.concatenate([table_horizontal, table_vertical], axis=0)
    bins = table_line.shape[0] + planes.shape[0]
    lines = jnp.broadcast_to(table_line.T[:, :, None], (heads, table_line.shape[0], B))
    planes = jnp.broadcast_to(planes.T[:, None, :], (heads, PACK, planes.shape[0]))
    pad = padding[:, None, :]
    bucket_line, bucket_horizontal, bucket_vertical = (
        pltpu.with_memory_space_constraint(x, pltpu.HBM)
        for x in (bucket_line, bucket_horizontal, bucket_vertical))

    flat = hidden.reshape(rows * slots, width)
    query = ((times(flat, attn_project[0], 1, 0) + attn_bias[0].astype(f32)).astype(low)
             * jnp.asarray(factor, low))
    key = times(flat, attn_project[1], 1, 0).astype(low)
    value = (times(flat, attn_project[2], 1, 0) + attn_bias[1].astype(f32)).astype(low)
    query, key, value = (pltpu.with_memory_space_constraint(x.reshape(rows, slots, local), pltpu.HBM)
                         for x in (query, key, value))

    def own(values):
        return lax.dynamic_slice_in_dim(values, offset, half, 0)

    def others(values):
        return lax.dynamic_slice_in_dim(values, half - offset, half, 0)

    fronts, attn_sum, attn_got = [], [], []
    for r in range(rows):
        if r == 1:
            lengths, down_got = lax.optimization_barrier((lengths, down_got))
            down_beside = lax.ppermute(down_got, "dp", flips(count, 1))
        probs, context = attn_fwd(r, lengths, query, key, value, pad, bucket_line,
                                  bucket_horizontal, bucket_vertical, lines, planes)
        if r == 1:
            context, down_beside = lax.optimization_barrier((context, down_beside))
        fronts.append((probs, context))
        send = times(others(context), out_project, 1, 0).astype(low)
        got = to_peer(send)
        attn_sum.append(times(own(context), out_project, 1, 0))
        attn_got.append(got)
    (send, hidden_project, down_project, cotangent, norm_rows, out_bias, down_bias, hidden_bias, bias_got,
     hidden) = lax.optimization_barrier(
        (send, hidden_project, down_project, cotangent, (attn_gain, attn_shift, final_gain, final_shift),
         out_bias, down_bias, hidden_bias, bias_got, hidden))
    biases = [jnp.concatenate([x, y]) for x, y in zip(split(hidden_bias, 0), split(bias_got, 0))]
    gain_first, shift_first, gain_last, shift_last = (x.astype(f32) for x in norm_rows)
    up_parts = [up_mine, lax.dynamic_slice_in_dim(hidden_project, (1 - core) * part, part, 1)]
    down_parts = split(down_project, 0)
    up_got, down_beside, attn_got = lax.optimization_barrier((up_got, down_beside, attn_got))
    down_got = in_order(side, down_got, down_beside)
    ups = joined(up_parts, up_got, 1)
    downs = joined(down_parts, down_got.reshape(part, width), 0)
    attn_sum = [x + got.astype(f32) for x, got in zip(attn_sum, attn_got)]
    tokens = lax.dynamic_slice_in_dim(hidden, offset, half, 1).reshape(rows * half, width).astype(f32)
    normed, scale = normalize(tokens + jnp.concatenate(attn_sum, axis=0) + out_bias.astype(f32))
    mid = normed * gain_first + shift_first
    mid_low = mid.astype(low)

    actives, slopes = [], []
    total = None
    for up, down, bias in zip(ups, downs, biases):
        inner = times(mid_low, up, 1, 0) + bias.astype(f32)
        bell = 0.5 * (1.0 + lax.erf(inner * math.sqrt(0.5)))
        actives.append((inner * bell).astype(low))
        slope = bell + inner * (jnp.exp(-0.5 * inner * inner) * (1.0 / math.sqrt(2.0 * math.pi)))
        slopes.append(slope.astype(low))
        term = times(actives[-1], down, 1, 0)
        total = term if total is None else total + term
    normed_final, scale_final = normalize(mid + total + down_bias.astype(f32))
    output = (normed_final * gain_last + shift_last).astype(low).reshape(rows, half, width)

    above = cotangent.reshape(rows * half, width).astype(f32)
    g_final = normalize_back(above, normed_final, scale_final, gain_last)
    g_low = g_final.astype(low)
    order = Order()
    total = None
    inners = []
    for up, down, slope in zip(ups, downs, slopes):
        g_inner = (times(g_low, down, 1, 1) * slope.astype(f32)).astype(low)
        inners.append(g_inner)
        term = times(g_inner, up, 1, 1)
        total = term if total is None else total + term
    g_mid = g_final + total
    g_attn = normalize_back(g_mid, normed, scale, gain_first)
    g_attn_low = g_attn.astype(low).reshape(rows, half, width)
    g_others = [to_peer(g_attn_low[r]) for r in range(rows)]
    order.mark(g_attn_low)
    down_out, up_out, attn_out = [], [], []
    g_low = order.tie(g_low)
    kept, given = (times(active, g_low, 0, 0).astype(low) for active in actives)
    down_chain = unit_steps(order, *(x.reshape(2, part, width) for x in (kept, given)), count, 1,
                            lambda v: (v[0], v[1]), down_out)
    advance(down_chain)
    mid_low = order.tie(mid_low)
    kept, given = (times(mid_low, g_inner, 0, 0).astype(low) for g_inner in inners)
    up_chain = unit_steps(order, kept, given, count, 0, lambda v: (v[:, :part], v[:, part:]), up_out)
    advance(up_chain, down_chain)
    g_attn = g_attn.reshape(rows, half, width)

    marks, three, grad_out = [], None, 0.0
    for r in range(rows):
        probs, context = fronts[r]
        g_all = in_order(head, g_attn_low[r], order.tie(g_others[r])).reshape(slots, width)
        g_context = times(g_all, out_project, 1, 1).astype(low)
        g_scores, three = attn_bwd(r, factor, lengths, query, key, value, g_context, context, probs, three)
        order.mark(g_scores)
        marks.append(g_scores)
        grad_out = grad_out + times(context, g_all, 0, 0)
        advance(up_chain if r == 0 else down_chain)
    grad_attn = times(flat, three.reshape(rows * slots, 3 * local), 0, 0).astype(low)
    grad_out = jnp.concatenate([grad_out[:, :local], grad_out[:, local:]], axis=0).astype(low)
    attn_chain = buffer_steps(order, jnp.concatenate([grad_attn, grad_out], axis=1), count, attn_out)
    advance(attn_chain)
    every_project = jnp.concatenate([attn_project[c] for c in range(3)], axis=1)
    room = width // 2

    def pack():
        sums = [jnp.sum(x.reshape(rows * half, width), axis=0, keepdims=True) for x in
                (g_attn, g_mid * normed, g_mid, g_final, above * normed_final, above)]
        sums, units_in, three_sums, tables = order.tie(
            (sums, inners, jnp.sum(three.astype(f32).reshape(rows * slots, 3 * local), axis=0,
                                       keepdims=True), sum(tables_out)))
        unit_sums = [jnp.sum(x.astype(f32), axis=0, keepdims=True) for x in units_in]
        ours, others_ = (jnp.concatenate(arranged(core, *(x[:, c * part:(c + 1) * part] for x in unit_sums)),
                                         axis=0) for c in range(2))
        pair = jnp.concatenate([three_sums[:, :local], three_sums[:, 2 * local:]], axis=1)
        tables = jnp.pad(tables, ((0, 0), (0, room - bins)))
        return jnp.concatenate(
            sums + list(arranged(head, ours, others_))
            + [jnp.where(head == slot, pair, 0.0) for slot in range(2)]
            + [jnp.zeros((4, width), f32),
               jnp.concatenate([jnp.where(head == slot, tables, 0.0) for slot in range(2)], axis=1)], axis=0)

    tables_out, small_out = [], []
    blocks = [(r, block) for r in range(rows) for block in range(slots // B)]
    chains = {"D": down_chain, "U": up_chain, "A": attn_chain}
    for name in ORDER:
        if name == "T":
            r, block = blocks[len(tables_out)]
            tables_out.append(table_grads(r, block, order.tie(lengths), bucket_line,
                                          bucket_horizontal, bucket_vertical, marks[r]))
            order.mark(tables_out[-1])
        elif name == "G":
            three = order.tie(three)
            theirs = lax.dynamic_slice_in_dim(three, half - offset, half, 1)
            give = times(theirs.reshape(rows * half, 3 * local), every_project, 1, 1).astype(low)
            order.mark(give)
            received = to_peer(give)
            mine = lax.dynamic_slice_in_dim(three, offset, half, 1)
            mine = times(mine.reshape(rows * half, 3 * local), every_project, 1, 1)
        elif name == "P":
            chains["S"] = small_steps(order, pack(), count, small_out)
        else:
            advance(chains[name])
    finish(*chains.values())
    packed = after(small_out[0], up_out[0])
    grads_in = (mine + received.astype(f32)).reshape(rows, half, width) + g_attn
    grad_down = in_order(core, *down_out).reshape(down_project.shape).astype(f32)
    mine, other = up_out
    grad_up = jnp.concatenate(arranged(core, mine, other), axis=1).astype(f32)
    buffer = attn_out[0].astype(f32)
    grad_attn = jnp.stack([buffer[:, c * local:(c + 1) * local] for c in range(3)])
    grad_out = jnp.concatenate([buffer[:local, 3 * local:], buffer[local:, 3 * local:]], axis=1)

    rows_of = lambda at, size: lax.dynamic_slice_in_dim(packed, at, size, 0)
    grad_bias = rows_of(6 + 2 * head, 2).reshape(-1)
    grad_attn_bias = rows_of(10 + head, 1).reshape(2, local)
    marks = jnp.where(head == 0, packed[16:, :bins], packed[16:, room:room + bins])[:heads].T
    first, second = table_line.shape[0], table_horizontal.shape[0]
    return (
        output,
        grads_in,
        grad_attn,
        grad_attn_bias,
        marks[:first],
        marks[first:first + second],
        marks[first + second:],
        grad_out,
        packed[0],
        packed[1],
        packed[2],
        grad_up,
        grad_bias,
        grad_down,
        packed[3],
        packed[4],
        packed[5],
    )


def solution(mesh):
    return jax.shard_map(
        functools.partial(body, mesh.shape["dp"]),
        mesh=mesh,
        in_specs=(
            P("dp", None, None),
            P("dp", None),
            P("dp", None),
            P("dp", None, None),
            P("dp", None, None),
            P("dp", None, None),
            P(None, None, "head"),
            P(None, "head"),
            P(None, "head"),
            P(None, "head"),
            P(None, "head"),
            P("head", None),
            P(),
            P(),
            P(),
            P(None, "head"),
            P("head"),
            P("head", None),
            P(),
            P(),
            P(),
            P("dp", "head", None),
        ),
        out_specs=(
            P("dp", "head", None),
            P("dp", "head", None),
            P(None, None, "head"),
            P(None, "head"),
            P(None, "head"),
            P(None, "head"),
            P(None, "head"),
            P("head", None),
            P(),
            P(),
            P(),
            P(None, "head"),
            P("head"),
            P("head", None),
            P(),
            P(),
            P(),
        ),
        check_vma=False,
    )
```

```python
import functools
import math

import jax
import jax.numpy as jnp
from jax import lax
from jax.experimental import pallas as pl
from jax.experimental.pallas import tpu as pltpu
from jax.sharding import PartitionSpec as P

B = 128

PACK = 16


def gather_dims(axis):
    return lax.GatherDimensionNumbers(
        offset_dims=(), collapsed_slice_dims=(axis,), start_index_map=(axis,),
        operand_batching_dims=(1 - axis,), start_indices_batching_dims=(1 - axis,))


def pick(table, index, axis):
    return lax.gather(table, index[:, :, None], gather_dims(axis), (1, 1),
                      mode=lax.GatherScatterMode.PROMISE_IN_BOUNDS)


def two_heads(values, left):
    zero = jnp.zeros_like(values)
    return jnp.concatenate([jnp.where(left, values, zero), jnp.where(left, zero, values)], axis=0)


def doc_span(len_ref, row, first, last):
    edge = 0
    start = 0
    stop = 0
    for k in range(len_ref.shape[1]):
        begin = edge
        edge = edge + len_ref[row, k]
        start = jnp.where(begin <= first, begin, start)
        stop = jnp.where(begin <= last, edge, stop)
    return start // B, (stop + (B - 1)) // B

def fwd_kernel(row, len_ref, q_ref, k_ref, v_ref, pad_ref, bl_ref, bh_ref, bv_ref, line_ref, plane_ref,
               probs_ref, ctx_ref, sc, qs, best, mass, mixed):
    qb = pl.program_id(0)
    heads = sc.shape[1]
    pairs = heads // 2
    lane = lax.broadcasted_iota(jnp.int32, (B, B), 1)
    left = lane < (B // 2)
    first = qb * B
    low, high = doc_span(len_ref, row, first, first + B - 1)
    sub = lax.broadcasted_iota(jnp.int32, (B, B), 0) + first
    edges = []
    edge = 0
    for k in range(len_ref.shape[1]):
        edge = edge + len_ref[row, k]
        edges.append(edge)
    seg_q = sum(((sub >= e).astype(jnp.int32) for e in edges))
    for p in range(pairs):
        qs[p] = two_heads(q_ref[:, p * B:(p + 1) * B], left)

    def scores(t, carry):
        key_at = lane + t * B
        at = pl.ds(pl.multiple_of(t * B, B), B)
        seg_k = sum(((key_at >= e).astype(jnp.int32) for e in edges))
        real = jnp.broadcast_to(pad_ref[:, at], (B, B)) > 0
        allowed = ((seg_q == seg_k) & real) | (sub == key_at)
        parts = []
        for g in range(B // PACK):
            rows = slice(g * PACK, g * PACK + PACK)
            line = bl_ref[rows, at].astype(jnp.int16)
            parts.append((line & jnp.int16(PACK - 1), line >= jnp.int16(PACK),
                          bh_ref[rows, at].astype(jnp.int16), (bv_ref[rows, at] + 64).astype(jnp.int16)))
        for p in range(pairs):
            raw = lax.dot_general(qs[p], k_ref[at, p * B:(p + 1) * B], (((1,), (1,)), ((), ())),
                                  preferred_element_type=jnp.float32)
            for s in range(2):
                h = 2 * p + s
                plane = plane_ref[h]
                for g, (place, upper, horiz, vert) in enumerate(parts):
                    rows = slice(g * PACK, g * PACK + PACK)
                    found = jnp.where(upper, pick(line_ref[h, PACK:2 * PACK, :], place, 0),
                                      pick(line_ref[h, 0:PACK, :], place, 0))
                    rel = ((found.astype(jnp.float32) + pick(plane, horiz, 1).astype(jnp.float32))
                           + pick(plane, vert, 1).astype(jnp.float32))
                    val = jnp.where(allowed[rows], raw[s * B + g * PACK:s * B + (g + 1) * PACK, :] + rel,
                                    -1000000000.0)
                    sc[t, h, rows, :] = val
                    best[h, rows, :] = jnp.maximum(best[h, rows, :], val)
        return carry

    best[...] = jnp.full(best.shape, -3.0e38, jnp.float32)
    mass[...] = jnp.zeros_like(mass)
    mixed[...] = jnp.zeros_like(mixed)
    lax.fori_loop(low, high, scores, 0)
    for h in range(heads):
        best[h] = jnp.broadcast_to(jnp.max(best[h], axis=-1, keepdims=True), (B, B))

    def expo(t, carry):
        for h in range(heads):
            e = jnp.exp(sc[t, h] - best[h])
            sc[t, h] = e
            mass[h] += e
        return carry

    lax.fori_loop(low, high, expo, 0)
    for h in range(heads):
        mass[h] = jnp.broadcast_to(1.0 / jnp.sum(mass[h], axis=-1, keepdims=True), (B, B))

    def mix(t, carry):
        at = pl.ds(pl.multiple_of(t * B, B), B)
        for p in range(pairs):
            low_pair = []
            for s in range(2):
                h = 2 * p + s
                pr = sc[t, h] * mass[h]
                probs_ref[t, h] = pr
                low_pair.append(pr.astype(jnp.bfloat16))
            mixed[p] += jnp.dot(jnp.concatenate(low_pair, axis=0), v_ref[at, p * B:(p + 1) * B],
                                preferred_element_type=jnp.float32)
        return carry

    lax.fori_loop(low, high, mix, 0)
    for p in range(pairs):
        ctx_ref[:, p * B:(p + 1) * B] = jnp.where(left, mixed[p, :B, :], mixed[p, B:, :]).astype(jnp.bfloat16)


def attn_fwd(row, lengths, q, k, v, pad, bl, bh, bv, line, plane):
    slots, width = q.shape[1:]
    pairs = width // B
    tiles = slots // B
    row_block = lambda n: pl.BlockSpec((None, B, n), lambda i, L: (row, i, 0))
    return pl.pallas_call(
        functools.partial(fwd_kernel, row),
        grid_spec=pltpu.PrefetchScalarGridSpec(
            num_scalar_prefetch=1, grid=(tiles,),
            in_specs=[
                row_block(width),
                pl.BlockSpec((None, slots, width), lambda i, L: (row, 0, 0)),
                pl.BlockSpec((None, slots, width), lambda i, L: (row, 0, 0)),
                pl.BlockSpec((None, 1, slots), lambda i, L: (row, 0, 0)),
                row_block(slots), row_block(slots), row_block(slots),
                pl.BlockSpec(line.shape, lambda i, L: (0, 0, 0)),
                pl.BlockSpec(plane.shape, lambda i, L: (0, 0, 0)),
            ],
            out_specs=[
                pl.BlockSpec((None, tiles, 2 * pairs, B, B), lambda i, L: (i, 0, 0, 0, 0)),
                pl.BlockSpec((B, width), lambda i, L: (i, 0)),
            ],
            scratch_shapes=[
                pltpu.VMEM((tiles, 2 * pairs, B, B), jnp.float32),
                pltpu.VMEM((pairs, 2 * B, B), jnp.bfloat16),
                pltpu.VMEM((2 * pairs, B, B), jnp.float32),
                pltpu.VMEM((2 * pairs, B, B), jnp.float32),
                pltpu.VMEM((pairs, 2 * B, B), jnp.float32),
            ]),
        out_shape=[
            jax.ShapeDtypeStruct((tiles, tiles, 2 * pairs, B, B), jnp.float32),
            jax.ShapeDtypeStruct((slots, width), jnp.bfloat16),
        ],
        compiler_params=pltpu.CompilerParams(vmem_limit_bytes=48 << 20),
        cost_estimate=pl.CostEstimate(flops=1, transcendentals=0, bytes_accessed=1),
        name="attn_forward",
    )(lengths, q, k, v, pad, bl, bh, bv, line, plane)


NT = (((1,), (1,)), ((), ()))
TN = (((0,), (0,)), ((), ()))

def bwd_kernel(row, factor, len_ref, q_ref, k_ref, v_ref, gctx_ref, ctx_ref, probs_ref, *rest):
    pairs, tiles = q_ref.shape[1] // B, probs_ref.shape[0]
    ds_ref, three_ref, *scratch = rest[len(rest) - 6 * pairs - 2:]
    dks, dvs, dqs, inner, qs, gs = (scratch[n * pairs:(n + 1) * pairs] for n in range(6))
    qb = pl.program_id(0)
    lane = lax.broadcasted_iota(jnp.int32, (B, B), 1)
    left = lane < (B // 2)

    @pl.when(qb == 0)
    def _():
        for ref in dks + dvs:
            ref[...] = jnp.zeros_like(ref)

    first = qb * B
    low, high = doc_span(len_ref, row, first, first + B - 1)
    for p in range(pairs):
        cols = slice(p * B, (p + 1) * B)
        gctx = gctx_ref[:, cols]
        qs[p][...] = two_heads(q_ref[:, cols], left)
        gs[p][...] = two_heads(gctx, left)
        prod = gctx.astype(jnp.float32) * ctx_ref[:, cols].astype(jnp.float32)
        inner[p][...] = jnp.broadcast_to(jnp.sum(two_heads(prod, left), axis=-1, keepdims=True), (2 * B, B))
        dqs[p][...] = jnp.zeros_like(dqs[p])

    def tile(t, carry):
        at = pl.ds(pl.multiple_of(t * B, B), B)
        for p in range(pairs):
            cols = slice(p * B, (p + 1) * B)
            gp = lax.dot_general(gs[p][...], v_ref[at, cols], NT, preferred_element_type=jnp.float32)
            probs_low, g_scores = [], []
            for s in range(2):
                rows = slice(s * B, (s + 1) * B)
                pr = probs_ref[t, 2 * p + s]
                ds = (pr * (gp[rows, :] - inner[p][rows, :])).astype(jnp.bfloat16)
                ds_ref[t, 2 * p + s] = ds
                g_scores.append(ds)
                probs_low.append(pr.astype(jnp.bfloat16))
            ds = jnp.concatenate(g_scores, axis=0)
            mix = jnp.concatenate(probs_low, axis=0)
            dvs[p][t] += lax.dot_general(mix, gs[p][...], TN, preferred_element_type=jnp.float32)
            dks[p][t] += lax.dot_general(ds, qs[p][...], TN, preferred_element_type=jnp.float32)
            dqs[p][...] += jnp.dot(ds, k_ref[at, cols], preferred_element_type=jnp.float32)
        return carry

    lax.fori_loop(low, high, tile, 0)
    for p in range(pairs):
        dq = jnp.where(left, dqs[p][0:B, :], dqs[p][B:2 * B, :]) * factor
        three_ref[pl.ds(pl.multiple_of(first, B), B), p * B:(p + 1) * B] = dq.astype(jnp.bfloat16)

    @pl.when(qb == tiles - 1)
    def _():
        for p in range(pairs):
            for t in range(tiles):
                rows = slice(t * B, (t + 1) * B)
                three_ref[rows, (pairs + p) * B:(pairs + p + 1) * B] = dks[p][t].astype(jnp.bfloat16)
                three_ref[rows, (2 * pairs + p) * B:(2 * pairs + p + 1) * B] = dvs[p][t].astype(jnp.bfloat16)


def attn_bwd(row, factor, lengths, q, k, v, gctx, ctx, probs, kept=None):
    slots, width = q.shape[1:]
    pairs, tiles = width // B, slots // B
    part = pl.BlockSpec((B, width), lambda i, L: (i, 0))
    three = pl.BlockSpec((None, slots, 3 * width), lambda i, L: (row, 0, 0))
    mine = pl.BlockSpec((None, B, width), lambda i, L: (row, i, 0))
    whole = pl.BlockSpec((None, slots, width), lambda i, L: (row, 0, 0))
    pairs_of = pl.BlockSpec((None, tiles, 2 * pairs, B, B), lambda i, L: (i, 0, 0, 0, 0))
    kept = () if kept is None else (kept,)
    return pl.pallas_call(
        functools.partial(bwd_kernel, row, factor),
        grid_spec=pltpu.PrefetchScalarGridSpec(
            num_scalar_prefetch=1, grid=(tiles,),
            in_specs=[mine, whole, whole, part, part, pairs_of]
            + [pl.BlockSpec(memory_space=pl.ANY)] * len(kept),
            out_specs=[pairs_of, three],
            scratch_shapes=[pltpu.VMEM((tiles, B, B), jnp.float32)] * (2 * pairs)
            + [pltpu.VMEM((2 * B, B), jnp.float32)] * (2 * pairs)
            + [pltpu.VMEM((2 * B, B), jnp.bfloat16)] * (2 * pairs)),
        out_shape=[jax.ShapeDtypeStruct(probs.shape, jnp.bfloat16),
                   jax.ShapeDtypeStruct((q.shape[0], slots, 3 * width), jnp.bfloat16)],
        input_output_aliases={7: 1} if kept else {},
        compiler_params=pltpu.CompilerParams(vmem_limit_bytes=48 << 20),
        cost_estimate=pl.CostEstimate(flops=1, transcendentals=0, bytes_accessed=1),
        name="attn_backward",
    )(lengths, q, k, v, gctx, ctx, probs, *kept)

BINS = 160
SPREADS = 3


def hist_kernel(row, step, len_ref, bl_ref, bh_ref, bv_ref, ds_ref, out_ref, *spreads):
    tiles, heads = ds_ref.shape[0], ds_ref.shape[1]
    docs = len_ref.shape[1]
    lane = lax.broadcasted_iota(jnp.int32, (PACK, B), 1)
    sub = lax.broadcasted_iota(jnp.int32, (PACK, B), 0)
    for spread in spreads:
        spread[...] = jnp.zeros_like(spread)

    floor, roof = step * B, (step + 1) * B
    starts, ends, firsts, lasts, upto, steps = [], [], [], [], [], []
    edge, count = 0, 0
    for d in range(docs):
        starts.append(edge)
        edge = edge + len_ref[row, d]
        ends.append(edge)
        firsts.append(jnp.maximum(starts[d], floor))
        lasts.append(jnp.maximum(jnp.minimum(edge, roof), firsts[d]))
        steps.append(jnp.where(edge - starts[d] <= B, 2, 1))
        here = ((lasts[d] + (PACK - 1)) // PACK - firsts[d] // PACK + (steps[d] - 1)) // steps[d]
        count = count + jnp.where(lasts[d] > firsts[d], here, 0)
        upto.append(count)

    def group(g, spread):
        start, end, first, last, pace = starts[0], ends[0], firsts[0], lasts[0], steps[0]
        block = firsts[0] // PACK + g * steps[0]
        for d in range(1, docs):
            past = g >= upto[d - 1]
            start, end, first, last, pace, block = (
                jnp.where(past, new, old) for new, old in
                ((starts[d], start), (ends[d], end), (firsts[d], first), (lasts[d], last), (steps[d], pace),
                 (firsts[d] // PACK + (g - upto[d - 1]) * steps[d], block)))
        last = jnp.where(g < count, last, first)
        start = jnp.minimum(start, tiles * B - 1)
        tile = start // B
        left = start - tile * B
        turn = jnp.where(left == 0, 0, B - left)
        halves = []
        for part in range(2):
            along, later = part * (pace - 1), part * (2 - pace)
            mine = block + along
            token = sub + mine * PACK
            live = (token >= first) & (token < last) & (lane + later * B < end - start)
            at = jnp.clip(mine - step * (B // PACK), 0, B // PACK - 1)
            halves.append((live, pl.ds(pl.multiple_of(at * PACK, PACK), PACK),
                           [jnp.minimum(tile + later + n, tiles - 1) for n in range(2)]))
        before = lane < B - left

        def moved(here, there):
            return jnp.where(before, pltpu.roll(here, turn, 1), pltpu.roll(there, turn, 1))

        codes = []
        for part, (live, rows, spots) in enumerate(halves):
            for h in range(heads):
                vals = moved(*(ds_ref[s, h, rows, :].astype(jnp.float32) for s in spots))
                spread[part, pl.ds(h, PACK, stride=8), :] = jnp.where(live, vals, 0.0)
            at = [pl.ds(pl.multiple_of(s * B, B), B) for s in spots]
            codes.append(moved(*(bl_ref[rows, x] + 32 * bh_ref[rows, x] + 2048 * bv_ref[rows, x]
                                 for x in at)))
        code = jnp.concatenate(codes, axis=1)
        index = [(code & 31).astype(jnp.int16), ((code >> 5) & 63).astype(jnp.int16),
                 (code >> 11).astype(jnp.int16)]
        one, zero = jnp.ones((), jnp.bfloat16), jnp.zeros((), jnp.bfloat16)
        grads, hots = [], []
        for r in range(PACK):
            hot = []
            for ix, n in zip(index, (32, 64, 64)):
                bins = lax.broadcasted_iota(jnp.int16, (n, 2 * B), 0)
                line = jnp.broadcast_to(ix[r:r + 1, :], (n, 2 * B))
                hot.append(jnp.where(bins == line, one, zero))
            hots.append(jnp.concatenate(hot, axis=0))
            grads += [spread[part, r * 8:r * 8 + 8, :].astype(jnp.bfloat16) for part in range(2)]
        return lax.dot_general(jnp.concatenate(grads, axis=1), jnp.concatenate(hots, axis=1), NT,
                               preferred_element_type=jnp.float32)

    def several(turn, sums):
        return tuple(x + group(len(spreads) * turn + n, spread)
                     for n, (x, spread) in enumerate(zip(sums, spreads)))

    none = jnp.zeros((8, BINS), jnp.float32)
    turns = (count + (len(spreads) - 1)) // len(spreads)
    out_ref[...] = sum(lax.fori_loop(0, turns, several, tuple(none for _ in spreads)))


def table_grads(row, step, lengths, bl, bh, bv, ds):
    slots = bl.shape[1]
    tiles, heads = ds.shape[0], ds.shape[2]
    block = pl.BlockSpec((None, B, slots), lambda i, L: (row, step, 0))
    return pl.pallas_call(
        functools.partial(hist_kernel, row, step),
        grid_spec=pltpu.PrefetchScalarGridSpec(
            num_scalar_prefetch=1, grid=(1,),
            in_specs=[block, block, block,
                      pl.BlockSpec((None, tiles, heads, B, B), lambda i, L: (step, 0, 0, 0, 0))],
            out_specs=pl.BlockSpec((8, BINS), lambda i, L: (0, 0)),
            scratch_shapes=[pltpu.VMEM((2, 8 * PACK, B), jnp.float32)] * SPREADS),
        out_shape=jax.ShapeDtypeStruct((8, BINS), jnp.float32),
        compiler_params=pltpu.CompilerParams(vmem_limit_bytes=48 << 20),
        cost_estimate=pl.CostEstimate(flops=1, transcendentals=0, bytes_accessed=1),
        name="table_grads",
    )(lengths, bl, bh, bv, ds)


f32, low = jnp.float32, jnp.bfloat16
SWAP = [(0, 1), (1, 0)]
ORDER = "UATDTADTGUATDTUADTTUADTPSUASDUSASSFUS"


def normalize(values):
    mean = jnp.mean(values, axis=-1, keepdims=True)
    centered = values - mean
    scale = lax.rsqrt(jnp.mean(centered * centered, axis=-1, keepdims=True) + 1e-12)
    return centered * scale, scale


def normalize_back(grad, normed, scale, gain):
    scaled = grad * gain
    first = jnp.mean(scaled, axis=-1, keepdims=True)
    second = jnp.mean(scaled * normed, axis=-1, keepdims=True)
    return scale * (scaled - first - normed * second)


def times(left, right, left_dim, right_dim):
    return lax.dot_general(left, right, (((left_dim,), (right_dim,)), ((), ())),
                           preferred_element_type=f32)


def flips(count, bit):
    return [(i, i ^ (1 << bit)) for i in range(count)]


def to_peer(values):
    return lax.ppermute(values, "head", SWAP)


def plus(left, right):
    return (left.astype(f32) + right.astype(f32)).astype(low)


def arranged(bit_value, mine, other):
    return jnp.where(bit_value == 0, mine, other), jnp.where(bit_value == 0, other, mine)


def in_order(bit_value, mine, other):
    return jnp.stack(arranged(bit_value, mine, other))


def nothing(*refs):
    pass


def after(values, earlier):
    anywhere = pl.BlockSpec(memory_space=pl.ANY)
    return pl.pallas_call(
        nothing, in_specs=[anywhere, anywhere], out_specs=anywhere,
        out_shape=jax.ShapeDtypeStruct(values.shape, values.dtype), input_output_aliases={0: 0},
        cost_estimate=pl.CostEstimate(flops=1, transcendentals=0, bytes_accessed=1), name="after")(values, earlier)


class Order:
    def __init__(self):
        self.last = None
        self.ends = []

    def tie(self, values):
        if self.last is None:
            return values
        values, self.last = lax.optimization_barrier((values, self.last))
        return values

    def mark(self, values):
        self.last = values


def total(terms, lift, size, axis):
    return sum(lax.dynamic_slice_in_dim(values, start + lift, size, axis).astype(f32)
               for values, start in terms)


def halve(order, terms, size, axis, count, bit):
    half = size // 2
    mine = (lax.axis_index("dp") >> bit) & 1
    send = total(terms, (1 - mine) * half, half, axis).astype(low)
    order.mark(send)
    got = lax.ppermute(send, "dp", flips(count, bit))
    yield
    return [(values, start + mine * half) for values, start in terms] + [(order.tie(got), 0)]


def gather_steps(order, values, count, bits):
    index = lax.axis_index("dp")
    for bit in reversed(bits):
        order.mark(values)
        got = lax.ppermute(values, "dp", flips(count, bit))
        yield
        both = in_order((index >> bit) & 1, values, order.tie(got))
        values = both.reshape((2 * values.shape[0],) + values.shape[1:])
    return values


def unit_steps(order, kept, given, count, axis, split, out):
    bits = list(range(1, count.bit_length() - 1))
    size = kept.shape[axis]
    given = order.tie(given)
    order.mark(given)
    got = lax.ppermute(given, "dp", flips(count, 0))
    yield
    terms = [(kept, 0), (order.tie(got), 0)]
    terms = yield from halve(order, terms, size, axis, count, bits[0])
    size //= 2
    mine, other = ([(split(values)[c], start) for values, start in terms] for c in range(2))
    send = total(other, 0, size, 0).astype(low)
    order.mark(send)
    got = to_peer(send)
    yield
    terms = mine + [(order.tie(got), 0)]
    for bit in bits[1:]:
        terms = yield from halve(order, terms, size, 0, count, bit)
        size //= 2
    mine = yield from gather_steps(order, total(terms, 0, size, 0).astype(low), count, bits)
    order.mark(mine)
    other = lax.ppermute(mine, "dp", flips(count, 0))
    yield
    out += [mine, order.tie(other)]


def buffer_steps(order, values, count, out):
    bits = list(range(count.bit_length() - 1))
    size = values.shape[0]
    terms = [(order.tie(values), 0)]
    for bit in bits:
        terms = yield from halve(order, terms, size, 0, count, bit)
        size //= 2
    values = yield from gather_steps(order, total(terms, 0, size, 0).astype(low), count, bits)
    order.mark(values)
    out.append(values)


def small_steps(order, values, count, out):
    values = order.tie(values)
    bits = [None, 0] + list(range(2, count.bit_length() - 1)) + [1]
    for bit in bits:
        order.mark(values)
        got = to_peer(values) if bit is None else lax.ppermute(values, "dp", flips(count, bit))
        yield
        got = order.tie(got)
        if bit == bits[-1]:
            for other in order.ends:
                got = after(got, other)
        values = values + got
    order.mark(values)
    out.append(values)


def advance(*chains):
    for chain in chains:
        next(chain, None)


def finish(*chains):
    left = list(chains)
    while left:
        for chain in list(left):
            try:
                next(chain)
            except StopIteration:
                left.remove(chain)


def body(
    count,
    hidden,
    lengths,
    padding,
    bucket_line,
    bucket_horizontal,
    bucket_vertical,
    attn_project,
    attn_bias,
    table_line,
    table_horizontal,
    table_vertical,
    out_project,
    out_bias,
    attn_gain,
    attn_shift,
    hidden_project,
    hidden_bias,
    down_project,
    down_bias,
    final_gain,
    final_shift,
    cotangent,
):
    rows, slots, width = hidden.shape
    half = cotangent.shape[1]
    heads = table_line.shape[1]
    local = attn_project.shape[2]
    units = hidden_project.shape[1]
    part = units // 2
    factor = 1.0 / math.sqrt(local // heads)
    head = lax.axis_index("head")
    index = lax.axis_index("dp")
    core = index & 1
    offset = head * half
    every = list(range(count.bit_length() - 1))

    def split(values, dim):
        return [lax.dynamic_slice_in_dim(values, c * part, part, dim) for c in (core, 1 - core)]

    def joined(own_parts, got, dim):
        mine, rest = own_parts
        beside = lax.ppermute(got, "dp", flips(count, 0))
        return [jnp.concatenate([mine, got], axis=dim), jnp.concatenate([rest, beside], axis=dim)]

    side = (index >> 1) & 1
    down_mine = lax.dynamic_slice_in_dim(down_project, core * part + side * (part // 2), part // 2, 0)
    down_got = to_peer(down_mine)
    down_mine, hidden_project = lax.optimization_barrier((down_mine, hidden_project))
    up_mine = lax.dynamic_slice_in_dim(hidden_project, core * part, part, 1)
    up_got = to_peer(up_mine)
    up_mine, hidden, hidden_project, down_project = lax.optimization_barrier(
        (up_mine, hidden, hidden_project, down_project))
    bias_got = to_peer(hidden_bias)

    planes = jnp.concatenate([table_horizontal, table_vertical], axis=0)
    bins = table_line.shape[0] + planes.shape[0]
    lines = jnp.broadcast_to(table_line.T[:, :, None], (heads, table_line.shape[0], B))
    planes = jnp.broadcast_to(planes.T[:, None, :], (heads, PACK, planes.shape[0]))
    pad = padding[:, None, :]
    bucket_line, bucket_horizontal, bucket_vertical = (
        pltpu.with_memory_space_constraint(x, pltpu.HBM)
        for x in (bucket_line, bucket_horizontal, bucket_vertical))

    flat = hidden.reshape(rows * slots, width)
    query = ((times(flat, attn_project[0], 1, 0) + attn_bias[0].astype(f32)).astype(low)
             * jnp.asarray(factor, low))
    key = times(flat, attn_project[1], 1, 0).astype(low)
    value = (times(flat, attn_project[2], 1, 0) + attn_bias[1].astype(f32)).astype(low)
    query, key, value = (pltpu.with_memory_space_constraint(x.reshape(rows, slots, local), pltpu.HBM)
                         for x in (query, key, value))

    def own(values):
        return lax.dynamic_slice_in_dim(values, offset, half, 0)

    def others(values):
        return lax.dynamic_slice_in_dim(values, half - offset, half, 0)

    fronts, attn_sum, attn_got = [], [], []
    for r in range(rows):
        if r == 1:
            lengths, down_got = lax.optimization_barrier((lengths, down_got))
            down_beside = lax.ppermute(down_got, "dp", flips(count, 1))
        probs, context = attn_fwd(r, lengths, query, key, value, pad, bucket_line,
                                  bucket_horizontal, bucket_vertical, lines, planes)
        if r == 1:
            context, down_beside = lax.optimization_barrier((context, down_beside))
        fronts.append((probs, context))
        send = times(others(context), out_project, 1, 0).astype(low)
        got = to_peer(send)
        attn_sum.append(times(own(context), out_project, 1, 0))
        attn_got.append(got)
    (send, hidden_project, down_project, cotangent, norm_rows, out_bias, down_bias, hidden_bias, bias_got,
     hidden) = lax.optimization_barrier(
        (send, hidden_project, down_project, cotangent, (attn_gain, attn_shift, final_gain, final_shift),
         out_bias, down_bias, hidden_bias, bias_got, hidden))
    biases = [jnp.concatenate([x, y]) for x, y in zip(split(hidden_bias, 0), split(bias_got, 0))]
    gain_first, shift_first, gain_last, shift_last = (x.astype(f32) for x in norm_rows)
    up_parts = [up_mine, lax.dynamic_slice_in_dim(hidden_project, (1 - core) * part, part, 1)]
    down_parts = split(down_project, 0)
    up_got, down_beside, attn_got = lax.optimization_barrier((up_got, down_beside, attn_got))
    down_got = in_order(side, down_got, down_beside)
    ups = joined(up_parts, up_got, 1)
    downs = joined(down_parts, down_got.reshape(part, width), 0)
    attn_sum = [x + got.astype(f32) for x, got in zip(attn_sum, attn_got)]
    tokens = lax.dynamic_slice_in_dim(hidden, offset, half, 1).reshape(rows * half, width).astype(f32)
    normed, scale = normalize(tokens + jnp.concatenate(attn_sum, axis=0) + out_bias.astype(f32))
    mid = normed * gain_first + shift_first
    mid_low = mid.astype(low)

    actives, slopes = [], []
    total = None
    for up, down, bias in zip(ups, downs, biases):
        inner = times(mid_low, up, 1, 0) + bias.astype(f32)
        bell = 0.5 * (1.0 + lax.erf(inner * math.sqrt(0.5)))
        actives.append((inner * bell).astype(low))
        slope = bell + inner * (jnp.exp(-0.5 * inner * inner) * (1.0 / math.sqrt(2.0 * math.pi)))
        slopes.append(slope.astype(low))
        term = times(actives[-1], down, 1, 0)
        total = term if total is None else total + term
    normed_final, scale_final = normalize(mid + total + down_bias.astype(f32))
    output = (normed_final * gain_last + shift_last).astype(low).reshape(rows, half, width)

    above = cotangent.reshape(rows * half, width).astype(f32)
    g_final = normalize_back(above, normed_final, scale_final, gain_last)
    g_low = g_final.astype(low)
    order = Order()
    total = None
    inners = []
    for up, down, slope in zip(ups, downs, slopes):
        g_inner = (times(g_low, down, 1, 1) * slope.astype(f32)).astype(low)
        inners.append(g_inner)
        term = times(g_inner, up, 1, 1)
        total = term if total is None else total + term
    g_mid = g_final + total
    g_attn = normalize_back(g_mid, normed, scale, gain_first)
    g_attn_low = g_attn.astype(low).reshape(rows, half, width)
    g_others = [to_peer(g_attn_low[r]) for r in range(rows)]
    order.mark(g_attn_low)
    down_out, up_out, attn_out = [], [], []
    g_low = order.tie(g_low)
    kept, given = (times(active, g_low, 0, 0).astype(low) for active in actives)
    down_chain = unit_steps(order, *(x.reshape(2, part, width) for x in (kept, given)), count, 1,
                            lambda v: (v[0], v[1]), down_out)
    advance(down_chain)
    mid_low = order.tie(mid_low)
    kept, given = (times(mid_low, g_inner, 0, 0).astype(low) for g_inner in inners)
    up_chain = unit_steps(order, kept, given, count, 0, lambda v: (v[:, :part], v[:, part:]), up_out)
    advance(up_chain, down_chain)
    g_attn = g_attn.reshape(rows, half, width)

    marks, three, grad_out = [], None, 0.0
    for r in range(rows):
        probs, context = fronts[r]
        g_all = in_order(head, g_attn_low[r], order.tie(g_others[r])).reshape(slots, width)
        g_context = times(g_all, out_project, 1, 1).astype(low)
        g_scores, three = attn_bwd(r, factor, lengths, query, key, value, g_context, context, probs, three)
        order.mark(g_scores)
        marks.append(g_scores)
        grad_out = grad_out + times(context, g_all, 0, 0)
        advance(up_chain if r == 0 else down_chain)
    grad_attn = times(flat, three.reshape(rows * slots, 3 * local), 0, 0).astype(low)
    grad_out = jnp.concatenate([grad_out[:, :local], grad_out[:, local:]], axis=0).astype(low)
    attn_chain = buffer_steps(order, jnp.concatenate([grad_attn, grad_out], axis=1), count, attn_out)
    advance(attn_chain)
    every_project = jnp.concatenate([attn_project[c] for c in range(3)], axis=1)
    room = width // 2

    def pack():
        sums = [jnp.sum(x.reshape(rows * half, width), axis=0, keepdims=True) for x in
                (g_attn, g_mid * normed, g_mid, g_final, above * normed_final, above)]
        sums, units_in, three_sums, tables = order.tie(
            (sums, inners, jnp.sum(three.astype(f32).reshape(rows * slots, 3 * local), axis=0,
                                       keepdims=True), sum(tables_out)))
        unit_sums = [jnp.sum(x.astype(f32), axis=0, keepdims=True) for x in units_in]
        ours, others_ = (jnp.concatenate(arranged(core, *(x[:, c * part:(c + 1) * part] for x in unit_sums)),
                                         axis=0) for c in range(2))
        pair = jnp.concatenate([three_sums[:, :local], three_sums[:, 2 * local:]], axis=1)
        tables = jnp.pad(tables, ((0, 0), (0, room - bins)))
        return jnp.concatenate(
            sums + list(arranged(head, ours, others_))
            + [jnp.where(head == slot, pair, 0.0) for slot in range(2)]
            + [jnp.zeros((4, width), f32),
               jnp.concatenate([jnp.where(head == slot, tables, 0.0) for slot in range(2)], axis=1)], axis=0)

    tables_out, small_out = [], []
    blocks = [(r, block) for r in range(rows) for block in range(slots // B)]
    chains = {"D": down_chain, "U": up_chain, "A": attn_chain}
    for name in ORDER:
        if name == "T":
            r, block = blocks[len(tables_out)]
            tables_out.append(table_grads(r, block, order.tie(lengths), bucket_line,
                                          bucket_horizontal, bucket_vertical, marks[r]))
            order.mark(tables_out[-1])
        elif name == "G":
            three = order.tie(three)
            theirs = lax.dynamic_slice_in_dim(three, half - offset, half, 1)
            give = times(theirs.reshape(rows * half, 3 * local), every_project, 1, 1).astype(low)
            order.mark(give)
            received = to_peer(give)
            mine = lax.dynamic_slice_in_dim(three, offset, half, 1)
            mine = times(mine.reshape(rows * half, 3 * local), every_project, 1, 1)
        elif name == "F":
            finish(down_chain, attn_chain)
            grad_down = in_order(core, *down_out).reshape(down_project.shape).astype(f32)
            buffer = attn_out[0].astype(f32)
            grad_attn = jnp.stack([buffer[:, c * local:(c + 1) * local] for c in range(3)])
            order.ends = [grad_down, grad_attn]
        elif name == "P":
            chains["S"] = small_steps(order, pack(), count, small_out)
        else:
            advance(chains[name])
    finish(*chains.values())
    packed = after(small_out[0], up_out[0])
    grads_in = (mine + received.astype(f32)).reshape(rows, half, width) + g_attn
    mine, other = up_out
    grad_up = jnp.concatenate(arranged(core, mine, other), axis=1).astype(f32)
    grad_out = jnp.concatenate([buffer[:local, 3 * local:], buffer[local:, 3 * local:]], axis=1)

    rows_of = lambda at, size: lax.dynamic_slice_in_dim(packed, at, size, 0)
    grad_bias = rows_of(6 + 2 * head, 2).reshape(-1)
    grad_attn_bias = rows_of(10 + head, 1).reshape(2, local)
    marks = jnp.where(head == 0, packed[16:, :bins], packed[16:, room:room + bins])[:heads].T
    first, second = table_line.shape[0], table_horizontal.shape[0]
    return (
        output,
        grads_in,
        grad_attn,
        grad_attn_bias,
        marks[:first],
        marks[first:first + second],
        marks[first + second:],
        grad_out,
        packed[0],
        packed[1],
        packed[2],
        grad_up,
        grad_bias,
        grad_down,
        packed[3],
        packed[4],
        packed[5],
    )


def solution(mesh):
    return jax.shard_map(
        functools.partial(body, mesh.shape["dp"]),
        mesh=mesh,
        in_specs=(
            P("dp", None, None),
            P("dp", None),
            P("dp", None),
            P("dp", None, None),
            P("dp", None, None),
            P("dp", None, None),
            P(None, None, "head"),
            P(None, "head"),
            P(None, "head"),
            P(None, "head"),
            P(None, "head"),
            P("head", None),
            P(),
            P(),
            P(),
            P(None, "head"),
            P("head"),
            P("head", None),
            P(),
            P(),
            P(),
            P("dp", "head", None),
        ),
        out_specs=(
            P("dp", "head", None),
            P("dp", "head", None),
            P(None, None, "head"),
            P(None, "head"),
            P(None, "head"),
            P(None, "head"),
            P(None, "head"),
            P("head", None),
            P(),
            P(),
            P(),
            P(None, "head"),
            P("head"),
            P("head", None),
            P(),
            P(),
            P(),
        ),
        check_vma=False,
    )
```

```python
import functools
import math

import jax
import jax.numpy as jnp
from jax import lax
from jax.experimental import pallas as pl
from jax.experimental.pallas import tpu as pltpu
from jax.sharding import PartitionSpec as P

B = 128

PACK = 16


def gather_dims(axis):
    return lax.GatherDimensionNumbers(
        offset_dims=(), collapsed_slice_dims=(axis,), start_index_map=(axis,),
        operand_batching_dims=(1 - axis,), start_indices_batching_dims=(1 - axis,))


def pick(table, index, axis):
    return lax.gather(table, index[:, :, None], gather_dims(axis), (1, 1),
                      mode=lax.GatherScatterMode.PROMISE_IN_BOUNDS)


def two_heads(values, left):
    zero = jnp.zeros_like(values)
    return jnp.concatenate([jnp.where(left, values, zero), jnp.where(left, zero, values)], axis=0)


def doc_span(len_ref, row, first, last):
    edge = 0
    start = 0
    stop = 0
    for k in range(len_ref.shape[1]):
        begin = edge
        edge = edge + len_ref[row, k]
        start = jnp.where(begin <= first, begin, start)
        stop = jnp.where(begin <= last, edge, stop)
    return start // B, (stop + (B - 1)) // B

def fwd_kernel(row, len_ref, q_ref, k_ref, v_ref, pad_ref, bl_ref, bh_ref, bv_ref, line_ref, plane_ref,
               probs_ref, ctx_ref, sc, qs, best, mass, mixed):
    qb = pl.program_id(0)
    heads = sc.shape[1]
    pairs = heads // 2
    lane = lax.broadcasted_iota(jnp.int32, (B, B), 1)
    left = lane < (B // 2)
    first = qb * B
    low, high = doc_span(len_ref, row, first, first + B - 1)
    sub = lax.broadcasted_iota(jnp.int32, (B, B), 0) + first
    edges = []
    edge = 0
    for k in range(len_ref.shape[1]):
        edge = edge + len_ref[row, k]
        edges.append(edge)
    seg_q = sum(((sub >= e).astype(jnp.int32) for e in edges))
    for p in range(pairs):
        qs[p] = two_heads(q_ref[:, p * B:(p + 1) * B], left)

    def scores(t, carry):
        key_at = lane + t * B
        at = pl.ds(pl.multiple_of(t * B, B), B)
        seg_k = sum(((key_at >= e).astype(jnp.int32) for e in edges))
        real = jnp.broadcast_to(pad_ref[:, at], (B, B)) > 0
        allowed = ((seg_q == seg_k) & real) | (sub == key_at)
        parts = []
        for g in range(B // PACK):
            rows = slice(g * PACK, g * PACK + PACK)
            line = bl_ref[rows, at].astype(jnp.int16)
            parts.append((line & jnp.int16(PACK - 1), line >= jnp.int16(PACK),
                          bh_ref[rows, at].astype(jnp.int16), (bv_ref[rows, at] + 64).astype(jnp.int16)))
        for p in range(pairs):
            raw = lax.dot_general(qs[p], k_ref[at, p * B:(p + 1) * B], (((1,), (1,)), ((), ())),
                                  preferred_element_type=jnp.float32)
            for s in range(2):
                h = 2 * p + s
                plane = plane_ref[h]
                for g, (place, upper, horiz, vert) in enumerate(parts):
                    rows = slice(g * PACK, g * PACK + PACK)
                    found = jnp.where(upper, pick(line_ref[h, PACK:2 * PACK, :], place, 0),
                                      pick(line_ref[h, 0:PACK, :], place, 0))
                    rel = ((found.astype(jnp.float32) + pick(plane, horiz, 1).astype(jnp.float32))
                           + pick(plane, vert, 1).astype(jnp.float32))
                    val = jnp.where(allowed[rows], raw[s * B + g * PACK:s * B + (g + 1) * PACK, :] + rel,
                                    -1000000000.0)
                    sc[t, h, rows, :] = val
                    best[h, rows, :] = jnp.maximum(best[h, rows, :], val)
        return carry

    best[...] = jnp.full(best.shape, -3.0e38, jnp.float32)
    mass[...] = jnp.zeros_like(mass)
    mixed[...] = jnp.zeros_like(mixed)
    lax.fori_loop(low, high, scores, 0)
    for h in range(heads):
        best[h] = jnp.broadcast_to(jnp.max(best[h], axis=-1, keepdims=True), (B, B))

    def expo(t, carry):
        for h in range(heads):
            e = jnp.exp(sc[t, h] - best[h])
            sc[t, h] = e
            mass[h] += e
        return carry

    lax.fori_loop(low, high, expo, 0)
    for h in range(heads):
        mass[h] = jnp.broadcast_to(1.0 / jnp.sum(mass[h], axis=-1, keepdims=True), (B, B))

    def mix(t, carry):
        at = pl.ds(pl.multiple_of(t * B, B), B)
        for p in range(pairs):
            low_pair = []
            for s in range(2):
                h = 2 * p + s
                pr = sc[t, h] * mass[h]
                probs_ref[t, h] = pr
                low_pair.append(pr.astype(jnp.bfloat16))
            mixed[p] += jnp.dot(jnp.concatenate(low_pair, axis=0), v_ref[at, p * B:(p + 1) * B],
                                preferred_element_type=jnp.float32)
        return carry

    lax.fori_loop(low, high, mix, 0)
    for p in range(pairs):
        ctx_ref[:, p * B:(p + 1) * B] = jnp.where(left, mixed[p, :B, :], mixed[p, B:, :]).astype(jnp.bfloat16)


def attn_fwd(row, lengths, q, k, v, pad, bl, bh, bv, line, plane):
    slots, width = q.shape[1:]
    pairs = width // B
    tiles = slots // B
    row_block = lambda n: pl.BlockSpec((None, B, n), lambda i, L: (row, i, 0))
    return pl.pallas_call(
        functools.partial(fwd_kernel, row),
        grid_spec=pltpu.PrefetchScalarGridSpec(
            num_scalar_prefetch=1, grid=(tiles,),
            in_specs=[
                row_block(width),
                pl.BlockSpec((None, slots, width), lambda i, L: (row, 0, 0)),
                pl.BlockSpec((None, slots, width), lambda i, L: (row, 0, 0)),
                pl.BlockSpec((None, 1, slots), lambda i, L: (row, 0, 0)),
                row_block(slots), row_block(slots), row_block(slots),
                pl.BlockSpec(line.shape, lambda i, L: (0, 0, 0)),
                pl.BlockSpec(plane.shape, lambda i, L: (0, 0, 0)),
            ],
            out_specs=[
                pl.BlockSpec((None, tiles, 2 * pairs, B, B), lambda i, L: (i, 0, 0, 0, 0)),
                pl.BlockSpec((B, width), lambda i, L: (i, 0)),
            ],
            scratch_shapes=[
                pltpu.VMEM((tiles, 2 * pairs, B, B), jnp.float32),
                pltpu.VMEM((pairs, 2 * B, B), jnp.bfloat16),
                pltpu.VMEM((2 * pairs, B, B), jnp.float32),
                pltpu.VMEM((2 * pairs, B, B), jnp.float32),
                pltpu.VMEM((pairs, 2 * B, B), jnp.float32),
            ]),
        out_shape=[
            jax.ShapeDtypeStruct((tiles, tiles, 2 * pairs, B, B), jnp.float32),
            jax.ShapeDtypeStruct((slots, width), jnp.bfloat16),
        ],
        compiler_params=pltpu.CompilerParams(vmem_limit_bytes=48 << 20),
        cost_estimate=pl.CostEstimate(flops=1, transcendentals=0, bytes_accessed=1),
        name="attn_forward",
    )(lengths, q, k, v, pad, bl, bh, bv, line, plane)


NT = (((1,), (1,)), ((), ()))
TN = (((0,), (0,)), ((), ()))

def bwd_kernel(row, factor, len_ref, q_ref, k_ref, v_ref, gctx_ref, ctx_ref, probs_ref, *rest):
    pairs, tiles = q_ref.shape[1] // B, probs_ref.shape[0]
    ds_ref, three_ref, *scratch = rest[len(rest) - 6 * pairs - 2:]
    dks, dvs, dqs, inner, qs, gs = (scratch[n * pairs:(n + 1) * pairs] for n in range(6))
    qb = pl.program_id(0)
    lane = lax.broadcasted_iota(jnp.int32, (B, B), 1)
    left = lane < (B // 2)

    @pl.when(qb == 0)
    def _():
        for ref in dks + dvs:
            ref[...] = jnp.zeros_like(ref)

    first = qb * B
    low, high = doc_span(len_ref, row, first, first + B - 1)
    for p in range(pairs):
        cols = slice(p * B, (p + 1) * B)
        gctx = gctx_ref[:, cols]
        qs[p][...] = two_heads(q_ref[:, cols], left)
        gs[p][...] = two_heads(gctx, left)
        prod = gctx.astype(jnp.float32) * ctx_ref[:, cols].astype(jnp.float32)
        inner[p][...] = jnp.broadcast_to(jnp.sum(two_heads(prod, left), axis=-1, keepdims=True), (2 * B, B))
        dqs[p][...] = jnp.zeros_like(dqs[p])

    def tile(t, carry):
        at = pl.ds(pl.multiple_of(t * B, B), B)
        for p in range(pairs):
            cols = slice(p * B, (p + 1) * B)
            gp = lax.dot_general(gs[p][...], v_ref[at, cols], NT, preferred_element_type=jnp.float32)
            probs_low, g_scores = [], []
            for s in range(2):
                rows = slice(s * B, (s + 1) * B)
                pr = probs_ref[t, 2 * p + s]
                ds = (pr * (gp[rows, :] - inner[p][rows, :])).astype(jnp.bfloat16)
                ds_ref[t, 2 * p + s] = ds
                g_scores.append(ds)
                probs_low.append(pr.astype(jnp.bfloat16))
            ds = jnp.concatenate(g_scores, axis=0)
            mix = jnp.concatenate(probs_low, axis=0)
            dvs[p][t] += lax.dot_general(mix, gs[p][...], TN, preferred_element_type=jnp.float32)
            dks[p][t] += lax.dot_general(ds, qs[p][...], TN, preferred_element_type=jnp.float32)
            dqs[p][...] += jnp.dot(ds, k_ref[at, cols], preferred_element_type=jnp.float32)
        return carry

    lax.fori_loop(low, high, tile, 0)
    for p in range(pairs):
        dq = jnp.where(left, dqs[p][0:B, :], dqs[p][B:2 * B, :]) * factor
        three_ref[pl.ds(pl.multiple_of(first, B), B), p * B:(p + 1) * B] = dq.astype(jnp.bfloat16)

    @pl.when(qb == tiles - 1)
    def _():
        for p in range(pairs):
            for t in range(tiles):
                rows = slice(t * B, (t + 1) * B)
                three_ref[rows, (pairs + p) * B:(pairs + p + 1) * B] = dks[p][t].astype(jnp.bfloat16)
                three_ref[rows, (2 * pairs + p) * B:(2 * pairs + p + 1) * B] = dvs[p][t].astype(jnp.bfloat16)


def attn_bwd(row, factor, lengths, q, k, v, gctx, ctx, probs, kept=None):
    slots, width = q.shape[1:]
    pairs, tiles = width // B, slots // B
    part = pl.BlockSpec((B, width), lambda i, L: (i, 0))
    three = pl.BlockSpec((None, slots, 3 * width), lambda i, L: (row, 0, 0))
    mine = pl.BlockSpec((None, B, width), lambda i, L: (row, i, 0))
    whole = pl.BlockSpec((None, slots, width), lambda i, L: (row, 0, 0))
    pairs_of = pl.BlockSpec((None, tiles, 2 * pairs, B, B), lambda i, L: (i, 0, 0, 0, 0))
    kept = () if kept is None else (kept,)
    return pl.pallas_call(
        functools.partial(bwd_kernel, row, factor),
        grid_spec=pltpu.PrefetchScalarGridSpec(
            num_scalar_prefetch=1, grid=(tiles,),
            in_specs=[mine, whole, whole, part, part, pairs_of]
            + [pl.BlockSpec(memory_space=pl.ANY)] * len(kept),
            out_specs=[pairs_of, three],
            scratch_shapes=[pltpu.VMEM((tiles, B, B), jnp.float32)] * (2 * pairs)
            + [pltpu.VMEM((2 * B, B), jnp.float32)] * (2 * pairs)
            + [pltpu.VMEM((2 * B, B), jnp.bfloat16)] * (2 * pairs)),
        out_shape=[jax.ShapeDtypeStruct(probs.shape, jnp.bfloat16),
                   jax.ShapeDtypeStruct((q.shape[0], slots, 3 * width), jnp.bfloat16)],
        input_output_aliases={7: 1} if kept else {},
        compiler_params=pltpu.CompilerParams(vmem_limit_bytes=48 << 20),
        cost_estimate=pl.CostEstimate(flops=1, transcendentals=0, bytes_accessed=1),
        name="attn_backward",
    )(lengths, q, k, v, gctx, ctx, probs, *kept)

BINS = 160
SPREADS = 3


def hist_kernel(row, step, len_ref, bl_ref, bh_ref, bv_ref, ds_ref, out_ref, *spreads):
    tiles, heads = ds_ref.shape[0], ds_ref.shape[1]
    docs = len_ref.shape[1]
    lane = lax.broadcasted_iota(jnp.int32, (PACK, B), 1)
    sub = lax.broadcasted_iota(jnp.int32, (PACK, B), 0)
    for spread in spreads:
        spread[...] = jnp.zeros_like(spread)

    floor, roof = step * B, (step + 1) * B
    starts, ends, firsts, lasts, upto, steps = [], [], [], [], [], []
    edge, count = 0, 0
    for d in range(docs):
        starts.append(edge)
        edge = edge + len_ref[row, d]
        ends.append(edge)
        firsts.append(jnp.maximum(starts[d], floor))
        lasts.append(jnp.maximum(jnp.minimum(edge, roof), firsts[d]))
        steps.append(jnp.where(edge - starts[d] <= B, 2, 1))
        here = ((lasts[d] + (PACK - 1)) // PACK - firsts[d] // PACK + (steps[d] - 1)) // steps[d]
        count = count + jnp.where(lasts[d] > firsts[d], here, 0)
        upto.append(count)

    def group(g, spread):
        start, end, first, last, pace = starts[0], ends[0], firsts[0], lasts[0], steps[0]
        block = firsts[0] // PACK + g * steps[0]
        for d in range(1, docs):
            past = g >= upto[d - 1]
            start, end, first, last, pace, block = (
                jnp.where(past, new, old) for new, old in
                ((starts[d], start), (ends[d], end), (firsts[d], first), (lasts[d], last), (steps[d], pace),
                 (firsts[d] // PACK + (g - upto[d - 1]) * steps[d], block)))
        last = jnp.where(g < count, last, first)
        start = jnp.minimum(start, tiles * B - 1)
        tile = start // B
        left = start - tile * B
        turn = jnp.where(left == 0, 0, B - left)
        halves = []
        for part in range(2):
            along, later = part * (pace - 1), part * (2 - pace)
            mine = block + along
            token = sub + mine * PACK
            live = (token >= first) & (token < last) & (lane + later * B < end - start)
            at = jnp.clip(mine - step * (B // PACK), 0, B // PACK - 1)
            halves.append((live, pl.ds(pl.multiple_of(at * PACK, PACK), PACK),
                           [jnp.minimum(tile + later + n, tiles - 1) for n in range(2)]))
        before = lane < B - left

        def moved(here, there):
            return jnp.where(before, pltpu.roll(here, turn, 1), pltpu.roll(there, turn, 1))

        codes = []
        for part, (live, rows, spots) in enumerate(halves):
            for h in range(heads):
                vals = moved(*(ds_ref[s, h, rows, :].astype(jnp.float32) for s in spots))
                spread[part, pl.ds(h, PACK, stride=8), :] = jnp.where(live, vals, 0.0)
            at = [pl.ds(pl.multiple_of(s * B, B), B) for s in spots]
            codes.append(moved(*(bl_ref[rows, x] + 32 * bh_ref[rows, x] + 2048 * bv_ref[rows, x]
                                 for x in at)))
        code = jnp.concatenate(codes, axis=1)
        index = [(code & 31).astype(jnp.int16), ((code >> 5) & 63).astype(jnp.int16),
                 (code >> 11).astype(jnp.int16)]
        one, zero = jnp.ones((), jnp.bfloat16), jnp.zeros((), jnp.bfloat16)
        grads, hots = [], []
        for r in range(PACK):
            hot = []
            for ix, n in zip(index, (32, 64, 64)):
                bins = lax.broadcasted_iota(jnp.int16, (n, 2 * B), 0)
                line = jnp.broadcast_to(ix[r:r + 1, :], (n, 2 * B))
                hot.append(jnp.where(bins == line, one, zero))
            hots.append(jnp.concatenate(hot, axis=0))
            grads += [spread[part, r * 8:r * 8 + 8, :].astype(jnp.bfloat16) for part in range(2)]
        return lax.dot_general(jnp.concatenate(grads, axis=1), jnp.concatenate(hots, axis=1), NT,
                               preferred_element_type=jnp.float32)

    def several(turn, sums):
        return tuple(x + group(len(spreads) * turn + n, spread)
                     for n, (x, spread) in enumerate(zip(sums, spreads)))

    none = jnp.zeros((8, BINS), jnp.float32)
    turns = (count + (len(spreads) - 1)) // len(spreads)
    out_ref[...] = sum(lax.fori_loop(0, turns, several, tuple(none for _ in spreads)))


def table_grads(row, step, lengths, bl, bh, bv, ds):
    slots = bl.shape[1]
    tiles, heads = ds.shape[0], ds.shape[2]
    block = pl.BlockSpec((None, B, slots), lambda i, L: (row, step, 0))
    return pl.pallas_call(
        functools.partial(hist_kernel, row, step),
        grid_spec=pltpu.PrefetchScalarGridSpec(
            num_scalar_prefetch=1, grid=(1,),
            in_specs=[block, block, block,
                      pl.BlockSpec((None, tiles, heads, B, B), lambda i, L: (step, 0, 0, 0, 0))],
            out_specs=pl.BlockSpec((8, BINS), lambda i, L: (0, 0)),
            scratch_shapes=[pltpu.VMEM((2, 8 * PACK, B), jnp.float32)] * SPREADS),
        out_shape=jax.ShapeDtypeStruct((8, BINS), jnp.float32),
        compiler_params=pltpu.CompilerParams(vmem_limit_bytes=48 << 20),
        cost_estimate=pl.CostEstimate(flops=1, transcendentals=0, bytes_accessed=1),
        name="table_grads",
    )(lengths, bl, bh, bv, ds)


f32, low = jnp.float32, jnp.bfloat16
SWAP = [(0, 1), (1, 0)]
ORDER = "UATDTADTUGATDUTATDTUADTPSUASDUSASSU"


def normalize(values):
    mean = jnp.mean(values, axis=-1, keepdims=True)
    centered = values - mean
    scale = lax.rsqrt(jnp.mean(centered * centered, axis=-1, keepdims=True) + 1e-12)
    return centered * scale, scale


def normalize_back(grad, normed, scale, gain):
    scaled = grad * gain
    first = jnp.mean(scaled, axis=-1, keepdims=True)
    second = jnp.mean(scaled * normed, axis=-1, keepdims=True)
    return scale * (scaled - first - normed * second)


def times(left, right, left_dim, right_dim):
    return lax.dot_general(left, right, (((left_dim,), (right_dim,)), ((), ())),
                           preferred_element_type=f32)


def flips(count, bit):
    return [(i, i ^ (1 << bit)) for i in range(count)]


def to_peer(values):
    return lax.ppermute(values, "head", SWAP)


def plus(left, right):
    return (left.astype(f32) + right.astype(f32)).astype(low)


def arranged(bit_value, mine, other):
    return jnp.where(bit_value == 0, mine, other), jnp.where(bit_value == 0, other, mine)


def in_order(bit_value, mine, other):
    return jnp.stack(arranged(bit_value, mine, other))


class Order:
    def __init__(self):
        self.last = None

    def tie(self, values):
        if self.last is None:
            return values
        values, self.last = lax.optimization_barrier((values, self.last))
        return values

    def mark(self, values):
        self.last = values


def total(terms, lift, size, axis):
    return sum(lax.dynamic_slice_in_dim(values, start + lift, size, axis).astype(f32)
               for values, start in terms)


def halve(order, terms, size, axis, count, bit):
    half = size // 2
    mine = (lax.axis_index("dp") >> bit) & 1
    send = total(terms, (1 - mine) * half, half, axis).astype(low)
    order.mark(send)
    got = lax.ppermute(send, "dp", flips(count, bit))
    yield
    return [(values, start + mine * half) for values, start in terms] + [(order.tie(got), 0)]


def gather_steps(order, values, count, bits):
    index = lax.axis_index("dp")
    for bit in reversed(bits):
        order.mark(values)
        got = lax.ppermute(values, "dp", flips(count, bit))
        yield
        both = in_order((index >> bit) & 1, values, order.tie(got))
        values = both.reshape((2 * values.shape[0],) + values.shape[1:])
    return values


def unit_steps(order, kept, given, count, axis, split, out):
    bits = list(range(1, count.bit_length() - 1))
    size = kept.shape[axis]
    given = order.tie(given)
    order.mark(given)
    got = lax.ppermute(given, "dp", flips(count, 0))
    yield
    terms = [(kept, 0), (order.tie(got), 0)]
    terms = yield from halve(order, terms, size, axis, count, bits[0])
    size //= 2
    mine, other = ([(split(values)[c], start) for values, start in terms] for c in range(2))
    send = total(other, 0, size, 0).astype(low)
    order.mark(send)
    got = to_peer(send)
    yield
    terms = mine + [(order.tie(got), 0)]
    for bit in bits[1:]:
        terms = yield from halve(order, terms, size, 0, count, bit)
        size //= 2
    mine = yield from gather_steps(order, total(terms, 0, size, 0).astype(low), count, bits)
    order.mark(mine)
    other = lax.ppermute(mine, "dp", flips(count, 0))
    yield
    out += [mine, order.tie(other)]


def buffer_steps(order, values, count, out):
    bits = list(range(count.bit_length() - 1))
    size = values.shape[0]
    terms = [(order.tie(values), 0)]
    for bit in bits:
        terms = yield from halve(order, terms, size, 0, count, bit)
        size //= 2
    values = yield from gather_steps(order, total(terms, 0, size, 0).astype(low), count, bits)
    order.mark(values)
    out.append(values)


def small_steps(order, values, count, out):
    values = order.tie(values)
    for bit in [None] + list(range(count.bit_length() - 1)):
        order.mark(values)
        got = to_peer(values) if bit is None else lax.ppermute(values, "dp", flips(count, bit))
        yield
        values = values + order.tie(got)
    order.mark(values)
    out.append(values)


def advance(*chains):
    for chain in chains:
        next(chain, None)


def finish(*chains):
    left = list(chains)
    while left:
        for chain in list(left):
            try:
                next(chain)
            except StopIteration:
                left.remove(chain)


def body(
    count,
    hidden,
    lengths,
    padding,
    bucket_line,
    bucket_horizontal,
    bucket_vertical,
    attn_project,
    attn_bias,
    table_line,
    table_horizontal,
    table_vertical,
    out_project,
    out_bias,
    attn_gain,
    attn_shift,
    hidden_project,
    hidden_bias,
    down_project,
    down_bias,
    final_gain,
    final_shift,
    cotangent,
):
    rows, slots, width = hidden.shape
    half = cotangent.shape[1]
    heads = table_line.shape[1]
    local = attn_project.shape[2]
    units = hidden_project.shape[1]
    part = units // 2
    factor = 1.0 / math.sqrt(local // heads)
    head = lax.axis_index("head")
    index = lax.axis_index("dp")
    core = index & 1
    offset = head * half
    every = list(range(count.bit_length() - 1))

    def split(values, dim):
        return [lax.dynamic_slice_in_dim(values, c * part, part, dim) for c in (core, 1 - core)]

    def joined(own_parts, got, dim):
        mine, rest = own_parts
        beside = lax.ppermute(got, "dp", flips(count, 0))
        return [jnp.concatenate([mine, got], axis=dim), jnp.concatenate([rest, beside], axis=dim)]

    side = (index >> 1) & 1
    down_mine = lax.dynamic_slice_in_dim(down_project, core * part + side * (part // 2), part // 2, 0)
    down_got = to_peer(down_mine)
    down_mine, hidden_project = lax.optimization_barrier((down_mine, hidden_project))
    up_mine = lax.dynamic_slice_in_dim(hidden_project, core * part, part, 1)
    up_got = to_peer(up_mine)
    up_mine, hidden, hidden_project, down_project = lax.optimization_barrier(
        (up_mine, hidden, hidden_project, down_project))
    bias_got = to_peer(hidden_bias)

    planes = jnp.concatenate([table_horizontal, table_vertical], axis=0)
    bins = table_line.shape[0] + planes.shape[0]
    lines = jnp.broadcast_to(table_line.T[:, :, None], (heads, table_line.shape[0], B))
    planes = jnp.broadcast_to(planes.T[:, None, :], (heads, PACK, planes.shape[0]))
    pad = padding[:, None, :]
    bucket_line, bucket_horizontal, bucket_vertical = (
        pltpu.with_memory_space_constraint(x, pltpu.HBM)
        for x in (bucket_line, bucket_horizontal, bucket_vertical))

    flat = hidden.reshape(rows * slots, width)
    query = ((times(flat, attn_project[0], 1, 0) + attn_bias[0].astype(f32)).astype(low)
             * jnp.asarray(factor, low))
    key = times(flat, attn_project[1], 1, 0).astype(low)
    value = (times(flat, attn_project[2], 1, 0) + attn_bias[1].astype(f32)).astype(low)
    query, key, value = (pltpu.with_memory_space_constraint(x.reshape(rows, slots, local), pltpu.HBM)
                         for x in (query, key, value))

    def own(values):
        return lax.dynamic_slice_in_dim(values, offset, half, 0)

    def others(values):
        return lax.dynamic_slice_in_dim(values, half - offset, half, 0)

    fronts, attn_sum, attn_got = [], [], []
    for r in range(rows):
        if r == 1:
            lengths, down_got = lax.optimization_barrier((lengths, down_got))
            down_beside = lax.ppermute(down_got, "dp", flips(count, 1))
        probs, context = attn_fwd(r, lengths, query, key, value, pad, bucket_line,
                                  bucket_horizontal, bucket_vertical, lines, planes)
        if r == 1:
            context, down_beside = lax.optimization_barrier((context, down_beside))
        fronts.append((probs, context))
        send = times(others(context), out_project, 1, 0).astype(low)
        got = to_peer(send)
        attn_sum.append(times(own(context), out_project, 1, 0))
        attn_got.append(got)
    (send, hidden_project, down_project, cotangent, norm_rows, out_bias, down_bias, hidden_bias, bias_got,
     hidden) = lax.optimization_barrier(
        (send, hidden_project, down_project, cotangent, (attn_gain, attn_shift, final_gain, final_shift),
         out_bias, down_bias, hidden_bias, bias_got, hidden))
    biases = [jnp.concatenate([x, y]) for x, y in zip(split(hidden_bias, 0), split(bias_got, 0))]
    gain_first, shift_first, gain_last, shift_last = (x.astype(f32) for x in norm_rows)
    up_parts = [up_mine, lax.dynamic_slice_in_dim(hidden_project, (1 - core) * part, part, 1)]
    down_parts = split(down_project, 0)
    up_got, down_beside, attn_got = lax.optimization_barrier((up_got, down_beside, attn_got))
    down_got = in_order(side, down_got, down_beside)
    ups = joined(up_parts, up_got, 1)
    downs = joined(down_parts, down_got.reshape(part, width), 0)
    attn_sum = [x + got.astype(f32) for x, got in zip(attn_sum, attn_got)]
    tokens = lax.dynamic_slice_in_dim(hidden, offset, half, 1).reshape(rows * half, width).astype(f32)
    normed, scale = normalize(tokens + jnp.concatenate(attn_sum, axis=0) + out_bias.astype(f32))
    mid = normed * gain_first + shift_first
    mid_low = mid.astype(low)

    actives, slopes = [], []
    total = None
    for up, down, bias in zip(ups, downs, biases):
        inner = times(mid_low, up, 1, 0) + bias.astype(f32)
        bell = 0.5 * (1.0 + lax.erf(inner * math.sqrt(0.5)))
        actives.append((inner * bell).astype(low))
        slope = bell + inner * (jnp.exp(-0.5 * inner * inner) * (1.0 / math.sqrt(2.0 * math.pi)))
        slopes.append(slope.astype(low))
        term = times(actives[-1], down, 1, 0)
        total = term if total is None else total + term
    normed_final, scale_final = normalize(mid + total + down_bias.astype(f32))
    output = (normed_final * gain_last + shift_last).astype(low).reshape(rows, half, width)

    above = cotangent.reshape(rows * half, width).astype(f32)
    g_final = normalize_back(above, normed_final, scale_final, gain_last)
    g_low = g_final.astype(low)
    order = Order()
    total = None
    inners = []
    for up, down, slope in zip(ups, downs, slopes):
        g_active = lax.optimization_barrier(times(g_low, down, 1, 1))
        g_inner = (g_active * slope.astype(f32)).astype(low)
        inners.append(g_inner)
        term = times(g_inner, up, 1, 1)
        total = term if total is None else total + term
    g_mid = g_final + total
    g_attn = normalize_back(g_mid, normed, scale, gain_first)
    g_attn_low = g_attn.astype(low).reshape(rows, half, width)
    g_others = [to_peer(g_attn_low[r]) for r in range(rows)]
    order.mark(g_attn_low)
    down_out, up_out, attn_out = [], [], []
    g_low = order.tie(g_low)
    kept, given = (times(active, g_low, 0, 0).astype(low) for active in actives)
    down_chain = unit_steps(order, *(x.reshape(2, part, width) for x in (kept, given)), count, 1,
                            lambda v: (v[0], v[1]), down_out)
    advance(down_chain)
    mid_low = order.tie(mid_low)
    kept, given = (times(mid_low, g_inner, 0, 0).astype(low) for g_inner in inners)
    up_chain = unit_steps(order, kept, given, count, 0, lambda v: (v[:, :part], v[:, part:]), up_out)
    advance(up_chain, down_chain)
    g_attn = g_attn.reshape(rows, half, width)

    marks, three, grad_out = [], None, 0.0
    for r in range(rows):
        probs, context = fronts[r]
        g_all = in_order(head, g_attn_low[r], order.tie(g_others[r])).reshape(slots, width)
        g_context = times(g_all, out_project, 1, 1).astype(low)
        g_scores, three = attn_bwd(r, factor, lengths, query, key, value, g_context, context, probs, three)
        order.mark(g_scores)
        marks.append(g_scores)
        grad_out = grad_out + times(context, g_all, 0, 0)
        advance(up_chain if r == 0 else down_chain)
    grad_attn = times(flat, three.reshape(rows * slots, 3 * local), 0, 0).astype(low)
    grad_out = jnp.concatenate([grad_out[:, :local], grad_out[:, local:]], axis=0).astype(low)
    attn_chain = buffer_steps(order, jnp.concatenate([grad_attn, grad_out], axis=1), count, attn_out)
    advance(attn_chain)
    every_project = jnp.concatenate([attn_project[c] for c in range(3)], axis=1)
    room = width // 2

    def pack():
        sums = [jnp.sum(x.reshape(rows * half, width), axis=0, keepdims=True) for x in
                (g_attn, g_mid * normed, g_mid, g_final, above * normed_final, above)]
        sums, units_in, three_sums, tables = order.tie(
            (sums, inners, jnp.sum(three.astype(f32).reshape(rows * slots, 3 * local), axis=0,
                                       keepdims=True), sum(tables_out)))
        unit_sums = [jnp.sum(x.astype(f32), axis=0, keepdims=True) for x in units_in]
        ours, others_ = (jnp.concatenate(arranged(core, *(x[:, c * part:(c + 1) * part] for x in unit_sums)),
                                         axis=0) for c in range(2))
        pair = jnp.concatenate([three_sums[:, :local], three_sums[:, 2 * local:]], axis=1)
        tables = jnp.pad(tables, ((0, 0), (0, room - bins)))
        return jnp.concatenate(
            sums + list(arranged(head, ours, others_))
            + [jnp.where(head == slot, pair, 0.0) for slot in range(2)]
            + [jnp.zeros((4, width), f32),
               jnp.concatenate([jnp.where(head == slot, tables, 0.0) for slot in range(2)], axis=1)], axis=0)

    tables_out, small_out = [], []
    blocks = [(r, block) for r in range(rows) for block in range(slots // B)]
    chains = {"D": down_chain, "U": up_chain, "A": attn_chain}
    for name in ORDER:
        if name == "T":
            r, block = blocks[len(tables_out)]
            tables_out.append(table_grads(r, block, order.tie(lengths), bucket_line,
                                          bucket_horizontal, bucket_vertical, marks[r]))
            order.mark(tables_out[-1])
        elif name == "G":
            three = order.tie(three)
            theirs = lax.dynamic_slice_in_dim(three, half - offset, half, 1)
            give = times(theirs.reshape(rows * half, 3 * local), every_project, 1, 1).astype(low)
            order.mark(give)
            received = to_peer(give)
            mine = lax.dynamic_slice_in_dim(three, offset, half, 1)
            mine = times(mine.reshape(rows * half, 3 * local), every_project, 1, 1)
        elif name == "P":
            chains["S"] = small_steps(order, pack(), count, small_out)
        else:
            advance(chains[name])
    finish(*chains.values())
    packed = small_out[0]
    grads_in = (mine + received.astype(f32)).reshape(rows, half, width) + g_attn
    grad_down = in_order(core, *down_out).reshape(down_project.shape).astype(f32)
    mine, other = up_out
    grad_up = jnp.concatenate(arranged(core, mine, other), axis=1).astype(f32)
    buffer = attn_out[0].astype(f32)
    grad_attn = jnp.stack([buffer[:, c * local:(c + 1) * local] for c in range(3)])
    grad_out = jnp.concatenate([buffer[:local, 3 * local:], buffer[local:, 3 * local:]], axis=1)

    rows_of = lambda at, size: lax.dynamic_slice_in_dim(packed, at, size, 0)
    grad_bias = rows_of(6 + 2 * head, 2).reshape(-1)
    grad_attn_bias = rows_of(10 + head, 1).reshape(2, local)
    marks = jnp.where(head == 0, packed[16:, :bins], packed[16:, room:room + bins])[:heads].T
    first, second = table_line.shape[0], table_horizontal.shape[0]
    return (
        output,
        grads_in,
        grad_attn,
        grad_attn_bias,
        marks[:first],
        marks[first:first + second],
        marks[first + second:],
        grad_out,
        packed[0],
        packed[1],
        packed[2],
        grad_up,
        grad_bias,
        grad_down,
        packed[3],
        packed[4],
        packed[5],
    )


def solution(mesh):
    return jax.shard_map(
        functools.partial(body, mesh.shape["dp"]),
        mesh=mesh,
        in_specs=(
            P("dp", None, None),
            P("dp", None),
            P("dp", None),
            P("dp", None, None),
            P("dp", None, None),
            P("dp", None, None),
            P(None, None, "head"),
            P(None, "head"),
            P(None, "head"),
            P(None, "head"),
            P(None, "head"),
            P("head", None),
            P(),
            P(),
            P(),
            P(None, "head"),
            P("head"),
            P("head", None),
            P(),
            P(),
            P(),
            P("dp", "head", None),
        ),
        out_specs=(
            P("dp", "head", None),
            P("dp", "head", None),
            P(None, None, "head"),
            P(None, "head"),
            P(None, "head"),
            P(None, "head"),
            P(None, "head"),
            P("head", None),
            P(),
            P(),
            P(),
            P(None, "head"),
            P("head"),
            P("head", None),
            P(),
            P(),
            P(),
        ),
        check_vma=False,
    )
```

```python
import functools
import math

import jax
import jax.numpy as jnp
from jax import lax
from jax.experimental import pallas as pl
from jax.experimental.pallas import tpu as pltpu
from jax.sharding import PartitionSpec as P

B = 128

PACK = 16


def gather_dims(axis):
    return lax.GatherDimensionNumbers(
        offset_dims=(), collapsed_slice_dims=(axis,), start_index_map=(axis,),
        operand_batching_dims=(1 - axis,), start_indices_batching_dims=(1 - axis,))


def pick(table, index, axis):
    return lax.gather(table, index[:, :, None], gather_dims(axis), (1, 1),
                      mode=lax.GatherScatterMode.PROMISE_IN_BOUNDS)


def two_heads(values, left):
    zero = jnp.zeros_like(values)
    return jnp.concatenate([jnp.where(left, values, zero), jnp.where(left, zero, values)], axis=0)


def doc_span(len_ref, row, first, last):
    edge = 0
    start = 0
    stop = 0
    for k in range(len_ref.shape[1]):
        begin = edge
        edge = edge + len_ref[row, k]
        start = jnp.where(begin <= first, begin, start)
        stop = jnp.where(begin <= last, edge, stop)
    return start // B, (stop + (B - 1)) // B

def fwd_kernel(row, len_ref, q_ref, k_ref, v_ref, pad_ref, bl_ref, bh_ref, bv_ref, line_ref, plane_ref,
               probs_ref, ctx_ref, sc, qs, best, mass, mixed):
    qb = pl.program_id(0)
    heads = sc.shape[1]
    pairs = heads // 2
    lane = lax.broadcasted_iota(jnp.int32, (B, B), 1)
    left = lane < (B // 2)
    first = qb * B
    low, high = doc_span(len_ref, row, first, first + B - 1)
    sub = lax.broadcasted_iota(jnp.int32, (B, B), 0) + first
    edges = []
    edge = 0
    for k in range(len_ref.shape[1]):
        edge = edge + len_ref[row, k]
        edges.append(edge)
    seg_q = sum(((sub >= e).astype(jnp.int32) for e in edges))
    for p in range(pairs):
        qs[p] = two_heads(q_ref[:, p * B:(p + 1) * B], left)

    def scores(t, carry):
        key_at = lane + t * B
        at = pl.ds(pl.multiple_of(t * B, B), B)
        seg_k = sum(((key_at >= e).astype(jnp.int32) for e in edges))
        real = jnp.broadcast_to(pad_ref[:, at], (B, B)) > 0
        allowed = ((seg_q == seg_k) & real) | (sub == key_at)
        parts = []
        for g in range(B // PACK):
            rows = slice(g * PACK, g * PACK + PACK)
            line = bl_ref[rows, at].astype(jnp.int16)
            parts.append((line & jnp.int16(PACK - 1), line >= jnp.int16(PACK),
                          bh_ref[rows, at].astype(jnp.int16), (bv_ref[rows, at] + 64).astype(jnp.int16)))
        for p in range(pairs):
            raw = lax.dot_general(qs[p], k_ref[at, p * B:(p + 1) * B], (((1,), (1,)), ((), ())),
                                  preferred_element_type=jnp.float32)
            for s in range(2):
                h = 2 * p + s
                plane = plane_ref[h]
                for g, (place, upper, horiz, vert) in enumerate(parts):
                    rows = slice(g * PACK, g * PACK + PACK)
                    found = jnp.where(upper, pick(line_ref[h, PACK:2 * PACK, :], place, 0),
                                      pick(line_ref[h, 0:PACK, :], place, 0))
                    rel = ((found.astype(jnp.float32) + pick(plane, horiz, 1).astype(jnp.float32))
                           + pick(plane, vert, 1).astype(jnp.float32))
                    val = jnp.where(allowed[rows], raw[s * B + g * PACK:s * B + (g + 1) * PACK, :] + rel,
                                    -1000000000.0)
                    sc[t, h, rows, :] = val
                    best[h, rows, :] = jnp.maximum(best[h, rows, :], val)
        return carry

    best[...] = jnp.full(best.shape, -3.0e38, jnp.float32)
    mass[...] = jnp.zeros_like(mass)
    mixed[...] = jnp.zeros_like(mixed)
    lax.fori_loop(low, high, scores, 0)
    for h in range(heads):
        best[h] = jnp.broadcast_to(jnp.max(best[h], axis=-1, keepdims=True), (B, B))

    def expo(t, carry):
        for h in range(heads):
            e = jnp.exp(sc[t, h] - best[h])
            sc[t, h] = e
            mass[h] += e
        return carry

    lax.fori_loop(low, high, expo, 0)
    for h in range(heads):
        mass[h] = jnp.broadcast_to(1.0 / jnp.sum(mass[h], axis=-1, keepdims=True), (B, B))

    def mix(t, carry):
        at = pl.ds(pl.multiple_of(t * B, B), B)
        for p in range(pairs):
            low_pair = []
            for s in range(2):
                h = 2 * p + s
                pr = sc[t, h] * mass[h]
                probs_ref[t, h] = pr
                low_pair.append(pr.astype(jnp.bfloat16))
            mixed[p] += jnp.dot(jnp.concatenate(low_pair, axis=0), v_ref[at, p * B:(p + 1) * B],
                                preferred_element_type=jnp.float32)
        return carry

    lax.fori_loop(low, high, mix, 0)
    for p in range(pairs):
        ctx_ref[:, p * B:(p + 1) * B] = jnp.where(left, mixed[p, :B, :], mixed[p, B:, :]).astype(jnp.bfloat16)


def attn_fwd(row, lengths, q, k, v, pad, bl, bh, bv, line, plane):
    slots, width = q.shape[1:]
    pairs = width // B
    tiles = slots // B
    row_block = lambda n: pl.BlockSpec((None, B, n), lambda i, L: (row, i, 0))
    return pl.pallas_call(
        functools.partial(fwd_kernel, row),
        grid_spec=pltpu.PrefetchScalarGridSpec(
            num_scalar_prefetch=1, grid=(tiles,),
            in_specs=[
                row_block(width),
                pl.BlockSpec((None, slots, width), lambda i, L: (row, 0, 0)),
                pl.BlockSpec((None, slots, width), lambda i, L: (row, 0, 0)),
                pl.BlockSpec((None, 1, slots), lambda i, L: (row, 0, 0)),
                row_block(slots), row_block(slots), row_block(slots),
                pl.BlockSpec(line.shape, lambda i, L: (0, 0, 0)),
                pl.BlockSpec(plane.shape, lambda i, L: (0, 0, 0)),
            ],
            out_specs=[
                pl.BlockSpec((None, tiles, 2 * pairs, B, B), lambda i, L: (i, 0, 0, 0, 0)),
                pl.BlockSpec((B, width), lambda i, L: (i, 0)),
            ],
            scratch_shapes=[
                pltpu.VMEM((tiles, 2 * pairs, B, B), jnp.float32),
                pltpu.VMEM((pairs, 2 * B, B), jnp.bfloat16),
                pltpu.VMEM((2 * pairs, B, B), jnp.float32),
                pltpu.VMEM((2 * pairs, B, B), jnp.float32),
                pltpu.VMEM((pairs, 2 * B, B), jnp.float32),
            ]),
        out_shape=[
            jax.ShapeDtypeStruct((tiles, tiles, 2 * pairs, B, B), jnp.float32),
            jax.ShapeDtypeStruct((slots, width), jnp.bfloat16),
        ],
        compiler_params=pltpu.CompilerParams(vmem_limit_bytes=48 << 20),
        cost_estimate=pl.CostEstimate(flops=1, transcendentals=0, bytes_accessed=1),
        name="attn_forward",
    )(lengths, q, k, v, pad, bl, bh, bv, line, plane)


NT = (((1,), (1,)), ((), ()))
TN = (((0,), (0,)), ((), ()))

def bwd_kernel(row, factor, len_ref, q_ref, k_ref, v_ref, gctx_ref, ctx_ref, probs_ref, *rest):
    pairs, tiles = q_ref.shape[1] // B, probs_ref.shape[0]
    ds_ref, three_ref, *scratch = rest[len(rest) - 6 * pairs - 2:]
    dks, dvs, dqs, inner, qs, gs = (scratch[n * pairs:(n + 1) * pairs] for n in range(6))
    qb = pl.program_id(0)
    lane = lax.broadcasted_iota(jnp.int32, (B, B), 1)
    left = lane < (B // 2)

    @pl.when(qb == 0)
    def _():
        for ref in dks + dvs:
            ref[...] = jnp.zeros_like(ref)

    first = qb * B
    low, high = doc_span(len_ref, row, first, first + B - 1)
    for p in range(pairs):
        cols = slice(p * B, (p + 1) * B)
        gctx = gctx_ref[:, cols]
        qs[p][...] = two_heads(q_ref[:, cols], left)
        gs[p][...] = two_heads(gctx, left)
        prod = gctx.astype(jnp.float32) * ctx_ref[:, cols].astype(jnp.float32)
        inner[p][...] = jnp.broadcast_to(jnp.sum(two_heads(prod, left), axis=-1, keepdims=True), (2 * B, B))
        dqs[p][...] = jnp.zeros_like(dqs[p])

    def tile(t, carry):
        at = pl.ds(pl.multiple_of(t * B, B), B)
        for p in range(pairs):
            cols = slice(p * B, (p + 1) * B)
            gp = lax.dot_general(gs[p][...], v_ref[at, cols], NT, preferred_element_type=jnp.float32)
            probs_low, g_scores = [], []
            for s in range(2):
                rows = slice(s * B, (s + 1) * B)
                pr = probs_ref[t, 2 * p + s]
                ds = (pr * (gp[rows, :] - inner[p][rows, :])).astype(jnp.bfloat16)
                ds_ref[t, 2 * p + s] = ds
                g_scores.append(ds)
                probs_low.append(pr.astype(jnp.bfloat16))
            ds = jnp.concatenate(g_scores, axis=0)
            mix = jnp.concatenate(probs_low, axis=0)
            dvs[p][t] += lax.dot_general(mix, gs[p][...], TN, preferred_element_type=jnp.float32)
            dks[p][t] += lax.dot_general(ds, qs[p][...], TN, preferred_element_type=jnp.float32)
            dqs[p][...] += jnp.dot(ds, k_ref[at, cols], preferred_element_type=jnp.float32)
        return carry

    lax.fori_loop(low, high, tile, 0)
    for p in range(pairs):
        dq = jnp.where(left, dqs[p][0:B, :], dqs[p][B:2 * B, :]) * factor
        three_ref[pl.ds(pl.multiple_of(first, B), B), p * B:(p + 1) * B] = dq.astype(jnp.bfloat16)

    @pl.when(qb == tiles - 1)
    def _():
        for p in range(pairs):
            for t in range(tiles):
                rows = slice(t * B, (t + 1) * B)
                three_ref[rows, (pairs + p) * B:(pairs + p + 1) * B] = dks[p][t].astype(jnp.bfloat16)
                three_ref[rows, (2 * pairs + p) * B:(2 * pairs + p + 1) * B] = dvs[p][t].astype(jnp.bfloat16)


def attn_bwd(row, factor, lengths, q, k, v, gctx, ctx, probs, kept=None):
    slots, width = q.shape[1:]
    pairs, tiles = width // B, slots // B
    part = pl.BlockSpec((B, width), lambda i, L: (i, 0))
    three = pl.BlockSpec((None, slots, 3 * width), lambda i, L: (row, 0, 0))
    mine = pl.BlockSpec((None, B, width), lambda i, L: (row, i, 0))
    whole = pl.BlockSpec((None, slots, width), lambda i, L: (row, 0, 0))
    pairs_of = pl.BlockSpec((None, tiles, 2 * pairs, B, B), lambda i, L: (i, 0, 0, 0, 0))
    kept = () if kept is None else (kept,)
    return pl.pallas_call(
        functools.partial(bwd_kernel, row, factor),
        grid_spec=pltpu.PrefetchScalarGridSpec(
            num_scalar_prefetch=1, grid=(tiles,),
            in_specs=[mine, whole, whole, part, part, pairs_of]
            + [pl.BlockSpec(memory_space=pl.ANY)] * len(kept),
            out_specs=[pairs_of, three],
            scratch_shapes=[pltpu.VMEM((tiles, B, B), jnp.float32)] * (2 * pairs)
            + [pltpu.VMEM((2 * B, B), jnp.float32)] * (2 * pairs)
            + [pltpu.VMEM((2 * B, B), jnp.bfloat16)] * (2 * pairs)),
        out_shape=[jax.ShapeDtypeStruct(probs.shape, jnp.bfloat16),
                   jax.ShapeDtypeStruct((q.shape[0], slots, 3 * width), jnp.bfloat16)],
        input_output_aliases={7: 1} if kept else {},
        compiler_params=pltpu.CompilerParams(vmem_limit_bytes=48 << 20),
        cost_estimate=pl.CostEstimate(flops=1, transcendentals=0, bytes_accessed=1),
        name="attn_backward",
    )(lengths, q, k, v, gctx, ctx, probs, *kept)

BINS = 160
SPREADS = 3


def hist_kernel(row, step, len_ref, bl_ref, bh_ref, bv_ref, ds_ref, out_ref, *spreads):
    tiles, heads = ds_ref.shape[0], ds_ref.shape[1]
    docs = len_ref.shape[1]
    lane = lax.broadcasted_iota(jnp.int32, (PACK, B), 1)
    sub = lax.broadcasted_iota(jnp.int32, (PACK, B), 0)
    for spread in spreads:
        spread[...] = jnp.zeros_like(spread)

    floor, roof = step * B, (step + 1) * B
    starts, ends, firsts, lasts, upto, steps = [], [], [], [], [], []
    edge, count = 0, 0
    for d in range(docs):
        starts.append(edge)
        edge = edge + len_ref[row, d]
        ends.append(edge)
        firsts.append(jnp.maximum(starts[d], floor))
        lasts.append(jnp.maximum(jnp.minimum(edge, roof), firsts[d]))
        steps.append(jnp.where(edge - starts[d] <= B, 2, 1))
        here = ((lasts[d] + (PACK - 1)) // PACK - firsts[d] // PACK + (steps[d] - 1)) // steps[d]
        count = count + jnp.where(lasts[d] > firsts[d], here, 0)
        upto.append(count)

    def group(g, spread):
        start, end, first, last, pace = starts[0], ends[0], firsts[0], lasts[0], steps[0]
        block = firsts[0] // PACK + g * steps[0]
        for d in range(1, docs):
            past = g >= upto[d - 1]
            start, end, first, last, pace, block = (
                jnp.where(past, new, old) for new, old in
                ((starts[d], start), (ends[d], end), (firsts[d], first), (lasts[d], last), (steps[d], pace),
                 (firsts[d] // PACK + (g - upto[d - 1]) * steps[d], block)))
        last = jnp.where(g < count, last, first)
        start = jnp.minimum(start, tiles * B - 1)
        tile = start // B
        left = start - tile * B
        turn = jnp.where(left == 0, 0, B - left)
        halves = []
        for part in range(2):
            along, later = part * (pace - 1), part * (2 - pace)
            mine = block + along
            token = sub + mine * PACK
            live = (token >= first) & (token < last) & (lane + later * B < end - start)
            at = jnp.clip(mine - step * (B // PACK), 0, B // PACK - 1)
            halves.append((live, pl.ds(pl.multiple_of(at * PACK, PACK), PACK),
                           [jnp.minimum(tile + later + n, tiles - 1) for n in range(2)]))
        before = lane < B - left

        def moved(here, there):
            return jnp.where(before, pltpu.roll(here, turn, 1), pltpu.roll(there, turn, 1))

        codes = []
        for part, (live, rows, spots) in enumerate(halves):
            for h in range(heads):
                vals = moved(*(ds_ref[s, h, rows, :].astype(jnp.float32) for s in spots))
                spread[part, pl.ds(h, PACK, stride=8), :] = jnp.where(live, vals, 0.0)
            at = [pl.ds(pl.multiple_of(s * B, B), B) for s in spots]
            codes.append(moved(*(bl_ref[rows, x] + 32 * bh_ref[rows, x] + 2048 * bv_ref[rows, x]
                                 for x in at)))
        code = jnp.concatenate(codes, axis=1)
        index = [(code & 31).astype(jnp.int16), ((code >> 5) & 63).astype(jnp.int16),
                 (code >> 11).astype(jnp.int16)]
        one, zero = jnp.ones((), jnp.bfloat16), jnp.zeros((), jnp.bfloat16)
        grads, hots = [], []
        for r in range(PACK):
            hot = []
            for ix, n in zip(index, (32, 64, 64)):
                bins = lax.broadcasted_iota(jnp.int16, (n, 2 * B), 0)
                line = jnp.broadcast_to(ix[r:r + 1, :], (n, 2 * B))
                hot.append(jnp.where(bins == line, one, zero))
            hots.append(jnp.concatenate(hot, axis=0))
            grads += [spread[part, r * 8:r * 8 + 8, :].astype(jnp.bfloat16) for part in range(2)]
        return lax.dot_general(jnp.concatenate(grads, axis=1), jnp.concatenate(hots, axis=1), NT,
                               preferred_element_type=jnp.float32)

    def several(turn, sums):
        return tuple(x + group(len(spreads) * turn + n, spread)
                     for n, (x, spread) in enumerate(zip(sums, spreads)))

    none = jnp.zeros((8, BINS), jnp.float32)
    turns = (count + (len(spreads) - 1)) // len(spreads)
    out_ref[...] = sum(lax.fori_loop(0, turns, several, tuple(none for _ in spreads)))


def table_grads(row, step, lengths, bl, bh, bv, ds):
    slots = bl.shape[1]
    tiles, heads = ds.shape[0], ds.shape[2]
    block = pl.BlockSpec((None, B, slots), lambda i, L: (row, step, 0))
    return pl.pallas_call(
        functools.partial(hist_kernel, row, step),
        grid_spec=pltpu.PrefetchScalarGridSpec(
            num_scalar_prefetch=1, grid=(1,),
            in_specs=[block, block, block,
                      pl.BlockSpec((None, tiles, heads, B, B), lambda i, L: (step, 0, 0, 0, 0))],
            out_specs=pl.BlockSpec((8, BINS), lambda i, L: (0, 0)),
            scratch_shapes=[pltpu.VMEM((2, 8 * PACK, B), jnp.float32)] * SPREADS),
        out_shape=jax.ShapeDtypeStruct((8, BINS), jnp.float32),
        compiler_params=pltpu.CompilerParams(vmem_limit_bytes=48 << 20),
        cost_estimate=pl.CostEstimate(flops=1, transcendentals=0, bytes_accessed=1),
        name="table_grads",
    )(lengths, bl, bh, bv, ds)


f32, low = jnp.float32, jnp.bfloat16
SWAP = [(0, 1), (1, 0)]
ORDER = "UATDTADTUGATDUTATDTUADTPSUASDUSASSU"


def normalize(values):
    mean = jnp.mean(values, axis=-1, keepdims=True)
    centered = values - mean
    scale = lax.rsqrt(jnp.mean(centered * centered, axis=-1, keepdims=True) + 1e-12)
    return centered * scale, scale


def normalize_back(grad, normed, scale, gain):
    scaled = grad * gain
    first = jnp.mean(scaled, axis=-1, keepdims=True)
    second = jnp.mean(scaled * normed, axis=-1, keepdims=True)
    return scale * (scaled - first - normed * second)


def times(left, right, left_dim, right_dim):
    return lax.dot_general(left, right, (((left_dim,), (right_dim,)), ((), ())),
                           preferred_element_type=f32)


def flips(count, bit):
    return [(i, i ^ (1 << bit)) for i in range(count)]


def to_peer(values):
    return lax.ppermute(values, "head", SWAP)


def plus(left, right):
    return (left.astype(f32) + right.astype(f32)).astype(low)


def arranged(bit_value, mine, other):
    return jnp.where(bit_value == 0, mine, other), jnp.where(bit_value == 0, other, mine)


def in_order(bit_value, mine, other):
    return jnp.stack(arranged(bit_value, mine, other))


class Order:
    def __init__(self):
        self.last = None

    def tie(self, values):
        if self.last is None:
            return values
        values, self.last = lax.optimization_barrier((values, self.last))
        return values

    def mark(self, values):
        self.last = values


def total(terms, lift, size, axis):
    return sum((values(start + lift, size) if callable(values) else
                lax.dynamic_slice_in_dim(values, start + lift, size, axis)).astype(f32)
               for values, start in terms)


def halve(order, terms, size, axis, count, bit):
    half = size // 2
    mine = (lax.axis_index("dp") >> bit) & 1
    send = total(terms, (1 - mine) * half, half, axis).astype(low)
    order.mark(send)
    got = lax.ppermute(send, "dp", flips(count, bit))
    yield
    return [(values, start + mine * half) for values, start in terms] + [(order.tie(got), 0)]


def gather_steps(order, values, count, bits):
    index = lax.axis_index("dp")
    for bit in reversed(bits):
        order.mark(values)
        got = lax.ppermute(values, "dp", flips(count, bit))
        yield
        both = in_order((index >> bit) & 1, values, order.tie(got))
        values = both.reshape((2 * values.shape[0],) + values.shape[1:])
    return values


def unit_steps(order, kept, given, count, axis, split, out):
    bits = list(range(1, count.bit_length() - 1))
    size = kept.shape[axis]
    given = order.tie(given)
    order.mark(given)
    got = lax.ppermute(given, "dp", flips(count, 0))
    yield
    terms = [(kept, 0), (order.tie(got), 0)]
    terms = yield from halve(order, terms, size, axis, count, bits[0])
    size //= 2
    mine, other = ([(functools.partial(split, values, c), start) for values, start in terms] for c in range(2))
    send = total(other, 0, size, 0).astype(low)
    order.mark(send)
    got = to_peer(send)
    yield
    terms = mine + [(order.tie(got), 0)]
    for bit in bits[1:]:
        terms = yield from halve(order, terms, size, 0, count, bit)
        size //= 2
    mine = yield from gather_steps(order, total(terms, 0, size, 0).astype(low), count, bits)
    order.mark(mine)
    other = lax.ppermute(mine, "dp", flips(count, 0))
    yield
    out += [mine, order.tie(other)]


def buffer_steps(order, values, count, out):
    bits = list(range(count.bit_length() - 1))
    size = values.shape[0]
    terms = [(order.tie(values), 0)]
    for bit in bits:
        terms = yield from halve(order, terms, size, 0, count, bit)
        size //= 2
    values = yield from gather_steps(order, total(terms, 0, size, 0).astype(low), count, bits)
    order.mark(values)
    out.append(values)


def small_steps(order, values, count, out):
    values = order.tie(values)
    for bit in [None] + list(range(count.bit_length() - 1)):
        order.mark(values)
        got = to_peer(values) if bit is None else lax.ppermute(values, "dp", flips(count, bit))
        yield
        values = values + order.tie(got)
    order.mark(values)
    out.append(values)


def advance(*chains):
    for chain in chains:
        next(chain, None)


def finish(*chains):
    left = list(chains)
    while left:
        for chain in list(left):
            try:
                next(chain)
            except StopIteration:
                left.remove(chain)


def body(
    count,
    hidden,
    lengths,
    padding,
    bucket_line,
    bucket_horizontal,
    bucket_vertical,
    attn_project,
    attn_bias,
    table_line,
    table_horizontal,
    table_vertical,
    out_project,
    out_bias,
    attn_gain,
    attn_shift,
    hidden_project,
    hidden_bias,
    down_project,
    down_bias,
    final_gain,
    final_shift,
    cotangent,
):
    rows, slots, width = hidden.shape
    half = cotangent.shape[1]
    heads = table_line.shape[1]
    local = attn_project.shape[2]
    units = hidden_project.shape[1]
    part = units // 2
    factor = 1.0 / math.sqrt(local // heads)
    head = lax.axis_index("head")
    index = lax.axis_index("dp")
    core = index & 1
    offset = head * half
    every = list(range(count.bit_length() - 1))

    def split(values, dim):
        return [lax.dynamic_slice_in_dim(values, c * part, part, dim) for c in (core, 1 - core)]

    def joined(own_parts, got, dim):
        mine, rest = own_parts
        beside = lax.ppermute(got, "dp", flips(count, 0))
        return [jnp.concatenate([mine, got], axis=dim), jnp.concatenate([rest, beside], axis=dim)]

    side = (index >> 1) & 1
    down_mine = lax.dynamic_slice_in_dim(down_project, core * part + side * (part // 2), part // 2, 0)
    down_got = to_peer(down_mine)
    down_mine, hidden_project = lax.optimization_barrier((down_mine, hidden_project))
    up_mine = lax.dynamic_slice_in_dim(hidden_project, core * part, part, 1)
    up_got = to_peer(up_mine)
    up_mine, hidden, hidden_project, down_project = lax.optimization_barrier(
        (up_mine, hidden, hidden_project, down_project))
    bias_got = to_peer(hidden_bias)

    planes = jnp.concatenate([table_horizontal, table_vertical], axis=0)
    bins = table_line.shape[0] + planes.shape[0]
    lines = jnp.broadcast_to(table_line.T[:, :, None], (heads, table_line.shape[0], B))
    planes = jnp.broadcast_to(planes.T[:, None, :], (heads, PACK, planes.shape[0]))
    pad = padding[:, None, :]
    bucket_line, bucket_horizontal, bucket_vertical = (
        pltpu.with_memory_space_constraint(x, pltpu.HBM)
        for x in (bucket_line, bucket_horizontal, bucket_vertical))

    flat = hidden.reshape(rows * slots, width)
    query = ((times(flat, attn_project[0], 1, 0) + attn_bias[0].astype(f32)).astype(low)
             * jnp.asarray(factor, low))
    key = times(flat, attn_project[1], 1, 0).astype(low)
    value = (times(flat, attn_project[2], 1, 0) + attn_bias[1].astype(f32)).astype(low)
    query, key, value = (pltpu.with_memory_space_constraint(x.reshape(rows, slots, local), pltpu.HBM)
                         for x in (query, key, value))

    def own(values):
        return lax.dynamic_slice_in_dim(values, offset, half, 0)

    def others(values):
        return lax.dynamic_slice_in_dim(values, half - offset, half, 0)

    fronts, attn_sum, attn_got = [], [], []
    for r in range(rows):
        if r == 1:
            lengths, down_got = lax.optimization_barrier((lengths, down_got))
            down_beside = lax.ppermute(down_got, "dp", flips(count, 1))
        probs, context = attn_fwd(r, lengths, query, key, value, pad, bucket_line,
                                  bucket_horizontal, bucket_vertical, lines, planes)
        if r == 1:
            context, down_beside = lax.optimization_barrier((context, down_beside))
        fronts.append((probs, context))
        send = times(others(context), out_project, 1, 0).astype(low)
        got = to_peer(send)
        attn_sum.append(times(own(context), out_project, 1, 0))
        attn_got.append(got)
    (send, hidden_project, down_project, cotangent, norm_rows, out_bias, down_bias, hidden_bias, bias_got,
     hidden) = lax.optimization_barrier(
        (send, hidden_project, down_project, cotangent, (attn_gain, attn_shift, final_gain, final_shift),
         out_bias, down_bias, hidden_bias, bias_got, hidden))
    biases = [jnp.concatenate([x, y]) for x, y in zip(split(hidden_bias, 0), split(bias_got, 0))]
    gain_first, shift_first, gain_last, shift_last = (x.astype(f32) for x in norm_rows)
    up_parts = [up_mine, lax.dynamic_slice_in_dim(hidden_project, (1 - core) * part, part, 1)]
    down_parts = split(down_project, 0)
    up_got, down_beside, attn_got = lax.optimization_barrier((up_got, down_beside, attn_got))
    down_got = in_order(side, down_got, down_beside)
    ups = joined(up_parts, up_got, 1)
    downs = joined(down_parts, down_got.reshape(part, width), 0)
    attn_sum = [x + got.astype(f32) for x, got in zip(attn_sum, attn_got)]
    tokens = lax.dynamic_slice_in_dim(hidden, offset, half, 1).reshape(rows * half, width).astype(f32)
    normed, scale = normalize(tokens + jnp.concatenate(attn_sum, axis=0) + out_bias.astype(f32))
    mid = normed * gain_first + shift_first
    mid_low = mid.astype(low)

    actives, slopes = [], []
    total = None
    for up, down, bias in zip(ups, downs, biases):
        inner = times(mid_low, up, 1, 0) + bias.astype(f32)
        bell = 0.5 * (1.0 + lax.erf(inner * math.sqrt(0.5)))
        actives.append((inner * bell).astype(low))
        slope = bell + inner * (jnp.exp(-0.5 * inner * inner) * (1.0 / math.sqrt(2.0 * math.pi)))
        slopes.append(slope.astype(low))
        term = times(actives[-1], down, 1, 0)
        total = term if total is None else total + term
    normed_final, scale_final = normalize(mid + total + down_bias.astype(f32))
    output = (normed_final * gain_last + shift_last).astype(low).reshape(rows, half, width)

    above = cotangent.reshape(rows * half, width).astype(f32)
    g_final = normalize_back(above, normed_final, scale_final, gain_last)
    g_low = g_final.astype(low)
    order = Order()
    total = None
    inners = []
    for up, down, slope in zip(ups, downs, slopes):
        g_active = lax.optimization_barrier(times(g_low, down, 1, 1))
        g_inner = (g_active * slope.astype(f32)).astype(low)
        inners.append(g_inner)
        term = times(g_inner, up, 1, 1)
        total = term if total is None else total + term
    g_mid = g_final + total
    g_attn = normalize_back(g_mid, normed, scale, gain_first)
    g_attn_low = g_attn.astype(low).reshape(rows, half, width)
    g_others = [to_peer(g_attn_low[r]) for r in range(rows)]
    order.mark(g_attn_low)
    down_out, up_out, attn_out = [], [], []
    g_low = order.tie(g_low)
    kept, given = (times(active, g_low, 0, 0).astype(low) for active in actives)
    def down_part(values, c, start, size):
        at = [jnp.asarray(x, jnp.int32) for x in (c, start, 0)]
        return lax.dynamic_slice(values, at, (1, size, width)).reshape(size, width)

    def up_part(values, c, start, size):
        return lax.dynamic_slice(values, [jnp.asarray(x, jnp.int32) for x in (start, c * part)], (size, part))

    down_chain = unit_steps(order, *(x.reshape(2, part, width) for x in (kept, given)), count, 1,
                            down_part, down_out)
    advance(down_chain)
    mid_low = order.tie(mid_low)
    kept, given = (times(mid_low, g_inner, 0, 0).astype(low) for g_inner in inners)
    up_chain = unit_steps(order, kept, given, count, 0, up_part, up_out)
    advance(up_chain, down_chain)
    g_attn = g_attn.reshape(rows, half, width)

    marks, three, grad_out = [], None, 0.0
    for r in range(rows):
        probs, context = fronts[r]
        g_all = in_order(head, g_attn_low[r], order.tie(g_others[r])).reshape(slots, width)
        g_context = times(g_all, out_project, 1, 1).astype(low)
        g_scores, three = attn_bwd(r, factor, lengths, query, key, value, g_context, context, probs, three)
        order.mark(g_scores)
        marks.append(g_scores)
        grad_out = grad_out + times(context, g_all, 0, 0)
        advance(up_chain if r == 0 else down_chain)
    grad_attn = times(flat, three.reshape(rows * slots, 3 * local), 0, 0).astype(low)
    grad_out = jnp.concatenate([grad_out[:, :local], grad_out[:, local:]], axis=0).astype(low)
    attn_chain = buffer_steps(order, jnp.concatenate([grad_attn, grad_out], axis=1), count, attn_out)
    advance(attn_chain)
    every_project = jnp.concatenate([attn_project[c] for c in range(3)], axis=1)
    room = width // 2

    def pack():
        sums = [jnp.sum(x.reshape(rows * half, width), axis=0, keepdims=True) for x in
                (g_attn, g_mid * normed, g_mid, g_final, above * normed_final, above)]
        sums, units_in, three_sums, tables = order.tie(
            (sums, inners, jnp.sum(three.astype(f32).reshape(rows * slots, 3 * local), axis=0,
                                       keepdims=True), sum(tables_out)))
        unit_sums = [jnp.sum(x.astype(f32), axis=0, keepdims=True) for x in units_in]
        ours, others_ = (jnp.concatenate(arranged(core, *(x[:, c * part:(c + 1) * part] for x in unit_sums)),
                                         axis=0) for c in range(2))
        pair = jnp.concatenate([three_sums[:, :local], three_sums[:, 2 * local:]], axis=1)
        tables = jnp.pad(tables, ((0, 0), (0, room - bins)))
        return jnp.concatenate(
            sums + list(arranged(head, ours, others_))
            + [jnp.where(head == slot, pair, 0.0) for slot in range(2)]
            + [jnp.zeros((4, width), f32),
               jnp.concatenate([jnp.where(head == slot, tables, 0.0) for slot in range(2)], axis=1)], axis=0)

    tables_out, small_out = [], []
    blocks = [(r, block) for r in range(rows) for block in range(slots // B)]
    chains = {"D": down_chain, "U": up_chain, "A": attn_chain}
    for name in ORDER:
        if name == "T":
            r, block = blocks[len(tables_out)]
            tables_out.append(table_grads(r, block, order.tie(lengths), bucket_line,
                                          bucket_horizontal, bucket_vertical, marks[r]))
            order.mark(tables_out[-1])
        elif name == "G":
            three = order.tie(three)
            theirs = lax.dynamic_slice_in_dim(three, half - offset, half, 1)
            give = times(theirs.reshape(rows * half, 3 * local), every_project, 1, 1).astype(low)
            order.mark(give)
            received = to_peer(give)
            mine = lax.dynamic_slice_in_dim(three, offset, half, 1)
            mine = times(mine.reshape(rows * half, 3 * local), every_project, 1, 1)
        elif name == "P":
            chains["S"] = small_steps(order, pack(), count, small_out)
        else:
            advance(chains[name])
    finish(*chains.values())
    packed = small_out[0]
    grads_in = (mine + received.astype(f32)).reshape(rows, half, width) + g_attn
    grad_down = in_order(core, *down_out).reshape(down_project.shape).astype(f32)
    mine, other = up_out
    grad_up = jnp.concatenate(arranged(core, mine, other), axis=1).astype(f32)
    buffer = attn_out[0].astype(f32)
    grad_attn = jnp.stack([buffer[:, c * local:(c + 1) * local] for c in range(3)])
    grad_out = jnp.concatenate([buffer[:local, 3 * local:], buffer[local:, 3 * local:]], axis=1)

    rows_of = lambda at, size: lax.dynamic_slice_in_dim(packed, at, size, 0)
    grad_bias = rows_of(6 + 2 * head, 2).reshape(-1)
    grad_attn_bias = rows_of(10 + head, 1).reshape(2, local)
    marks = jnp.where(head == 0, packed[16:, :bins], packed[16:, room:room + bins])[:heads].T
    first, second = table_line.shape[0], table_horizontal.shape[0]
    return (
        output,
        grads_in,
        grad_attn,
        grad_attn_bias,
        marks[:first],
        marks[first:first + second],
        marks[first + second:],
        grad_out,
        packed[0],
        packed[1],
        packed[2],
        grad_up,
        grad_bias,
        grad_down,
        packed[3],
        packed[4],
        packed[5],
    )


def solution(mesh):
    return jax.shard_map(
        functools.partial(body, mesh.shape["dp"]),
        mesh=mesh,
        in_specs=(
            P("dp", None, None),
            P("dp", None),
            P("dp", None),
            P("dp", None, None),
            P("dp", None, None),
            P("dp", None, None),
            P(None, None, "head"),
            P(None, "head"),
            P(None, "head"),
            P(None, "head"),
            P(None, "head"),
            P("head", None),
            P(),
            P(),
            P(),
            P(None, "head"),
            P("head"),
            P("head", None),
            P(),
            P(),
            P(),
            P("dp", "head", None),
        ),
        out_specs=(
            P("dp", "head", None),
            P("dp", "head", None),
            P(None, None, "head"),
            P(None, "head"),
            P(None, "head"),
            P(None, "head"),
            P(None, "head"),
            P("head", None),
            P(),
            P(),
            P(),
            P(None, "head"),
            P("head"),
            P("head", None),
            P(),
            P(),
            P(),
        ),
        check_vma=False,
    )
```

```python
import functools
import math

import jax
import jax.numpy as jnp
from jax import lax
from jax.experimental import pallas as pl
from jax.experimental.pallas import tpu as pltpu
from jax.sharding import PartitionSpec as P

B = 128

PACK = 16


def gather_dims(axis):
    return lax.GatherDimensionNumbers(
        offset_dims=(), collapsed_slice_dims=(axis,), start_index_map=(axis,),
        operand_batching_dims=(1 - axis,), start_indices_batching_dims=(1 - axis,))


def pick(table, index, axis):
    return lax.gather(table, index[:, :, None], gather_dims(axis), (1, 1),
                      mode=lax.GatherScatterMode.PROMISE_IN_BOUNDS)


def two_heads(values, left):
    zero = jnp.zeros_like(values)
    return jnp.concatenate([jnp.where(left, values, zero), jnp.where(left, zero, values)], axis=0)


def doc_span(len_ref, row, first, last):
    edge = 0
    start = 0
    stop = 0
    for k in range(len_ref.shape[1]):
        begin = edge
        edge = edge + len_ref[row, k]
        start = jnp.where(begin <= first, begin, start)
        stop = jnp.where(begin <= last, edge, stop)
    return start // B, (stop + (B - 1)) // B

def fwd_kernel(row, len_ref, q_ref, k_ref, v_ref, pad_ref, bl_ref, bh_ref, bv_ref, line_ref, plane_ref,
               probs_ref, ctx_ref, sc, qs, best, mass, mixed):
    qb = pl.program_id(0)
    heads = sc.shape[1]
    pairs = heads // 2
    lane = lax.broadcasted_iota(jnp.int32, (B, B), 1)
    left = lane < (B // 2)
    first = qb * B
    low, high = doc_span(len_ref, row, first, first + B - 1)
    sub = lax.broadcasted_iota(jnp.int32, (B, B), 0) + first
    edges = []
    edge = 0
    for k in range(len_ref.shape[1]):
        edge = edge + len_ref[row, k]
        edges.append(edge)
    seg_q = sum(((sub >= e).astype(jnp.int32) for e in edges))
    for p in range(pairs):
        qs[p] = two_heads(q_ref[:, p * B:(p + 1) * B], left)

    def scores(t, carry):
        key_at = lane + t * B
        at = pl.ds(pl.multiple_of(t * B, B), B)
        seg_k = sum(((key_at >= e).astype(jnp.int32) for e in edges))
        real = jnp.broadcast_to(pad_ref[:, at], (B, B)) > 0
        allowed = ((seg_q == seg_k) & real) | (sub == key_at)
        parts = []
        for g in range(B // PACK):
            rows = slice(g * PACK, g * PACK + PACK)
            line = bl_ref[rows, at].astype(jnp.int16)
            parts.append((line & jnp.int16(PACK - 1), line >= jnp.int16(PACK),
                          bh_ref[rows, at].astype(jnp.int16), (bv_ref[rows, at] + 64).astype(jnp.int16)))
        for p in range(pairs):
            raw = lax.dot_general(qs[p], k_ref[at, p * B:(p + 1) * B], (((1,), (1,)), ((), ())),
                                  preferred_element_type=jnp.float32)
            for s in range(2):
                h = 2 * p + s
                plane = plane_ref[h]
                for g, (place, upper, horiz, vert) in enumerate(parts):
                    rows = slice(g * PACK, g * PACK + PACK)
                    found = jnp.where(upper, pick(line_ref[h, PACK:2 * PACK, :], place, 0),
                                      pick(line_ref[h, 0:PACK, :], place, 0))
                    rel = ((found.astype(jnp.float32) + pick(plane, horiz, 1).astype(jnp.float32))
                           + pick(plane, vert, 1).astype(jnp.float32))
                    val = jnp.where(allowed[rows], raw[s * B + g * PACK:s * B + (g + 1) * PACK, :] + rel,
                                    -1000000000.0)
                    sc[t, h, rows, :] = val
                    best[h, rows, :] = jnp.maximum(best[h, rows, :], val)
        return carry

    best[...] = jnp.full(best.shape, -3.0e38, jnp.float32)
    mass[...] = jnp.zeros_like(mass)
    mixed[...] = jnp.zeros_like(mixed)
    lax.fori_loop(low, high, scores, 0)
    for h in range(heads):
        best[h] = jnp.broadcast_to(jnp.max(best[h], axis=-1, keepdims=True), (B, B))

    def expo(t, carry):
        for h in range(heads):
            e = jnp.exp(sc[t, h] - best[h])
            sc[t, h] = e
            mass[h] += e
        return carry

    lax.fori_loop(low, high, expo, 0)
    for h in range(heads):
        mass[h] = jnp.broadcast_to(1.0 / jnp.sum(mass[h], axis=-1, keepdims=True), (B, B))

    def mix(t, carry):
        at = pl.ds(pl.multiple_of(t * B, B), B)
        for p in range(pairs):
            low_pair = []
            for s in range(2):
                h = 2 * p + s
                pr = sc[t, h] * mass[h]
                probs_ref[t, h] = pr
                low_pair.append(pr.astype(jnp.bfloat16))
            mixed[p] += jnp.dot(jnp.concatenate(low_pair, axis=0), v_ref[at, p * B:(p + 1) * B],
                                preferred_element_type=jnp.float32)
        return carry

    lax.fori_loop(low, high, mix, 0)
    for p in range(pairs):
        ctx_ref[:, p * B:(p + 1) * B] = jnp.where(left, mixed[p, :B, :], mixed[p, B:, :]).astype(jnp.bfloat16)


def attn_fwd(row, lengths, q, k, v, pad, bl, bh, bv, line, plane):
    slots, width = q.shape[1:]
    pairs = width // B
    tiles = slots // B
    row_block = lambda n: pl.BlockSpec((None, B, n), lambda i, L: (row, i, 0))
    return pl.pallas_call(
        functools.partial(fwd_kernel, row),
        grid_spec=pltpu.PrefetchScalarGridSpec(
            num_scalar_prefetch=1, grid=(tiles,),
            in_specs=[
                row_block(width),
                pl.BlockSpec((None, slots, width), lambda i, L: (row, 0, 0)),
                pl.BlockSpec((None, slots, width), lambda i, L: (row, 0, 0)),
                pl.BlockSpec((None, 1, slots), lambda i, L: (row, 0, 0)),
                row_block(slots), row_block(slots), row_block(slots),
                pl.BlockSpec(line.shape, lambda i, L: (0, 0, 0)),
                pl.BlockSpec(plane.shape, lambda i, L: (0, 0, 0)),
            ],
            out_specs=[
                pl.BlockSpec((None, tiles, 2 * pairs, B, B), lambda i, L: (i, 0, 0, 0, 0)),
                pl.BlockSpec((B, width), lambda i, L: (i, 0)),
            ],
            scratch_shapes=[
                pltpu.VMEM((tiles, 2 * pairs, B, B), jnp.float32),
                pltpu.VMEM((pairs, 2 * B, B), jnp.bfloat16),
                pltpu.VMEM((2 * pairs, B, B), jnp.float32),
                pltpu.VMEM((2 * pairs, B, B), jnp.float32),
                pltpu.VMEM((pairs, 2 * B, B), jnp.float32),
            ]),
        out_shape=[
            jax.ShapeDtypeStruct((tiles, tiles, 2 * pairs, B, B), jnp.float32),
            jax.ShapeDtypeStruct((slots, width), jnp.bfloat16),
        ],
        compiler_params=pltpu.CompilerParams(vmem_limit_bytes=48 << 20),
        cost_estimate=pl.CostEstimate(flops=1, transcendentals=0, bytes_accessed=1),
        name="attn_forward",
    )(lengths, q, k, v, pad, bl, bh, bv, line, plane)


NT = (((1,), (1,)), ((), ()))
TN = (((0,), (0,)), ((), ()))

def bwd_kernel(row, factor, len_ref, q_ref, k_ref, v_ref, gctx_ref, ctx_ref, probs_ref, *rest):
    pairs, tiles = q_ref.shape[1] // B, probs_ref.shape[0]
    ds_ref, three_ref, *scratch = rest[len(rest) - 6 * pairs - 2:]
    dks, dvs, dqs, inner, qs, gs = (scratch[n * pairs:(n + 1) * pairs] for n in range(6))
    qb = pl.program_id(0)
    lane = lax.broadcasted_iota(jnp.int32, (B, B), 1)
    left = lane < (B // 2)

    @pl.when(qb == 0)
    def _():
        for ref in dks + dvs:
            ref[...] = jnp.zeros_like(ref)

    first = qb * B
    low, high = doc_span(len_ref, row, first, first + B - 1)
    for p in range(pairs):
        cols = slice(p * B, (p + 1) * B)
        gctx = gctx_ref[:, cols]
        qs[p][...] = two_heads(q_ref[:, cols], left)
        gs[p][...] = two_heads(gctx, left)
        prod = gctx.astype(jnp.float32) * ctx_ref[:, cols].astype(jnp.float32)
        inner[p][...] = jnp.broadcast_to(jnp.sum(two_heads(prod, left), axis=-1, keepdims=True), (2 * B, B))
        dqs[p][...] = jnp.zeros_like(dqs[p])

    def tile(t, carry):
        at = pl.ds(pl.multiple_of(t * B, B), B)
        for p in range(pairs):
            cols = slice(p * B, (p + 1) * B)
            gp = lax.dot_general(gs[p][...], v_ref[at, cols], NT, preferred_element_type=jnp.float32)
            probs_low, g_scores = [], []
            for s in range(2):
                rows = slice(s * B, (s + 1) * B)
                pr = probs_ref[t, 2 * p + s]
                ds = (pr * (gp[rows, :] - inner[p][rows, :])).astype(jnp.bfloat16)
                ds_ref[t, 2 * p + s] = ds
                g_scores.append(ds)
                probs_low.append(pr.astype(jnp.bfloat16))
            ds = jnp.concatenate(g_scores, axis=0)
            mix = jnp.concatenate(probs_low, axis=0)
            dvs[p][t] += lax.dot_general(mix, gs[p][...], TN, preferred_element_type=jnp.float32)
            dks[p][t] += lax.dot_general(ds, qs[p][...], TN, preferred_element_type=jnp.float32)
            dqs[p][...] += jnp.dot(ds, k_ref[at, cols], preferred_element_type=jnp.float32)
        return carry

    lax.fori_loop(low, high, tile, 0)
    for p in range(pairs):
        dq = jnp.where(left, dqs[p][0:B, :], dqs[p][B:2 * B, :]) * factor
        three_ref[pl.ds(pl.multiple_of(first, B), B), p * B:(p + 1) * B] = dq.astype(jnp.bfloat16)

    @pl.when(qb == tiles - 1)
    def _():
        for p in range(pairs):
            for t in range(tiles):
                rows = slice(t * B, (t + 1) * B)
                three_ref[rows, (pairs + p) * B:(pairs + p + 1) * B] = dks[p][t].astype(jnp.bfloat16)
                three_ref[rows, (2 * pairs + p) * B:(2 * pairs + p + 1) * B] = dvs[p][t].astype(jnp.bfloat16)


def attn_bwd(row, factor, lengths, q, k, v, gctx, ctx, probs, kept=None):
    slots, width = q.shape[1:]
    pairs, tiles = width // B, slots // B
    part = pl.BlockSpec((B, width), lambda i, L: (i, 0))
    three = pl.BlockSpec((None, slots, 3 * width), lambda i, L: (row, 0, 0))
    mine = pl.BlockSpec((None, B, width), lambda i, L: (row, i, 0))
    whole = pl.BlockSpec((None, slots, width), lambda i, L: (row, 0, 0))
    pairs_of = pl.BlockSpec((None, tiles, 2 * pairs, B, B), lambda i, L: (i, 0, 0, 0, 0))
    kept = () if kept is None else (kept,)
    return pl.pallas_call(
        functools.partial(bwd_kernel, row, factor),
        grid_spec=pltpu.PrefetchScalarGridSpec(
            num_scalar_prefetch=1, grid=(tiles,),
            in_specs=[mine, whole, whole, part, part, pairs_of]
            + [pl.BlockSpec(memory_space=pl.ANY)] * len(kept),
            out_specs=[pairs_of, three],
            scratch_shapes=[pltpu.VMEM((tiles, B, B), jnp.float32)] * (2 * pairs)
            + [pltpu.VMEM((2 * B, B), jnp.float32)] * (2 * pairs)
            + [pltpu.VMEM((2 * B, B), jnp.bfloat16)] * (2 * pairs)),
        out_shape=[jax.ShapeDtypeStruct(probs.shape, jnp.bfloat16),
                   jax.ShapeDtypeStruct((q.shape[0], slots, 3 * width), jnp.bfloat16)],
        input_output_aliases={7: 1} if kept else {},
        compiler_params=pltpu.CompilerParams(vmem_limit_bytes=48 << 20),
        cost_estimate=pl.CostEstimate(flops=1, transcendentals=0, bytes_accessed=1),
        name="attn_backward",
    )(lengths, q, k, v, gctx, ctx, probs, *kept)

BINS = 160
SPREADS = 3


def hist_kernel(row, step, len_ref, bl_ref, bh_ref, bv_ref, ds_ref, out_ref, *spreads):
    tiles, heads = ds_ref.shape[0], ds_ref.shape[1]
    docs = len_ref.shape[1]
    lane = lax.broadcasted_iota(jnp.int32, (PACK, B), 1)
    sub = lax.broadcasted_iota(jnp.int32, (PACK, B), 0)
    for spread in spreads:
        spread[...] = jnp.zeros_like(spread)

    floor, roof = step * B, (step + 1) * B
    starts, ends, firsts, lasts, upto, steps = [], [], [], [], [], []
    edge, count = 0, 0
    for d in range(docs):
        starts.append(edge)
        edge = edge + len_ref[row, d]
        ends.append(edge)
        firsts.append(jnp.maximum(starts[d], floor))
        lasts.append(jnp.maximum(jnp.minimum(edge, roof), firsts[d]))
        steps.append(jnp.where(edge - starts[d] <= B, 2, 1))
        here = ((lasts[d] + (PACK - 1)) // PACK - firsts[d] // PACK + (steps[d] - 1)) // steps[d]
        count = count + jnp.where(lasts[d] > firsts[d], here, 0)
        upto.append(count)

    def group(g, spread):
        start, end, first, last, pace = starts[0], ends[0], firsts[0], lasts[0], steps[0]
        block = firsts[0] // PACK + g * steps[0]
        for d in range(1, docs):
            past = g >= upto[d - 1]
            start, end, first, last, pace, block = (
                jnp.where(past, new, old) for new, old in
                ((starts[d], start), (ends[d], end), (firsts[d], first), (lasts[d], last), (steps[d], pace),
                 (firsts[d] // PACK + (g - upto[d - 1]) * steps[d], block)))
        last = jnp.where(g < count, last, first)
        start = jnp.minimum(start, tiles * B - 1)
        tile = start // B
        left = start - tile * B
        turn = jnp.where(left == 0, 0, B - left)
        halves = []
        for part in range(2):
            along, later = part * (pace - 1), part * (2 - pace)
            mine = block + along
            token = sub + mine * PACK
            live = (token >= first) & (token < last) & (lane + later * B < end - start)
            at = jnp.clip(mine - step * (B // PACK), 0, B // PACK - 1)
            halves.append((live, pl.ds(pl.multiple_of(at * PACK, PACK), PACK),
                           [jnp.minimum(tile + later + n, tiles - 1) for n in range(2)]))
        before = lane < B - left

        def moved(here, there):
            return jnp.where(before, pltpu.roll(here, turn, 1), pltpu.roll(there, turn, 1))

        codes = []
        for part, (live, rows, spots) in enumerate(halves):
            for h in range(heads):
                vals = moved(*(ds_ref[s, h, rows, :].astype(jnp.float32) for s in spots))
                spread[part, pl.ds(h, PACK, stride=8), :] = jnp.where(live, vals, 0.0)
            at = [pl.ds(pl.multiple_of(s * B, B), B) for s in spots]
            codes.append(moved(*(bl_ref[rows, x] + 32 * bh_ref[rows, x] + 2048 * bv_ref[rows, x]
                                 for x in at)))
        code = jnp.concatenate(codes, axis=1)
        index = [(code & 31).astype(jnp.int16), ((code >> 5) & 63).astype(jnp.int16),
                 (code >> 11).astype(jnp.int16)]
        one, zero = jnp.ones((), jnp.bfloat16), jnp.zeros((), jnp.bfloat16)
        grads, hots = [], []
        for r in range(PACK):
            hot = []
            for ix, n in zip(index, (32, 64, 64)):
                bins = lax.broadcasted_iota(jnp.int16, (n, 2 * B), 0)
                line = jnp.broadcast_to(ix[r:r + 1, :], (n, 2 * B))
                hot.append(jnp.where(bins == line, one, zero))
            hots.append(jnp.concatenate(hot, axis=0))
            grads += [spread[part, r * 8:r * 8 + 8, :].astype(jnp.bfloat16) for part in range(2)]
        return lax.dot_general(jnp.concatenate(grads, axis=1), jnp.concatenate(hots, axis=1), NT,
                               preferred_element_type=jnp.float32)

    def several(turn, sums):
        return tuple(x + group(len(spreads) * turn + n, spread)
                     for n, (x, spread) in enumerate(zip(sums, spreads)))

    none = jnp.zeros((8, BINS), jnp.float32)
    turns = (count + (len(spreads) - 1)) // len(spreads)
    out_ref[...] = sum(lax.fori_loop(0, turns, several, tuple(none for _ in spreads)))


def table_grads(row, step, lengths, bl, bh, bv, ds):
    slots = bl.shape[1]
    tiles, heads = ds.shape[0], ds.shape[2]
    block = pl.BlockSpec((None, B, slots), lambda i, L: (row, step, 0))
    return pl.pallas_call(
        functools.partial(hist_kernel, row, step),
        grid_spec=pltpu.PrefetchScalarGridSpec(
            num_scalar_prefetch=1, grid=(1,),
            in_specs=[block, block, block,
                      pl.BlockSpec((None, tiles, heads, B, B), lambda i, L: (step, 0, 0, 0, 0))],
            out_specs=pl.BlockSpec((8, BINS), lambda i, L: (0, 0)),
            scratch_shapes=[pltpu.VMEM((2, 8 * PACK, B), jnp.float32)] * SPREADS),
        out_shape=jax.ShapeDtypeStruct((8, BINS), jnp.float32),
        compiler_params=pltpu.CompilerParams(vmem_limit_bytes=48 << 20),
        cost_estimate=pl.CostEstimate(flops=1, transcendentals=0, bytes_accessed=1),
        name="table_grads",
    )(lengths, bl, bh, bv, ds)


f32, low = jnp.float32, jnp.bfloat16
SWAP = [(0, 1), (1, 0)]
ORDER = "UATDTADTUATDUTATDTUADGTPSUASDUSASSU"


def normalize(values):
    mean = jnp.mean(values, axis=-1, keepdims=True)
    centered = values - mean
    scale = lax.rsqrt(jnp.mean(centered * centered, axis=-1, keepdims=True) + 1e-12)
    return centered * scale, scale


def normalize_back(grad, normed, scale, gain):
    scaled = grad * gain
    first = jnp.mean(scaled, axis=-1, keepdims=True)
    second = jnp.mean(scaled * normed, axis=-1, keepdims=True)
    return scale * (scaled - first - normed * second)


def times(left, right, left_dim, right_dim):
    return lax.dot_general(left, right, (((left_dim,), (right_dim,)), ((), ())),
                           preferred_element_type=f32)


def flips(count, bit):
    return [(i, i ^ (1 << bit)) for i in range(count)]


def to_peer(values):
    return lax.ppermute(values, "head", SWAP)


def plus(left, right):
    return (left.astype(f32) + right.astype(f32)).astype(low)


def arranged(bit_value, mine, other):
    return jnp.where(bit_value == 0, mine, other), jnp.where(bit_value == 0, other, mine)


def in_order(bit_value, mine, other):
    return jnp.stack(arranged(bit_value, mine, other))


class Order:
    def __init__(self):
        self.last = None

    def tie(self, values):
        if self.last is None:
            return values
        values, self.last = lax.optimization_barrier((values, self.last))
        return values

    def mark(self, values):
        self.last = values


def total(terms, lift, size, axis):
    return sum((values(start + lift, size) if callable(values) else
                lax.dynamic_slice_in_dim(values, start + lift, size, axis)).astype(f32)
               for values, start in terms)


def halve(order, terms, size, axis, count, bit):
    half = size // 2
    mine = (lax.axis_index("dp") >> bit) & 1
    send = total(terms, (1 - mine) * half, half, axis).astype(low)
    order.mark(send)
    got = lax.ppermute(send, "dp", flips(count, bit))
    yield
    return [(values, start + mine * half) for values, start in terms] + [(order.tie(got), 0)]


def gather_steps(order, values, count, bits):
    index = lax.axis_index("dp")
    for bit in reversed(bits):
        order.mark(values)
        got = lax.ppermute(values, "dp", flips(count, bit))
        yield
        both = in_order((index >> bit) & 1, values, order.tie(got))
        values = both.reshape((2 * values.shape[0],) + values.shape[1:])
    return values


def unit_steps(order, kept, given, count, axis, split, out):
    bits = list(range(1, count.bit_length() - 1))
    size = kept.shape[axis]
    given = order.tie(given)
    order.mark(given)
    got = lax.ppermute(given, "dp", flips(count, 0))
    yield
    terms = [(kept, 0), (order.tie(got), 0)]
    terms = yield from halve(order, terms, size, axis, count, bits[0])
    size //= 2
    mine, other = ([(functools.partial(split, values, c), start) for values, start in terms] for c in range(2))
    send = total(other, 0, size, 0).astype(low)
    order.mark(send)
    got = to_peer(send)
    yield
    terms = mine + [(order.tie(got), 0)]
    for bit in bits[1:]:
        terms = yield from halve(order, terms, size, 0, count, bit)
        size //= 2
    mine = yield from gather_steps(order, total(terms, 0, size, 0).astype(low), count, bits)
    order.mark(mine)
    other = lax.ppermute(mine, "dp", flips(count, 0))
    yield
    out += [mine, order.tie(other)]


def buffer_steps(order, values, count, out):
    bits = list(range(count.bit_length() - 1))
    size = values.shape[0]
    terms = [(order.tie(values), 0)]
    for bit in bits:
        terms = yield from halve(order, terms, size, 0, count, bit)
        size //= 2
    values = yield from gather_steps(order, total(terms, 0, size, 0).astype(low), count, bits)
    order.mark(values)
    out.append(values)


def small_steps(order, values, count, out):
    values = order.tie(values)
    for bit in [None] + list(range(count.bit_length() - 1)):
        order.mark(values)
        got = to_peer(values) if bit is None else lax.ppermute(values, "dp", flips(count, bit))
        yield
        values = values + order.tie(got)
    order.mark(values)
    out.append(values)


def advance(*chains):
    for chain in chains:
        next(chain, None)


def finish(*chains):
    left = list(chains)
    while left:
        for chain in list(left):
            try:
                next(chain)
            except StopIteration:
                left.remove(chain)


def body(
    count,
    hidden,
    lengths,
    padding,
    bucket_line,
    bucket_horizontal,
    bucket_vertical,
    attn_project,
    attn_bias,
    table_line,
    table_horizontal,
    table_vertical,
    out_project,
    out_bias,
    attn_gain,
    attn_shift,
    hidden_project,
    hidden_bias,
    down_project,
    down_bias,
    final_gain,
    final_shift,
    cotangent,
):
    rows, slots, width = hidden.shape
    half = cotangent.shape[1]
    heads = table_line.shape[1]
    local = attn_project.shape[2]
    units = hidden_project.shape[1]
    part = units // 2
    factor = 1.0 / math.sqrt(local // heads)
    head = lax.axis_index("head")
    index = lax.axis_index("dp")
    core = index & 1
    offset = head * half
    every = list(range(count.bit_length() - 1))

    def split(values, dim):
        return [lax.dynamic_slice_in_dim(values, c * part, part, dim) for c in (core, 1 - core)]

    def joined(own_parts, got, dim):
        mine, rest = own_parts
        beside = lax.ppermute(got, "dp", flips(count, 0))
        return [jnp.concatenate([mine, got], axis=dim), jnp.concatenate([rest, beside], axis=dim)]

    side = (index >> 1) & 1
    down_mine = lax.dynamic_slice_in_dim(down_project, core * part + side * (part // 2), part // 2, 0)
    down_got = to_peer(down_mine)
    down_mine, hidden_project = lax.optimization_barrier((down_mine, hidden_project))
    up_mine = lax.dynamic_slice_in_dim(hidden_project, core * part, part, 1)
    up_got = to_peer(up_mine)
    up_mine, hidden, hidden_project, down_project = lax.optimization_barrier(
        (up_mine, hidden, hidden_project, down_project))
    bias_got = to_peer(hidden_bias)

    planes = jnp.concatenate([table_horizontal, table_vertical], axis=0)
    bins = table_line.shape[0] + planes.shape[0]
    lines = jnp.broadcast_to(table_line.T[:, :, None], (heads, table_line.shape[0], B))
    planes = jnp.broadcast_to(planes.T[:, None, :], (heads, PACK, planes.shape[0]))
    pad = padding[:, None, :]
    bucket_line, bucket_horizontal, bucket_vertical = (
        pltpu.with_memory_space_constraint(x, pltpu.HBM)
        for x in (bucket_line, bucket_horizontal, bucket_vertical))

    flat = hidden.reshape(rows * slots, width)
    query = ((times(flat, attn_project[0], 1, 0) + attn_bias[0].astype(f32)).astype(low)
             * jnp.asarray(factor, low))
    key = times(flat, attn_project[1], 1, 0).astype(low)
    value = (times(flat, attn_project[2], 1, 0) + attn_bias[1].astype(f32)).astype(low)
    query, key, value = (pltpu.with_memory_space_constraint(x.reshape(rows, slots, local), pltpu.HBM)
                         for x in (query, key, value))

    def own(values):
        return lax.dynamic_slice_in_dim(values, offset, half, 0)

    def others(values):
        return lax.dynamic_slice_in_dim(values, half - offset, half, 0)

    fronts, attn_sum, attn_got = [], [], []
    for r in range(rows):
        if r == 1:
            lengths, down_got = lax.optimization_barrier((lengths, down_got))
            down_beside = lax.ppermute(down_got, "dp", flips(count, 1))
        probs, context = attn_fwd(r, lengths, query, key, value, pad, bucket_line,
                                  bucket_horizontal, bucket_vertical, lines, planes)
        if r == 1:
            context, down_beside = lax.optimization_barrier((context, down_beside))
        fronts.append((probs, context))
        send = times(others(context), out_project, 1, 0).astype(low)
        got = to_peer(send)
        attn_sum.append(times(own(context), out_project, 1, 0))
        attn_got.append(got)
    (send, hidden_project, down_project, cotangent, norm_rows, out_bias, down_bias, hidden_bias, bias_got,
     hidden) = lax.optimization_barrier(
        (send, hidden_project, down_project, cotangent, (attn_gain, attn_shift, final_gain, final_shift),
         out_bias, down_bias, hidden_bias, bias_got, hidden))
    biases = [jnp.concatenate([x, y]) for x, y in zip(split(hidden_bias, 0), split(bias_got, 0))]
    gain_first, shift_first, gain_last, shift_last = (x.astype(f32) for x in norm_rows)
    up_parts = [up_mine, lax.dynamic_slice_in_dim(hidden_project, (1 - core) * part, part, 1)]
    down_parts = split(down_project, 0)
    up_got, down_beside, attn_got = lax.optimization_barrier((up_got, down_beside, attn_got))
    down_got = in_order(side, down_got, down_beside)
    ups = joined(up_parts, up_got, 1)
    downs = joined(down_parts, down_got.reshape(part, width), 0)
    attn_sum = [x + got.astype(f32) for x, got in zip(attn_sum, attn_got)]
    tokens = lax.dynamic_slice_in_dim(hidden, offset, half, 1).reshape(rows * half, width).astype(f32)
    normed, scale = normalize(tokens + jnp.concatenate(attn_sum, axis=0) + out_bias.astype(f32))
    mid = normed * gain_first + shift_first
    mid_low = mid.astype(low)

    actives, slopes = [], []
    total = None
    for up, down, bias in zip(ups, downs, biases):
        inner = times(mid_low, up, 1, 0) + bias.astype(f32)
        bell = 0.5 * (1.0 + lax.erf(inner * math.sqrt(0.5)))
        actives.append((inner * bell).astype(low))
        slope = bell + inner * (jnp.exp(-0.5 * inner * inner) * (1.0 / math.sqrt(2.0 * math.pi)))
        slopes.append(slope.astype(low))
        term = times(actives[-1], down, 1, 0)
        total = term if total is None else total + term
    normed_final, scale_final = normalize(mid + total + down_bias.astype(f32))
    output = (normed_final * gain_last + shift_last).astype(low).reshape(rows, half, width)

    above = cotangent.reshape(rows * half, width).astype(f32)
    g_final = normalize_back(above, normed_final, scale_final, gain_last)
    g_low = g_final.astype(low)
    order = Order()
    total = None
    inners = []
    for up, down, slope in zip(ups, downs, slopes):
        g_active = lax.optimization_barrier(times(g_low, down, 1, 1))
        g_inner = (g_active * slope.astype(f32)).astype(low)
        inners.append(g_inner)
        term = times(g_inner, up, 1, 1)
        total = term if total is None else total + term
    g_mid = g_final + total
    g_attn = normalize_back(g_mid, normed, scale, gain_first)
    g_attn_low = g_attn.astype(low).reshape(rows, half, width)
    g_others = [to_peer(g_attn_low[r]) for r in range(rows)]
    order.mark(g_attn_low)
    down_out, up_out, attn_out = [], [], []
    g_low = order.tie(g_low)
    kept, given = (times(active, g_low, 0, 0).astype(low) for active in actives)
    def down_part(values, c, start, size):
        at = [jnp.asarray(x, jnp.int32) for x in (c, start, 0)]
        return lax.dynamic_slice(values, at, (1, size, width)).reshape(size, width)

    def up_part(values, c, start, size):
        return lax.dynamic_slice(values, [jnp.asarray(x, jnp.int32) for x in (start, c * part)], (size, part))

    down_chain = unit_steps(order, *(x.reshape(2, part, width) for x in (kept, given)), count, 1,
                            down_part, down_out)
    advance(down_chain)
    mid_low = order.tie(mid_low)
    kept, given = (times(mid_low, g_inner, 0, 0).astype(low) for g_inner in inners)
    up_chain = unit_steps(order, kept, given, count, 0, up_part, up_out)
    advance(up_chain, down_chain)
    g_attn = g_attn.reshape(rows, half, width)

    marks, three, grad_out = [], None, 0.0
    for r in range(rows):
        probs, context = fronts[r]
        g_all = in_order(head, g_attn_low[r], order.tie(g_others[r])).reshape(slots, width)
        g_context = times(g_all, out_project, 1, 1).astype(low)
        g_scores, three = attn_bwd(r, factor, lengths, query, key, value, g_context, context, probs, three)
        order.mark(g_scores)
        marks.append(g_scores)
        grad_out = grad_out + times(context, g_all, 0, 0)
        advance(up_chain if r == 0 else down_chain)
    grad_attn = times(flat, three.reshape(rows * slots, 3 * local), 0, 0).astype(low)
    grad_out = jnp.concatenate([grad_out[:, :local], grad_out[:, local:]], axis=0).astype(low)
    attn_chain = buffer_steps(order, jnp.concatenate([grad_attn, grad_out], axis=1), count, attn_out)
    advance(attn_chain)
    every_project = jnp.concatenate([attn_project[c] for c in range(3)], axis=1)
    room = width // 2

    def pack():
        sums = [jnp.sum(x.reshape(rows * half, width), axis=0, keepdims=True) for x in
                (g_attn, g_mid * normed, g_mid, g_final, above * normed_final, above)]
        sums, units_in, three_sums, tables = order.tie(
            (sums, inners, jnp.sum(three.astype(f32).reshape(rows * slots, 3 * local), axis=0,
                                       keepdims=True), sum(tables_out)))
        unit_sums = [jnp.sum(x.astype(f32), axis=0, keepdims=True) for x in units_in]
        ours, others_ = (jnp.concatenate(arranged(core, *(x[:, c * part:(c + 1) * part] for x in unit_sums)),
                                         axis=0) for c in range(2))
        pair = jnp.concatenate([three_sums[:, :local], three_sums[:, 2 * local:]], axis=1)
        tables = jnp.pad(tables, ((0, 0), (0, room - bins)))
        return jnp.concatenate(
            sums + list(arranged(head, ours, others_))
            + [jnp.where(head == slot, pair, 0.0) for slot in range(2)]
            + [jnp.zeros((4, width), f32),
               jnp.concatenate([jnp.where(head == slot, tables, 0.0) for slot in range(2)], axis=1)], axis=0)

    tables_out, small_out = [], []
    blocks = [(r, block) for r in range(rows) for block in range(slots // B)]
    chains = {"D": down_chain, "U": up_chain, "A": attn_chain}
    for name in ORDER:
        if name == "T":
            r, block = blocks[len(tables_out)]
            tables_out.append(table_grads(r, block, order.tie(lengths), bucket_line,
                                          bucket_horizontal, bucket_vertical, marks[r]))
            order.mark(tables_out[-1])
        elif name == "G":
            three = order.tie(three)
            theirs = lax.dynamic_slice_in_dim(three, half - offset, half, 1)
            give = times(theirs.reshape(rows * half, 3 * local), every_project, 1, 1).astype(low)
            order.mark(give)
            received = to_peer(give)
            mine = lax.dynamic_slice_in_dim(three, offset, half, 1)
            mine = times(mine.reshape(rows * half, 3 * local), every_project, 1, 1)
        elif name == "P":
            chains["S"] = small_steps(order, pack(), count, small_out)
        else:
            advance(chains[name])
    finish(*chains.values())
    packed = small_out[0]
    grads_in = (mine + received.astype(f32)).reshape(rows, half, width) + g_attn
    grad_down = in_order(core, *down_out).reshape(down_project.shape).astype(f32)
    mine, other = up_out
    grad_up = jnp.concatenate(arranged(core, mine, other), axis=1).astype(f32)
    buffer = attn_out[0].astype(f32)
    grad_attn = jnp.stack([buffer[:, c * local:(c + 1) * local] for c in range(3)])
    grad_out = jnp.concatenate([buffer[:local, 3 * local:], buffer[local:, 3 * local:]], axis=1)

    rows_of = lambda at, size: lax.dynamic_slice_in_dim(packed, at, size, 0)
    grad_bias = rows_of(6 + 2 * head, 2).reshape(-1)
    grad_attn_bias = rows_of(10 + head, 1).reshape(2, local)
    marks = jnp.where(head == 0, packed[16:, :bins], packed[16:, room:room + bins])[:heads].T
    first, second = table_line.shape[0], table_horizontal.shape[0]
    return (
        output,
        grads_in,
        grad_attn,
        grad_attn_bias,
        marks[:first],
        marks[first:first + second],
        marks[first + second:],
        grad_out,
        packed[0],
        packed[1],
        packed[2],
        grad_up,
        grad_bias,
        grad_down,
        packed[3],
        packed[4],
        packed[5],
    )


def solution(mesh):
    return jax.shard_map(
        functools.partial(body, mesh.shape["dp"]),
        mesh=mesh,
        in_specs=(
            P("dp", None, None),
            P("dp", None),
            P("dp", None),
            P("dp", None, None),
            P("dp", None, None),
            P("dp", None, None),
            P(None, None, "head"),
            P(None, "head"),
            P(None, "head"),
            P(None, "head"),
            P(None, "head"),
            P("head", None),
            P(),
            P(),
            P(),
            P(None, "head"),
            P("head"),
            P("head", None),
            P(),
            P(),
            P(),
            P("dp", "head", None),
        ),
        out_specs=(
            P("dp", "head", None),
            P("dp", "head", None),
            P(None, None, "head"),
            P(None, "head"),
            P(None, "head"),
            P(None, "head"),
            P(None, "head"),
            P("head", None),
            P(),
            P(),
            P(),
            P(None, "head"),
            P("head"),
            P("head", None),
            P(),
            P(),
            P(),
        ),
        check_vma=False,
    )
```
